32 devices in a mesh: dp: 16 (over z, y, core), tensor: 2 (over x).
Axes of the slice: x: 2, y: 2, z: 4, core: 2. Of those that a mesh axis runs over, the one named last changes fastest.
Arguments:
- inputs: bfloat16 [4096, 1024], P('dp'), may hold values from -6 to 6
- qkv_weight: bfloat16 [2, 3, 1024, 1024], P(None, None, None, 'tensor'), may hold values from -0.1875 to 0.1875
- conv_taps: bfloat16 [2, 3, 4, 1024], P(None, None, None, 'tensor'), may hold values from -3 to 3
- beta_weight: bfloat16 [2, 1024, 8], P(None, None, 'tensor'), may hold values from -0.1875 to 0.1875
- out_gain: bfloat16 [2, 128], replicated, may hold values from 0.5 to 1.5
- out_weight: bfloat16 [2, 1024, 1024], P(None, 'tensor'), may hold values from -0.1875 to 0.1875
- norm_gain: bfloat16 [2, 2, 1024], replicated, may hold values from 0.5 to 1.5
- gate_up_weight: bfloat16 [2, 2, 1024, 2816], P(None, None, None, 'tensor'), may hold values from -0.1875 to 0.1875
- down_weight: bfloat16 [2, 2816, 1024], P(None, 'tensor'), may hold values from -0.109375 to 0.109375
- cotangent: bfloat16 [4096, 1024], P('dp'), may hold values from -6 to 6
Outputs:
- outputs: bfloat16 [4096, 1024], P('dp')
- input_grad: bfloat16 [4096, 1024], P('dp')
- grad_qkv: float32 [2, 3, 1024, 1024], P(None, None, None, 'tensor')
- grad_conv: float32 [2, 3, 4, 1024], P(None, None, None, 'tensor')
- grad_beta: float32 [2, 1024, 8], P(None, None, 'tensor')
- grad_out_gain: float32 [2, 128], replicated
- grad_out: float32 [2, 1024, 1024], P(None, 'tensor')
- grad_norm: float32 [2, 2, 1024], replicated
- grad_gate_up: float32 [2, 2, 1024, 2816], P(None, None, None, 'tensor')
- grad_down: float32 [2, 2816, 1024], P(None, 'tensor')
The draws below stay inside these ranges and needn't reach their ends.
All inputs are finite; a program needn't handle non-finite values.
Results may differ from the reference program's by a relative error of at most 0.033.
Values may be sent and summed in bfloat16 or wider, within the bound.
A program may use at most 384 MiB of HBM per device.

```python
import jax
import jax.numpy as jnp
from jax import lax

D = 1024
HEADS = 8
DK = 128
FF = 2816
KCONV = 4
SPAN = 64
LAYERS = 2
SEQ_LEN = 256
TOKENS = 4096
N_DP = 16


def shard_levels(stream_key, dims, split, low, largest):
    level, own = 1.0, jax.random.fold_in(stream_key, 6)
    for dim, parts in split:
        heights = jnp.exp(jax.random.uniform(jax.random.fold_in(own, dim), (parts,), jnp.float32, low / len(split), largest / len(split)))
        level = level * jnp.repeat(heights, dims[dim] // parts).reshape([-1 if axis == dim else 1 for axis in range(len(dims))])
    return level


def normal_values(stream_key, extent, width, reach, pieces=(), held_as=jnp.bfloat16):
    values = width * jax.random.normal(stream_key, extent, jnp.float32)
    if pieces:
        values = values * shard_levels(stream_key, extent, pieces, -0.22, 0.18)
    return jnp.clip(values, -reach, reach).astype(held_as)


def setup_inputs(seed: int = 0) -> dict:
    seeds = jax.random.split(jax.random.key(seed), 11)
    inputs = normal_values(seeds[0], (TOKENS, D), 1.0, 6.0, ((0, 16),))
    qkv_weight = normal_values(seeds[1], (LAYERS, 3, D, D), D ** -0.5, 0.1875, ((3, 2),))
    conv_taps = normal_values(seeds[2], (LAYERS, 3, KCONV, D), KCONV ** -0.5, 3.0, ((3, 2),))
    beta_weight = normal_values(seeds[3], (LAYERS, D, HEADS), D ** -0.5, 0.1875, ((2, 2),))
    out_gain = jnp.clip(1.0 + 0.1 * jax.random.normal(seeds[4], (LAYERS, DK), jnp.float32), 0.5, 1.5).astype(jnp.bfloat16)
    out_weight = normal_values(seeds[5], (LAYERS, D, D), D ** -0.5, 0.1875, ((1, 2),))
    norm_gain = jnp.clip(1.0 + 0.1 * jax.random.normal(seeds[6], (LAYERS, 2, D), jnp.float32), 0.5, 1.5).astype(jnp.bfloat16)
    gate_up_weight = normal_values(seeds[7], (LAYERS, 2, D, FF), D ** -0.5, 0.1875, ((3, 2),))
    down_weight = normal_values(seeds[8], (LAYERS, FF, D), FF ** -0.5, 0.109375, ((1, 2),))
    cotangent = normal_values(seeds[9], (TOKENS, D), 1.0, 6.0, ((0, 16),))
    return dict(inputs=inputs, qkv_weight=qkv_weight, conv_taps=conv_taps, beta_weight=beta_weight, out_gain=out_gain, out_weight=out_weight, norm_gain=norm_gain, gate_up_weight=gate_up_weight, down_weight=down_weight, cotangent=cotangent)


HIGHEST = lax.Precision.HIGHEST

@jax.custom_vjp
def low(v):
    return lax.optimization_barrier(v.astype(jnp.bfloat16)).astype(jnp.float32)

@jax.custom_vjp
def low_back(v):
    return v

def low_keep(v):
    return (low(v), None)

def low_pass(kept, grad):
    return (grad,)

def back_keep(v):
    return (v, None)

def back_low(kept, grad):
    return (low(grad),)
low.defvjp(low_keep, low_pass)
low_back.defvjp(back_keep, back_low)

def rms_norm(source, gain):
    return source * lax.rsqrt(lax.optimization_barrier(jnp.mean(source * source, axis=-1, keepdims=True)) + 1e-05) * gain

def head_norm(source, gain):
    return source * lax.rsqrt(lax.optimization_barrier(jnp.mean(source * source, axis=-1, keepdims=True)) + 0.01) * gain

def unit_heads(source):
    return source * lax.rsqrt(lax.optimization_barrier(jnp.sum(source * source, axis=-1, keepdims=True)) + 0.001)

def prepare(project, taps, logits):
    length = project.shape[1]
    padded = jnp.pad(project, ((0, 0), (KCONV - 1, 0), (0, 0)))
    conv_sum = taps[:, 0, None, :] * padded[:, 0:length, :]
    for offset in range(1, KCONV):
        conv_sum = conv_sum + taps[:, offset, None, :] * padded[:, offset:offset + length, :]
    active = jax.nn.silu(conv_sum)
    per_head = active.reshape(3, length, -1, DK)
    return (unit_heads(per_head[0]), unit_heads(per_head[1]), per_head[2], jax.nn.sigmoid(logits))

def delta_rule(query_vec, key_vec, value_vec, beta_gate):
    length, head_count, head_size = query_vec.shape
    num_blocks = length // SPAN

    def blocked(source):
        return source.reshape(num_blocks, SPAN, head_count, -1).transpose(0, 2, 1, 3)
    beta_blocks = beta_gate.reshape(num_blocks, SPAN, head_count).transpose(0, 2, 1)
    strict = jnp.tril(jnp.ones((SPAN, SPAN), jnp.float32), -1)
    inclusive = jnp.tril(jnp.ones((SPAN, SPAN), jnp.float32))
    identity = jnp.eye(SPAN, dtype=jnp.float32)

    def block_step(memory, block):
        query_blk, key_blk, value_blk, beta_blk = block
        key_gram = jnp.einsum('hid,hjd->hij', key_blk, key_blk, precision=HIGHEST)
        unit_lower = identity + strict * (beta_blk[:, :, None] * key_gram)
        right_side = jnp.concatenate([key_blk, value_blk], axis=-1) * beta_blk[:, :, None]
        solved = lax.linalg.triangular_solve(unit_lower, right_side, left_side=True, lower=True, unit_diagonal=True)
        key_mix = solved[..., :head_size]
        value_mix = solved[..., head_size:]
        new_values = value_mix - jnp.einsum('hcd,hde->hce', key_mix, memory, precision=HIGHEST)
        scores = jnp.einsum('hid,hjd->hij', query_blk, key_blk, precision=HIGHEST) * inclusive
        result = jnp.einsum('hid,hde->hie', query_blk, memory, precision=HIGHEST)
        result = result + jnp.einsum('hij,hje->hie', scores, new_values, precision=HIGHEST)
        memory = memory + jnp.einsum('hjd,hje->hde', key_blk, new_values, precision=HIGHEST)
        return (memory, result)
    start_state = jnp.zeros((head_count, head_size, head_size), jnp.float32)
    _, results = lax.scan(jax.checkpoint(block_step), start_state, (blocked(query_vec), blocked(key_vec), blocked(value_vec), beta_blocks))
    return results.transpose(0, 2, 1, 3).reshape(length, head_count, head_size)

def block_layer(residual, weights):
    qkv_w, taps, beta_w, head_gain, out_w, norm_gains, gate_up_w, down_w = weights
    length = residual.shape[0]
    normed = low(rms_norm(residual, norm_gains[0]))
    project = low_back(jnp.einsum('td,sdc->stc', normed, qkv_w, precision=HIGHEST))
    logits = low_back(jnp.dot(normed, beta_w, precision=HIGHEST))
    query_vec, key_vec, value_vec, beta_gate = prepare(project, taps, logits)
    mixer_out = delta_rule(low(query_vec), low(key_vec), low(value_vec), beta_gate)
    heads_out = low(head_norm(mixer_out, head_gain)).reshape(length, -1)
    hidden = residual + low_back(jnp.dot(heads_out, out_w, precision=HIGHEST))
    normed_two = low(rms_norm(hidden, norm_gains[1]))
    gate_up = low_back(jnp.einsum('td,sdf->stf', normed_two, gate_up_w, precision=HIGHEST))
    inner_act = low(jax.nn.silu(gate_up[0]) * gate_up[1])
    return hidden + low_back(jnp.dot(inner_act, down_w, precision=HIGHEST))

def model(source, params):
    residual = source
    for level in range(LAYERS):
        residual = block_layer(residual, tuple((table[level] for table in params)))
    return residual

def reference(inputs, qkv_weight, conv_taps, beta_weight, out_gain, out_weight, norm_gain, gate_up_weight, down_weight, cotangent):
    params = tuple((table.astype(jnp.float32) for table in (qkv_weight, conv_taps, beta_weight, out_gain, out_weight, norm_gain, gate_up_weight, down_weight)))
    group_in = inputs.astype(jnp.float32).reshape(N_DP, SEQ_LEN, D)
    group_co = cotangent.astype(jnp.float32).reshape(N_DP, SEQ_LEN, D)

    def one_group(totals, pair):
        seq_in, seq_co = pair
        result, pullback = jax.vjp(model, seq_in, params)
        grad_in, grad_params = pullback(seq_co)
        totals = tuple((first + second for first, second in zip(totals, grad_params)))
        return (totals, (result.astype(jnp.bfloat16), grad_in.astype(jnp.bfloat16)))
    zeros_start = tuple((jnp.zeros_like(table) for table in params))
    totals, (results, grads_in) = lax.scan(one_group, zeros_start, (group_in, group_co))
    return (results.reshape(TOKENS, D), grads_in.reshape(TOKENS, D), totals[0], totals[1], totals[2], totals[3], totals[4], totals[5], totals[6], totals[7])
```

```python
import functools
import math

import jax
import jax.numpy as jnp
from jax import lax
from jax.experimental import pallas as pl
from jax.experimental.pallas import tpu as pltpu
from jax.sharding import PartitionSpec as P

DK = 128
KCONV = 4
LAYERS = 2
LANES = 128
F32 = jnp.float32
BF16 = jnp.bfloat16
VMEM_LIMIT = 60 * 1024 * 1024


def dot_nn(a, b):
    return lax.dot_general(a, b, (((1,), (0,)), ((), ())), preferred_element_type=F32)


def dot_nt(a, b):
    return lax.dot_general(a, b, (((1,), (1,)), ((), ())), preferred_element_type=F32)


def dot_tn(a, b):
    return lax.dot_general(a, b, (((0,), (0,)), ((), ())), preferred_element_type=F32)


def halves(a):
    hi = a.astype(BF16)
    return hi, (a - hi.astype(F32)).astype(BF16)


def split_dot(dot, a, b):
    return dot(a[0], b[0]) + (dot(a[0], b[1]) + dot(a[1], b[0]))


def low(a):
    return a.astype(BF16)


def sigmoid(a):
    return 1.0 / (1.0 + jnp.exp(-a))


def rms_scale(a):
    return lax.rsqrt(jnp.mean(a * a, axis=-1, keepdims=True) + 1e-05)


def rms_back(hidden, gain, grad_normed):
    scale = rms_scale(hidden)
    weighted = gain * grad_normed
    inner = jnp.mean(hidden * weighted, axis=-1, keepdims=True)
    grad_hidden = scale * weighted - hidden * (scale * scale * scale) * inner
    rows = jnp.sum(grad_normed * hidden * scale, axis=0, keepdims=True)
    return grad_hidden, rows


def shift_down(a, count):
    if count == 0:
        return a
    row = lax.broadcasted_iota(jnp.int32, a.shape, 0)
    return jnp.where(row >= count, pltpu.roll(a, count, 0), 0.0)


def shift_up(a, count):
    if count == 0:
        return a
    length = a.shape[0]
    row = lax.broadcasted_iota(jnp.int32, a.shape, 0)
    return jnp.where(row < length - count, pltpu.roll(a, length - count, 0), 0.0)


def conv_silu(project, taps):
    total = taps[KCONV - 1 : KCONV, :] * project
    for tap in range(KCONV - 1):
        total = total + taps[tap : tap + 1, :] * shift_down(project, KCONV - 1 - tap)
    gate = sigmoid(total)
    return total, gate, total * gate


def positions(length):
    row = lax.broadcasted_iota(jnp.int32, (length, length), 0)
    col = lax.broadcasted_iota(jnp.int32, (length, length), 1)
    return row, col


def unit_lower_inverse(lower_list):
    length = lower_list[0].shape[0]
    row, col = positions(length)
    eye = jnp.where(row == col, 1.0, 0.0)
    diag_list = [jnp.where(row // 4 == col // 4, lower, 0.0) for lower in lower_list]
    parts = [halves(diag) for diag in diag_list]
    squares = [split_dot(dot_nn, part, part) for part in parts]
    firsts = [eye - diag for diag in diag_list]
    inverse = [
        first + split_dot(dot_nn, halves(first), halves(square))
        for first, square in zip(firsts, squares)
    ]
    size = 4
    while size < length:
        fresh = (row // (2 * size) == col // (2 * size)) & (row // size != col // size)
        offs = [halves(jnp.where(fresh, lower, 0.0)) for lower in lower_list]
        held = [halves(inv) for inv in inverse]
        mids = [split_dot(dot_nn, inv, off) for inv, off in zip(held, offs)]
        inverse = [
            inv - split_dot(dot_nn, halves(mid), part)
            for inv, mid, part in zip(inverse, mids, held)
        ]
        size = 2 * size
    return inverse


def head_cols(head):
    return slice(head * DK, (head + 1) * DK)


def mixer_forward_kernel(level, heads, n_add, *refs):
    (x_ref, *adds) = refs[: 1 + n_add]
    (gain_ref, taps_ref, head_gain_ref, wb_ref, wq_hbm, wo_hbm) = refs[1 + n_add : 7 + n_add]
    (x_out, n1_out, p_out, logit_out, t_out, u_out, o_out, on_out, part_out) = refs[
        7 + n_add : 16 + n_add
    ]
    wq, wo, sems = refs[16 + n_add :]
    loads = [
        pltpu.make_async_copy(wq_hbm.at[level], wq, sems.at[0]),
        pltpu.make_async_copy(wo_hbm.at[level], wo, sems.at[1]),
    ]
    for load in loads:
        load.start()
    x = x_ref[...].astype(F32)
    for add in adds:
        x = x + add[...].astype(F32)
    x_out[...] = x
    length = x.shape[0]
    n1 = low(x * rms_scale(x) * gain_ref[level, 0:1, :].astype(F32))
    n1_out[...] = n1
    logits = dot_nn(n1, wb_ref[level])
    logit_out[...] = logits
    beta = sigmoid(logits)
    loads[0].wait()
    acts = []
    for part in range(3):
        p = dot_nn(n1, wq[part])
        p_out[part] = p
        acts.append(conv_silu(p, taps_ref[level, part].astype(F32))[2])
    row, col = positions(length)
    lowers, scores, values = [], [], []
    for head in range(heads):
        cols = head_cols(head)
        c0, c1, c2 = (act[:, cols] for act in acts)
        q = low(c0 * lax.rsqrt(jnp.sum(c0 * c0, axis=-1, keepdims=True) + 0.001))
        k = low(c1 * lax.rsqrt(jnp.sum(c1 * c1, axis=-1, keepdims=True) + 0.001))
        v = low(c2).astype(F32)
        gate = beta[:, head : head + 1]
        lowers.append(jnp.where(row > col, gate * dot_nt(k, k), 0.0))
        scores.append(low(jnp.where(row >= col, dot_nt(q, k), 0.0)))
        values.append(halves(gate * v))
    inverse = unit_lower_inverse(lowers)
    head_gain = head_gain_ref[level : level + 1, :].astype(F32)
    for head in range(heads):
        cols = head_cols(head)
        t_hi, t_lo = halves(inverse[head])
        t_out[0, head] = t_hi
        t_out[1, head] = t_lo
        u = split_dot(dot_nn, (t_hi, t_lo), values[head])
        u_low = low(u)
        u_out[:, cols] = u_low
        o = dot_nn(scores[head], u_low)
        o_out[:, cols] = o
        scale = lax.rsqrt(jnp.mean(o * o, axis=-1, keepdims=True) + 0.01)
        on_out[:, cols] = low(o * scale * head_gain)
    loads[1].wait()
    part_out[...] = low(dot_nn(on_out[...], wo[...]))


def mixer_forward(level, x, adds, norm_gain, taps, head_gain, wb, wq, wo):
    length, width = x.shape
    chans = wq.shape[-1]
    heads = chans // DK
    sds = jax.ShapeDtypeStruct
    vmem = pl.BlockSpec(memory_space=pltpu.VMEM)
    hbm = pl.BlockSpec(memory_space=pl.ANY)
    return pl.pallas_call(
        functools.partial(mixer_forward_kernel, level, heads, len(adds)),
        out_shape=(
            sds((length, width), F32),
            sds((length, width), BF16),
            sds((3, length, chans), F32),
            sds((length, LANES), F32),
            sds((2, heads, length, length), BF16),
            sds((length, chans), BF16),
            sds((length, chans), F32),
            sds((length, chans), BF16),
            sds((length, width), BF16),
        ),
        in_specs=[vmem] * (5 + len(adds)) + [hbm, hbm],
        out_specs=(vmem,) * 9,
        scratch_shapes=[
            pltpu.VMEM((3, width, chans), BF16),
            pltpu.VMEM((chans, width), BF16),
            pltpu.SemaphoreType.DMA((2,)),
        ],
        compiler_params=pltpu.CompilerParams(vmem_limit_bytes=VMEM_LIMIT),
        name="mixer_forward",
    )(x, *adds, norm_gain, taps, head_gain, wb, wq, wo)


def mlp_forward_kernel(level, n_add, *refs):
    (x_ref, *adds) = refs[: 1 + n_add]
    (gain_ref, wgu_hbm, wd_hbm) = refs[1 + n_add : 4 + n_add]
    (h_out, n2_out, gu_out, z_out, part_out) = refs[4 + n_add : 9 + n_add]
    wgu, wd, sems = refs[9 + n_add :]
    loads = [
        pltpu.make_async_copy(wgu_hbm.at[level, 0], wgu.at[0], sems.at[0]),
        pltpu.make_async_copy(wgu_hbm.at[level, 1], wgu.at[1], sems.at[1]),
        pltpu.make_async_copy(wd_hbm.at[level], wd, sems.at[2]),
    ]
    for load in loads:
        load.start()
    h = x_ref[...].astype(F32)
    for add in adds:
        h = h + add[...].astype(F32)
    h_out[...] = h
    n2 = low(h * rms_scale(h) * gain_ref[level, 1:2, :].astype(F32))
    n2_out[...] = n2
    loads[0].wait()
    g = dot_nn(n2, wgu[0])
    gu_out[0] = g
    loads[1].wait()
    u = dot_nn(n2, wgu[1])
    gu_out[1] = u
    z = low(g * sigmoid(g) * u)
    z_out[...] = z
    loads[2].wait()
    part_out[...] = low(dot_nn(z, wd[...]))


def mlp_forward(level, x, adds, norm_gain, wgu, wd):
    length, width = x.shape
    hidden = wgu.shape[-1]
    sds = jax.ShapeDtypeStruct
    vmem = pl.BlockSpec(memory_space=pltpu.VMEM)
    hbm = pl.BlockSpec(memory_space=pl.ANY)
    return pl.pallas_call(
        functools.partial(mlp_forward_kernel, level, len(adds)),
        out_shape=(
            sds((length, width), F32),
            sds((length, width), BF16),
            sds((2, length, hidden), F32),
            sds((length, hidden), BF16),
            sds((length, width), BF16),
        ),
        in_specs=[vmem] * (2 + len(adds)) + [hbm, hbm],
        out_specs=(vmem,) * 5,
        scratch_shapes=[
            pltpu.VMEM((2, width, hidden), BF16),
            pltpu.VMEM((hidden, width), BF16),
            pltpu.SemaphoreType.DMA((3,)),
        ],
        compiler_params=pltpu.CompilerParams(vmem_limit_bytes=VMEM_LIMIT),
        name="mlp_forward",
    )(x, *adds, norm_gain, wgu, wd)


def back_through_norm(level, which, gain_ref, e_ref, hid_ref, adds, rows_out):
    e = e_ref[...].astype(F32)
    if not adds:
        rows_out[...] = jnp.zeros_like(rows_out)
        return e
    total = adds[0][...].astype(F32)
    for add in adds[1:]:
        total = total + add[...].astype(F32)
    gain = gain_ref[level, which : which + 1, :].astype(F32)
    grad_hidden, rows = rms_back(hid_ref[...], gain, total)
    rows_out[...] = rows
    return e + grad_hidden


def mlp_backward_kernel(level, n_add, *refs):
    (e_ref, hid_ref, *adds) = refs[: 2 + n_add]
    (gain_ref, n2_ref, gu_ref, z_ref, wgu_hbm, wd_hbm) = refs[2 + n_add : 8 + n_add]
    (e_out, rows_out, part_out, gd_out, ggu_out) = refs[8 + n_add : 13 + n_add]
    wgu, wd, dgu_ref, sems = refs[13 + n_add :]
    loads = [
        pltpu.make_async_copy(wd_hbm.at[level], wd, sems.at[0]),
        pltpu.make_async_copy(wgu_hbm.at[level], wgu, sems.at[1]),
    ]
    for load in loads:
        load.start()
    e = back_through_norm(level + 1, 0, gain_ref, e_ref, hid_ref, adds, rows_out)
    e_out[...] = e
    ef = low(e)
    loads[0].wait()
    dz = dot_nt(ef, wd[...])
    g, u = gu_ref[0], gu_ref[1]
    s = sigmoid(g)
    dgu_ref[0] = low(dz * u * (s * (1.0 + g * (1.0 - s))))
    dgu_ref[1] = low(dz * (g * s))
    loads[1].wait()
    part_out[...] = low(dot_nt(dgu_ref[0], wgu[0]) + dot_nt(dgu_ref[1], wgu[1]))
    gd_out[...] = low(dot_tn(z_ref[...], ef))
    for half in range(2):
        ggu_out[half] = low(dot_tn(n2_ref[...], dgu_ref[half]))


def mlp_backward(level, e, hid, adds, norm_gain, n2, gu, z, wgu, wd):
    length, width = e.shape
    hidden = wgu.shape[-1]
    sds = jax.ShapeDtypeStruct
    vmem = pl.BlockSpec(memory_space=pltpu.VMEM)
    hbm = pl.BlockSpec(memory_space=pl.ANY)
    return pl.pallas_call(
        functools.partial(mlp_backward_kernel, level, len(adds)),
        out_shape=(
            sds((length, width), F32),
            sds((1, width), F32),
            sds((length, width), BF16),
            sds((hidden, width), BF16),
            sds((2, width, hidden), BF16),
        ),
        in_specs=[vmem] * (6 + len(adds)) + [hbm, hbm],
        out_specs=(vmem,) * 5,
        scratch_shapes=[
            pltpu.VMEM((2, width, hidden), BF16),
            pltpu.VMEM((hidden, width), BF16),
            pltpu.VMEM((2, length, hidden), BF16),
            pltpu.SemaphoreType.DMA((2,)),
        ],
        compiler_params=pltpu.CompilerParams(vmem_limit_bytes=VMEM_LIMIT),
        name="mlp_backward",
    )(e, hid, *adds, norm_gain, n2, gu, z, wgu, wd)


def mixer_backward_kernel(level, heads, n_add, *refs):
    (e_ref, hid_ref, *adds) = refs[: 2 + n_add]
    (gain_ref, taps_ref, head_gain_ref, wb_ref, n1_ref, p_ref, logit_ref, t_ref, u_ref, o_ref) = (
        refs[2 + n_add : 12 + n_add]
    )
    (on_ref, wq_hbm, wo_hbm) = refs[12 + n_add : 15 + n_add]
    (e_out, rows_out, part_out, gq_out, gc_out, gb_out, gh_out, go_out) = refs[
        15 + n_add : 23 + n_add
    ]
    wq, wo, grads, dp_ref, sems = refs[23 + n_add :]
    loads = [
        pltpu.make_async_copy(wo_hbm.at[level], wo, sems.at[0]),
        pltpu.make_async_copy(wq_hbm.at[level], wq, sems.at[1]),
    ]
    for load in loads:
        load.start()
    e = back_through_norm(level, 1, gain_ref, e_ref, hid_ref, adds, rows_out)
    e_out[...] = e
    em = low(e)
    length = e.shape[0]
    loads[0].wait()
    don = dot_nt(em, wo[...])
    go_out[...] = low(dot_tn(on_ref[...], em))
    beta = sigmoid(logit_ref[...])
    row, col = positions(length)
    lane = lax.broadcasted_iota(jnp.int32, (length, LANES), 1)
    head_gain = head_gain_ref[level : level + 1, :].astype(F32)
    convs = [conv_silu(p_ref[part], taps_ref[level, part].astype(F32)) for part in range(3)]
    gain_rows = jnp.zeros((1, DK), F32)
    dlogit = jnp.zeros((length, LANES), F32)
    for head in range(heads):
        cols = head_cols(head)
        c0, c1, c2 = (conv[2][:, cols] for conv in convs)
        rho0 = lax.rsqrt(jnp.sum(c0 * c0, axis=-1, keepdims=True) + 0.001)
        rho1 = lax.rsqrt(jnp.sum(c1 * c1, axis=-1, keepdims=True) + 0.001)
        q, k, v = low(c0 * rho0), low(c1 * rho1), low(c2).astype(F32)
        gate = beta[:, head : head + 1]
        o = o_ref[:, cols]
        scale = lax.rsqrt(jnp.mean(o * o, axis=-1, keepdims=True) + 0.01)
        dn = don[:, cols]
        weighted = dn * head_gain
        inner = jnp.mean(o * weighted, axis=-1, keepdims=True)
        do = low(scale * weighted - o * (scale * scale * scale) * inner)
        gain_rows = gain_rows + jnp.sum(dn * o * scale, axis=0, keepdims=True)
        u = u_ref[:, cols]
        score_t = low(jnp.where(row <= col, dot_nt(k, q), 0.0))
        du = dot_nn(score_t, do)
        ds = low(jnp.where(row >= col, dot_nt(do, u), 0.0))
        ds_t = low(jnp.where(row <= col, dot_nt(u, do), 0.0))
        dq = dot_nn(ds, k)
        dk = dot_nn(ds_t, q)
        r = split_dot(dot_tn, (t_ref[0, head], t_ref[1, head]), halves(du))
        dv = gate * r
        dv_low = low(dv)
        gram = low(jnp.where(row > col, dot_nt(k, k), 0.0))
        w = v - dot_nn(gram, u)
        dbeta = jnp.sum(r * w, axis=-1, keepdims=True)
        dgram = jnp.where(row > col, dot_nt(dv_low, u), 0.0) + jnp.where(
            row < col, dot_nt(u, dv_low), 0.0
        )
        dk = dk - dot_nn(low(dgram), k)
        grads[0, :, cols] = rho0 * dq - c0 * (rho0 * rho0 * rho0) * jnp.sum(
            c0 * dq, axis=-1, keepdims=True
        )
        grads[1, :, cols] = rho1 * dk - c1 * (rho1 * rho1 * rho1) * jnp.sum(
            c1 * dk, axis=-1, keepdims=True
        )
        grads[2, :, cols] = dv
        dlogit = dlogit + jnp.where(lane == head, dbeta * gate * (1.0 - gate), 0.0)
    gh_out[...] = gain_rows
    dlogit_low = low(dlogit)
    n1 = n1_ref[...]
    gb_out[...] = dot_tn(n1, dlogit_low)
    for part in range(3):
        taps = taps_ref[level, part].astype(F32)
        total, gate, _ = convs[part]
        dsum = grads[part] * (gate * (1.0 + total * (1.0 - gate)))
        p = p_ref[part]
        dp = taps[KCONV - 1 : KCONV, :] * dsum
        for tap in range(KCONV):
            back = KCONV - 1 - tap
            gc_out[part, tap : tap + 1, :] = jnp.sum(
                dsum * shift_down(p, back), axis=0, keepdims=True
            )
            if back:
                dp = dp + taps[tap : tap + 1, :] * shift_up(dsum, back)
        dp_ref[part] = low(dp)
    loads[1].wait()
    dn1 = dot_nt(dlogit_low, wb_ref[level])
    for part in range(3):
        dn1 = dn1 + dot_nt(dp_ref[part], wq[part])
    part_out[...] = low(dn1)
    for part in range(3):
        gq_out[part] = low(dot_tn(n1, dp_ref[part]))


def mixer_backward(level, e, hid, adds, norm_gain, taps, head_gain, wb, kept, wq, wo):
    length, width = e.shape
    chans = wq.shape[-1]
    heads = chans // DK
    sds = jax.ShapeDtypeStruct
    vmem = pl.BlockSpec(memory_space=pltpu.VMEM)
    hbm = pl.BlockSpec(memory_space=pl.ANY)
    return pl.pallas_call(
        functools.partial(mixer_backward_kernel, level, heads, len(adds)),
        out_shape=(
            sds((length, width), F32),
            sds((1, width), F32),
            sds((length, width), BF16),
            sds((3, width, chans), BF16),
            sds((3, KCONV, chans), F32),
            sds((width, LANES), F32),
            sds((1, DK), F32),
            sds((chans, width), BF16),
        ),
        in_specs=[vmem] * (13 + len(adds)) + [hbm, hbm],
        out_specs=(vmem,) * 8,
        scratch_shapes=[
            pltpu.VMEM((3, width, chans), BF16),
            pltpu.VMEM((chans, width), BF16),
            pltpu.VMEM((3, length, chans), F32),
            pltpu.VMEM((3, length, chans), BF16),
            pltpu.SemaphoreType.DMA((2,)),
        ],
        compiler_params=pltpu.CompilerParams(vmem_limit_bytes=VMEM_LIMIT),
        name="mixer_backward",
    )(e, hid, *adds, norm_gain, taps, head_gain, wb, *kept, wq, wo)


def branch_parts(part):
    count = lax.axis_size("tensor")
    if count == 1:
        return (part,)
    if count == 2:
        return (part, lax.ppermute(part, "tensor", [(0, 1), (1, 0)]))
    return (lax.psum(part, "tensor"),)


def sum_over_dp(tables):
    shapes = [table.shape for table in tables]
    flat = jnp.concatenate([table.reshape(-1) for table in tables])
    size = flat.shape[0]
    count = lax.axis_size("dp")
    pad = -size % (count * 1024)
    flat = jnp.pad(flat, (0, pad))
    shard = lax.psum_scatter(flat, "dp", scatter_dimension=0, tiled=True)
    joined = lax.all_gather(shard, "dp", axis=0, tiled=True).astype(F32)
    pieces = []
    offset = 0
    for shape in shapes:
        size = math.prod(shape)
        pieces.append(joined[offset : offset + size].reshape(shape))
        offset = offset + size
    return pieces


def body(
    inputs,
    qkv_weight,
    conv_taps,
    beta_weight,
    out_gain,
    out_weight,
    norm_gain,
    gate_up_weight,
    down_weight,
    cotangent,
):
    heads = beta_weight.shape[-1]
    wb = jnp.pad(beta_weight, ((0, 0), (0, 0), (0, LANES - heads)))
    base, adds = inputs, ()
    kept = []
    for level in range(LAYERS):
        x, n1, p, logits, t, u, o, on, part = mixer_forward(
            level, base, adds, norm_gain, conv_taps, out_gain, wb, qkv_weight, out_weight
        )
        h, n2, gu, z, part_two = mlp_forward(
            level, x, branch_parts(part), norm_gain, gate_up_weight, down_weight
        )
        kept.append((x, h, (n1, p, logits, t, u, o, on), (n2, gu, z)))
        base, adds = h, branch_parts(part_two)
    total = base
    for add in adds:
        total = total + add.astype(F32)
    outputs = total.astype(BF16)

    e, hid, adds = cotangent, kept[-1][0], ()
    gain_rows = {}
    small = [None] * LAYERS
    big = [None] * LAYERS
    for level in reversed(range(LAYERS)):
        x, h, mixer_kept, mlp_kept = kept[level]
        e, rows, part, grad_down, grad_gate_up = mlp_backward(
            level, e, hid, adds, norm_gain, *mlp_kept, gate_up_weight, down_weight
        )
        gain_rows[(level + 1, 0)] = rows
        e, rows, part, grad_qkv, grad_conv, grad_beta, head_rows, grad_out = mixer_backward(
            level,
            e,
            h,
            branch_parts(part),
            norm_gain,
            conv_taps,
            out_gain,
            wb,
            mixer_kept,
            qkv_weight,
            out_weight,
        )
        gain_rows[(level, 1)] = rows
        hid, adds = x, branch_parts(part)
        small[level] = (grad_conv, grad_beta[:, :heads], head_rows[0])
        big[level] = (grad_qkv, grad_out, grad_gate_up, grad_down)
    branch = adds[0].astype(F32)
    for add in adds[1:]:
        branch = branch + add.astype(F32)
    grad_hidden, rows = rms_back(hid, norm_gain[0, 0:1].astype(F32), branch)
    gain_rows[(0, 0)] = rows
    input_grad = (e + grad_hidden).astype(BF16)

    norm_rows = jnp.stack(
        [jnp.concatenate([gain_rows[(level, 0)], gain_rows[(level, 1)]]) for level in range(LAYERS)]
    )
    norm_rows = norm_rows / lax.axis_size("tensor")
    grad_norm, grad_out_gain = lax.psum(
        (norm_rows, jnp.stack([group[2] for group in small])), ("dp", "tensor")
    )
    grad_conv, grad_beta = lax.psum(
        (jnp.stack([group[0] for group in small]), jnp.stack([group[1] for group in small])), "dp"
    )
    sums = [sum_over_dp(big[level]) for level in range(LAYERS)]
    grad_qkv, grad_out, grad_gate_up, grad_down = (
        jnp.stack([sums[level][index] for level in range(LAYERS)]) for index in range(4)
    )
    return (
        outputs,
        input_grad,
        grad_qkv,
        grad_conv,
        grad_beta,
        grad_out_gain,
        grad_out,
        grad_norm,
        grad_gate_up,
        grad_down,
    )


def solution(mesh):
    in_specs = (
        P("dp", None),
        P(None, None, None, "tensor"),
        P(None, None, None, "tensor"),
        P(None, None, "tensor"),
        P(),
        P(None, "tensor", None),
        P(),
        P(None, None, None, "tensor"),
        P(None, "tensor", None),
        P("dp", None),
    )
    out_specs = (
        P("dp", None),
        P("dp", None),
        P(None, None, None, "tensor"),
        P(None, None, None, "tensor"),
        P(None, None, "tensor"),
        P(),
        P(None, "tensor", None),
        P(),
        P(None, None, None, "tensor"),
        P(None, "tensor", None),
    )
    return jax.shard_map(body, mesh=mesh, in_specs=in_specs, out_specs=out_specs, check_vma=False)
```

```python
import functools
import math

import jax
import jax.numpy as jnp
from jax import lax
from jax.experimental import pallas as pl
from jax.experimental.pallas import tpu as pltpu
from jax.sharding import PartitionSpec as P

DK = 128
KCONV = 4
LAYERS = 2
LANES = 128
SIDE = 512
F32 = jnp.float32
BF16 = jnp.bfloat16
VMEM_LIMIT = 60 * 1024 * 1024


def dot_nn(a, b):
    return lax.dot_general(a, b, (((1,), (0,)), ((), ())), preferred_element_type=F32)


def dot_nt(a, b):
    return lax.dot_general(a, b, (((1,), (1,)), ((), ())), preferred_element_type=F32)


def dot_tn(a, b):
    return lax.dot_general(a, b, (((0,), (0,)), ((), ())), preferred_element_type=F32)


def halves(a):
    hi = a.astype(BF16)
    return hi, (a - hi.astype(F32)).astype(BF16)


def split_dot(dot, a, b):
    return dot(a[0], b[0]) + (dot(a[0], b[1]) + dot(a[1], b[0]))


def low(a):
    return a.astype(BF16)


def sigmoid(a):
    return 1.0 / (1.0 + jnp.exp(-a))


def rms_scale(a):
    return lax.rsqrt(jnp.mean(a * a, axis=-1, keepdims=True) + 1e-05)


def rms_back(hidden, gain, grad_normed):
    scale = rms_scale(hidden)
    weighted = gain * grad_normed
    inner = jnp.mean(hidden * weighted, axis=-1, keepdims=True)
    grad_hidden = scale * weighted - hidden * (scale * scale * scale) * inner
    rows = jnp.sum(grad_normed * hidden * scale, axis=0, keepdims=True)
    return grad_hidden, rows


def shift_down(a, count):
    if count == 0:
        return a
    row = lax.broadcasted_iota(jnp.int32, a.shape, 0)
    return jnp.where(row >= count, pltpu.roll(a, count, 0), 0.0)


def shift_up(a, count):
    if count == 0:
        return a
    length = a.shape[0]
    row = lax.broadcasted_iota(jnp.int32, a.shape, 0)
    return jnp.where(row < length - count, pltpu.roll(a, length - count, 0), 0.0)


def conv_silu(project, taps):
    total = taps[KCONV - 1 : KCONV, :] * project
    for tap in range(KCONV - 1):
        total = total + taps[tap : tap + 1, :] * shift_down(project, KCONV - 1 - tap)
    gate = sigmoid(total)
    return total, gate, total * gate


def positions(length):
    row = lax.broadcasted_iota(jnp.int32, (length, length), 0)
    col = lax.broadcasted_iota(jnp.int32, (length, length), 1)
    return row, col


def unit_lower_inverse(lower_list):
    length = lower_list[0].shape[0]
    row, col = positions(length)
    eye = jnp.where(row == col, 1.0, 0.0)
    diag_list = [jnp.where(row // 4 == col // 4, lower, 0.0) for lower in lower_list]
    parts = [halves(diag) for diag in diag_list]
    squares = [split_dot(dot_nn, part, part) for part in parts]
    firsts = [eye - diag for diag in diag_list]
    inverse = [
        first + split_dot(dot_nn, halves(first), halves(square))
        for first, square in zip(firsts, squares)
    ]
    size = 4
    while size < length:
        fresh = (row // (2 * size) == col // (2 * size)) & (row // size != col // size)
        offs = [halves(jnp.where(fresh, lower, 0.0)) for lower in lower_list]
        held = [halves(inv) for inv in inverse]
        mids = [split_dot(dot_nn, inv, off) for inv, off in zip(held, offs)]
        inverse = [
            inv - split_dot(dot_nn, halves(mid), part)
            for inv, mid, part in zip(inverse, mids, held)
        ]
        size = 2 * size
    return inverse


def head_cols(head):
    return slice(head * DK, (head + 1) * DK)


def mixer_forward_kernel(level, heads, n_add, *refs):
    (x_ref, *adds) = refs[: 1 + n_add]
    (gain_ref, taps_ref, head_gain_ref, wb_ref, wq_hbm, wo_hbm) = refs[1 + n_add : 7 + n_add]
    (x_out, n1_out, p_out, logit_out, t_out, u_out, o_out, on_out, part_out) = refs[
        7 + n_add : 16 + n_add
    ]
    wq, wo, sems = refs[16 + n_add :]
    loads = [
        pltpu.make_async_copy(wq_hbm.at[level], wq, sems.at[0]),
        pltpu.make_async_copy(wo_hbm.at[level], wo, sems.at[1]),
    ]
    for load in loads:
        load.start()
    x = x_ref[...].astype(F32)
    for add in adds:
        x = x + add[...].astype(F32)
    x_out[...] = x
    length = x.shape[0]
    n1 = low(x * rms_scale(x) * gain_ref[level, 0:1, :].astype(F32))
    n1_out[...] = n1
    logits = dot_nn(n1, wb_ref[level])
    logit_out[...] = logits
    beta = sigmoid(logits)
    loads[0].wait()
    acts = []
    for part in range(3):
        p = dot_nn(n1, wq[part])
        p_out[part] = p
        acts.append(conv_silu(p, taps_ref[level, part].astype(F32))[2])
    row, col = positions(length)
    lowers, scores, values = [], [], []
    for head in range(heads):
        cols = head_cols(head)
        c0, c1, c2 = (act[:, cols] for act in acts)
        q = low(c0 * lax.rsqrt(jnp.sum(c0 * c0, axis=-1, keepdims=True) + 0.001))
        k = low(c1 * lax.rsqrt(jnp.sum(c1 * c1, axis=-1, keepdims=True) + 0.001))
        v = low(c2).astype(F32)
        gate = beta[:, head : head + 1]
        lowers.append(jnp.where(row > col, gate * dot_nt(k, k), 0.0))
        scores.append(low(jnp.where(row >= col, dot_nt(q, k), 0.0)))
        values.append(halves(gate * v))
    inverse = unit_lower_inverse(lowers)
    head_gain = head_gain_ref[level : level + 1, :].astype(F32)
    for head in range(heads):
        cols = head_cols(head)
        t_hi, t_lo = halves(inverse[head])
        t_out[0, head] = t_hi
        t_out[1, head] = t_lo
        u = split_dot(dot_nn, (t_hi, t_lo), values[head])
        u_low = low(u)
        u_out[:, cols] = u_low
        o = dot_nn(scores[head], u_low)
        o_out[:, cols] = o
        scale = lax.rsqrt(jnp.mean(o * o, axis=-1, keepdims=True) + 0.01)
        on_out[:, cols] = low(o * scale * head_gain)
    loads[1].wait()
    part_out[...] = low(dot_nn(on_out[...], wo[...]))


def mixer_forward(level, x, adds, norm_gain, taps, head_gain, wb, wq, wo):
    length, width = x.shape
    chans = wq.shape[-1]
    heads = chans // DK
    sds = jax.ShapeDtypeStruct
    vmem = pl.BlockSpec(memory_space=pltpu.VMEM)
    hbm = pl.BlockSpec(memory_space=pl.ANY)
    return pl.pallas_call(
        functools.partial(mixer_forward_kernel, level, heads, len(adds)),
        out_shape=(
            sds((length, width), F32),
            sds((length, width), BF16),
            sds((3, length, chans), F32),
            sds((length, LANES), F32),
            sds((2, heads, length, length), BF16),
            sds((length, chans), BF16),
            sds((length, chans), F32),
            sds((length, chans), BF16),
            sds((length, width), BF16),
        ),
        in_specs=[vmem] * (5 + len(adds)) + [hbm, hbm],
        out_specs=(vmem,) * 9,
        scratch_shapes=[
            pltpu.VMEM((3, width, chans), BF16),
            pltpu.VMEM((chans, width), BF16),
            pltpu.SemaphoreType.DMA((2,)),
        ],
        compiler_params=pltpu.CompilerParams(vmem_limit_bytes=VMEM_LIMIT),
        name="mixer_forward",
    )(x, *adds, norm_gain, taps, head_gain, wb, wq, wo)


def mlp_forward_kernel(level, n_add, *refs):
    (x_ref, *adds) = refs[: 1 + n_add]
    (gain_ref, wgu_hbm, wd_hbm) = refs[1 + n_add : 4 + n_add]
    (h_out, n2_out, gu_out, z_out, part_out) = refs[4 + n_add : 9 + n_add]
    wgu, wd, sems = refs[9 + n_add :]
    loads = [
        pltpu.make_async_copy(wgu_hbm.at[level, 0], wgu.at[0], sems.at[0]),
        pltpu.make_async_copy(wgu_hbm.at[level, 1], wgu.at[1], sems.at[1]),
        pltpu.make_async_copy(wd_hbm.at[level], wd, sems.at[2]),
    ]
    for load in loads:
        load.start()
    h = x_ref[...].astype(F32)
    for add in adds:
        h = h + add[...].astype(F32)
    h_out[...] = h
    n2 = low(h * rms_scale(h) * gain_ref[level, 1:2, :].astype(F32))
    n2_out[...] = n2
    loads[0].wait()
    g = dot_nn(n2, wgu[0])
    gu_out[0] = g
    loads[1].wait()
    u = dot_nn(n2, wgu[1])
    gu_out[1] = u
    z = low(g * sigmoid(g) * u)
    z_out[...] = z
    loads[2].wait()
    part_out[...] = low(dot_nn(z, wd[...]))


def mlp_forward(level, x, adds, norm_gain, wgu, wd):
    length, width = x.shape
    hidden = wgu.shape[-1]
    sds = jax.ShapeDtypeStruct
    vmem = pl.BlockSpec(memory_space=pltpu.VMEM)
    hbm = pl.BlockSpec(memory_space=pl.ANY)
    return pl.pallas_call(
        functools.partial(mlp_forward_kernel, level, len(adds)),
        out_shape=(
            sds((length, width), F32),
            sds((length, width), BF16),
            sds((2, length, hidden), F32),
            sds((length, hidden), BF16),
            sds((length, width), BF16),
        ),
        in_specs=[vmem] * (2 + len(adds)) + [hbm, hbm],
        out_specs=(vmem,) * 5,
        scratch_shapes=[
            pltpu.VMEM((2, width, hidden), BF16),
            pltpu.VMEM((hidden, width), BF16),
            pltpu.SemaphoreType.DMA((3,)),
        ],
        compiler_params=pltpu.CompilerParams(vmem_limit_bytes=VMEM_LIMIT),
        name="mlp_forward",
    )(x, *adds, norm_gain, wgu, wd)


def back_through_norm(level, which, gain_ref, e_ref, hid_ref, adds, rows_out):
    e = e_ref[...].astype(F32)
    if not adds:
        rows_out[...] = jnp.zeros_like(rows_out)
        return e
    total = adds[0][...].astype(F32)
    for add in adds[1:]:
        total = total + add[...].astype(F32)
    gain = gain_ref[level, which : which + 1, :].astype(F32)
    grad_hidden, rows = rms_back(hid_ref[...], gain, total)
    rows_out[...] = rows
    return e + grad_hidden


def mlp_backward_kernel(level, n_add, *refs):
    (e_ref, hid_ref, *adds) = refs[: 2 + n_add]
    (gain_ref, n2_ref, gu_ref, z_ref, wgu_hbm, wd_hbm) = refs[2 + n_add : 8 + n_add]
    (e_out, rows_out, part_out, gd_out, ggu_out) = refs[8 + n_add : 13 + n_add]
    wgu, wd, dgu_ref, sems = refs[13 + n_add :]
    loads = [
        pltpu.make_async_copy(wd_hbm.at[level], wd, sems.at[0]),
        pltpu.make_async_copy(wgu_hbm.at[level], wgu, sems.at[1]),
    ]
    for load in loads:
        load.start()
    e = back_through_norm(level + 1, 0, gain_ref, e_ref, hid_ref, adds, rows_out)
    e_out[...] = e
    ef = low(e)
    loads[0].wait()
    dz = dot_nt(ef, wd[...])
    g, u = gu_ref[0], gu_ref[1]
    s = sigmoid(g)
    dgu_ref[0] = low(dz * u * (s * (1.0 + g * (1.0 - s))))
    dgu_ref[1] = low(dz * (g * s))
    loads[1].wait()
    part_out[...] = low(dot_nt(dgu_ref[0], wgu[0]) + dot_nt(dgu_ref[1], wgu[1]))
    gd_out[...] = low(dot_tn(z_ref[...], ef))
    for half in range(2):
        ggu_out[half] = low(dot_tn(n2_ref[...], dgu_ref[half]))


def mlp_backward(level, e, hid, adds, norm_gain, n2, gu, z, wgu, wd):
    length, width = e.shape
    hidden = wgu.shape[-1]
    sds = jax.ShapeDtypeStruct
    vmem = pl.BlockSpec(memory_space=pltpu.VMEM)
    hbm = pl.BlockSpec(memory_space=pl.ANY)
    return pl.pallas_call(
        functools.partial(mlp_backward_kernel, level, len(adds)),
        out_shape=(
            sds((length, width), F32),
            sds((1, width), F32),
            sds((length, width), BF16),
            sds((hidden, width), BF16),
            sds((2, width, hidden), BF16),
        ),
        in_specs=[vmem] * (6 + len(adds)) + [hbm, hbm],
        out_specs=(vmem,) * 5,
        scratch_shapes=[
            pltpu.VMEM((2, width, hidden), BF16),
            pltpu.VMEM((hidden, width), BF16),
            pltpu.VMEM((2, length, hidden), BF16),
            pltpu.SemaphoreType.DMA((2,)),
        ],
        compiler_params=pltpu.CompilerParams(vmem_limit_bytes=VMEM_LIMIT),
        name="mlp_backward",
    )(e, hid, *adds, norm_gain, n2, gu, z, wgu, wd)


def mixer_backward_kernel(level, heads, n_add, *refs):
    (e_ref, hid_ref, *adds) = refs[: 2 + n_add]
    (gain_ref, taps_ref, head_gain_ref, wb_ref, n1_ref, p_ref, logit_ref, t_ref, u_ref, o_ref) = (
        refs[2 + n_add : 12 + n_add]
    )
    (on_ref, wq_hbm, wo_hbm) = refs[12 + n_add : 15 + n_add]
    (e_out, part_out, small_out, gq_out, go_out) = refs[15 + n_add : 20 + n_add]
    wq, wo, grads, dp_ref, rows_out, sems = refs[20 + n_add :]
    loads = [
        pltpu.make_async_copy(wo_hbm.at[level], wo, sems.at[0]),
        pltpu.make_async_copy(wq_hbm.at[level], wq, sems.at[1]),
    ]
    for load in loads:
        load.start()
    e = back_through_norm(level, 1, gain_ref, e_ref, hid_ref, adds, rows_out)
    e_out[...] = e
    em = low(e)
    length = e.shape[0]
    loads[0].wait()
    don = dot_nt(em, wo[...])
    go_out[...] = low(dot_tn(on_ref[...], em))
    beta = sigmoid(logit_ref[...])
    row, col = positions(length)
    lane = lax.broadcasted_iota(jnp.int32, (length, LANES), 1)
    head_gain = head_gain_ref[level : level + 1, :].astype(F32)
    convs = [conv_silu(p_ref[part], taps_ref[level, part].astype(F32)) for part in range(3)]
    gain_rows = jnp.zeros((1, DK), F32)
    dlogit = jnp.zeros((length, LANES), F32)
    for head in range(heads):
        cols = head_cols(head)
        c0, c1, c2 = (conv[2][:, cols] for conv in convs)
        rho0 = lax.rsqrt(jnp.sum(c0 * c0, axis=-1, keepdims=True) + 0.001)
        rho1 = lax.rsqrt(jnp.sum(c1 * c1, axis=-1, keepdims=True) + 0.001)
        q, k, v = low(c0 * rho0), low(c1 * rho1), low(c2).astype(F32)
        gate = beta[:, head : head + 1]
        o = o_ref[:, cols]
        scale = lax.rsqrt(jnp.mean(o * o, axis=-1, keepdims=True) + 0.01)
        dn = don[:, cols]
        weighted = dn * head_gain
        inner = jnp.mean(o * weighted, axis=-1, keepdims=True)
        do = low(scale * weighted - o * (scale * scale * scale) * inner)
        gain_rows = gain_rows + jnp.sum(dn * o * scale, axis=0, keepdims=True)
        u = u_ref[:, cols]
        score_t = low(jnp.where(row <= col, dot_nt(k, q), 0.0))
        du = dot_nn(score_t, do)
        ds = low(jnp.where(row >= col, dot_nt(do, u), 0.0))
        ds_t = low(jnp.where(row <= col, dot_nt(u, do), 0.0))
        dq = dot_nn(ds, k)
        dk = dot_nn(ds_t, q)
        r = split_dot(dot_tn, (t_ref[0, head], t_ref[1, head]), halves(du))
        dv = gate * r
        dv_low = low(dv)
        gram = low(jnp.where(row > col, dot_nt(k, k), 0.0))
        w = v - dot_nn(gram, u)
        dbeta = jnp.sum(r * w, axis=-1, keepdims=True)
        dgram = jnp.where(row > col, dot_nt(dv_low, u), 0.0) + jnp.where(
            row < col, dot_nt(u, dv_low), 0.0
        )
        dk = dk - dot_nn(low(dgram), k)
        grads[0, :, cols] = rho0 * dq - c0 * (rho0 * rho0 * rho0) * jnp.sum(
            c0 * dq, axis=-1, keepdims=True
        )
        grads[1, :, cols] = rho1 * dk - c1 * (rho1 * rho1 * rho1) * jnp.sum(
            c1 * dk, axis=-1, keepdims=True
        )
        grads[2, :, cols] = dv
        dlogit = dlogit + jnp.where(lane == head, dbeta * gate * (1.0 - gate), 0.0)
    chans = grads.shape[-1]
    small_out[...] = jnp.zeros_like(small_out)
    small_out[0:1, SIDE : SIDE + DK] = gain_rows
    half = rows_out.shape[-1] // 2
    small_out[1:2, SIDE:] = rows_out[:, :half]
    small_out[2:3, SIDE:] = rows_out[:, half:]
    dlogit_low = low(dlogit)
    n1 = n1_ref[...]
    small_out[3 * KCONV : 3 * KCONV + heads, :] = dot_tn(dlogit_low, n1)[:heads, :]
    for part in range(3):
        taps = taps_ref[level, part].astype(F32)
        total, gate, _ = convs[part]
        dsum = grads[part] * (gate * (1.0 + total * (1.0 - gate)))
        p = p_ref[part]
        dp = taps[KCONV - 1 : KCONV, :] * dsum
        for tap in range(KCONV):
            back = KCONV - 1 - tap
            spot = part * KCONV + tap
            small_out[spot : spot + 1, :chans] = jnp.sum(
                dsum * shift_down(p, back), axis=0, keepdims=True
            )
            if back:
                dp = dp + taps[tap : tap + 1, :] * shift_up(dsum, back)
        dp_ref[part] = low(dp)
    loads[1].wait()
    dn1 = dot_nt(dlogit_low, wb_ref[level])
    for part in range(3):
        dn1 = dn1 + dot_nt(dp_ref[part], wq[part])
    part_out[...] = low(dn1)
    for part in range(3):
        gq_out[part] = low(dot_tn(n1, dp_ref[part]))


def mixer_backward(level, e, hid, adds, norm_gain, taps, head_gain, wb, kept, wq, wo):
    length, width = e.shape
    chans = wq.shape[-1]
    heads = chans // DK
    sds = jax.ShapeDtypeStruct
    vmem = pl.BlockSpec(memory_space=pltpu.VMEM)
    hbm = pl.BlockSpec(memory_space=pl.ANY)
    return pl.pallas_call(
        functools.partial(mixer_backward_kernel, level, heads, len(adds)),
        out_shape=(
            sds((length, width), F32),
            sds((length, width), BF16),
            sds((16, width), F32),
            sds((3, width, chans), BF16),
            sds((chans, width), BF16),
        ),
        in_specs=[vmem] * (13 + len(adds)) + [hbm, hbm],
        out_specs=(vmem,) * 5,
        scratch_shapes=[
            pltpu.VMEM((3, width, chans), BF16),
            pltpu.VMEM((chans, width), BF16),
            pltpu.VMEM((3, length, chans), F32),
            pltpu.VMEM((3, length, chans), BF16),
            pltpu.VMEM((1, width), F32),
            pltpu.SemaphoreType.DMA((2,)),
        ],
        compiler_params=pltpu.CompilerParams(vmem_limit_bytes=VMEM_LIMIT),
        name="mixer_backward",
    )(e, hid, *adds, norm_gain, taps, head_gain, wb, *kept, wq, wo)


def branch_parts(part):
    count = lax.axis_size("tensor")
    if count == 1:
        return (part,)
    if count == 2:
        return (part, lax.ppermute(part, "tensor", [(0, 1), (1, 0)]))
    return (lax.psum(part, "tensor"),)


def sum_over_dp(tables):
    shapes = [table.shape for table in tables]
    flat = jnp.concatenate([table.reshape(-1) for table in tables])
    size = flat.shape[0]
    count = lax.axis_size("dp")
    pad = -size % (count * 1024)
    flat = jnp.pad(flat, (0, pad))
    shard = lax.psum_scatter(flat, "dp", scatter_dimension=0, tiled=True)
    joined = lax.all_gather(shard, "dp", axis=0, tiled=True)
    pieces = []
    offset = 0
    for shape in shapes:
        size = math.prod(shape)
        pieces.append(joined[offset : offset + size].reshape(shape))
        offset = offset + size
    return pieces


def ring_place(n_dp):
    spot = lax.axis_index("dp")
    core = lax.rem(spot, 2)
    side = lax.rem(lax.div(spot, 2), 2)
    depth = lax.div(spot, 4)
    length = n_dp // 2
    return core, depth + side * (length - 1 - 2 * depth), length


def ring_spot(place, core, length):
    side = lax.div(place, length // 2)
    depth = place + side * (length - 1 - 2 * place)
    return (depth * 2 + side) * 2 + core


def ring_kernel(n_dp, kinds, *refs):
    count = len(kinds)
    given = refs[:count]
    total = refs[count : 2 * count]
    own = refs[2 * count : 3 * count]
    peer = refs[3 * count : 4 * count]
    slots = refs[4 * count : 5 * count]
    load_sem, core_sems, send_sems, recv_sems, fan_sems, keep_sem = refs[5 * count :]
    core, place, length = ring_place(n_dp)
    partner = {"dp": ring_spot(place, 1 - core, length)}
    places = [lax.rem(place + 1, length), lax.rem(place + length - 1, length)]
    nexts = [{"dp": ring_spot(spot, core, length)} for spot in places]
    streams = [(index, way) for index in range(count) for way in range(2)]

    def share(ref, index, half):
        kind = kinds[index]
        if kind == "rows":
            return ref.at[:, half]
        if kind == "cols":
            wide = ref.shape[-1] // 2
            return ref.at[:, :, pl.ds(pl.multiple_of(half * wide, LANES), wide)]
        return ref.at[half]

    def piece(ref, index, chunk, way):
        kind = kinds[index]
        if kind == "rows":
            high = ref.shape[1] // 2
            return ref.at[chunk, way * high : (way + 1) * high]
        if kind == "cols":
            wide = ref.shape[-1] // 2
            return ref.at[chunk, :, way * wide : (way + 1) * wide]
        return ref.at[way, :, pl.ds(pl.multiple_of(chunk * LANES, LANES), LANES)]

    def spot_of(ref, index, half, chunk, way):
        kind = kinds[index]
        if kind == "rows":
            high = ref.shape[2] // 2
            return ref.at[chunk, half, way * high : (way + 1) * high]
        if kind == "cols":
            wide = ref.shape[-1] // 4
            start = pl.multiple_of(half * (2 * wide) + way * wide, LANES)
            return ref.at[chunk, :, pl.ds(start, wide)]
        return ref.at[half, way, :, pl.ds(pl.multiple_of(chunk * LANES, LANES), LANES)]

    def turned(way, steps):
        if way == 0:
            return lax.rem(place + 2 * length - steps, length)
        return lax.rem(place + steps + length, length)

    def remote(source, target, send, recv, device):
        return pltpu.make_async_remote_copy(
            src_ref=source,
            dst_ref=target,
            send_sem=send,
            recv_sem=recv,
            device_id=device,
            device_id_type=pl.DeviceIdType.MESH,
        )

    def scatter_copy(index, way, step):
        return remote(
            piece(own[index], index, turned(way, step), way),
            slots[index].at[way, step],
            send_sems.at[0, index, way, step],
            recv_sems.at[0, index, way, step],
            nexts[way],
        )

    def gather_copy(index, way, step, first):
        chunk = turned(way, step - 1 + length)
        target = spot_of(total[index], index, core, chunk, way)
        source = piece(own[index], index, chunk, way) if first else target
        return remote(
            source,
            target,
            send_sems.at[1, index, way, step],
            recv_sems.at[1, index, way, step],
            nexts[way],
        )

    def fan_copy(index, way, step, first):
        chunk = turned(way, step - 1 + length)
        target = spot_of(total[index], index, core, chunk, way)
        source = piece(own[index], index, chunk, way) if first else target
        return remote(
            source,
            target,
            fan_sems.at[0, index, way, step],
            fan_sems.at[1, index, way, step],
            partner,
        )

    barrier = pltpu.get_barrier_semaphore()
    for device in (*nexts, partner):
        pl.semaphore_signal(barrier, inc=1, device_id=device, device_id_type=pl.DeviceIdType.MESH)
    pl.semaphore_wait(barrier, 3)

    loads = [
        pltpu.make_async_copy(share(given[index], index, core), own[index], load_sem.at[index])
        for index in range(count)
    ]
    swaps = [
        remote(
            share(given[index], index, 1 - core),
            peer[index],
            core_sems.at[0, index],
            core_sems.at[1, index],
            partner,
        )
        for index in range(count)
    ]
    for load, swap in zip(loads, swaps):
        swap.start()
        load.start()
    for index in range(count):
        loads[index].wait()
        swaps[index].wait_recv()
        for way in range(2):
            chunk = turned(way, 0)
            mine = piece(own[index], index, chunk, way)
            theirs = piece(peer[index], index, chunk, way)
            mine[...] = (mine[...].astype(F32) + theirs[...].astype(F32)).astype(mine.dtype)
            scatter_copy(index, way, 0).start()

    def absorb(index, way, step):
        scatter_copy(index, way, step - 1).wait_recv()
        chunk = turned(way, step)
        mine = piece(own[index], index, chunk, way)
        theirs = piece(peer[index], index, chunk, way)
        came = slots[index][way, step - 1]
        both = mine[...].astype(F32) + theirs[...].astype(F32) + came.astype(F32)
        mine[...] = both.astype(mine.dtype)

    def scatter_step(step, carry):
        for index, way in streams:
            absorb(index, way, step)
            scatter_copy(index, way, step).start()
        return carry

    lax.fori_loop(1, length - 1, scatter_step, 0)
    for index, way in streams:
        absorb(index, way, length - 1)
        gather_copy(index, way, 0, True).start()
        fan_copy(index, way, 0, True).start()
        chunk = turned(way, length - 1)
        pltpu.make_async_copy(
            piece(own[index], index, chunk, way),
            spot_of(total[index], index, core, chunk, way),
            keep_sem.at[index, way],
        ).start()

    def gather_step(step, carry):
        for index, way in streams:
            gather_copy(index, way, step - 1, False).wait_recv()
            gather_copy(index, way, step, False).start()
            fan_copy(index, way, step, False).start()
        return carry

    lax.fori_loop(1, length - 1, gather_step, 0)
    for index, way in streams:
        gather_copy(index, way, length - 2, False).wait_recv()
        fan_copy(index, way, length - 1, False).start()

    for index in range(count):
        swaps[index].wait_send()

    def drain(step, carry):
        for index, way in streams:
            scatter_copy(index, way, step).wait_send()
            gather_copy(index, way, step, False).wait_send()
            fan_copy(index, way, step, False).wait()
        return carry

    lax.fori_loop(0, length - 1, drain, 0)
    for index, way in streams:
        fan_copy(index, way, length - 1, False).wait()
        chunk = turned(way, length - 1)
        pltpu.make_async_copy(
            piece(own[index], index, chunk, way),
            spot_of(total[index], index, core, chunk, way),
            keep_sem.at[index, way],
        ).wait()


def ring_kind(table, length):
    rows, cols = math.prod(table.shape[:-1]), table.shape[-1]
    if rows % (length * 4 * 16) == 0 and cols % LANES == 0:
        return "rows", (length, 2, rows // (2 * length), cols)
    if rows % (length * 16) == 0 and cols % (4 * LANES) == 0:
        return "cols", (length, rows // length, cols)
    return None


def ring_sum(tables, small):
    n_dp = lax.axis_size("dp")
    length = n_dp // 2
    cuts = [ring_kind(table, length) for table in tables]
    if n_dp % 4 or length < 4 or any(cut is None for cut in cuts):
        return None
    if small.shape != (32, length * LANES):
        return None
    views = [table.reshape(cut[1]) for table, cut in zip(tables, cuts)]
    views.append(small.reshape(2, 2, 8, small.shape[-1]))
    kinds = [cut[0] for cut in cuts] + ["small"]
    own, slots = [], []
    for view, kind in zip(views, kinds):
        shape = view.shape
        if kind == "rows":
            half = (shape[0], shape[2], shape[3])
            part = (shape[2] // 2, shape[3])
        elif kind == "cols":
            half = (shape[0], shape[1], shape[2] // 2)
            part = (shape[1], shape[2] // 4)
        else:
            half = shape[1:]
            part = (shape[2], LANES)
        own.append(pltpu.VMEM(half, view.dtype))
        slots.append(pltpu.VMEM((2, length - 1, *part), view.dtype))
    count = len(views)
    hbm = pl.BlockSpec(memory_space=pl.ANY)
    moved = sum(view.size * view.dtype.itemsize for view in views)
    sums = pl.pallas_call(
        functools.partial(ring_kernel, n_dp, tuple(kinds)),
        out_shape=tuple(jax.ShapeDtypeStruct(view.shape, view.dtype) for view in views),
        in_specs=[hbm] * count,
        out_specs=(hbm,) * count,
        scratch_shapes=[
            *own,
            *own,
            *slots,
            pltpu.SemaphoreType.DMA((count,)),
            pltpu.SemaphoreType.DMA((2, count)),
            pltpu.SemaphoreType.DMA((2, count, 2, length - 1)),
            pltpu.SemaphoreType.DMA((2, count, 2, length - 1)),
            pltpu.SemaphoreType.DMA((2, count, 2, length)),
            pltpu.SemaphoreType.DMA((count, 2)),
        ],
        compiler_params=pltpu.CompilerParams(
            vmem_limit_bytes=VMEM_LIMIT, collective_id=0, has_side_effects=True
        ),
        cost_estimate=pl.CostEstimate(flops=0, bytes_accessed=30 * moved, transcendentals=0),
        name="ring_sum",
    )(*views)
    return [
        result.reshape(table.shape) for result, table in zip(sums, [*tables, small])
    ]


def body(
    inputs,
    qkv_weight,
    conv_taps,
    beta_weight,
    out_gain,
    out_weight,
    norm_gain,
    gate_up_weight,
    down_weight,
    cotangent,
):
    heads = beta_weight.shape[-1]
    wb = jnp.pad(beta_weight, ((0, 0), (0, 0), (0, LANES - heads)))
    base, adds = inputs, ()
    kept = []
    for level in range(LAYERS):
        x, n1, p, logits, t, u, o, on, part = mixer_forward(
            level, base, adds, norm_gain, conv_taps, out_gain, wb, qkv_weight, out_weight
        )
        h, n2, gu, z, part_two = mlp_forward(
            level, x, branch_parts(part), norm_gain, gate_up_weight, down_weight
        )
        kept.append((x, h, (n1, p, logits, t, u, o, on), (n2, gu, z)))
        base, adds = h, branch_parts(part_two)
    total = base
    for add in adds:
        total = total + add.astype(F32)
    outputs = total.astype(BF16)

    e, hid, adds = cotangent, kept[-1][0], ()
    gain_rows = {}
    small = [None] * LAYERS
    big = [None] * LAYERS
    for level in reversed(range(LAYERS)):
        x, h, mixer_kept, mlp_kept = kept[level]
        e, rows, part, grad_down, grad_gate_up = mlp_backward(
            level, e, hid, adds, norm_gain, *mlp_kept, gate_up_weight, down_weight
        )
        gain_rows[(level + 1, 0)] = rows
        e, part, small[level], grad_qkv, grad_out = mixer_backward(
            level,
            e,
            h,
            branch_parts(part),
            norm_gain,
            conv_taps,
            out_gain,
            wb,
            mixer_kept,
            qkv_weight,
            out_weight,
        )
        hid, adds = x, branch_parts(part)
        big[level] = (grad_out, grad_down, grad_qkv, grad_gate_up)
    branch = adds[0].astype(F32)
    for add in adds[1:]:
        branch = branch + add.astype(F32)
    grad_hidden, rows = rms_back(hid, norm_gain[0, 0:1].astype(F32), branch)
    gain_rows[(0, 0)] = rows
    input_grad = (e + grad_hidden).astype(BF16)

    half = rows.shape[-1] // 2
    small_all = jnp.concatenate(
        [
            small[level].at[3:5, SIDE:].set(gain_rows[(level, 0)].reshape(2, half))
            for level in range(LAYERS)
        ]
    )
    tables = [table for level in reversed(range(LAYERS)) for table in big[level]]
    sums = ring_sum(tables, small_all)
    if sums is None:
        sums = [*sum_over_dp(tables), lax.psum(small_all, "dp")]
    small_all = sums[-1].reshape(LAYERS, 16, -1)
    chans = conv_taps.shape[-1]
    grad_conv = small_all[:, : 3 * KCONV, :chans].reshape(conv_taps.shape)
    grad_beta = small_all[:, 3 * KCONV : 3 * KCONV + heads].transpose(0, 2, 1)
    grad_norm = jnp.stack(
        [
            small_all[:, 3:5, SIDE:].reshape(LAYERS, -1),
            small_all[:, 1:3, SIDE:].reshape(LAYERS, -1),
        ],
        axis=1,
    )
    grad_out_gain = small_all[:, 0, SIDE : SIDE + DK]
    grad_out_gain = sum(branch_parts(grad_out_gain))
    grad_out, grad_down, grad_qkv, grad_gate_up = (
        jnp.stack([sums[4 + index], sums[index]]).astype(F32) for index in range(4)
    )
    return (
        outputs,
        input_grad,
        grad_qkv,
        grad_conv,
        grad_beta,
        grad_out_gain,
        grad_out,
        grad_norm,
        grad_gate_up,
        grad_down,
    )


def solution(mesh):
    in_specs = (
        P("dp", None),
        P(None, None, None, "tensor"),
        P(None, None, None, "tensor"),
        P(None, None, "tensor"),
        P(),
        P(None, "tensor", None),
        P(),
        P(None, None, None, "tensor"),
        P(None, "tensor", None),
        P("dp", None),
    )
    out_specs = (
        P("dp", None),
        P("dp", None),
        P(None, None, None, "tensor"),
        P(None, None, None, "tensor"),
        P(None, None, "tensor"),
        P(),
        P(None, "tensor", None),
        P(),
        P(None, None, None, "tensor"),
        P(None, "tensor", None),
    )
    return jax.shard_map(body, mesh=mesh, in_specs=in_specs, out_specs=out_specs, check_vma=False)
```

```python
import functools
import math

import jax
import jax.numpy as jnp
from jax import lax
from jax.experimental import pallas as pl
from jax.experimental.pallas import tpu as pltpu
from jax.sharding import PartitionSpec as P

DK = 128
KCONV = 4
LAYERS = 2
LANES = 128
SIDE = 512
F32 = jnp.float32
BF16 = jnp.bfloat16
VMEM_LIMIT = 60 * 1024 * 1024


def dot_nn(a, b):
    return lax.dot_general(a, b, (((1,), (0,)), ((), ())), preferred_element_type=F32)


def dot_nt(a, b):
    return lax.dot_general(a, b, (((1,), (1,)), ((), ())), preferred_element_type=F32)


def dot_tn(a, b):
    return lax.dot_general(a, b, (((0,), (0,)), ((), ())), preferred_element_type=F32)


def halves(a):
    hi = a.astype(BF16)
    return hi, (a - hi.astype(F32)).astype(BF16)


def split_dot(dot, a, b):
    return dot(a[0], b[0]) + (dot(a[0], b[1]) + dot(a[1], b[0]))


def low(a):
    return a.astype(BF16)


def sigmoid(a):
    return 1.0 / (1.0 + jnp.exp(-a))


def rms_scale(a):
    return lax.rsqrt(jnp.mean(a * a, axis=-1, keepdims=True) + 1e-05)


def rms_back(hidden, gain, grad_normed):
    scale = rms_scale(hidden)
    weighted = gain * grad_normed
    inner = jnp.mean(hidden * weighted, axis=-1, keepdims=True)
    grad_hidden = scale * weighted - hidden * (scale * scale * scale) * inner
    rows = jnp.sum(grad_normed * hidden * scale, axis=0, keepdims=True)
    return grad_hidden, rows


def shift_down(a, count):
    if count == 0:
        return a
    row = lax.broadcasted_iota(jnp.int32, a.shape, 0)
    return jnp.where(row >= count, pltpu.roll(a, count, 0), 0.0)


def shift_up(a, count):
    if count == 0:
        return a
    length = a.shape[0]
    row = lax.broadcasted_iota(jnp.int32, a.shape, 0)
    return jnp.where(row < length - count, pltpu.roll(a, length - count, 0), 0.0)


def conv_silu(project, taps):
    total = taps[KCONV - 1 : KCONV, :] * project
    for tap in range(KCONV - 1):
        total = total + taps[tap : tap + 1, :] * shift_down(project, KCONV - 1 - tap)
    gate = sigmoid(total)
    return total, gate, total * gate


def positions(length):
    row = lax.broadcasted_iota(jnp.int32, (length, length), 0)
    col = lax.broadcasted_iota(jnp.int32, (length, length), 1)
    return row, col


def unit_lower_inverse(lower_list):
    length = lower_list[0].shape[0]
    row, col = positions(length)
    eye = jnp.where(row == col, 1.0, 0.0)
    diag_list = [jnp.where(row // 4 == col // 4, lower, 0.0) for lower in lower_list]
    parts = [halves(diag) for diag in diag_list]
    squares = [split_dot(dot_nn, part, part) for part in parts]
    firsts = [eye - diag for diag in diag_list]
    inverse = [
        first + split_dot(dot_nn, halves(first), halves(square))
        for first, square in zip(firsts, squares)
    ]
    size = 4
    while size < length:
        fresh = (row // (2 * size) == col // (2 * size)) & (row // size != col // size)
        offs = [halves(jnp.where(fresh, lower, 0.0)) for lower in lower_list]
        held = [halves(inv) for inv in inverse]
        mids = [split_dot(dot_nn, inv, off) for inv, off in zip(held, offs)]
        inverse = [
            inv - split_dot(dot_nn, halves(mid), part)
            for inv, mid, part in zip(inverse, mids, held)
        ]
        size = 2 * size
    return inverse


def head_cols(head):
    return slice(head * DK, (head + 1) * DK)


KEPT = ("x", "n1", "p", "logits", "t", "u", "o", "on", "h", "n2", "gu", "z")


def kept_shapes(length, width, chans, hidden):
    heads = chans // DK
    shapes = dict(
        x=((length, width), F32),
        n1=((length, width), BF16),
        p=((3, length, chans), F32),
        logits=((length, LANES), F32),
        t=((2, heads, length, length), BF16),
        u=((length, chans), BF16),
        o=((length, chans), F32),
        on=((length, chans), BF16),
        h=((length, width), F32),
        n2=((length, width), BF16),
        gu=((2, length, hidden), F32),
        z=((length, hidden), BF16),
    )
    return [((LAYERS, *shapes[name][0]), shapes[name][1]) for name in KEPT]


class Exchange:
    def __init__(self, slots, send_sems, recv_sems):
        self.slots, self.send_sems, self.recv_sems = slots, send_sems, recv_sems
        self.count = slots.shape[1]
        self.me = lax.axis_index("tensor")
        self.pending = []

    def greet(self):
        barrier = pltpu.get_barrier_semaphore()
        for away in range(1, self.count):
            pl.semaphore_signal(
                barrier,
                inc=1,
                device_id={"tensor": lax.rem(self.me + away, self.count)},
                device_id_type=pl.DeviceIdType.MESH,
            )
        pl.semaphore_wait(barrier, self.count - 1)

    def copies(self, spot, part, rows):
        mine = self.slots.at[spot, self.me, rows]
        return [
            pltpu.make_async_remote_copy(
                src_ref=mine,
                dst_ref=mine,
                send_sem=self.send_sems.at[spot, part, away - 1],
                recv_sem=self.recv_sems.at[spot, part, away - 1],
                device_id={"tensor": lax.rem(self.me + away, self.count)},
                device_id_type=pl.DeviceIdType.MESH,
            )
            for away in range(1, self.count)
        ]

    def give(self, spot, part, rows, value):
        self.slots[spot, self.me, rows] = value
        for copy in self.copies(spot, part, rows):
            copy.start()
            self.pending.append(copy)

    def take(self, spot, part, rows):
        for copy in self.copies(spot, part, rows):
            copy.wait_recv()
        total = self.slots[spot, 0, rows].astype(F32)
        for index in range(1, self.count):
            total = total + self.slots[spot, index, rows].astype(F32)
        return total

    def finish(self):
        for copy in self.pending:
            copy.wait_send()


def forward_kernel(n_parts, *refs):
    (x_ref, gain_ref, taps_ref, head_gain_ref, wb_ref) = refs[:5]
    (wq_hbm, wo_hbm, wgu_hbm, wd_hbm) = refs[5:9]
    count = len(KEPT)
    outs = dict(zip(KEPT, refs[9 : 9 + count]))
    last_out = refs[9 + count]
    held = dict(zip(KEPT, refs[10 + count : 10 + 2 * count]))
    (wq, wo, wgu, wd, slots, last, load_sems, keep_sems, send_sems, recv_sems) = refs[
        10 + 2 * count :
    ]
    exchange = Exchange(slots, send_sems, recv_sems)
    sources = ((wq_hbm, wq), (wo_hbm, wo), (wgu_hbm, wgu), (wd_hbm, wd))
    loads = [
        [
            pltpu.make_async_copy(source.at[level], target.at[level], load_sems.at[level, index])
            for index, (source, target) in enumerate(sources)
        ]
        for level in range(LAYERS)
    ]
    for group in loads:
        for load in group:
            load.start()
    exchange.greet()
    keeps = []

    def keep(name, level):
        copy = pltpu.make_async_copy(
            held[name].at[level], outs[name].at[level], keep_sems.at[KEPT.index(name), level]
        )
        copy.start()
        keeps.append(copy)

    length = x_ref.shape[0]
    heads = wo.shape[1] // DK
    high = length // n_parts
    parts = [(part, slice(part * high, (part + 1) * high)) for part in range(n_parts)]
    row, col = positions(length)
    for level in range(LAYERS):
        for part, rows in parts:
            if level == 0:
                x = x_ref[rows].astype(F32)
            else:
                x = held["h"][level - 1, rows] + exchange.take(2 * level - 1, part, rows)
            held["x"][level, rows] = x
            n1 = low(x * rms_scale(x) * gain_ref[level, 0:1, :].astype(F32))
            held["n1"][level, rows] = n1
            held["logits"][level, rows] = dot_nn(n1, wb_ref[level])
            if part == 0:
                loads[level][0].wait()
            for index in range(3):
                held["p"][level, index, rows] = dot_nn(n1, wq[level, index])
        for name in ("x", "n1", "logits", "p"):
            keep(name, level)
        beta = sigmoid(held["logits"][level])
        acts = [
            conv_silu(held["p"][level, index], taps_ref[level, index].astype(F32))[2]
            for index in range(3)
        ]
        lowers, scores, values = [], [], []
        for head in range(heads):
            cols = head_cols(head)
            c0, c1, c2 = (act[:, cols] for act in acts)
            q = low(c0 * lax.rsqrt(jnp.sum(c0 * c0, axis=-1, keepdims=True) + 0.001))
            k = low(c1 * lax.rsqrt(jnp.sum(c1 * c1, axis=-1, keepdims=True) + 0.001))
            v = low(c2).astype(F32)
            gate = beta[:, head : head + 1]
            lowers.append(jnp.where(row > col, gate * dot_nt(k, k), 0.0))
            scores.append(low(jnp.where(row >= col, dot_nt(q, k), 0.0)))
            values.append(halves(gate * v))
        inverse = unit_lower_inverse(lowers)
        head_gain = head_gain_ref[level : level + 1, :].astype(F32)
        for head in range(heads):
            cols = head_cols(head)
            t_hi, t_lo = halves(inverse[head])
            held["t"][level, 0, head] = t_hi
            held["t"][level, 1, head] = t_lo
            u_low = low(split_dot(dot_nn, (t_hi, t_lo), values[head]))
            held["u"][level, :, cols] = u_low
            o = dot_nn(scores[head], u_low)
            held["o"][level, :, cols] = o
            scale = lax.rsqrt(jnp.mean(o * o, axis=-1, keepdims=True) + 0.01)
            held["on"][level, :, cols] = low(o * scale * head_gain)
        loads[level][1].wait()
        for part, rows in parts:
            out = dot_nn(held["on"][level, rows], wo[level])
            exchange.give(2 * level, part, rows, low(out))
        for name in ("t", "u", "o", "on"):
            keep(name, level)
        for part, rows in parts:
            h = held["x"][level, rows] + exchange.take(2 * level, part, rows)
            held["h"][level, rows] = h
            n2 = low(h * rms_scale(h) * gain_ref[level, 1:2, :].astype(F32))
            held["n2"][level, rows] = n2
            if part == 0:
                loads[level][2].wait()
            g = dot_nn(n2, wgu[level, 0])
            held["gu"][level, 0, rows] = g
            u = dot_nn(n2, wgu[level, 1])
            held["gu"][level, 1, rows] = u
            z = low(g * sigmoid(g) * u)
            held["z"][level, rows] = z
            if part == 0:
                loads[level][3].wait()
            out = low(dot_nn(z, wd[level]))
            if level < LAYERS - 1:
                exchange.give(2 * level + 1, part, rows, out)
            else:
                last[rows] = out
        for name in ("h", "n2", "gu", "z"):
            keep(name, level)
    final = pltpu.make_async_copy(last, last_out, load_sems.at[0, 0])
    final.start()
    for copy in keeps:
        copy.wait()
    final.wait()
    exchange.finish()


def forward(x, norm_gain, taps, head_gain, wb, wq, wo, wgu, wd):
    length, width = x.shape
    chans, hidden = wq.shape[-1], wgu.shape[-1]
    n_tensor = lax.axis_size("tensor")
    n_parts = 2
    kept = kept_shapes(length, width, chans, hidden)
    vmem = pl.BlockSpec(memory_space=pltpu.VMEM)
    hbm = pl.BlockSpec(memory_space=pl.ANY)
    spots = 2 * LAYERS - 1
    *kept, part = pl.pallas_call(
        functools.partial(forward_kernel, n_parts),
        out_shape=(
            *(jax.ShapeDtypeStruct(*spec) for spec in kept),
            jax.ShapeDtypeStruct((length, width), BF16),
        ),
        in_specs=[vmem] * 5 + [hbm] * 4,
        out_specs=(hbm,) * (len(kept) + 1),
        scratch_shapes=[
            *(pltpu.VMEM(*spec) for spec in kept),
            pltpu.VMEM((LAYERS, 3, width, chans), BF16),
            pltpu.VMEM((LAYERS, chans, width), BF16),
            pltpu.VMEM((LAYERS, 2, width, hidden), BF16),
            pltpu.VMEM((LAYERS, hidden, width), BF16),
            pltpu.VMEM((spots, n_tensor, length, width), BF16),
            pltpu.VMEM((length, width), BF16),
            pltpu.SemaphoreType.DMA((LAYERS, 4)),
            pltpu.SemaphoreType.DMA((len(kept), LAYERS)),
            pltpu.SemaphoreType.DMA((spots, n_parts, n_tensor - 1)),
            pltpu.SemaphoreType.DMA((spots, n_parts, n_tensor - 1)),
        ],
        compiler_params=pltpu.CompilerParams(
            vmem_limit_bytes=VMEM_LIMIT, collective_id=1, has_side_effects=True
        ),
        name="forward",
    )(x, norm_gain, taps, head_gain, wb, wq, wo, wgu, wd)
    return dict(zip(KEPT, kept)), part


def back_through_norm(level, which, gain_ref, e_ref, hid_ref, adds, rows_out):
    e = e_ref[...].astype(F32)
    if not adds:
        rows_out[...] = jnp.zeros_like(rows_out)
        return e
    total = adds[0][...].astype(F32)
    for add in adds[1:]:
        total = total + add[...].astype(F32)
    gain = gain_ref[level, which : which + 1, :].astype(F32)
    grad_hidden, rows = rms_back(hid_ref[...], gain, total)
    rows_out[...] = rows
    return e + grad_hidden


def mlp_backward_kernel(level, n_add, *refs):
    (e_ref, hid_ref, *adds) = refs[: 2 + n_add]
    (gain_ref, n2_ref, gu_ref, z_ref, wgu_hbm, wd_hbm) = refs[2 + n_add : 8 + n_add]
    (e_out, rows_out, part_out, gd_out, ggu_out) = refs[8 + n_add : 13 + n_add]
    wgu, wd, dgu_ref, sems = refs[13 + n_add :]
    loads = [
        pltpu.make_async_copy(wd_hbm.at[level], wd, sems.at[0]),
        pltpu.make_async_copy(wgu_hbm.at[level], wgu, sems.at[1]),
    ]
    for load in loads:
        load.start()
    e = back_through_norm(level + 1, 0, gain_ref, e_ref, hid_ref, adds, rows_out)
    e_out[...] = e
    ef = low(e)
    loads[0].wait()
    dz = dot_nt(ef, wd[...])
    g, u = gu_ref[0], gu_ref[1]
    s = sigmoid(g)
    dgu_ref[0] = low(dz * u * (s * (1.0 + g * (1.0 - s))))
    dgu_ref[1] = low(dz * (g * s))
    loads[1].wait()
    part_out[...] = low(dot_nt(dgu_ref[0], wgu[0]) + dot_nt(dgu_ref[1], wgu[1]))
    gd_out[...] = low(dot_tn(z_ref[...], ef))
    for half in range(2):
        ggu_out[half] = low(dot_tn(n2_ref[...], dgu_ref[half]))


def mlp_backward(level, e, hid, adds, norm_gain, n2, gu, z, wgu, wd):
    length, width = e.shape
    hidden = wgu.shape[-1]
    sds = jax.ShapeDtypeStruct
    vmem = pl.BlockSpec(memory_space=pltpu.VMEM)
    hbm = pl.BlockSpec(memory_space=pl.ANY)
    return pl.pallas_call(
        functools.partial(mlp_backward_kernel, level, len(adds)),
        out_shape=(
            sds((length, width), F32),
            sds((1, width), F32),
            sds((length, width), BF16),
            sds((hidden, width), BF16),
            sds((2, width, hidden), BF16),
        ),
        in_specs=[vmem] * (6 + len(adds)) + [hbm, hbm],
        out_specs=(vmem,) * 5,
        scratch_shapes=[
            pltpu.VMEM((2, width, hidden), BF16),
            pltpu.VMEM((hidden, width), BF16),
            pltpu.VMEM((2, length, hidden), BF16),
            pltpu.SemaphoreType.DMA((2,)),
        ],
        compiler_params=pltpu.CompilerParams(vmem_limit_bytes=VMEM_LIMIT),
        name="mlp_backward",
    )(e, hid, *adds, norm_gain, n2, gu, z, wgu, wd)


def mixer_backward_kernel(level, heads, n_add, *refs):
    (e_ref, hid_ref, *adds) = refs[: 2 + n_add]
    (gain_ref, taps_ref, head_gain_ref, wb_ref, n1_ref, p_ref, logit_ref, t_ref, u_ref, o_ref) = (
        refs[2 + n_add : 12 + n_add]
    )
    (on_ref, wq_hbm, wo_hbm) = refs[12 + n_add : 15 + n_add]
    (e_out, part_out, small_out, gq_out, go_out) = refs[15 + n_add : 20 + n_add]
    wq, wo, grads, dp_ref, rows_out, sems = refs[20 + n_add :]
    loads = [
        pltpu.make_async_copy(wo_hbm.at[level], wo, sems.at[0]),
        pltpu.make_async_copy(wq_hbm.at[level], wq, sems.at[1]),
    ]
    for load in loads:
        load.start()
    e = back_through_norm(level, 1, gain_ref, e_ref, hid_ref, adds, rows_out)
    e_out[...] = e
    em = low(e)
    length = e.shape[0]
    loads[0].wait()
    don = dot_nt(em, wo[...])
    go_out[...] = low(dot_tn(on_ref[...], em))
    beta = sigmoid(logit_ref[...])
    row, col = positions(length)
    lane = lax.broadcasted_iota(jnp.int32, (length, LANES), 1)
    head_gain = head_gain_ref[level : level + 1, :].astype(F32)
    convs = [conv_silu(p_ref[part], taps_ref[level, part].astype(F32)) for part in range(3)]
    gain_rows = jnp.zeros((1, DK), F32)
    dlogit = jnp.zeros((length, LANES), F32)
    for head in range(heads):
        cols = head_cols(head)
        c0, c1, c2 = (conv[2][:, cols] for conv in convs)
        rho0 = lax.rsqrt(jnp.sum(c0 * c0, axis=-1, keepdims=True) + 0.001)
        rho1 = lax.rsqrt(jnp.sum(c1 * c1, axis=-1, keepdims=True) + 0.001)
        q, k, v = low(c0 * rho0), low(c1 * rho1), low(c2).astype(F32)
        gate = beta[:, head : head + 1]
        o = o_ref[:, cols]
        scale = lax.rsqrt(jnp.mean(o * o, axis=-1, keepdims=True) + 0.01)
        dn = don[:, cols]
        weighted = dn * head_gain
        inner = jnp.mean(o * weighted, axis=-1, keepdims=True)
        do = low(scale * weighted - o * (scale * scale * scale) * inner)
        gain_rows = gain_rows + jnp.sum(dn * o * scale, axis=0, keepdims=True)
        u = u_ref[:, cols]
        score_t = low(jnp.where(row <= col, dot_nt(k, q), 0.0))
        du = dot_nn(score_t, do)
        ds = low(jnp.where(row >= col, dot_nt(do, u), 0.0))
        ds_t = low(jnp.where(row <= col, dot_nt(u, do), 0.0))
        dq = dot_nn(ds, k)
        dk = dot_nn(ds_t, q)
        r = split_dot(dot_tn, (t_ref[0, head], t_ref[1, head]), halves(du))
        dv = gate * r
        dv_low = low(dv)
        gram = low(jnp.where(row > col, dot_nt(k, k), 0.0))
        w = v - dot_nn(gram, u)
        dbeta = jnp.sum(r * w, axis=-1, keepdims=True)
        dgram = jnp.where(row > col, dot_nt(dv_low, u), 0.0) + jnp.where(
            row < col, dot_nt(u, dv_low), 0.0
        )
        dk = dk - dot_nn(low(dgram), k)
        grads[0, :, cols] = rho0 * dq - c0 * (rho0 * rho0 * rho0) * jnp.sum(
            c0 * dq, axis=-1, keepdims=True
        )
        grads[1, :, cols] = rho1 * dk - c1 * (rho1 * rho1 * rho1) * jnp.sum(
            c1 * dk, axis=-1, keepdims=True
        )
        grads[2, :, cols] = dv
        dlogit = dlogit + jnp.where(lane == head, dbeta * gate * (1.0 - gate), 0.0)
    chans = grads.shape[-1]
    small_out[...] = jnp.zeros_like(small_out)
    small_out[0:1, SIDE : SIDE + DK] = gain_rows
    half = rows_out.shape[-1] // 2
    small_out[1:2, SIDE:] = rows_out[:, :half]
    small_out[2:3, SIDE:] = rows_out[:, half:]
    dlogit_low = low(dlogit)
    n1 = n1_ref[...]
    small_out[3 * KCONV : 3 * KCONV + heads, :] = dot_tn(dlogit_low, n1)[:heads, :]
    for part in range(3):
        taps = taps_ref[level, part].astype(F32)
        total, gate, _ = convs[part]
        dsum = grads[part] * (gate * (1.0 + total * (1.0 - gate)))
        p = p_ref[part]
        dp = taps[KCONV - 1 : KCONV, :] * dsum
        for tap in range(KCONV):
            back = KCONV - 1 - tap
            spot = part * KCONV + tap
            small_out[spot : spot + 1, :chans] = jnp.sum(
                dsum * shift_down(p, back), axis=0, keepdims=True
            )
            if back:
                dp = dp + taps[tap : tap + 1, :] * shift_up(dsum, back)
        dp_ref[part] = low(dp)
    loads[1].wait()
    dn1 = dot_nt(dlogit_low, wb_ref[level])
    for part in range(3):
        dn1 = dn1 + dot_nt(dp_ref[part], wq[part])
    part_out[...] = low(dn1)
    for part in range(3):
        gq_out[part] = low(dot_tn(n1, dp_ref[part]))


def mixer_backward(level, e, hid, adds, norm_gain, taps, head_gain, wb, kept, wq, wo):
    length, width = e.shape
    chans = wq.shape[-1]
    heads = chans // DK
    sds = jax.ShapeDtypeStruct
    vmem = pl.BlockSpec(memory_space=pltpu.VMEM)
    hbm = pl.BlockSpec(memory_space=pl.ANY)
    return pl.pallas_call(
        functools.partial(mixer_backward_kernel, level, heads, len(adds)),
        out_shape=(
            sds((length, width), F32),
            sds((length, width), BF16),
            sds((16, width), F32),
            sds((3, width, chans), BF16),
            sds((chans, width), BF16),
        ),
        in_specs=[vmem] * (13 + len(adds)) + [hbm, hbm],
        out_specs=(vmem,) * 5,
        scratch_shapes=[
            pltpu.VMEM((3, width, chans), BF16),
            pltpu.VMEM((chans, width), BF16),
            pltpu.VMEM((3, length, chans), F32),
            pltpu.VMEM((3, length, chans), BF16),
            pltpu.VMEM((1, width), F32),
            pltpu.SemaphoreType.DMA((2,)),
        ],
        compiler_params=pltpu.CompilerParams(vmem_limit_bytes=VMEM_LIMIT),
        name="mixer_backward",
    )(e, hid, *adds, norm_gain, taps, head_gain, wb, *kept, wq, wo)


def branch_parts(part):
    count = lax.axis_size("tensor")
    if count == 1:
        return (part,)
    if count == 2:
        return (part, lax.ppermute(part, "tensor", [(0, 1), (1, 0)]))
    return (lax.psum(part, "tensor"),)


def sum_over_dp(tables):
    shapes = [table.shape for table in tables]
    flat = jnp.concatenate([table.reshape(-1) for table in tables])
    size = flat.shape[0]
    count = lax.axis_size("dp")
    pad = -size % (count * 1024)
    flat = jnp.pad(flat, (0, pad))
    shard = lax.psum_scatter(flat, "dp", scatter_dimension=0, tiled=True)
    joined = lax.all_gather(shard, "dp", axis=0, tiled=True)
    pieces = []
    offset = 0
    for shape in shapes:
        size = math.prod(shape)
        pieces.append(joined[offset : offset + size].reshape(shape))
        offset = offset + size
    return pieces


def ring_place(n_dp):
    spot = lax.axis_index("dp")
    core = lax.rem(spot, 2)
    side = lax.rem(lax.div(spot, 2), 2)
    depth = lax.div(spot, 4)
    length = n_dp // 2
    return core, depth + side * (length - 1 - 2 * depth), length


def ring_spot(place, core, length):
    side = lax.div(place, length // 2)
    depth = place + side * (length - 1 - 2 * place)
    return (depth * 2 + side) * 2 + core


def ring_kernel(n_dp, kinds, *refs):
    count = len(kinds)
    given = refs[:count]
    total = refs[count : 2 * count]
    own = refs[2 * count : 3 * count]
    peer = refs[3 * count : 4 * count]
    slots = refs[4 * count : 5 * count]
    load_sem, core_sems, send_sems, recv_sems, fan_sems, keep_sem = refs[5 * count :]
    core, place, length = ring_place(n_dp)
    partner = {"dp": ring_spot(place, 1 - core, length)}
    places = [lax.rem(place + 1, length), lax.rem(place + length - 1, length)]
    nexts = [{"dp": ring_spot(spot, core, length)} for spot in places]
    streams = [(index, way) for index in range(count) for way in range(2)]

    def share(ref, index, half):
        kind = kinds[index]
        if kind == "rows":
            return ref.at[:, half]
        if kind == "cols":
            wide = ref.shape[-1] // 2
            return ref.at[:, :, pl.ds(pl.multiple_of(half * wide, LANES), wide)]
        return ref.at[half]

    def piece(ref, index, chunk, way):
        kind = kinds[index]
        if kind == "rows":
            high = ref.shape[1] // 2
            return ref.at[chunk, way * high : (way + 1) * high]
        if kind == "cols":
            wide = ref.shape[-1] // 2
            return ref.at[chunk, :, way * wide : (way + 1) * wide]
        return ref.at[way, :, pl.ds(pl.multiple_of(chunk * LANES, LANES), LANES)]

    def spot_of(ref, index, half, chunk, way):
        kind = kinds[index]
        if kind == "rows":
            high = ref.shape[2] // 2
            return ref.at[chunk, half, way * high : (way + 1) * high]
        if kind == "cols":
            wide = ref.shape[-1] // 4
            start = pl.multiple_of(half * (2 * wide) + way * wide, LANES)
            return ref.at[chunk, :, pl.ds(start, wide)]
        return ref.at[half, way, :, pl.ds(pl.multiple_of(chunk * LANES, LANES), LANES)]

    def turned(way, steps):
        if way == 0:
            return lax.rem(place + 2 * length - steps, length)
        return lax.rem(place + steps + length, length)

    def remote(source, target, send, recv, device):
        return pltpu.make_async_remote_copy(
            src_ref=source,
            dst_ref=target,
            send_sem=send,
            recv_sem=recv,
            device_id=device,
            device_id_type=pl.DeviceIdType.MESH,
        )

    def scatter_copy(index, way, step):
        return remote(
            piece(own[index], index, turned(way, step), way),
            slots[index].at[way, step],
            send_sems.at[0, index, way, step],
            recv_sems.at[0, index, way, step],
            nexts[way],
        )

    def gather_copy(index, way, step, first):
        chunk = turned(way, step - 1 + length)
        target = spot_of(total[index], index, core, chunk, way)
        source = piece(own[index], index, chunk, way) if first else target
        return remote(
            source,
            target,
            send_sems.at[1, index, way, step],
            recv_sems.at[1, index, way, step],
            nexts[way],
        )

    def fan_copy(index, way, step, first):
        chunk = turned(way, step - 1 + length)
        target = spot_of(total[index], index, core, chunk, way)
        source = piece(own[index], index, chunk, way) if first else target
        return remote(
            source,
            target,
            fan_sems.at[0, index, way, step],
            fan_sems.at[1, index, way, step],
            partner,
        )

    barrier = pltpu.get_barrier_semaphore()
    for device in (*nexts, partner):
        pl.semaphore_signal(barrier, inc=1, device_id=device, device_id_type=pl.DeviceIdType.MESH)
    pl.semaphore_wait(barrier, 3)

    loads = [
        pltpu.make_async_copy(share(given[index], index, core), own[index], load_sem.at[index])
        for index in range(count)
    ]
    swaps = [
        remote(
            share(given[index], index, 1 - core),
            peer[index],
            core_sems.at[0, index],
            core_sems.at[1, index],
            partner,
        )
        for index in range(count)
    ]
    for load, swap in zip(loads, swaps):
        swap.start()
        load.start()
    for index in range(count):
        loads[index].wait()
        swaps[index].wait_recv()
        for way in range(2):
            chunk = turned(way, 0)
            mine = piece(own[index], index, chunk, way)
            theirs = piece(peer[index], index, chunk, way)
            mine[...] = (mine[...].astype(F32) + theirs[...].astype(F32)).astype(mine.dtype)
            scatter_copy(index, way, 0).start()

    def absorb(index, way, step):
        scatter_copy(index, way, step - 1).wait_recv()
        chunk = turned(way, step)
        mine = piece(own[index], index, chunk, way)
        theirs = piece(peer[index], index, chunk, way)
        came = slots[index][way, step - 1]
        both = mine[...].astype(F32) + theirs[...].astype(F32) + came.astype(F32)
        mine[...] = both.astype(mine.dtype)

    def scatter_step(step, carry):
        for index, way in streams:
            absorb(index, way, step)
            scatter_copy(index, way, step).start()
        return carry

    lax.fori_loop(1, length - 1, scatter_step, 0)
    for index, way in streams:
        absorb(index, way, length - 1)
        gather_copy(index, way, 0, True).start()
        fan_copy(index, way, 0, True).start()
        chunk = turned(way, length - 1)
        pltpu.make_async_copy(
            piece(own[index], index, chunk, way),
            spot_of(total[index], index, core, chunk, way),
            keep_sem.at[index, way],
        ).start()

    def gather_step(step, carry):
        for index, way in streams:
            gather_copy(index, way, step - 1, False).wait_recv()
            gather_copy(index, way, step, False).start()
            fan_copy(index, way, step, False).start()
        return carry

    lax.fori_loop(1, length - 1, gather_step, 0)
    for index, way in streams:
        gather_copy(index, way, length - 2, False).wait_recv()
        fan_copy(index, way, length - 1, False).start()

    for index in range(count):
        swaps[index].wait_send()

    def drain(step, carry):
        for index, way in streams:
            scatter_copy(index, way, step).wait_send()
            gather_copy(index, way, step, False).wait_send()
            fan_copy(index, way, step, False).wait()
        return carry

    lax.fori_loop(0, length - 1, drain, 0)
    for index, way in streams:
        fan_copy(index, way, length - 1, False).wait()
        chunk = turned(way, length - 1)
        pltpu.make_async_copy(
            piece(own[index], index, chunk, way),
            spot_of(total[index], index, core, chunk, way),
            keep_sem.at[index, way],
        ).wait()


def ring_kind(table, length):
    rows, cols = math.prod(table.shape[:-1]), table.shape[-1]
    if rows % (length * 4 * 16) == 0 and cols % LANES == 0:
        return "rows", (length, 2, rows // (2 * length), cols)
    if rows % (length * 16) == 0 and cols % (4 * LANES) == 0:
        return "cols", (length, rows // length, cols)
    return None


def ring_sum(tables, small):
    n_dp = lax.axis_size("dp")
    length = n_dp // 2
    cuts = [ring_kind(table, length) for table in tables]
    if n_dp % 4 or length < 4 or any(cut is None for cut in cuts):
        return None
    if small.shape != (32, length * LANES):
        return None
    views = [table.reshape(cut[1]) for table, cut in zip(tables, cuts)]
    views.append(small.reshape(2, 2, 8, small.shape[-1]))
    kinds = [cut[0] for cut in cuts] + ["small"]
    own, slots = [], []
    for view, kind in zip(views, kinds):
        shape = view.shape
        if kind == "rows":
            half = (shape[0], shape[2], shape[3])
            part = (shape[2] // 2, shape[3])
        elif kind == "cols":
            half = (shape[0], shape[1], shape[2] // 2)
            part = (shape[1], shape[2] // 4)
        else:
            half = shape[1:]
            part = (shape[2], LANES)
        own.append(pltpu.VMEM(half, view.dtype))
        slots.append(pltpu.VMEM((2, length - 1, *part), view.dtype))
    count = len(views)
    hbm = pl.BlockSpec(memory_space=pl.ANY)
    moved = sum(view.size * view.dtype.itemsize for view in views)
    sums = pl.pallas_call(
        functools.partial(ring_kernel, n_dp, tuple(kinds)),
        out_shape=tuple(jax.ShapeDtypeStruct(view.shape, view.dtype) for view in views),
        in_specs=[hbm] * count,
        out_specs=(hbm,) * count,
        scratch_shapes=[
            *own,
            *own,
            *slots,
            pltpu.SemaphoreType.DMA((count,)),
            pltpu.SemaphoreType.DMA((2, count)),
            pltpu.SemaphoreType.DMA((2, count, 2, length - 1)),
            pltpu.SemaphoreType.DMA((2, count, 2, length - 1)),
            pltpu.SemaphoreType.DMA((2, count, 2, length)),
            pltpu.SemaphoreType.DMA((count, 2)),
        ],
        compiler_params=pltpu.CompilerParams(
            vmem_limit_bytes=VMEM_LIMIT, collective_id=0, has_side_effects=True
        ),
        cost_estimate=pl.CostEstimate(flops=0, bytes_accessed=30 * moved, transcendentals=0),
        name="ring_sum",
    )(*views)
    return [
        result.reshape(table.shape) for result, table in zip(sums, [*tables, small])
    ]


def body(
    inputs,
    qkv_weight,
    conv_taps,
    beta_weight,
    out_gain,
    out_weight,
    norm_gain,
    gate_up_weight,
    down_weight,
    cotangent,
):
    heads = beta_weight.shape[-1]
    wb = jnp.pad(beta_weight, ((0, 0), (0, 0), (0, LANES - heads)))
    saved, part = forward(
        inputs,
        norm_gain,
        conv_taps,
        out_gain,
        wb,
        qkv_weight,
        out_weight,
        gate_up_weight,
        down_weight,
    )
    kept = []
    for level in range(LAYERS):
        at = {name: saved[name][level] for name in KEPT}
        kept.append(
            (
                at["x"],
                at["h"],
                tuple(at[name] for name in ("n1", "p", "logits", "t", "u", "o", "on")),
                tuple(at[name] for name in ("n2", "gu", "z")),
            )
        )
    total = kept[-1][1]
    for add in branch_parts(part):
        total = total + add.astype(F32)
    outputs = total.astype(BF16)

    e, hid, adds = cotangent, kept[-1][0], ()
    gain_rows = {}
    small = [None] * LAYERS
    big = [None] * LAYERS
    for level in reversed(range(LAYERS)):
        x, h, mixer_kept, mlp_kept = kept[level]
        e, rows, part, grad_down, grad_gate_up = mlp_backward(
            level, e, hid, adds, norm_gain, *mlp_kept, gate_up_weight, down_weight
        )
        gain_rows[(level + 1, 0)] = rows
        e, part, small[level], grad_qkv, grad_out = mixer_backward(
            level,
            e,
            h,
            branch_parts(part),
            norm_gain,
            conv_taps,
            out_gain,
            wb,
            mixer_kept,
            qkv_weight,
            out_weight,
        )
        hid, adds = x, branch_parts(part)
        big[level] = (grad_out, grad_down, grad_qkv, grad_gate_up)
    branch = adds[0].astype(F32)
    for add in adds[1:]:
        branch = branch + add.astype(F32)
    grad_hidden, rows = rms_back(hid, norm_gain[0, 0:1].astype(F32), branch)
    gain_rows[(0, 0)] = rows
    input_grad = (e + grad_hidden).astype(BF16)

    half = rows.shape[-1] // 2
    small_all = jnp.concatenate(
        [
            small[level].at[3:5, SIDE:].set(gain_rows[(level, 0)].reshape(2, half))
            for level in range(LAYERS)
        ]
    )
    tables = [table for level in reversed(range(LAYERS)) for table in big[level]]
    sums = ring_sum(tables, small_all)
    if sums is None:
        sums = [*sum_over_dp(tables), lax.psum(small_all, "dp")]
    small_all = sums[-1].reshape(LAYERS, 16, -1)
    chans = conv_taps.shape[-1]
    grad_conv = small_all[:, : 3 * KCONV, :chans].reshape(conv_taps.shape)
    grad_beta = small_all[:, 3 * KCONV : 3 * KCONV + heads].transpose(0, 2, 1)
    grad_norm = jnp.stack(
        [
            small_all[:, 3:5, SIDE:].reshape(LAYERS, -1),
            small_all[:, 1:3, SIDE:].reshape(LAYERS, -1),
        ],
        axis=1,
    )
    grad_out_gain = small_all[:, 0, SIDE : SIDE + DK]
    grad_out_gain = sum(branch_parts(grad_out_gain))
    grad_out, grad_down, grad_qkv, grad_gate_up = (
        jnp.stack([sums[4 + index], sums[index]]).astype(F32) for index in range(4)
    )
    return (
        outputs,
        input_grad,
        grad_qkv,
        grad_conv,
        grad_beta,
        grad_out_gain,
        grad_out,
        grad_norm,
        grad_gate_up,
        grad_down,
    )


def solution(mesh):
    in_specs = (
        P("dp", None),
        P(None, None, None, "tensor"),
        P(None, None, None, "tensor"),
        P(None, None, "tensor"),
        P(),
        P(None, "tensor", None),
        P(),
        P(None, None, None, "tensor"),
        P(None, "tensor", None),
        P("dp", None),
    )
    out_specs = (
        P("dp", None),
        P("dp", None),
        P(None, None, None, "tensor"),
        P(None, None, None, "tensor"),
        P(None, None, "tensor"),
        P(),
        P(None, "tensor", None),
        P(),
        P(None, None, None, "tensor"),
        P(None, "tensor", None),
    )
    return jax.shard_map(body, mesh=mesh, in_specs=in_specs, out_specs=out_specs, check_vma=False)
```

```python
import functools
import math

import jax
import jax.numpy as jnp
from jax import lax
from jax.experimental import pallas as pl
from jax.experimental.pallas import tpu as pltpu
from jax.sharding import PartitionSpec as P

DK = 128
KCONV = 4
LAYERS = 2
LANES = 128
SIDE = 512
F32 = jnp.float32
BF16 = jnp.bfloat16
VMEM_LIMIT = 60 * 1024 * 1024


def dot_nn(a, b):
    return lax.dot_general(a, b, (((1,), (0,)), ((), ())), preferred_element_type=F32)


def dot_nt(a, b):
    return lax.dot_general(a, b, (((1,), (1,)), ((), ())), preferred_element_type=F32)


def dot_tn(a, b):
    return lax.dot_general(a, b, (((0,), (0,)), ((), ())), preferred_element_type=F32)


def halves(a):
    hi = a.astype(BF16)
    return hi, (a - hi.astype(F32)).astype(BF16)


def split_dot(dot, a, b):
    return dot(a[0], b[0]) + (dot(a[0], b[1]) + dot(a[1], b[0]))


def low(a):
    return a.astype(BF16)


def sigmoid(a):
    return 1.0 / (1.0 + jnp.exp(-a))


def rms_scale(a):
    return lax.rsqrt(jnp.mean(a * a, axis=-1, keepdims=True) + 1e-05)


def rms_back(hidden, gain, grad_normed):
    scale = rms_scale(hidden)
    weighted = gain * grad_normed
    inner = jnp.mean(hidden * weighted, axis=-1, keepdims=True)
    grad_hidden = scale * weighted - hidden * (scale * scale * scale) * inner
    rows = jnp.sum(grad_normed * hidden * scale, axis=0, keepdims=True)
    return grad_hidden, rows


def shift_down(a, count):
    if count == 0:
        return a
    row = lax.broadcasted_iota(jnp.int32, a.shape, 0)
    return jnp.where(row >= count, pltpu.roll(a, count, 0), 0.0)


def shift_up(a, count):
    if count == 0:
        return a
    length = a.shape[0]
    row = lax.broadcasted_iota(jnp.int32, a.shape, 0)
    return jnp.where(row < length - count, pltpu.roll(a, length - count, 0), 0.0)


def conv_silu(project, taps):
    total = taps[KCONV - 1 : KCONV, :] * project
    for tap in range(KCONV - 1):
        total = total + taps[tap : tap + 1, :] * shift_down(project, KCONV - 1 - tap)
    gate = sigmoid(total)
    return total, gate, total * gate


def positions(length):
    row = lax.broadcasted_iota(jnp.int32, (length, length), 0)
    col = lax.broadcasted_iota(jnp.int32, (length, length), 1)
    return row, col


def unit_lower_inverse(lower_list):
    length = lower_list[0].shape[0]
    row, col = positions(length)
    eye = jnp.where(row == col, 1.0, 0.0)
    diag_list = [jnp.where(row // 4 == col // 4, lower, 0.0) for lower in lower_list]
    parts = [halves(diag) for diag in diag_list]
    squares = [split_dot(dot_nn, part, part) for part in parts]
    firsts = [eye - diag for diag in diag_list]
    inverse = [
        first + split_dot(dot_nn, halves(first), halves(square))
        for first, square in zip(firsts, squares)
    ]
    size = 4
    while size < length:
        fresh = (row // (2 * size) == col // (2 * size)) & (row // size != col // size)
        offs = [halves(jnp.where(fresh, lower, 0.0)) for lower in lower_list]
        held = [halves(inv) for inv in inverse]
        mids = [split_dot(dot_nn, inv, off) for inv, off in zip(held, offs)]
        inverse = [
            inv - split_dot(dot_nn, halves(mid), part)
            for inv, mid, part in zip(inverse, mids, held)
        ]
        size = 2 * size
    return inverse


def head_cols(head):
    return slice(head * DK, (head + 1) * DK)


KEPT = ("x", "n1", "p", "logits", "t", "u", "o", "on", "h", "n2", "gu", "z")


def kept_shapes(length, width, chans, hidden):
    heads = chans // DK
    shapes = dict(
        x=((length, width), F32),
        n1=((length, width), BF16),
        p=((3, length, chans), F32),
        logits=((length, LANES), F32),
        t=((2, heads, length, length), BF16),
        u=((length, chans), BF16),
        o=((length, chans), F32),
        on=((length, chans), BF16),
        h=((length, width), F32),
        n2=((length, width), BF16),
        gu=((2, length, hidden), F32),
        z=((length, hidden), BF16),
    )
    return [((LAYERS, *shapes[name][0]), shapes[name][1]) for name in KEPT]


class Exchange:
    def __init__(self, slots, send_sems, recv_sems):
        self.slots, self.send_sems, self.recv_sems = slots, send_sems, recv_sems
        self.count = slots.shape[1]
        self.me = lax.axis_index("tensor")
        self.others = [
            {"tensor": lax.rem(self.me + away, self.count)} for away in range(1, self.count)
        ]
        self.pending = []

    def greet(self, others=0):
        barrier = pltpu.get_barrier_semaphore()
        for device in self.others:
            pl.semaphore_signal(
                barrier, inc=1, device_id=device, device_id_type=pl.DeviceIdType.MESH
            )
        pl.semaphore_wait(barrier, self.count - 1 + others)

    def copies(self, spot, part, rows):
        mine = self.slots.at[spot, self.me, rows]
        return [
            pltpu.make_async_remote_copy(
                src_ref=mine,
                dst_ref=mine,
                send_sem=self.send_sems.at[spot, part, away],
                recv_sem=self.recv_sems.at[spot, part, away],
                device_id=device,
                device_id_type=pl.DeviceIdType.MESH,
            )
            for away, device in enumerate(self.others)
        ]

    def give(self, spot, part, rows, value):
        self.slots[spot, self.me, rows] = value
        self.send(spot, part, rows)

    def send(self, spot, part, rows):
        for copy in self.copies(spot, part, rows):
            copy.start()
        self.pending.append((spot, part, rows))

    def take(self, spot, part, rows):
        for copy in self.copies(spot, part, rows):
            copy.wait_recv()
        total = self.slots[spot, 0, rows].astype(F32)
        for index in range(1, self.count):
            total = total + self.slots[spot, index, rows].astype(F32)
        return total

    def finish(self):
        for sent in self.pending:
            for copy in self.copies(*sent):
                copy.wait_send()


def forward_kernel(n_parts, *refs):
    (x_ref, gain_ref, taps_ref, head_gain_ref, wb_ref) = refs[:5]
    (wq_hbm, wo_hbm, wgu_hbm, wd_hbm) = refs[5:9]
    count = len(KEPT)
    outs = dict(zip(KEPT, refs[9 : 9 + count]))
    last_out = refs[9 + count]
    held = dict(zip(KEPT, refs[10 + count : 10 + 2 * count]))
    (wq, wo, wgu, wd, slots, last, load_sems, keep_sems, send_sems, recv_sems) = refs[
        10 + 2 * count :
    ]
    exchange = Exchange(slots, send_sems, recv_sems)
    sources = ((wq_hbm, wq), (wo_hbm, wo), (wgu_hbm, wgu), (wd_hbm, wd))
    loads = [
        [
            pltpu.make_async_copy(source.at[level], target.at[level], load_sems.at[level, index])
            for index, (source, target) in enumerate(sources)
        ]
        for level in range(LAYERS)
    ]
    for group in loads:
        for load in group:
            load.start()
    exchange.greet()
    keeps = []

    def keep(name, level):
        copy = pltpu.make_async_copy(
            held[name].at[level], outs[name].at[level], keep_sems.at[KEPT.index(name), level]
        )
        copy.start()
        keeps.append(copy)

    length = x_ref.shape[0]
    heads = wo.shape[1] // DK
    high = length // n_parts
    parts = [(part, slice(part * high, (part + 1) * high)) for part in range(n_parts)]
    row, col = positions(length)
    for level in range(LAYERS):
        for part, rows in parts:
            if level == 0:
                x = x_ref[rows].astype(F32)
            else:
                x = held["h"][level - 1, rows] + exchange.take(2 * level - 1, part, rows)
            held["x"][level, rows] = x
            n1 = low(x * rms_scale(x) * gain_ref[level, 0:1, :].astype(F32))
            held["n1"][level, rows] = n1
            held["logits"][level, rows] = dot_nn(n1, wb_ref[level])
            if part == 0:
                loads[level][0].wait()
            for index in range(3):
                held["p"][level, index, rows] = dot_nn(n1, wq[level, index])
        for name in ("x", "n1", "logits", "p"):
            keep(name, level)
        beta = sigmoid(held["logits"][level])
        acts = [
            conv_silu(held["p"][level, index], taps_ref[level, index].astype(F32))[2]
            for index in range(3)
        ]
        lowers, scores, values = [], [], []
        for head in range(heads):
            cols = head_cols(head)
            c0, c1, c2 = (act[:, cols] for act in acts)
            q = low(c0 * lax.rsqrt(jnp.sum(c0 * c0, axis=-1, keepdims=True) + 0.001))
            k = low(c1 * lax.rsqrt(jnp.sum(c1 * c1, axis=-1, keepdims=True) + 0.001))
            v = low(c2).astype(F32)
            gate = beta[:, head : head + 1]
            lowers.append(jnp.where(row > col, gate * dot_nt(k, k), 0.0))
            scores.append(low(jnp.where(row >= col, dot_nt(q, k), 0.0)))
            values.append(halves(gate * v))
        inverse = unit_lower_inverse(lowers)
        head_gain = head_gain_ref[level : level + 1, :].astype(F32)
        for head in range(heads):
            cols = head_cols(head)
            t_hi, t_lo = halves(inverse[head])
            held["t"][level, 0, head] = t_hi
            held["t"][level, 1, head] = t_lo
            u_low = low(split_dot(dot_nn, (t_hi, t_lo), values[head]))
            held["u"][level, :, cols] = u_low
            o = dot_nn(scores[head], u_low)
            held["o"][level, :, cols] = o
            scale = lax.rsqrt(jnp.mean(o * o, axis=-1, keepdims=True) + 0.01)
            held["on"][level, :, cols] = low(o * scale * head_gain)
        loads[level][1].wait()
        for part, rows in parts:
            out = dot_nn(held["on"][level, rows], wo[level])
            exchange.give(2 * level, part, rows, low(out))
        for name in ("t", "u", "o", "on"):
            keep(name, level)
        for part, rows in parts:
            h = held["x"][level, rows] + exchange.take(2 * level, part, rows)
            held["h"][level, rows] = h
            n2 = low(h * rms_scale(h) * gain_ref[level, 1:2, :].astype(F32))
            held["n2"][level, rows] = n2
            if part == 0:
                loads[level][2].wait()
            g = dot_nn(n2, wgu[level, 0])
            held["gu"][level, 0, rows] = g
            u = dot_nn(n2, wgu[level, 1])
            held["gu"][level, 1, rows] = u
            z = low(g * sigmoid(g) * u)
            held["z"][level, rows] = z
            if part == 0:
                loads[level][3].wait()
            out = low(dot_nn(z, wd[level]))
            if level < LAYERS - 1:
                exchange.give(2 * level + 1, part, rows, out)
            else:
                last[rows] = out
        for name in ("h", "n2", "gu", "z"):
            keep(name, level)
    final = pltpu.make_async_copy(last, last_out, load_sems.at[0, 0])
    final.start()
    for copy in keeps:
        copy.wait()
    final.wait()
    exchange.finish()


def forward(x, norm_gain, taps, head_gain, wb, wq, wo, wgu, wd):
    length, width = x.shape
    chans, hidden = wq.shape[-1], wgu.shape[-1]
    n_tensor = lax.axis_size("tensor")
    n_parts = 2
    kept = kept_shapes(length, width, chans, hidden)
    vmem = pl.BlockSpec(memory_space=pltpu.VMEM)
    hbm = pl.BlockSpec(memory_space=pl.ANY)
    spots = 2 * LAYERS - 1
    *kept, part = pl.pallas_call(
        functools.partial(forward_kernel, n_parts),
        out_shape=(
            *(jax.ShapeDtypeStruct(*spec) for spec in kept),
            jax.ShapeDtypeStruct((length, width), BF16),
        ),
        in_specs=[vmem] * 5 + [hbm] * 4,
        out_specs=(hbm,) * (len(kept) + 1),
        scratch_shapes=[
            *(pltpu.VMEM(*spec) for spec in kept),
            pltpu.VMEM((LAYERS, 3, width, chans), BF16),
            pltpu.VMEM((LAYERS, chans, width), BF16),
            pltpu.VMEM((LAYERS, 2, width, hidden), BF16),
            pltpu.VMEM((LAYERS, hidden, width), BF16),
            pltpu.VMEM((spots, n_tensor, length, width), BF16),
            pltpu.VMEM((length, width), BF16),
            pltpu.SemaphoreType.DMA((LAYERS, 4)),
            pltpu.SemaphoreType.DMA((len(kept), LAYERS)),
            pltpu.SemaphoreType.DMA((spots, n_parts, n_tensor - 1)),
            pltpu.SemaphoreType.DMA((spots, n_parts, n_tensor - 1)),
        ],
        compiler_params=pltpu.CompilerParams(
            vmem_limit_bytes=VMEM_LIMIT, collective_id=1, has_side_effects=True
        ),
        name="forward",
    )(x, norm_gain, taps, head_gain, wb, wq, wo, wgu, wd)
    return dict(zip(KEPT, kept)), part


def back_through_norm(level, which, gain_ref, e_ref, hid_ref, adds, rows_out):
    e = e_ref[...].astype(F32)
    if not adds:
        rows_out[...] = jnp.zeros_like(rows_out)
        return e
    total = adds[0][...].astype(F32)
    for add in adds[1:]:
        total = total + add[...].astype(F32)
    gain = gain_ref[level, which : which + 1, :].astype(F32)
    grad_hidden, rows = rms_back(hid_ref[...], gain, total)
    rows_out[...] = rows
    return e + grad_hidden


def mlp_backward_kernel(level, n_add, *refs):
    (e_ref, hid_ref, *adds) = refs[: 2 + n_add]
    (gain_ref, n2_ref, gu_ref, z_ref, wgu_hbm, wd_hbm) = refs[2 + n_add : 8 + n_add]
    (e_out, rows_out, part_out, gd_out, ggu_out) = refs[8 + n_add : 13 + n_add]
    wgu, wd, dgu_ref, sems = refs[13 + n_add :]
    loads = [
        pltpu.make_async_copy(wd_hbm.at[level], wd, sems.at[0]),
        pltpu.make_async_copy(wgu_hbm.at[level], wgu, sems.at[1]),
    ]
    for load in loads:
        load.start()
    e = back_through_norm(level + 1, 0, gain_ref, e_ref, hid_ref, adds, rows_out)
    e_out[...] = e
    ef = low(e)
    loads[0].wait()
    dz = dot_nt(ef, wd[...])
    g, u = gu_ref[0], gu_ref[1]
    s = sigmoid(g)
    dgu_ref[0] = low(dz * u * (s * (1.0 + g * (1.0 - s))))
    dgu_ref[1] = low(dz * (g * s))
    loads[1].wait()
    part_out[...] = low(dot_nt(dgu_ref[0], wgu[0]) + dot_nt(dgu_ref[1], wgu[1]))
    gd_out[...] = low(dot_tn(z_ref[...], ef))
    for half in range(2):
        ggu_out[half] = low(dot_tn(n2_ref[...], dgu_ref[half]))


def mlp_backward(level, e, hid, adds, norm_gain, n2, gu, z, wgu, wd):
    length, width = e.shape
    hidden = wgu.shape[-1]
    sds = jax.ShapeDtypeStruct
    vmem = pl.BlockSpec(memory_space=pltpu.VMEM)
    hbm = pl.BlockSpec(memory_space=pl.ANY)
    return pl.pallas_call(
        functools.partial(mlp_backward_kernel, level, len(adds)),
        out_shape=(
            sds((length, width), F32),
            sds((1, width), F32),
            sds((length, width), BF16),
            sds((hidden, width), BF16),
            sds((2, width, hidden), BF16),
        ),
        in_specs=[vmem] * (6 + len(adds)) + [hbm, hbm],
        out_specs=(vmem,) * 5,
        scratch_shapes=[
            pltpu.VMEM((2, width, hidden), BF16),
            pltpu.VMEM((hidden, width), BF16),
            pltpu.VMEM((2, length, hidden), BF16),
            pltpu.SemaphoreType.DMA((2,)),
        ],
        compiler_params=pltpu.CompilerParams(vmem_limit_bytes=VMEM_LIMIT),
        name="mlp_backward",
    )(e, hid, *adds, norm_gain, n2, gu, z, wgu, wd)


def mixer_backward_kernel(level, heads, n_add, *refs):
    (e_ref, hid_ref, *adds) = refs[: 2 + n_add]
    (gain_ref, taps_ref, head_gain_ref, wb_ref, n1_ref, p_ref, logit_ref, t_ref, u_ref, o_ref) = (
        refs[2 + n_add : 12 + n_add]
    )
    (on_ref, wq_hbm, wo_hbm) = refs[12 + n_add : 15 + n_add]
    (e_out, part_out, small_out, gq_out, go_out) = refs[15 + n_add : 20 + n_add]
    wq, wo, grads, dp_ref, rows_out, sems = refs[20 + n_add :]
    loads = [
        pltpu.make_async_copy(wo_hbm.at[level], wo, sems.at[0]),
        pltpu.make_async_copy(wq_hbm.at[level], wq, sems.at[1]),
    ]
    for load in loads:
        load.start()
    e = back_through_norm(level, 1, gain_ref, e_ref, hid_ref, adds, rows_out)
    e_out[...] = e
    em = low(e)
    length = e.shape[0]
    loads[0].wait()
    don = dot_nt(em, wo[...])
    go_out[...] = low(dot_tn(on_ref[...], em))
    beta = sigmoid(logit_ref[...])
    row, col = positions(length)
    lane = lax.broadcasted_iota(jnp.int32, (length, LANES), 1)
    head_gain = head_gain_ref[level : level + 1, :].astype(F32)
    convs = [conv_silu(p_ref[part], taps_ref[level, part].astype(F32)) for part in range(3)]
    gain_rows = jnp.zeros((1, DK), F32)
    dlogit = jnp.zeros((length, LANES), F32)
    for head in range(heads):
        cols = head_cols(head)
        c0, c1, c2 = (conv[2][:, cols] for conv in convs)
        rho0 = lax.rsqrt(jnp.sum(c0 * c0, axis=-1, keepdims=True) + 0.001)
        rho1 = lax.rsqrt(jnp.sum(c1 * c1, axis=-1, keepdims=True) + 0.001)
        q, k, v = low(c0 * rho0), low(c1 * rho1), low(c2).astype(F32)
        gate = beta[:, head : head + 1]
        o = o_ref[:, cols]
        scale = lax.rsqrt(jnp.mean(o * o, axis=-1, keepdims=True) + 0.01)
        dn = don[:, cols]
        weighted = dn * head_gain
        inner = jnp.mean(o * weighted, axis=-1, keepdims=True)
        do = low(scale * weighted - o * (scale * scale * scale) * inner)
        gain_rows = gain_rows + jnp.sum(dn * o * scale, axis=0, keepdims=True)
        u = u_ref[:, cols]
        score_t = low(jnp.where(row <= col, dot_nt(k, q), 0.0))
        du = dot_nn(score_t, do)
        ds = low(jnp.where(row >= col, dot_nt(do, u), 0.0))
        ds_t = low(jnp.where(row <= col, dot_nt(u, do), 0.0))
        dq = dot_nn(ds, k)
        dk = dot_nn(ds_t, q)
        r = split_dot(dot_tn, (t_ref[0, head], t_ref[1, head]), halves(du))
        dv = gate * r
        dv_low = low(dv)
        gram = low(jnp.where(row > col, dot_nt(k, k), 0.0))
        w = v - dot_nn(gram, u)
        dbeta = jnp.sum(r * w, axis=-1, keepdims=True)
        dgram = jnp.where(row > col, dot_nt(dv_low, u), 0.0) + jnp.where(
            row < col, dot_nt(u, dv_low), 0.0
        )
        dk = dk - dot_nn(low(dgram), k)
        grads[0, :, cols] = rho0 * dq - c0 * (rho0 * rho0 * rho0) * jnp.sum(
            c0 * dq, axis=-1, keepdims=True
        )
        grads[1, :, cols] = rho1 * dk - c1 * (rho1 * rho1 * rho1) * jnp.sum(
            c1 * dk, axis=-1, keepdims=True
        )
        grads[2, :, cols] = dv
        dlogit = dlogit + jnp.where(lane == head, dbeta * gate * (1.0 - gate), 0.0)
    chans = grads.shape[-1]
    small_out[...] = jnp.zeros_like(small_out)
    small_out[0:1, SIDE : SIDE + DK] = gain_rows
    half = rows_out.shape[-1] // 2
    small_out[1:2, SIDE:] = rows_out[:, :half]
    small_out[2:3, SIDE:] = rows_out[:, half:]
    dlogit_low = low(dlogit)
    n1 = n1_ref[...]
    small_out[3 * KCONV : 3 * KCONV + heads, :] = dot_tn(dlogit_low, n1)[:heads, :]
    for part in range(3):
        taps = taps_ref[level, part].astype(F32)
        total, gate, _ = convs[part]
        dsum = grads[part] * (gate * (1.0 + total * (1.0 - gate)))
        p = p_ref[part]
        dp = taps[KCONV - 1 : KCONV, :] * dsum
        for tap in range(KCONV):
            back = KCONV - 1 - tap
            spot = part * KCONV + tap
            small_out[spot : spot + 1, :chans] = jnp.sum(
                dsum * shift_down(p, back), axis=0, keepdims=True
            )
            if back:
                dp = dp + taps[tap : tap + 1, :] * shift_up(dsum, back)
        dp_ref[part] = low(dp)
    loads[1].wait()
    dn1 = dot_nt(dlogit_low, wb_ref[level])
    for part in range(3):
        dn1 = dn1 + dot_nt(dp_ref[part], wq[part])
    part_out[...] = low(dn1)
    for part in range(3):
        gq_out[part] = low(dot_tn(n1, dp_ref[part]))


def mixer_backward(level, e, hid, adds, norm_gain, taps, head_gain, wb, kept, wq, wo):
    length, width = e.shape
    chans = wq.shape[-1]
    heads = chans // DK
    sds = jax.ShapeDtypeStruct
    vmem = pl.BlockSpec(memory_space=pltpu.VMEM)
    hbm = pl.BlockSpec(memory_space=pl.ANY)
    return pl.pallas_call(
        functools.partial(mixer_backward_kernel, level, heads, len(adds)),
        out_shape=(
            sds((length, width), F32),
            sds((length, width), BF16),
            sds((16, width), F32),
            sds((3, width, chans), BF16),
            sds((chans, width), BF16),
        ),
        in_specs=[vmem] * (13 + len(adds)) + [hbm, hbm],
        out_specs=(vmem,) * 5,
        scratch_shapes=[
            pltpu.VMEM((3, width, chans), BF16),
            pltpu.VMEM((chans, width), BF16),
            pltpu.VMEM((3, length, chans), F32),
            pltpu.VMEM((3, length, chans), BF16),
            pltpu.VMEM((1, width), F32),
            pltpu.SemaphoreType.DMA((2,)),
        ],
        compiler_params=pltpu.CompilerParams(vmem_limit_bytes=VMEM_LIMIT),
        name="mixer_backward",
    )(e, hid, *adds, norm_gain, taps, head_gain, wb, *kept, wq, wo)


def branch_parts(part):
    count = lax.axis_size("tensor")
    if count == 1:
        return (part,)
    if count == 2:
        return (part, lax.ppermute(part, "tensor", [(0, 1), (1, 0)]))
    return (lax.psum(part, "tensor"),)


def sum_over_dp(tables):
    shapes = [table.shape for table in tables]
    flat = jnp.concatenate([table.reshape(-1) for table in tables])
    size = flat.shape[0]
    count = lax.axis_size("dp")
    pad = -size % (count * 1024)
    flat = jnp.pad(flat, (0, pad))
    shard = lax.psum_scatter(flat, "dp", scatter_dimension=0, tiled=True)
    joined = lax.all_gather(shard, "dp", axis=0, tiled=True)
    pieces = []
    offset = 0
    for shape in shapes:
        size = math.prod(shape)
        pieces.append(joined[offset : offset + size].reshape(shape))
        offset = offset + size
    return pieces


def ring_place(n_dp):
    spot = lax.axis_index("dp")
    core = lax.rem(spot, 2)
    side = lax.rem(lax.div(spot, 2), 2)
    depth = lax.div(spot, 4)
    length = n_dp // 2
    return core, depth + side * (length - 1 - 2 * depth), length


def ring_spot(place, core, length):
    side = lax.div(place, length // 2)
    depth = place + side * (length - 1 - 2 * place)
    return (depth * 2 + side) * 2 + core


def remote(source, target, send, recv, device):
    return pltpu.make_async_remote_copy(
        src_ref=source,
        dst_ref=target,
        send_sem=send,
        recv_sem=recv,
        device_id=device,
        device_id_type=pl.DeviceIdType.MESH,
    )


class Ring:
    def __init__(self, n_dp, cuts, own, slots, totals, sems):
        self.cuts, self.own, self.slots, self.totals = cuts, own, slots, totals
        self.send_sems, self.recv_sems, self.fan_sems, self.keep_sems = sems
        self.core, self.place, self.length = ring_place(n_dp)
        self.partner = {"dp": ring_spot(self.place, 1 - self.core, self.length)}
        spots = (
            lax.rem(self.place + 1, self.length),
            lax.rem(self.place + self.length - 1, self.length),
        )
        self.nexts = [{"dp": ring_spot(spot, self.core, self.length)} for spot in spots]
        self.chunks = [
            [
                lax.rem(self.place + self.length + (steps if way else -steps), self.length)
                for steps in range(self.length)
            ]
            for way in range(2)
        ]
        self.done = [0] * len(cuts)
        self.last = 2 * self.length - 2

    def turned(self, way, steps):
        if isinstance(steps, int):
            return self.chunks[way][steps % self.length]
        turn = steps if way else self.length - steps
        return lax.rem(self.place + self.length + turn, self.length)

    def piece(self, index, chunk, way):
        kind, rows, cols = self.cuts[index]
        ref = self.own[index]
        if kind == "cols":
            return ref.at[
                pl.ds(pl.multiple_of(chunk * rows, rows), rows), way * cols : (way + 1) * cols
            ]
        if kind == "rows":
            start = pl.multiple_of(chunk * (2 * rows) + way * rows, rows)
            return ref.at[pl.ds(start, rows), :]
        return ref.at[
            way * rows : (way + 1) * rows, pl.ds(pl.multiple_of(chunk * cols, cols), cols)
        ]

    def spot_of(self, index, chunk, way):
        kind, rows, cols = self.cuts[index]
        ref = self.totals[index]
        if kind == "cols":
            start = pl.multiple_of(self.core * (2 * cols) + way * cols, cols)
            return ref.at[pl.ds(pl.multiple_of(chunk * rows, rows), rows), pl.ds(start, cols)]
        if kind == "rows":
            start = pl.multiple_of(chunk * (2 * rows) + way * rows, rows)
            return ref.at[self.core, pl.ds(start, rows), :]
        start = pl.multiple_of(self.core * (2 * rows) + way * rows, rows)
        return ref.at[pl.ds(start, rows), pl.ds(pl.multiple_of(chunk * cols, cols), cols)]

    def scatter_copy(self, index, way, step):
        return remote(
            self.piece(index, self.turned(way, step), way),
            self.slots[index].at[way, step],
            self.send_sems.at[0, index, way, step],
            self.recv_sems.at[0, index, way, step],
            self.nexts[way],
        )

    def gather_copy(self, index, way, step, first):
        chunk = self.turned(way, step - 1 + self.length)
        target = self.spot_of(index, chunk, way)
        return remote(
            self.piece(index, chunk, way) if first else target,
            target,
            self.send_sems.at[1, index, way, step],
            self.recv_sems.at[1, index, way, step],
            self.nexts[way],
        )

    def fan_copy(self, index, way, step, first):
        chunk = self.turned(way, step - 1 + self.length)
        target = self.spot_of(index, chunk, way)
        return remote(
            self.piece(index, chunk, way) if first else target,
            target,
            self.fan_sems.at[0, index, way, step],
            self.fan_sems.at[1, index, way, step],
            self.partner,
        )

    def keep_copy(self, index, way):
        chunk = self.turned(way, self.length - 1)
        return pltpu.make_async_copy(
            self.piece(index, chunk, way),
            self.spot_of(index, chunk, way),
            self.keep_sems.at[index, way],
        )

    def absorb(self, index, way, step):
        self.scatter_copy(index, way, step - 1).wait_recv()
        mine = self.piece(index, self.turned(way, step), way)
        both = mine[...].astype(F32) + self.slots[index][way, step - 1].astype(F32)
        mine[...] = both.astype(mine.dtype)

    def advance(self, index):
        step = self.done[index]
        if step > self.last:
            return False
        self.done[index] = step + 1
        turn = self.length - 1
        for way in range(2):
            if step < turn:
                if step:
                    self.absorb(index, way, step)
                self.scatter_copy(index, way, step).start()
            elif step == turn:
                self.absorb(index, way, step)
                self.gather_copy(index, way, 0, True).start()
                self.fan_copy(index, way, 0, True).start()
                self.keep_copy(index, way).start()
            else:
                hop = step - turn
                self.gather_copy(index, way, hop - 1, False).wait_recv()
                if hop < turn:
                    self.gather_copy(index, way, hop, False).start()
                self.fan_copy(index, way, hop, False).start()
        return True

    def drain(self):
        streams = [(index, way) for index in range(len(self.cuts)) for way in range(2)]

        def step_waits(step, carry):
            for index, way in streams:
                self.scatter_copy(index, way, step).wait_send()
                self.gather_copy(index, way, step, False).wait_send()
                self.fan_copy(index, way, step, False).wait()
            return carry

        lax.fori_loop(0, self.length - 1, step_waits, 0)
        for index, way in streams:
            self.fan_copy(index, way, self.length - 1, False).wait()
            self.keep_copy(index, way).wait()


def ring_cuts(length, width, chans, hidden):
    if length < 4 or length % 2 or width != length * LANES or chans % (4 * LANES):
        return None
    if hidden % LANES or any(rows % (16 * length) for rows in (hidden, chans, width)):
        return None
    layer = [
        ("cols", hidden // length, width // 4),
        ("rows", width // (2 * length), hidden),
        ("cols", chans // length, width // 4),
        ("cols", 3 * width // length, chans // 4),
    ]
    return layer * LAYERS + [("small", 8, LANES)]


DOWN, GATE_UP, OUT, QKV = range(4)
SMALL = 4 * LAYERS
MLP_KEPT = ("gu", "z", "n2")
MIXER_KEPT = ("n1", "p", "logits", "t", "u", "o", "on", "h")
PEERS = ("z", "n2", "ef", "dgu", "n1", "on", "em", "dp")


def backward_kernel(n_dp, n_parts, cuts, *refs):
    refs = list(refs)

    def taken(count):
        group = refs[:count]
        del refs[:count]
        return group

    (cot_ref, gain_ref, taps_ref, head_gain_ref, wb_ref) = taken(5)
    (part_hbm, wq_hbm, wo_hbm, wgu_hbm, wd_hbm) = taken(5)
    kept = dict(zip(KEPT, taken(len(KEPT))))
    (out_ref, in_grad_ref, *totals) = taken(2 + 5)
    own = taken(len(cuts))
    ring_slots = taken(len(cuts))
    peers = dict(zip(PEERS, taken(len(PEERS))))
    (e_ref, small, small_peer, slots, don_ref) = taken(5)
    (load_sems, send_sems, recv_sems, peer_sems) = taken(4)
    ring_sems = taken(4)

    per_table = [totals[index].at[level] for level in range(LAYERS) for index in range(4)]
    ring = Ring(n_dp, cuts, own, ring_slots, [*per_table, totals[4]], ring_sems)
    core = ring.core
    exchange = Exchange(slots, send_sems, recv_sems)
    barrier = pltpu.get_barrier_semaphore()
    friends = [*ring.nexts, ring.partner]
    for device in friends:
        pl.semaphore_signal(barrier, inc=1, device_id=device, device_id_type=pl.DeviceIdType.MESH)
    exchange.greet(len(friends))

    length, width = e_ref.shape
    chans = wo_hbm.shape[1]
    hidden = wd_hbm.shape[1]
    heads = chans // DK
    high = length // n_parts
    parts = [(part, slice(part * high, (part + 1) * high)) for part in range(n_parts)]
    row, col = positions(length)
    lane = lax.broadcasted_iota(jnp.int32, (length, LANES), 1)
    side = width - SIDE
    half_width, half_chans = width // 2, chans // 2

    def to_peer(name, level, source):
        spot = PEERS.index(name)
        return remote(
            source,
            peers[name].at[level],
            peer_sems.at[0, spot, level],
            peer_sems.at[1, spot, level],
            ring.partner,
        )

    early = [
        to_peer(name, level, kept[name].at[level])
        for level in reversed(range(LAYERS))
        for name in ("z", "n2", "on", "n1")
    ]
    first = pltpu.make_async_copy(part_hbm, slots.at[0, exchange.me], load_sems.at[0, 0, 0])
    first.start()
    small[...] = jnp.zeros_like(small)

    active = []

    def serve(count=1):
        for _ in range(count):
            if not active:
                return
            index = active.pop(0)
            ring.advance(index)
            if ring.done[index] <= ring.last:
                active.append(index)

    def other_half(wide):
        return pl.ds(pl.multiple_of((1 - core) * wide, LANES), wide)

    def own_half(wide):
        return pl.ds(pl.multiple_of(core * wide, LANES), wide)

    def norm_step(level, which, spot, part, rows, hid):
        total = exchange.take(spot, part, rows)
        gain = gain_ref[level, which : which + 1, :].astype(F32)
        grad_hidden, sums = rms_back(hid, gain, total)
        base = 16 * level + (1 if which else 3)
        for index in range(2):
            spot_row = slice(base + index, base + index + 1)
            small[spot_row, SIDE:] += sums[:, index * side : (index + 1) * side]
        return e_ref[rows] + grad_hidden

    def mlp_stage(level):
        def scope(wgu, wd, gu, z, n2, hid, dgu, ef):
            held = dict(gu=gu, z=z, n2=n2)
            loads = {
                "wd": pltpu.make_async_copy(wd_hbm.at[level], wd, load_sems.at[level, 0, 1]),
                "wgu": pltpu.make_async_copy(wgu_hbm.at[level], wgu, load_sems.at[level, 0, 2]),
            }
            for index, name in enumerate(MLP_KEPT):
                loads[name] = pltpu.make_async_copy(
                    kept[name].at[level], held[name], load_sems.at[level, 0, 3 + index]
                )
            if level < LAYERS - 1:
                loads["hid"] = pltpu.make_async_copy(
                    kept["x"].at[level + 1], hid, load_sems.at[level, 0, 6]
                )
                loads["hid"].start()
            for name in ("wd", "gu", "wgu", "z", "n2"):
                loads[name].start()
            if level == LAYERS - 1:
                first.wait()
                for part, rows in parts:
                    exchange.send(0, part, rows)
                for copy in early:
                    copy.start()
            for part, rows in parts:
                serve(3)
                if level == LAYERS - 1:
                    e = cot_ref[rows].astype(F32)
                else:
                    if part == 0:
                        loads["hid"].wait()
                    e = norm_step(level + 1, 0, 2 * (LAYERS - 1 - level), part, rows, hid[rows])
                e_ref[rows] = e
                e_low = low(e)
                ef[rows] = e_low
                if part == 0:
                    loads["wd"].wait()
                dz = dot_nt(e_low, wd[...])
                if part == 0:
                    loads["gu"].wait()
                g, u = gu[0, rows], gu[1, rows]
                s = sigmoid(g)
                dgu[0, rows] = low(dz * u * (s * (1.0 + g * (1.0 - s))))
                dgu[1, rows] = low(dz * (g * s))
                if part == 0:
                    loads["wgu"].wait()
                partial = dot_nt(dgu[0, rows], wgu[0]) + dot_nt(dgu[1, rows], wgu[1])
                exchange.give(2 * (LAYERS - 1 - level) + 1, part, rows, low(partial))
            sends = [
                to_peer("ef", level, ef.at[:, other_half(half_width)]),
                to_peer("dgu", level, dgu.at[1 - core]),
            ]
            for send in sends:
                send.start()
            serve(2)
            loads["z"].wait()
            loads["n2"].wait()
            for name in ("z", "n2", "ef", "dgu"):
                to_peer(name, level, peers[name].at[level]).wait_recv()
            index = 4 * level
            own[index + DOWN][...] = low(
                dot_tn(z[...], ef[:, own_half(half_width)])
                + dot_tn(peers["z"][level], peers["ef"][level])
            )
            active.append(index + DOWN)
            serve(2)
            own[index + GATE_UP][...] = low(
                dot_tn(n2[...], dgu[core]) + dot_tn(peers["n2"][level], peers["dgu"][level])
            )
            active.append(index + GATE_UP)
            serve(2)
            for send in sends:
                send.wait_send()

        pl.run_scoped(
            scope,
            pltpu.VMEM((2, width, hidden), BF16),
            pltpu.VMEM((hidden, width), BF16),
            pltpu.VMEM((2, length, hidden), F32),
            pltpu.VMEM((length, hidden), BF16),
            pltpu.VMEM((length, width), BF16),
            pltpu.VMEM((length, width), F32),
            pltpu.VMEM((2, length, hidden), BF16),
            pltpu.VMEM((length, width), BF16),
        )

    def mixer_stage(level):
        def scope(wq, wo, n1, p, logits, t, u_all, o_all, on, h, grads, dp, em):
            held = dict(n1=n1, p=p, logits=logits, t=t, u=u_all, o=o_all, on=on, h=h)
            loads = {
                "wo": pltpu.make_async_copy(wo_hbm.at[level], wo, load_sems.at[level, 1, 0]),
                "wq": pltpu.make_async_copy(wq_hbm.at[level], wq, load_sems.at[level, 1, 1]),
            }
            for index, name in enumerate(MIXER_KEPT):
                loads[name] = pltpu.make_async_copy(
                    kept[name].at[level], held[name], load_sems.at[level, 1, 2 + index]
                )
            for name in ("h", "wo", "p", "o", "u", "logits", "t", "wq", "n1", "on"):
                loads[name].start()
            serve(1)
            loads["p"].wait()
            convs = [
                conv_silu(p[index], taps_ref[level, index].astype(F32)) for index in range(3)
            ]
            spot = 2 * (LAYERS - 1 - level) + 1
            loads["h"].wait()
            if level == LAYERS - 1:
                for part, rows in parts:
                    out_ref[rows] = low(h[rows] + exchange.take(0, part, rows))
            for part, rows in parts:
                serve(1)
                e = norm_step(level, 1, spot, part, rows, h[rows])
                e_ref[rows] = e
                e_low = low(e)
                em[rows] = e_low
                if part == 0:
                    loads["wo"].wait()
                don_ref[rows] = dot_nt(e_low, wo[...])
            send_em = to_peer("em", level, em.at[:, other_half(half_width)])
            send_em.start()
            for name in ("o", "u", "logits", "t"):
                loads[name].wait()
            beta = sigmoid(logits[...])
            head_gain = head_gain_ref[level : level + 1, :].astype(F32)
            gain_rows = jnp.zeros((1, DK), F32)
            dlogit = jnp.zeros((length, LANES), F32)
            serve(1)
            for head in range(heads):
                cols = head_cols(head)
                c0, c1, c2 = (conv[2][:, cols] for conv in convs)
                rho0 = lax.rsqrt(jnp.sum(c0 * c0, axis=-1, keepdims=True) + 0.001)
                rho1 = lax.rsqrt(jnp.sum(c1 * c1, axis=-1, keepdims=True) + 0.001)
                q, k, v = low(c0 * rho0), low(c1 * rho1), low(c2).astype(F32)
                gate = beta[:, head : head + 1]
                o = o_all[:, cols]
                scale = lax.rsqrt(jnp.mean(o * o, axis=-1, keepdims=True) + 0.01)
                dn = don_ref[:, cols]
                weighted = dn * head_gain
                inner = jnp.mean(o * weighted, axis=-1, keepdims=True)
                do = low(scale * weighted - o * (scale * scale * scale) * inner)
                gain_rows = gain_rows + jnp.sum(dn * o * scale, axis=0, keepdims=True)
                u = u_all[:, cols]
                score_t = low(jnp.where(row <= col, dot_nt(k, q), 0.0))
                du = dot_nn(score_t, do)
                ds = low(jnp.where(row >= col, dot_nt(do, u), 0.0))
                ds_t = low(jnp.where(row <= col, dot_nt(u, do), 0.0))
                dq = dot_nn(ds, k)
                dk = dot_nn(ds_t, q)
                r = split_dot(dot_tn, (t[0, head], t[1, head]), halves(du))
                dv = gate * r
                dv_low = low(dv)
                gram = low(jnp.where(row > col, dot_nt(k, k), 0.0))
                w = v - dot_nn(gram, u)
                dbeta = jnp.sum(r * w, axis=-1, keepdims=True)
                dgram = jnp.where(row > col, dot_nt(dv_low, u), 0.0) + jnp.where(
                    row < col, dot_nt(u, dv_low), 0.0
                )
                dk = dk - dot_nn(low(dgram), k)
                grads[0, :, cols] = rho0 * dq - c0 * (rho0 * rho0 * rho0) * jnp.sum(
                    c0 * dq, axis=-1, keepdims=True
                )
                grads[1, :, cols] = rho1 * dk - c1 * (rho1 * rho1 * rho1) * jnp.sum(
                    c1 * dk, axis=-1, keepdims=True
                )
                grads[2, :, cols] = dv
                dlogit = dlogit + jnp.where(lane == head, dbeta * gate * (1.0 - gate), 0.0)
                if head % 2:
                    serve(1)
            base = 16 * level
            small[base : base + 1, SIDE : SIDE + DK] = gain_rows
            for index in range(3):
                taps = taps_ref[level, index].astype(F32)
                total, gate, _ = convs[index]
                dsum = grads[index] * (gate * (1.0 + total * (1.0 - gate)))
                project = p[index]
                dproject = taps[KCONV - 1 : KCONV, :] * dsum
                for tap in range(KCONV):
                    back = KCONV - 1 - tap
                    line = base + index * KCONV + tap
                    small[line : line + 1, :chans] = jnp.sum(
                        dsum * shift_down(project, back), axis=0, keepdims=True
                    )
                    if back:
                        dproject = dproject + taps[tap : tap + 1, :] * shift_up(dsum, back)
                dp[index] = low(dproject)
            dlogit_low = low(dlogit)
            loads["wq"].wait()
            for part, rows in parts:
                dn1 = dot_nt(dlogit_low[rows], wb_ref[level])
                for index in range(3):
                    dn1 = dn1 + dot_nt(dp[index, rows], wq[index])
                exchange.give(spot + 1, part, rows, low(dn1))
            send_dp = to_peer("dp", level, dp.at[:, :, other_half(half_chans)])
            send_dp.start()
            serve(1)
            loads["n1"].wait()
            loads["on"].wait()
            line = base + 3 * KCONV
            small[line : line + heads, :] = dot_tn(dlogit_low, n1[...])[:heads, :]
            for name in ("em", "on", "n1", "dp"):
                to_peer(name, level, peers[name].at[level]).wait_recv()
            own[4 * level + OUT][...] = low(
                dot_tn(on[...], em[:, own_half(half_width)])
                + dot_tn(peers["on"][level], peers["em"][level])
            )
            active.append(4 * level + OUT)
            serve(1)
            for index in range(3):
                own[4 * level + QKV][index * width : (index + 1) * width] = low(
                    dot_tn(n1[...], dp[index, :, own_half(half_chans)])
                    + dot_tn(peers["n1"][level], peers["dp"][level, index])
                )
            active.append(4 * level + QKV)
            serve(1)
            send_em.wait_send()
            send_dp.wait_send()

        pl.run_scoped(
            scope,
            pltpu.VMEM((3, width, chans), BF16),
            pltpu.VMEM((chans, width), BF16),
            pltpu.VMEM((length, width), BF16),
            pltpu.VMEM((3, length, chans), F32),
            pltpu.VMEM((length, LANES), F32),
            pltpu.VMEM((2, heads, length, length), BF16),
            pltpu.VMEM((length, chans), BF16),
            pltpu.VMEM((length, chans), F32),
            pltpu.VMEM((length, chans), BF16),
            pltpu.VMEM((length, width), F32),
            pltpu.VMEM((3, length, chans), F32),
            pltpu.VMEM((3, length, chans), BF16),
            pltpu.VMEM((length, width), BF16),
        )

    for level in reversed(range(LAYERS)):
        mlp_stage(level)
        mixer_stage(level)

    def last_scope(hid):
        load = pltpu.make_async_copy(kept["x"].at[0], hid, load_sems.at[0, 0, 7])
        load.start()
        serve(len(active))
        load.wait()
        for part, rows in parts:
            in_grad_ref[rows] = low(norm_step(0, 0, 2 * LAYERS, part, rows, hid[rows]))

    pl.run_scoped(last_scope, pltpu.VMEM((length, width), F32))

    def small_half(which):
        return small.at[pl.ds(pl.multiple_of(which * 16, 16), 16)]

    send_small = remote(
        small_half(1 - core),
        small_peer,
        load_sems.at[1, 0, 6],
        load_sems.at[1, 0, 7],
        ring.partner,
    )
    send_small.start()
    serve(len(active))
    send_small.wait_recv()
    own[SMALL][...] = small_half(core)[...] + small_peer[...]
    active.append(SMALL)
    while active:
        serve(1)
    send_small.wait_send()
    for copy in early:
        copy.wait_send()
    exchange.finish()
    ring.drain()


def backward(cot, part, saved, norm_gain, taps, head_gain, wb, wq, wo, wgu, wd):
    length, width = cot.shape
    chans, hidden = wq.shape[-1], wgu.shape[-1]
    heads = chans // DK
    n_dp, n_tensor = lax.axis_size("dp"), lax.axis_size("tensor")
    size = n_dp // 2
    cuts = ring_cuts(size, width, chans, hidden)
    n_parts = 2
    sds = jax.ShapeDtypeStruct
    vmem = pl.BlockSpec(memory_space=pltpu.VMEM)
    hbm = pl.BlockSpec(memory_space=pl.ANY)
    own, slots = [], []
    for kind, rows, cols in cuts:
        dtype = F32 if kind == "small" else BF16
        half = {
            "cols": (rows * size, 2 * cols),
            "rows": (2 * rows * size, cols),
            "small": (2 * rows, cols * size),
        }[kind]
        own.append(pltpu.VMEM(half, dtype))
        slots.append(pltpu.VMEM((2, size - 1, rows, cols), dtype))
    peers = dict(
        z=(length, hidden),
        n2=(length, width),
        ef=(length, width // 2),
        dgu=(length, hidden),
        n1=(length, width),
        on=(length, chans),
        em=(length, width // 2),
        dp=(3, length, chans // 2),
    )
    spots = 2 * LAYERS + 1
    count = len(cuts)
    return pl.pallas_call(
        functools.partial(backward_kernel, n_dp, n_parts, cuts),
        out_shape=(
            sds((length, width), BF16),
            sds((length, width), BF16),
            sds((LAYERS, hidden, width), BF16),
            sds((LAYERS, 2, width, hidden), BF16),
            sds((LAYERS, chans, width), BF16),
            sds((LAYERS, 3 * width, chans), BF16),
            sds((16 * LAYERS, width), F32),
        ),
        in_specs=[vmem] * 5 + [hbm] * (5 + len(KEPT)),
        out_specs=(vmem, vmem) + (hbm,) * 5,
        scratch_shapes=[
            *own,
            *slots,
            *(pltpu.VMEM((LAYERS, *peers[name]), BF16) for name in PEERS),
            pltpu.VMEM((length, width), F32),
            pltpu.VMEM((16 * LAYERS, width), F32),
            pltpu.VMEM((16, width), F32),
            pltpu.VMEM((spots, n_tensor, length, width), BF16),
            pltpu.VMEM((length, chans), F32),
            pltpu.SemaphoreType.DMA((LAYERS, 2, 10)),
            pltpu.SemaphoreType.DMA((spots, n_parts, n_tensor - 1)),
            pltpu.SemaphoreType.DMA((spots, n_parts, n_tensor - 1)),
            pltpu.SemaphoreType.DMA((2, len(PEERS), LAYERS)),
            pltpu.SemaphoreType.DMA((2, count, 2, size - 1)),
            pltpu.SemaphoreType.DMA((2, count, 2, size - 1)),
            pltpu.SemaphoreType.DMA((2, count, 2, size)),
            pltpu.SemaphoreType.DMA((count, 2)),
        ],
        compiler_params=pltpu.CompilerParams(
            vmem_limit_bytes=VMEM_LIMIT, collective_id=0, has_side_effects=True
        ),
        name="backward",
    )(cot, norm_gain, taps, head_gain, wb, part, wq, wo, wgu, wd, *(saved[name] for name in KEPT))


def staged_backward(cot, part, saved, norm_gain, taps, head_gain, wb, wq, wo, wgu, wd):
    total = saved["h"][LAYERS - 1]
    for add in branch_parts(part):
        total = total + add.astype(F32)
    outputs = total.astype(BF16)
    e, hid, adds = cot, saved["x"][LAYERS - 1], ()
    gain_rows = {}
    small = [None] * LAYERS
    big = [None] * LAYERS
    for level in reversed(range(LAYERS)):
        at = {name: saved[name][level] for name in KEPT}
        mlp_kept = tuple(at[name] for name in ("n2", "gu", "z"))
        mixer_kept = tuple(at[name] for name in ("n1", "p", "logits", "t", "u", "o", "on"))
        e, rows, part, grad_down, grad_gate_up = mlp_backward(
            level, e, hid, adds, norm_gain, *mlp_kept, wgu, wd
        )
        gain_rows[level + 1] = rows
        e, part, small[level], grad_qkv, grad_out = mixer_backward(
            level,
            e,
            at["h"],
            branch_parts(part),
            norm_gain,
            taps,
            head_gain,
            wb,
            mixer_kept,
            wq,
            wo,
        )
        hid, adds = at["x"], branch_parts(part)
        big[level] = (grad_down, grad_gate_up, grad_out, grad_qkv)
    branch = adds[0].astype(F32)
    for add in adds[1:]:
        branch = branch + add.astype(F32)
    grad_hidden, rows = rms_back(hid, norm_gain[0, 0:1].astype(F32), branch)
    gain_rows[0] = rows
    input_grad = (e + grad_hidden).astype(BF16)
    side = rows.shape[-1] - SIDE
    small_all = jnp.concatenate(
        [
            small[level].at[3:5, SIDE:].set(gain_rows[level].reshape(2, side))
            for level in range(LAYERS)
        ]
    )
    tables = [table for group in big for table in group]
    sums = sum_over_dp(tables)
    stacked = [jnp.stack([sums[index], sums[4 + index]]) for index in range(4)]
    return (outputs, input_grad, *stacked, lax.psum(small_all, "dp"))


def body(
    inputs,
    qkv_weight,
    conv_taps,
    beta_weight,
    out_gain,
    out_weight,
    norm_gain,
    gate_up_weight,
    down_weight,
    cotangent,
):
    heads = beta_weight.shape[-1]
    wb = jnp.pad(beta_weight, ((0, 0), (0, 0), (0, LANES - heads)))
    saved, part = forward(
        inputs,
        norm_gain,
        conv_taps,
        out_gain,
        wb,
        qkv_weight,
        out_weight,
        gate_up_weight,
        down_weight,
    )
    length, width = inputs.shape
    chans, hidden = conv_taps.shape[-1], down_weight.shape[1]
    n_dp = lax.axis_size("dp")
    ringed = n_dp % 4 == 0 and ring_cuts(n_dp // 2, width, chans, hidden) is not None
    if ringed:
        outputs, input_grad, *big, small_all = backward(
            cotangent,
            part,
            saved,
            norm_gain,
            conv_taps,
            out_gain,
            wb,
            qkv_weight,
            out_weight,
            gate_up_weight,
            down_weight,
        )
    else:
        outputs, input_grad, *big, small_all = staged_backward(
            cotangent,
            part,
            saved,
            norm_gain,
            conv_taps,
            out_gain,
            wb,
            qkv_weight,
            out_weight,
            gate_up_weight,
            down_weight,
        )
    small_all = small_all.reshape(LAYERS, 16, -1)
    grad_conv = small_all[:, : 3 * KCONV, :chans].reshape(conv_taps.shape)
    grad_beta = small_all[:, 3 * KCONV : 3 * KCONV + heads].transpose(0, 2, 1)
    grad_norm = jnp.stack(
        [
            small_all[:, 3:5, SIDE:].reshape(LAYERS, -1),
            small_all[:, 1:3, SIDE:].reshape(LAYERS, -1),
        ],
        axis=1,
    )
    grad_out_gain = small_all[:, 0, SIDE : SIDE + DK]
    grad_out_gain = sum(branch_parts(grad_out_gain))
    shapes = (down_weight.shape, gate_up_weight.shape, out_weight.shape, qkv_weight.shape)
    grad_down, grad_gate_up, grad_out, grad_qkv = (
        table.reshape(shape).astype(F32) for table, shape in zip(big, shapes)
    )
    return (
        outputs,
        input_grad,
        grad_qkv,
        grad_conv,
        grad_beta,
        grad_out_gain,
        grad_out,
        grad_norm,
        grad_gate_up,
        grad_down,
    )


def solution(mesh):
    in_specs = (
        P("dp", None),
        P(None, None, None, "tensor"),
        P(None, None, None, "tensor"),
        P(None, None, "tensor"),
        P(),
        P(None, "tensor", None),
        P(),
        P(None, None, None, "tensor"),
        P(None, "tensor", None),
        P("dp", None),
    )
    out_specs = (
        P("dp", None),
        P("dp", None),
        P(None, None, None, "tensor"),
        P(None, None, None, "tensor"),
        P(None, None, "tensor"),
        P(),
        P(None, "tensor", None),
        P(),
        P(None, None, None, "tensor"),
        P(None, "tensor", None),
    )
    return jax.shard_map(body, mesh=mesh, in_specs=in_specs, out_specs=out_specs, check_vma=False)
```

```python
import functools
import math

import jax
import jax.numpy as jnp
from jax import lax
from jax.experimental import pallas as pl
from jax.experimental.pallas import tpu as pltpu
from jax.sharding import PartitionSpec as P

DK = 128
KCONV = 4
LAYERS = 2
LANES = 128
SIDE = 512
F32 = jnp.float32
BF16 = jnp.bfloat16
VMEM_LIMIT = 60 * 1024 * 1024


def dot_nn(a, b):
    return lax.dot_general(a, b, (((1,), (0,)), ((), ())), preferred_element_type=F32)


def dot_nt(a, b):
    return lax.dot_general(a, b, (((1,), (1,)), ((), ())), preferred_element_type=F32)


def dot_tn(a, b):
    return lax.dot_general(a, b, (((0,), (0,)), ((), ())), preferred_element_type=F32)


def halves(a):
    hi = a.astype(BF16)
    return hi, (a - hi.astype(F32)).astype(BF16)


def split_dot(dot, a, b):
    return dot(a[0], b[0]) + (dot(a[0], b[1]) + dot(a[1], b[0]))


def low(a):
    return a.astype(BF16)


def sigmoid(a):
    return 1.0 / (1.0 + jnp.exp(-a))


def rms_scale(a):
    return lax.rsqrt(jnp.mean(a * a, axis=-1, keepdims=True) + 1e-05)


def rms_back(hidden, gain, grad_normed):
    scale = rms_scale(hidden)
    weighted = gain * grad_normed
    inner = jnp.mean(hidden * weighted, axis=-1, keepdims=True)
    grad_hidden = scale * weighted - hidden * (scale * scale * scale) * inner
    rows = jnp.sum(grad_normed * hidden * scale, axis=0, keepdims=True)
    return grad_hidden, rows


def shift_down(a, count):
    if count == 0:
        return a
    row = lax.broadcasted_iota(jnp.int32, a.shape, 0)
    return jnp.where(row >= count, pltpu.roll(a, count, 0), 0.0)


def shift_up(a, count):
    if count == 0:
        return a
    length = a.shape[0]
    row = lax.broadcasted_iota(jnp.int32, a.shape, 0)
    return jnp.where(row < length - count, pltpu.roll(a, length - count, 0), 0.0)


def conv_silu(project, taps):
    total = taps[KCONV - 1 : KCONV, :] * project
    for tap in range(KCONV - 1):
        total = total + taps[tap : tap + 1, :] * shift_down(project, KCONV - 1 - tap)
    gate = sigmoid(total)
    return total, gate, total * gate


def positions(length):
    row = lax.broadcasted_iota(jnp.int32, (length, length), 0)
    col = lax.broadcasted_iota(jnp.int32, (length, length), 1)
    return row, col


def unit_lower_inverse(lower_list):
    length = lower_list[0].shape[0]
    row, col = positions(length)
    eye = jnp.where(row == col, 1.0, 0.0)
    diag_list = [jnp.where(row // 4 == col // 4, lower, 0.0) for lower in lower_list]
    parts = [halves(diag) for diag in diag_list]
    squares = [split_dot(dot_nn, part, part) for part in parts]
    firsts = [eye - diag for diag in diag_list]
    inverse = [
        first + split_dot(dot_nn, halves(first), halves(square))
        for first, square in zip(firsts, squares)
    ]
    size = 4
    while size < length:
        fresh = (row // (2 * size) == col // (2 * size)) & (row // size != col // size)
        offs = [halves(jnp.where(fresh, lower, 0.0)) for lower in lower_list]
        held = [halves(inv) for inv in inverse]
        mids = [split_dot(dot_nn, inv, off) for inv, off in zip(held, offs)]
        inverse = [
            inv - split_dot(dot_nn, halves(mid), part)
            for inv, mid, part in zip(inverse, mids, held)
        ]
        size = 2 * size
    return inverse


def head_cols(head):
    return slice(head * DK, (head + 1) * DK)


KEPT = ("x", "n1", "p", "logits", "t", "u", "o", "on", "h", "n2", "gu", "z")


def kept_shapes(length, width, chans, hidden):
    heads = chans // DK
    shapes = dict(
        x=((length, width), F32),
        n1=((length, width), BF16),
        p=((3, length, chans), F32),
        logits=((length, LANES), F32),
        t=((2, heads, length, length), BF16),
        u=((length, chans), BF16),
        o=((length, chans), F32),
        on=((length, chans), BF16),
        h=((length, width), F32),
        n2=((length, width), BF16),
        gu=((2, length, hidden), F32),
        z=((length, hidden), BF16),
    )
    return [((LAYERS, *shapes[name][0]), shapes[name][1]) for name in KEPT]


class Exchange:
    def __init__(self, slots, send_sems, recv_sems):
        self.slots, self.send_sems, self.recv_sems = slots, send_sems, recv_sems
        self.count = slots.shape[1]
        self.me = lax.axis_index("tensor")
        self.others = [
            {"tensor": lax.rem(self.me + away, self.count)} for away in range(1, self.count)
        ]
        self.pending = []

    def greet(self, others=0):
        barrier = pltpu.get_barrier_semaphore()
        for device in self.others:
            pl.semaphore_signal(
                barrier, inc=1, device_id=device, device_id_type=pl.DeviceIdType.MESH
            )
        pl.semaphore_wait(barrier, self.count - 1 + others)

    def copies(self, spot, part, rows):
        mine = self.slots.at[spot, self.me, rows]
        return [
            pltpu.make_async_remote_copy(
                src_ref=mine,
                dst_ref=mine,
                send_sem=self.send_sems.at[spot, part, away],
                recv_sem=self.recv_sems.at[spot, part, away],
                device_id=device,
                device_id_type=pl.DeviceIdType.MESH,
            )
            for away, device in enumerate(self.others)
        ]

    def give(self, spot, part, rows, value):
        self.slots[spot, self.me, rows] = value
        self.send(spot, part, rows)

    def send(self, spot, part, rows):
        for copy in self.copies(spot, part, rows):
            copy.start()
        self.pending.append((spot, part, rows))

    def take(self, spot, part, rows):
        for copy in self.copies(spot, part, rows):
            copy.wait_recv()
        total = self.slots[spot, 0, rows].astype(F32)
        for index in range(1, self.count):
            total = total + self.slots[spot, index, rows].astype(F32)
        return total

    def finish(self):
        for sent in self.pending:
            for copy in self.copies(*sent):
                copy.wait_send()


def forward_kernel(n_parts, *refs):
    (x_ref, gain_ref, taps_ref, head_gain_ref, wb_ref) = refs[:5]
    (wq_hbm, wo_hbm, wgu_hbm, wd_hbm) = refs[5:9]
    count = len(KEPT)
    outs = dict(zip(KEPT, refs[9 : 9 + count]))
    last_out = refs[9 + count]
    held = dict(zip(KEPT, refs[10 + count : 10 + 2 * count]))
    (wq, wo, wgu, wd, slots, last, load_sems, keep_sems, send_sems, recv_sems) = refs[
        10 + 2 * count :
    ]
    exchange = Exchange(slots, send_sems, recv_sems)
    sources = ((wq_hbm, wq), (wo_hbm, wo), (wgu_hbm, wgu), (wd_hbm, wd))
    loads = [
        [
            pltpu.make_async_copy(source.at[level], target.at[level], load_sems.at[level, index])
            for index, (source, target) in enumerate(sources)
        ]
        for level in range(LAYERS)
    ]
    for group in loads:
        for load in group:
            load.start()
    exchange.greet()
    keeps = []

    def keep(name, level):
        copy = pltpu.make_async_copy(
            held[name].at[level], outs[name].at[level], keep_sems.at[KEPT.index(name), level]
        )
        copy.start()
        keeps.append(copy)

    length = x_ref.shape[0]
    heads = wo.shape[1] // DK
    high = length // n_parts
    parts = [(part, slice(part * high, (part + 1) * high)) for part in range(n_parts)]
    row, col = positions(length)
    for level in range(LAYERS):
        for part, rows in parts:
            if level == 0:
                x = x_ref[rows].astype(F32)
            else:
                x = held["h"][level - 1, rows] + exchange.take(2 * level - 1, part, rows)
            held["x"][level, rows] = x
            n1 = low(x * rms_scale(x) * gain_ref[level, 0:1, :].astype(F32))
            held["n1"][level, rows] = n1
            held["logits"][level, rows] = dot_nn(n1, wb_ref[level])
            if part == 0:
                loads[level][0].wait()
            for index in range(3):
                held["p"][level, index, rows] = dot_nn(n1, wq[level, index])
        for name in ("x", "n1", "logits", "p"):
            keep(name, level)
        beta = sigmoid(held["logits"][level])
        acts = [
            conv_silu(held["p"][level, index], taps_ref[level, index].astype(F32))[2]
            for index in range(3)
        ]
        lowers, scores, values = [], [], []
        for head in range(heads):
            cols = head_cols(head)
            c0, c1, c2 = (act[:, cols] for act in acts)
            q = low(c0 * lax.rsqrt(jnp.sum(c0 * c0, axis=-1, keepdims=True) + 0.001))
            k = low(c1 * lax.rsqrt(jnp.sum(c1 * c1, axis=-1, keepdims=True) + 0.001))
            v = low(c2).astype(F32)
            gate = beta[:, head : head + 1]
            lowers.append(jnp.where(row > col, gate * dot_nt(k, k), 0.0))
            scores.append(low(jnp.where(row >= col, dot_nt(q, k), 0.0)))
            values.append(halves(gate * v))
        inverse = unit_lower_inverse(lowers)
        head_gain = head_gain_ref[level : level + 1, :].astype(F32)
        for head in range(heads):
            cols = head_cols(head)
            t_hi, t_lo = halves(inverse[head])
            held["t"][level, 0, head] = t_hi
            held["t"][level, 1, head] = t_lo
            u_low = low(split_dot(dot_nn, (t_hi, t_lo), values[head]))
            held["u"][level, :, cols] = u_low
            o = dot_nn(scores[head], u_low)
            held["o"][level, :, cols] = o
            scale = lax.rsqrt(jnp.mean(o * o, axis=-1, keepdims=True) + 0.01)
            held["on"][level, :, cols] = low(o * scale * head_gain)
        loads[level][1].wait()
        for part, rows in parts:
            out = dot_nn(held["on"][level, rows], wo[level])
            exchange.give(2 * level, part, rows, low(out))
        for name in ("t", "u", "o", "on"):
            keep(name, level)
        for part, rows in parts:
            h = held["x"][level, rows] + exchange.take(2 * level, part, rows)
            held["h"][level, rows] = h
            n2 = low(h * rms_scale(h) * gain_ref[level, 1:2, :].astype(F32))
            held["n2"][level, rows] = n2
            if part == 0:
                loads[level][2].wait()
            g = dot_nn(n2, wgu[level, 0])
            held["gu"][level, 0, rows] = g
            u = dot_nn(n2, wgu[level, 1])
            held["gu"][level, 1, rows] = u
            z = low(g * sigmoid(g) * u)
            held["z"][level, rows] = z
            if part == 0:
                loads[level][3].wait()
            out = low(dot_nn(z, wd[level]))
            if level < LAYERS - 1:
                exchange.give(2 * level + 1, part, rows, out)
            else:
                last[rows] = out
        for name in ("h", "n2", "gu", "z"):
            keep(name, level)
    final = pltpu.make_async_copy(last, last_out, load_sems.at[0, 0])
    final.start()
    for copy in keeps:
        copy.wait()
    final.wait()
    exchange.finish()


def forward(x, norm_gain, taps, head_gain, wb, wq, wo, wgu, wd):
    length, width = x.shape
    chans, hidden = wq.shape[-1], wgu.shape[-1]
    n_tensor = lax.axis_size("tensor")
    n_parts = 2
    kept = kept_shapes(length, width, chans, hidden)
    vmem = pl.BlockSpec(memory_space=pltpu.VMEM)
    hbm = pl.BlockSpec(memory_space=pl.ANY)
    spots = 2 * LAYERS - 1
    *kept, part = pl.pallas_call(
        functools.partial(forward_kernel, n_parts),
        out_shape=(
            *(jax.ShapeDtypeStruct(*spec) for spec in kept),
            jax.ShapeDtypeStruct((length, width), BF16),
        ),
        in_specs=[vmem] * 5 + [hbm] * 4,
        out_specs=(hbm,) * (len(kept) + 1),
        scratch_shapes=[
            *(pltpu.VMEM(*spec) for spec in kept),
            pltpu.VMEM((LAYERS, 3, width, chans), BF16),
            pltpu.VMEM((LAYERS, chans, width), BF16),
            pltpu.VMEM((LAYERS, 2, width, hidden), BF16),
            pltpu.VMEM((LAYERS, hidden, width), BF16),
            pltpu.VMEM((spots, n_tensor, length, width), BF16),
            pltpu.VMEM((length, width), BF16),
            pltpu.SemaphoreType.DMA((LAYERS, 4)),
            pltpu.SemaphoreType.DMA((len(kept), LAYERS)),
            pltpu.SemaphoreType.DMA((spots, n_parts, n_tensor - 1)),
            pltpu.SemaphoreType.DMA((spots, n_parts, n_tensor - 1)),
        ],
        compiler_params=pltpu.CompilerParams(
            vmem_limit_bytes=VMEM_LIMIT, collective_id=1, has_side_effects=True
        ),
        name="forward",
    )(x, norm_gain, taps, head_gain, wb, wq, wo, wgu, wd)
    return dict(zip(KEPT, kept)), part


def back_through_norm(level, which, gain_ref, e_ref, hid_ref, adds, rows_out):
    e = e_ref[...].astype(F32)
    if not adds:
        rows_out[...] = jnp.zeros_like(rows_out)
        return e
    total = adds[0][...].astype(F32)
    for add in adds[1:]:
        total = total + add[...].astype(F32)
    gain = gain_ref[level, which : which + 1, :].astype(F32)
    grad_hidden, rows = rms_back(hid_ref[...], gain, total)
    rows_out[...] = rows
    return e + grad_hidden


def mlp_backward_kernel(level, n_add, *refs):
    (e_ref, hid_ref, *adds) = refs[: 2 + n_add]
    (gain_ref, n2_ref, gu_ref, z_ref, wgu_hbm, wd_hbm) = refs[2 + n_add : 8 + n_add]
    (e_out, rows_out, part_out, gd_out, ggu_out) = refs[8 + n_add : 13 + n_add]
    wgu, wd, dgu_ref, sems = refs[13 + n_add :]
    loads = [
        pltpu.make_async_copy(wd_hbm.at[level], wd, sems.at[0]),
        pltpu.make_async_copy(wgu_hbm.at[level], wgu, sems.at[1]),
    ]
    for load in loads:
        load.start()
    e = back_through_norm(level + 1, 0, gain_ref, e_ref, hid_ref, adds, rows_out)
    e_out[...] = e
    ef = low(e)
    loads[0].wait()
    dz = dot_nt(ef, wd[...])
    g, u = gu_ref[0], gu_ref[1]
    s = sigmoid(g)
    dgu_ref[0] = low(dz * u * (s * (1.0 + g * (1.0 - s))))
    dgu_ref[1] = low(dz * (g * s))
    loads[1].wait()
    part_out[...] = low(dot_nt(dgu_ref[0], wgu[0]) + dot_nt(dgu_ref[1], wgu[1]))
    gd_out[...] = low(dot_tn(z_ref[...], ef))
    for half in range(2):
        ggu_out[half] = low(dot_tn(n2_ref[...], dgu_ref[half]))


def mlp_backward(level, e, hid, adds, norm_gain, n2, gu, z, wgu, wd):
    length, width = e.shape
    hidden = wgu.shape[-1]
    sds = jax.ShapeDtypeStruct
    vmem = pl.BlockSpec(memory_space=pltpu.VMEM)
    hbm = pl.BlockSpec(memory_space=pl.ANY)
    return pl.pallas_call(
        functools.partial(mlp_backward_kernel, level, len(adds)),
        out_shape=(
            sds((length, width), F32),
            sds((1, width), F32),
            sds((length, width), BF16),
            sds((hidden, width), BF16),
            sds((2, width, hidden), BF16),
        ),
        in_specs=[vmem] * (6 + len(adds)) + [hbm, hbm],
        out_specs=(vmem,) * 5,
        scratch_shapes=[
            pltpu.VMEM((2, width, hidden), BF16),
            pltpu.VMEM((hidden, width), BF16),
            pltpu.VMEM((2, length, hidden), BF16),
            pltpu.SemaphoreType.DMA((2,)),
        ],
        compiler_params=pltpu.CompilerParams(vmem_limit_bytes=VMEM_LIMIT),
        name="mlp_backward",
    )(e, hid, *adds, norm_gain, n2, gu, z, wgu, wd)


def mixer_backward_kernel(level, heads, n_add, *refs):
    (e_ref, hid_ref, *adds) = refs[: 2 + n_add]
    (gain_ref, taps_ref, head_gain_ref, wb_ref, n1_ref, p_ref, logit_ref, t_ref, u_ref, o_ref) = (
        refs[2 + n_add : 12 + n_add]
    )
    (on_ref, wq_hbm, wo_hbm) = refs[12 + n_add : 15 + n_add]
    (e_out, part_out, small_out, gq_out, go_out) = refs[15 + n_add : 20 + n_add]
    wq, wo, grads, dp_ref, rows_out, sems = refs[20 + n_add :]
    loads = [
        pltpu.make_async_copy(wo_hbm.at[level], wo, sems.at[0]),
        pltpu.make_async_copy(wq_hbm.at[level], wq, sems.at[1]),
    ]
    for load in loads:
        load.start()
    e = back_through_norm(level, 1, gain_ref, e_ref, hid_ref, adds, rows_out)
    e_out[...] = e
    em = low(e)
    length = e.shape[0]
    loads[0].wait()
    don = dot_nt(em, wo[...])
    go_out[...] = low(dot_tn(on_ref[...], em))
    beta = sigmoid(logit_ref[...])
    row, col = positions(length)
    lane = lax.broadcasted_iota(jnp.int32, (length, LANES), 1)
    head_gain = head_gain_ref[level : level + 1, :].astype(F32)
    convs = [conv_silu(p_ref[part], taps_ref[level, part].astype(F32)) for part in range(3)]
    gain_rows = jnp.zeros((1, DK), F32)
    dlogit = jnp.zeros((length, LANES), F32)
    for head in range(heads):
        cols = head_cols(head)
        c0, c1, c2 = (conv[2][:, cols] for conv in convs)
        rho0 = lax.rsqrt(jnp.sum(c0 * c0, axis=-1, keepdims=True) + 0.001)
        rho1 = lax.rsqrt(jnp.sum(c1 * c1, axis=-1, keepdims=True) + 0.001)
        q, k, v = low(c0 * rho0), low(c1 * rho1), low(c2).astype(F32)
        gate = beta[:, head : head + 1]
        o = o_ref[:, cols]
        scale = lax.rsqrt(jnp.mean(o * o, axis=-1, keepdims=True) + 0.01)
        dn = don[:, cols]
        weighted = dn * head_gain
        inner = jnp.mean(o * weighted, axis=-1, keepdims=True)
        do = low(scale * weighted - o * (scale * scale * scale) * inner)
        gain_rows = gain_rows + jnp.sum(dn * o * scale, axis=0, keepdims=True)
        u = u_ref[:, cols]
        score_t = low(jnp.where(row <= col, dot_nt(k, q), 0.0))
        du = dot_nn(score_t, do)
        ds = low(jnp.where(row >= col, dot_nt(do, u), 0.0))
        ds_t = low(jnp.where(row <= col, dot_nt(u, do), 0.0))
        dq = dot_nn(ds, k)
        dk = dot_nn(ds_t, q)
        r = split_dot(dot_tn, (t_ref[0, head], t_ref[1, head]), halves(du))
        dv = gate * r
        dv_low = low(dv)
        gram = low(jnp.where(row > col, dot_nt(k, k), 0.0))
        w = v - dot_nn(gram, u)
        dbeta = jnp.sum(r * w, axis=-1, keepdims=True)
        dgram = jnp.where(row > col, dot_nt(dv_low, u), 0.0) + jnp.where(
            row < col, dot_nt(u, dv_low), 0.0
        )
        dk = dk - dot_nn(low(dgram), k)
        grads[0, :, cols] = rho0 * dq - c0 * (rho0 * rho0 * rho0) * jnp.sum(
            c0 * dq, axis=-1, keepdims=True
        )
        grads[1, :, cols] = rho1 * dk - c1 * (rho1 * rho1 * rho1) * jnp.sum(
            c1 * dk, axis=-1, keepdims=True
        )
        grads[2, :, cols] = dv
        dlogit = dlogit + jnp.where(lane == head, dbeta * gate * (1.0 - gate), 0.0)
    chans = grads.shape[-1]
    small_out[...] = jnp.zeros_like(small_out)
    small_out[0:1, SIDE : SIDE + DK] = gain_rows
    half = rows_out.shape[-1] // 2
    small_out[1:2, SIDE:] = rows_out[:, :half]
    small_out[2:3, SIDE:] = rows_out[:, half:]
    dlogit_low = low(dlogit)
    n1 = n1_ref[...]
    small_out[3 * KCONV : 3 * KCONV + heads, :] = dot_tn(dlogit_low, n1)[:heads, :]
    for part in range(3):
        taps = taps_ref[level, part].astype(F32)
        total, gate, _ = convs[part]
        dsum = grads[part] * (gate * (1.0 + total * (1.0 - gate)))
        p = p_ref[part]
        dp = taps[KCONV - 1 : KCONV, :] * dsum
        for tap in range(KCONV):
            back = KCONV - 1 - tap
            spot = part * KCONV + tap
            small_out[spot : spot + 1, :chans] = jnp.sum(
                dsum * shift_down(p, back), axis=0, keepdims=True
            )
            if back:
                dp = dp + taps[tap : tap + 1, :] * shift_up(dsum, back)
        dp_ref[part] = low(dp)
    loads[1].wait()
    dn1 = dot_nt(dlogit_low, wb_ref[level])
    for part in range(3):
        dn1 = dn1 + dot_nt(dp_ref[part], wq[part])
    part_out[...] = low(dn1)
    for part in range(3):
        gq_out[part] = low(dot_tn(n1, dp_ref[part]))


def mixer_backward(level, e, hid, adds, norm_gain, taps, head_gain, wb, kept, wq, wo):
    length, width = e.shape
    chans = wq.shape[-1]
    heads = chans // DK
    sds = jax.ShapeDtypeStruct
    vmem = pl.BlockSpec(memory_space=pltpu.VMEM)
    hbm = pl.BlockSpec(memory_space=pl.ANY)
    return pl.pallas_call(
        functools.partial(mixer_backward_kernel, level, heads, len(adds)),
        out_shape=(
            sds((length, width), F32),
            sds((length, width), BF16),
            sds((16, width), F32),
            sds((3, width, chans), BF16),
            sds((chans, width), BF16),
        ),
        in_specs=[vmem] * (13 + len(adds)) + [hbm, hbm],
        out_specs=(vmem,) * 5,
        scratch_shapes=[
            pltpu.VMEM((3, width, chans), BF16),
            pltpu.VMEM((chans, width), BF16),
            pltpu.VMEM((3, length, chans), F32),
            pltpu.VMEM((3, length, chans), BF16),
            pltpu.VMEM((1, width), F32),
            pltpu.SemaphoreType.DMA((2,)),
        ],
        compiler_params=pltpu.CompilerParams(vmem_limit_bytes=VMEM_LIMIT),
        name="mixer_backward",
    )(e, hid, *adds, norm_gain, taps, head_gain, wb, *kept, wq, wo)


def branch_parts(part):
    count = lax.axis_size("tensor")
    if count == 1:
        return (part,)
    if count == 2:
        return (part, lax.ppermute(part, "tensor", [(0, 1), (1, 0)]))
    return (lax.psum(part, "tensor"),)


def sum_over_dp(tables):
    shapes = [table.shape for table in tables]
    flat = jnp.concatenate([table.reshape(-1) for table in tables])
    size = flat.shape[0]
    count = lax.axis_size("dp")
    pad = -size % (count * 1024)
    flat = jnp.pad(flat, (0, pad))
    shard = lax.psum_scatter(flat, "dp", scatter_dimension=0, tiled=True)
    joined = lax.all_gather(shard, "dp", axis=0, tiled=True)
    pieces = []
    offset = 0
    for shape in shapes:
        size = math.prod(shape)
        pieces.append(joined[offset : offset + size].reshape(shape))
        offset = offset + size
    return pieces


def fold_spot(depth, side, core):
    return (depth * 2 + side) * 2 + core


def remote(source, target, send, recv, device):
    return pltpu.make_async_remote_copy(
        src_ref=source,
        dst_ref=target,
        send_sem=send,
        recv_sem=recv,
        device_id=device,
        device_id_type=pl.DeviceIdType.MESH,
    )


DEPTH = 4
CHUNKS = 8
STEPS = CHUNKS // 2
SLOTS = ("p1", "p2", "p3", "e1", "e2", "e3", "e4")
KINDS = (*SLOTS, "p4e", "p4y", "pf0", "pf1", "pk", "e5", "e6", "e7", "ef0", "ef1", "ek")


class Fold:
    def __init__(self, cuts, own, slots, totals, sems):
        self.cuts, self.own, self.slots, self.totals = cuts, own, slots, totals
        self.send_sems, self.recv_sems = sems
        spot = lax.axis_index("dp")
        self.core = lax.rem(spot, 2)
        side = lax.rem(lax.div(spot, 2), 2)
        depth = lax.div(spot, 4)
        self.is_mid = (depth == 1) | (depth == 2)
        self.is_end = (depth == 0) | (depth == 3)
        folded = depth + 1 - 2 * lax.rem(depth, 2)
        across = DEPTH - 1 - depth
        half = lax.div(depth, 2)
        self.partner = {"dp": fold_spot(depth, side, 1 - self.core)}
        self.beside = {"dp": fold_spot(depth, 1 - side, self.core)}
        self.folded = {"dp": fold_spot(folded, side, self.core)}
        self.across = {"dp": fold_spot(across, side, self.core)}
        self.mine = [[base * STEPS + step for step in range(STEPS)] for base in (side, half)]
        self.others = [
            [(1 - base) * STEPS + step for step in range(STEPS)] for base in (side, half)
        ]
        self.done = [0] * len(cuts)
        self.active, self.waiting = [], []

    def piece(self, index, chunk, way):
        kind, rows, cols = self.cuts[index]
        ref = self.own[index]
        if kind == "cols":
            return ref.at[
                pl.ds(pl.multiple_of(chunk * rows, rows), rows), way * cols : (way + 1) * cols
            ]
        if kind == "rows":
            start = pl.multiple_of(chunk * (2 * rows) + way * rows, rows)
            return ref.at[pl.ds(start, rows), :]
        return ref.at[
            way * rows : (way + 1) * rows, pl.ds(pl.multiple_of(chunk * cols, cols), cols)
        ]

    def spot(self, index, chunk, way):
        kind, rows, cols = self.cuts[index]
        ref = self.totals[index]
        if kind == "cols":
            start = pl.multiple_of(self.core * (2 * cols) + way * cols, cols)
            return ref.at[pl.ds(pl.multiple_of(chunk * rows, rows), rows), pl.ds(start, cols)]
        if kind == "rows":
            start = pl.multiple_of(chunk * (2 * rows) + way * rows, rows)
            return ref.at[self.core, pl.ds(start, rows), :]
        start = pl.multiple_of(self.core * (2 * rows) + way * rows, rows)
        return ref.at[pl.ds(start, rows), pl.ds(pl.multiple_of(chunk * cols, cols), cols)]

    def family(self, index):
        return index % 4 if index < SMALL else 4

    def slot(self, name, index, step):
        return self.slots[self.family(index)].at[SLOTS.index(name), step]

    def copy(self, name, index, step, kept=True):
        way = 1 if name[0] == "e" else 0
        far = name in ("p1", "pf1", "e1", "e2", "e7", "ef1")
        chunk = (self.others if far else self.mine)[way][step]
        device = self.folded
        if name in ("p1", "p4y", "e4"):
            device = self.beside
        elif name in ("p3", "e2", "e6"):
            device = self.across
        elif name[1] == "f":
            device = self.partner
        source = self.piece(index, chunk, way)
        if name in SLOTS:
            target = self.slot(name, index, step)
        else:
            target = self.spot(index, chunk, way)
            if name in ("pf1", "ef1", "e6", "e7") or not kept:
                source = target
        at = (KINDS.index(name), index, step)
        if name[1] == "k":
            return pltpu.make_async_copy(source, target, self.recv_sems.at[at])
        return remote(source, target, self.send_sems.at[at], self.recv_sems.at[at], device)

    def start(self, names, index, step, kept=True):
        for name in names:
            self.copy(name, index, step, kept).start()

    def add(self, name, index, step, chunk):
        self.copy(name, index, step).wait_recv()
        mine = self.piece(index, chunk, 1 if name[0] == "e" else 0)
        both = mine[...].astype(F32) + self.slot(name, index, step)[...].astype(F32)
        mine[...] = both.astype(mine.dtype)

    def stage_one(self, index, step):
        self.start(("p1",), index, step)

        @pl.when(self.is_end)
        def _():
            self.start(("e1",), index, step)

    def stage_two(self, index, step):
        self.add("p1", index, step, self.mine[0][step])

        @pl.when(self.is_end)
        def _():
            self.start(("p2",), index, step)

        @pl.when(self.is_mid)
        def _():
            self.add("e1", index, step, self.others[1][step])
            self.start(("e2",), index, step)

    def stage_three(self, index, step):
        @pl.when(self.is_mid)
        def _():
            self.add("p2", index, step, self.mine[0][step])
            self.start(("p3",), index, step)
            self.add("e2", index, step, self.mine[1][step])
            self.start(("e3",), index, step)

    def stage_four(self, index, step):
        @pl.when(self.is_mid)
        def _():
            self.copy("p3", index, step).wait_send()
            self.add("p3", index, step, self.mine[0][step])
            self.start(("p4e", "p4y", "pf0", "pk"), index, step)

        @pl.when(self.is_end)
        def _():
            self.add("e3", index, step, self.mine[1][step])
            self.start(("e4",), index, step)

    def stage_five(self, index, step):
        @pl.when(self.is_end)
        def _():
            self.copy("e4", index, step).wait_send()
            self.add("e4", index, step, self.mine[1][step])
            self.start(("e5", "ef0", "ek"), index, step)
            self.copy("p4e", index, step).wait_recv()
            self.start(("p4y", "pf0"), index, step, False)

    def stage_six(self, index, step):
        self.copy("p4y", index, step).wait_recv()
        self.start(("pf1",), index, step)

        @pl.when(self.is_mid)
        def _():
            self.copy("e5", index, step).wait_recv()
            self.start(("e6", "ef0"), index, step, False)

    def stage_seven(self, index, step):
        @pl.when(self.is_mid)
        def _():
            self.copy("e6", index, step).wait_recv()
            self.start(("e7", "ef1"), index, step)

    def stage_eight(self, index, step):
        @pl.when(self.is_end)
        def _():
            self.copy("e7", index, step).wait_recv()
            self.start(("ef1",), index, step)

    def settle(self, index, step):
        for name in ("p1", "p4y"):
            self.copy(name, index, step).wait_send()
        for name in ("pf0", "pf1", "ef0", "ef1"):
            self.copy(name, index, step).wait()

        @pl.when(self.is_end)
        def _():
            for name in ("e1", "p2", "e5"):
                self.copy(name, index, step).wait_send()
            self.copy("ek", index, step).wait()

        @pl.when(self.is_mid)
        def _():
            for name in ("e2", "e3", "p4e", "e6", "e7"):
                self.copy(name, index, step).wait_send()
            self.copy("pk", index, step).wait()

    def advance(self, index):
        stages = (
            self.stage_one,
            self.stage_two,
            self.stage_three,
            self.stage_four,
            self.stage_five,
            self.stage_six,
            self.stage_seven,
            self.stage_eight,
        )
        tick = self.done[index]
        self.done[index] = tick + 1
        last = STEPS + len(stages) - 1
        if tick == last:
            for step in range(STEPS):
                self.settle(index, step)
            return False
        for offset, stage in reversed(list(enumerate(stages))):
            if 0 <= tick - offset < STEPS:
                stage(index, tick - offset)
        return True

    def begin(self, index):
        if any(self.family(index) == self.family(held) for held in self.active):
            self.waiting.append(index)
        else:
            self.active.append(index)

    def serve(self, count=1):
        for _ in range(count):
            if not self.active:
                return
            index = self.active.pop(0)
            if self.advance(index):
                self.active.append(index)
                continue
            for other in self.waiting:
                if self.family(other) == self.family(index):
                    self.waiting.remove(other)
                    self.active.append(other)
                    break


def fold_cuts(n_dp, width, chans, hidden):
    if n_dp != 4 * DEPTH or width != CHUNKS * LANES or chans % (4 * LANES) or hidden % LANES:
        return None
    if any(rows % (16 * CHUNKS) for rows in (hidden, chans, width)):
        return None
    layer = [
        ("cols", hidden // CHUNKS, width // 4),
        ("rows", width // (2 * CHUNKS), hidden),
        ("cols", chans // CHUNKS, width // 4),
        ("cols", 3 * width // CHUNKS, chans // 4),
    ]
    return layer * LAYERS + [("small", 8, LANES)]


DOWN, GATE_UP, OUT, QKV = range(4)
SMALL = 4 * LAYERS
MLP_KEPT = ("gu", "z", "n2")
MIXER_KEPT = ("n1", "p", "logits", "t", "u", "o", "on", "h")
PEERS = ("z", "n2", "ef", "dgu", "n1", "on", "em", "dp")


def backward_kernel(n_parts, cuts, *refs):
    refs = list(refs)

    def taken(count):
        group = refs[:count]
        del refs[:count]
        return group

    (cot_ref, gain_ref, taps_ref, head_gain_ref, wb_ref) = taken(5)
    (part_hbm, wq_hbm, wo_hbm, wgu_hbm, wd_hbm) = taken(5)
    kept = dict(zip(KEPT, taken(len(KEPT))))
    (out_ref, in_grad_ref, *totals) = taken(2 + 5)
    own = taken(len(cuts))
    fold_slots = taken(5)
    peers = dict(zip(PEERS, taken(len(PEERS))))
    (e_ref, small, small_peer, slots, don_ref) = taken(5)
    (load_sems, send_sems, recv_sems, peer_sems) = taken(4)
    fold_sems = taken(2)

    per_table = [totals[index].at[level] for level in range(LAYERS) for index in range(4)]
    fold = Fold(cuts, own, fold_slots, [*per_table, totals[4]], fold_sems)
    core, serve = fold.core, fold.serve
    exchange = Exchange(slots, send_sems, recv_sems)
    barrier = pltpu.get_barrier_semaphore()
    for device in (fold.partner, fold.beside, fold.folded, fold.across):
        pl.semaphore_signal(barrier, inc=1, device_id=device, device_id_type=pl.DeviceIdType.MESH)
    exchange.greet(4)

    length, width = e_ref.shape
    chans = wo_hbm.shape[1]
    hidden = wd_hbm.shape[1]
    heads = chans // DK
    high = length // n_parts
    parts = [(part, slice(part * high, (part + 1) * high)) for part in range(n_parts)]
    row, col = positions(length)
    lane = lax.broadcasted_iota(jnp.int32, (length, LANES), 1)
    side = width - SIDE
    half_width, half_chans = width // 2, chans // 2

    def other_half(wide):
        return pl.ds(pl.multiple_of((1 - core) * wide, LANES), wide)

    def own_half(wide):
        return pl.ds(pl.multiple_of(core * wide, LANES), wide)

    def to_peer(name, level, source):
        spot = PEERS.index(name)
        return remote(
            source,
            peers[name].at[level],
            peer_sems.at[0, spot, level],
            peer_sems.at[1, spot, level],
            fold.partner,
        )

    top = LAYERS - 1
    early = [
        to_peer(name, level, kept[name].at[level])
        for level in reversed(range(LAYERS))
        for name in ("z", "n2", "on", "n1")
    ]
    early.insert(1, to_peer("ef", top, cot_ref.at[:, other_half(width // 2)]))
    for copy in early:
        copy.start()
    first = pltpu.make_async_copy(part_hbm, slots.at[0, exchange.me], load_sems.at[0, 0, 0])
    first.start()
    small[...] = jnp.zeros_like(small)

    def norm_step(level, which, spot, part, rows, hid):
        total = exchange.take(spot, part, rows)
        gain = gain_ref[level, which : which + 1, :].astype(F32)
        grad_hidden, sums = rms_back(hid, gain, total)
        base = 16 * level + (1 if which else 3)
        for index in range(2):
            spot_row = slice(base + index, base + index + 1)
            small[spot_row, SIDE:] += sums[:, index * side : (index + 1) * side]
        return e_ref[rows] + grad_hidden

    def mlp_stage(level):
        def scope(wgu, wd, gu, z, n2, hid, dgu, ef):
            held = dict(gu=gu, z=z, n2=n2)
            loads = {
                "wd": pltpu.make_async_copy(wd_hbm.at[level], wd, load_sems.at[level, 0, 1]),
                "wgu": pltpu.make_async_copy(wgu_hbm.at[level], wgu, load_sems.at[level, 0, 2]),
            }
            for index, name in enumerate(MLP_KEPT):
                loads[name] = pltpu.make_async_copy(
                    kept[name].at[level], held[name], load_sems.at[level, 0, 3 + index]
                )
            if level < LAYERS - 1:
                loads["hid"] = pltpu.make_async_copy(
                    kept["x"].at[level + 1], hid, load_sems.at[level, 0, 6]
                )
                loads["hid"].start()
            for name in ("z", "wd", "gu", "wgu", "n2"):
                loads[name].start()
            index = 4 * level
            if level == top:
                first.wait()
                for part, rows in parts:
                    exchange.send(0, part, rows)
                loads["z"].wait()
                for name in ("z", "ef"):
                    to_peer(name, level, peers[name].at[level]).wait_recv()
                own[index + DOWN][...] = low(
                    dot_tn(z[...], cot_ref[:, own_half(half_width)])
                    + dot_tn(peers["z"][level], peers["ef"][level])
                )
                fold.begin(index + DOWN)
            for part, rows in parts:
                serve()
                if level == LAYERS - 1:
                    e = cot_ref[rows].astype(F32)
                else:
                    if part == 0:
                        loads["hid"].wait()
                    e = norm_step(level + 1, 0, 2 * (LAYERS - 1 - level), part, rows, hid[rows])
                e_ref[rows] = e
                e_low = low(e)
                ef[rows] = e_low
                if part == 0:
                    loads["wd"].wait()
                dz = dot_nt(e_low, wd[...])
                if part == 0:
                    loads["gu"].wait()
                g, u = gu[0, rows], gu[1, rows]
                s = sigmoid(g)
                dgu[0, rows] = low(dz * u * (s * (1.0 + g * (1.0 - s))))
                dgu[1, rows] = low(dz * (g * s))
                if part == 0:
                    loads["wgu"].wait()
                partial = dot_nt(dgu[0, rows], wgu[0]) + dot_nt(dgu[1, rows], wgu[1])
                exchange.give(2 * (LAYERS - 1 - level) + 1, part, rows, low(partial))
            sends = [to_peer("dgu", level, dgu.at[1 - core])]
            if level != top:
                sends.append(to_peer("ef", level, ef.at[:, other_half(half_width)]))
            for send in sends:
                send.start()
            serve()
            loads["n2"].wait()
            for name in ("n2", "dgu"):
                to_peer(name, level, peers[name].at[level]).wait_recv()
            own[index + GATE_UP][...] = low(
                dot_tn(n2[...], dgu[core]) + dot_tn(peers["n2"][level], peers["dgu"][level])
            )
            fold.begin(index + GATE_UP)
            serve()
            if level != top:
                loads["z"].wait()
                for name in ("z", "ef"):
                    to_peer(name, level, peers[name].at[level]).wait_recv()
                own[index + DOWN][...] = low(
                    dot_tn(z[...], ef[:, own_half(half_width)])
                    + dot_tn(peers["z"][level], peers["ef"][level])
                )
                fold.begin(index + DOWN)
                serve()
            for send in sends:
                send.wait_send()

        pl.run_scoped(
            scope,
            pltpu.VMEM((2, width, hidden), BF16),
            pltpu.VMEM((hidden, width), BF16),
            pltpu.VMEM((2, length, hidden), F32),
            pltpu.VMEM((length, hidden), BF16),
            pltpu.VMEM((length, width), BF16),
            pltpu.VMEM((length, width), F32),
            pltpu.VMEM((2, length, hidden), BF16),
            pltpu.VMEM((length, width), BF16),
        )

    def mixer_stage(level):
        def scope(wq, wo, n1, p, logits, t, u_all, o_all, on, h, grads, dp, em):
            held = dict(n1=n1, p=p, logits=logits, t=t, u=u_all, o=o_all, on=on, h=h)
            loads = {
                "wo": pltpu.make_async_copy(wo_hbm.at[level], wo, load_sems.at[level, 1, 0]),
                "wq": pltpu.make_async_copy(wq_hbm.at[level], wq, load_sems.at[level, 1, 1]),
            }
            for index, name in enumerate(MIXER_KEPT):
                loads[name] = pltpu.make_async_copy(
                    kept[name].at[level], held[name], load_sems.at[level, 1, 2 + index]
                )
            for name in ("h", "wo", "p", "o", "u", "logits", "t", "wq", "n1", "on"):
                loads[name].start()
            serve()
            loads["p"].wait()
            convs = [
                conv_silu(p[index], taps_ref[level, index].astype(F32)) for index in range(3)
            ]
            spot = 2 * (LAYERS - 1 - level) + 1
            loads["h"].wait()
            if level == LAYERS - 1:
                for part, rows in parts:
                    out_ref[rows] = low(h[rows] + exchange.take(0, part, rows))
            for part, rows in parts:
                serve()
                e = norm_step(level, 1, spot, part, rows, h[rows])
                e_ref[rows] = e
                e_low = low(e)
                em[rows] = e_low
                if part == 0:
                    loads["wo"].wait()
                don_ref[rows] = dot_nt(e_low, wo[...])
            send_em = to_peer("em", level, em.at[:, other_half(half_width)])
            send_em.start()
            for name in ("o", "u", "logits", "t"):
                loads[name].wait()
            beta = sigmoid(logits[...])
            head_gain = head_gain_ref[level : level + 1, :].astype(F32)
            gain_rows = jnp.zeros((1, DK), F32)
            dlogit = jnp.zeros((length, LANES), F32)
            serve()
            for head in range(heads):
                cols = head_cols(head)
                c0, c1, c2 = (conv[2][:, cols] for conv in convs)
                rho0 = lax.rsqrt(jnp.sum(c0 * c0, axis=-1, keepdims=True) + 0.001)
                rho1 = lax.rsqrt(jnp.sum(c1 * c1, axis=-1, keepdims=True) + 0.001)
                q, k, v = low(c0 * rho0), low(c1 * rho1), low(c2).astype(F32)
                gate = beta[:, head : head + 1]
                o = o_all[:, cols]
                scale = lax.rsqrt(jnp.mean(o * o, axis=-1, keepdims=True) + 0.01)
                dn = don_ref[:, cols]
                weighted = dn * head_gain
                inner = jnp.mean(o * weighted, axis=-1, keepdims=True)
                do = low(scale * weighted - o * (scale * scale * scale) * inner)
                gain_rows = gain_rows + jnp.sum(dn * o * scale, axis=0, keepdims=True)
                u = u_all[:, cols]
                score_t = low(jnp.where(row <= col, dot_nt(k, q), 0.0))
                du = dot_nn(score_t, do)
                ds = low(jnp.where(row >= col, dot_nt(do, u), 0.0))
                ds_t = low(jnp.where(row <= col, dot_nt(u, do), 0.0))
                dq = dot_nn(ds, k)
                dk = dot_nn(ds_t, q)
                r = split_dot(dot_tn, (t[0, head], t[1, head]), halves(du))
                dv = gate * r
                dv_low = low(dv)
                gram = low(jnp.where(row > col, dot_nt(k, k), 0.0))
                w = v - dot_nn(gram, u)
                dbeta = jnp.sum(r * w, axis=-1, keepdims=True)
                dgram = jnp.where(row > col, dot_nt(dv_low, u), 0.0) + jnp.where(
                    row < col, dot_nt(u, dv_low), 0.0
                )
                dk = dk - dot_nn(low(dgram), k)
                grads[0, :, cols] = rho0 * dq - c0 * (rho0 * rho0 * rho0) * jnp.sum(
                    c0 * dq, axis=-1, keepdims=True
                )
                grads[1, :, cols] = rho1 * dk - c1 * (rho1 * rho1 * rho1) * jnp.sum(
                    c1 * dk, axis=-1, keepdims=True
                )
                grads[2, :, cols] = dv
                dlogit = dlogit + jnp.where(lane == head, dbeta * gate * (1.0 - gate), 0.0)
                if head % 2:
                    serve()
            base = 16 * level
            small[base : base + 1, SIDE : SIDE + DK] = gain_rows
            for index in range(3):
                taps = taps_ref[level, index].astype(F32)
                total, gate, _ = convs[index]
                dsum = grads[index] * (gate * (1.0 + total * (1.0 - gate)))
                project = p[index]
                dproject = taps[KCONV - 1 : KCONV, :] * dsum
                for tap in range(KCONV):
                    back = KCONV - 1 - tap
                    line = base + index * KCONV + tap
                    small[line : line + 1, :chans] = jnp.sum(
                        dsum * shift_down(project, back), axis=0, keepdims=True
                    )
                    if back:
                        dproject = dproject + taps[tap : tap + 1, :] * shift_up(dsum, back)
                dp[index] = low(dproject)
            dlogit_low = low(dlogit)
            loads["wq"].wait()
            for part, rows in parts:
                dn1 = dot_nt(dlogit_low[rows], wb_ref[level])
                for index in range(3):
                    dn1 = dn1 + dot_nt(dp[index, rows], wq[index])
                exchange.give(spot + 1, part, rows, low(dn1))
            send_dp = to_peer("dp", level, dp.at[:, :, other_half(half_chans)])
            send_dp.start()
            serve()
            loads["n1"].wait()
            loads["on"].wait()
            line = base + 3 * KCONV
            small[line : line + heads, :] = dot_tn(dlogit_low, n1[...])[:heads, :]
            for name in ("em", "on", "n1", "dp"):
                to_peer(name, level, peers[name].at[level]).wait_recv()
            own[4 * level + OUT][...] = low(
                dot_tn(on[...], em[:, own_half(half_width)])
                + dot_tn(peers["on"][level], peers["em"][level])
            )
            fold.begin(4 * level + OUT)
            serve()
            for index in range(3):
                own[4 * level + QKV][index * width : (index + 1) * width] = low(
                    dot_tn(n1[...], dp[index, :, own_half(half_chans)])
                    + dot_tn(peers["n1"][level], peers["dp"][level, index])
                )
            fold.begin(4 * level + QKV)
            serve()
            send_em.wait_send()
            send_dp.wait_send()

        pl.run_scoped(
            scope,
            pltpu.VMEM((3, width, chans), BF16),
            pltpu.VMEM((chans, width), BF16),
            pltpu.VMEM((length, width), BF16),
            pltpu.VMEM((3, length, chans), F32),
            pltpu.VMEM((length, LANES), F32),
            pltpu.VMEM((2, heads, length, length), BF16),
            pltpu.VMEM((length, chans), BF16),
            pltpu.VMEM((length, chans), F32),
            pltpu.VMEM((length, chans), BF16),
            pltpu.VMEM((length, width), F32),
            pltpu.VMEM((3, length, chans), F32),
            pltpu.VMEM((3, length, chans), BF16),
            pltpu.VMEM((length, width), BF16),
        )

    for level in reversed(range(LAYERS)):
        mlp_stage(level)
        mixer_stage(level)

    def last_scope(hid):
        load = pltpu.make_async_copy(kept["x"].at[0], hid, load_sems.at[0, 0, 7])
        load.start()
        serve(len(fold.active))
        load.wait()
        for part, rows in parts:
            in_grad_ref[rows] = low(norm_step(0, 0, 2 * LAYERS, part, rows, hid[rows]))

    pl.run_scoped(last_scope, pltpu.VMEM((length, width), F32))

    def small_half(which):
        return small.at[pl.ds(pl.multiple_of(which * 16, 16), 16)]

    send_small = remote(
        small_half(1 - core),
        small_peer,
        load_sems.at[1, 0, 6],
        load_sems.at[1, 0, 7],
        fold.partner,
    )
    send_small.start()
    serve(len(fold.active))
    send_small.wait_recv()
    own[SMALL][...] = small_half(core)[...] + small_peer[...]
    fold.begin(SMALL)
    while fold.active:
        serve()
    send_small.wait_send()
    for copy in early:
        copy.wait_send()
    exchange.finish()


def backward(cot, part, saved, norm_gain, taps, head_gain, wb, wq, wo, wgu, wd):
    length, width = cot.shape
    chans, hidden = wq.shape[-1], wgu.shape[-1]
    heads = chans // DK
    n_tensor = lax.axis_size("tensor")
    cuts = fold_cuts(lax.axis_size("dp"), width, chans, hidden)
    n_parts = 2
    sds = jax.ShapeDtypeStruct
    vmem = pl.BlockSpec(memory_space=pltpu.VMEM)
    hbm = pl.BlockSpec(memory_space=pl.ANY)
    own, slots = [], []
    for index, (kind, rows, cols) in enumerate(cuts):
        dtype = F32 if kind == "small" else BF16
        half = {
            "cols": (rows * CHUNKS, 2 * cols),
            "rows": (2 * rows * CHUNKS, cols),
            "small": (2 * rows, cols * CHUNKS),
        }[kind]
        own.append(pltpu.VMEM(half, dtype))
        if index < 4 or index == SMALL:
            slots.append(pltpu.VMEM((len(SLOTS), STEPS, rows, cols), dtype))
    peers = dict(
        z=(length, hidden),
        n2=(length, width),
        ef=(length, width // 2),
        dgu=(length, hidden),
        n1=(length, width),
        on=(length, chans),
        em=(length, width // 2),
        dp=(3, length, chans // 2),
    )
    spots = 2 * LAYERS + 1
    return pl.pallas_call(
        functools.partial(backward_kernel, n_parts, cuts),
        out_shape=(
            sds((length, width), BF16),
            sds((length, width), BF16),
            sds((LAYERS, hidden, width), BF16),
            sds((LAYERS, 2, width, hidden), BF16),
            sds((LAYERS, chans, width), BF16),
            sds((LAYERS, 3 * width, chans), BF16),
            sds((16 * LAYERS, width), F32),
        ),
        in_specs=[vmem] * 5 + [hbm] * (5 + len(KEPT)),
        out_specs=(vmem, vmem) + (hbm,) * 5,
        scratch_shapes=[
            *own,
            *slots,
            *(pltpu.VMEM((LAYERS, *peers[name]), BF16) for name in PEERS),
            pltpu.VMEM((length, width), F32),
            pltpu.VMEM((16 * LAYERS, width), F32),
            pltpu.VMEM((16, width), F32),
            pltpu.VMEM((spots, n_tensor, length, width), BF16),
            pltpu.VMEM((length, chans), F32),
            pltpu.SemaphoreType.DMA((LAYERS, 2, 10)),
            pltpu.SemaphoreType.DMA((spots, n_parts, n_tensor - 1)),
            pltpu.SemaphoreType.DMA((spots, n_parts, n_tensor - 1)),
            pltpu.SemaphoreType.DMA((2, len(PEERS), LAYERS)),
            pltpu.SemaphoreType.DMA((len(KINDS), len(cuts), STEPS)),
            pltpu.SemaphoreType.DMA((len(KINDS), len(cuts), STEPS)),
        ],
        compiler_params=pltpu.CompilerParams(
            vmem_limit_bytes=VMEM_LIMIT, collective_id=0, has_side_effects=True
        ),
        name="backward",
    )(cot, norm_gain, taps, head_gain, wb, part, wq, wo, wgu, wd, *(saved[name] for name in KEPT))


def staged_backward(cot, part, saved, norm_gain, taps, head_gain, wb, wq, wo, wgu, wd):
    total = saved["h"][LAYERS - 1]
    for add in branch_parts(part):
        total = total + add.astype(F32)
    outputs = total.astype(BF16)
    e, hid, adds = cot, saved["x"][LAYERS - 1], ()
    gain_rows = {}
    small = [None] * LAYERS
    big = [None] * LAYERS
    for level in reversed(range(LAYERS)):
        at = {name: saved[name][level] for name in KEPT}
        mlp_kept = tuple(at[name] for name in ("n2", "gu", "z"))
        mixer_kept = tuple(at[name] for name in ("n1", "p", "logits", "t", "u", "o", "on"))
        e, rows, part, grad_down, grad_gate_up = mlp_backward(
            level, e, hid, adds, norm_gain, *mlp_kept, wgu, wd
        )
        gain_rows[level + 1] = rows
        e, part, small[level], grad_qkv, grad_out = mixer_backward(
            level,
            e,
            at["h"],
            branch_parts(part),
            norm_gain,
            taps,
            head_gain,
            wb,
            mixer_kept,
            wq,
            wo,
        )
        hid, adds = at["x"], branch_parts(part)
        big[level] = (grad_down, grad_gate_up, grad_out, grad_qkv)
    branch = adds[0].astype(F32)
    for add in adds[1:]:
        branch = branch + add.astype(F32)
    grad_hidden, rows = rms_back(hid, norm_gain[0, 0:1].astype(F32), branch)
    gain_rows[0] = rows
    input_grad = (e + grad_hidden).astype(BF16)
    side = rows.shape[-1] - SIDE
    small_all = jnp.concatenate(
        [
            small[level].at[3:5, SIDE:].set(gain_rows[level].reshape(2, side))
            for level in range(LAYERS)
        ]
    )
    tables = [table for group in big for table in group]
    sums = sum_over_dp(tables)
    stacked = [jnp.stack([sums[index], sums[4 + index]]) for index in range(4)]
    return (outputs, input_grad, *stacked, lax.psum(small_all, "dp"))


def body(
    inputs,
    qkv_weight,
    conv_taps,
    beta_weight,
    out_gain,
    out_weight,
    norm_gain,
    gate_up_weight,
    down_weight,
    cotangent,
):
    heads = beta_weight.shape[-1]
    wb = jnp.pad(beta_weight, ((0, 0), (0, 0), (0, LANES - heads)))
    saved, part = forward(
        inputs,
        norm_gain,
        conv_taps,
        out_gain,
        wb,
        qkv_weight,
        out_weight,
        gate_up_weight,
        down_weight,
    )
    length, width = inputs.shape
    chans, hidden = conv_taps.shape[-1], down_weight.shape[1]
    if fold_cuts(lax.axis_size("dp"), width, chans, hidden) is not None:
        outputs, input_grad, *big, small_all = backward(
            cotangent,
            part,
            saved,
            norm_gain,
            conv_taps,
            out_gain,
            wb,
            qkv_weight,
            out_weight,
            gate_up_weight,
            down_weight,
        )
    else:
        outputs, input_grad, *big, small_all = staged_backward(
            cotangent,
            part,
            saved,
            norm_gain,
            conv_taps,
            out_gain,
            wb,
            qkv_weight,
            out_weight,
            gate_up_weight,
            down_weight,
        )
    small_all = small_all.reshape(LAYERS, 16, -1)
    grad_conv = small_all[:, : 3 * KCONV, :chans].reshape(conv_taps.shape)
    grad_beta = small_all[:, 3 * KCONV : 3 * KCONV + heads].transpose(0, 2, 1)
    grad_norm = jnp.stack(
        [
            small_all[:, 3:5, SIDE:].reshape(LAYERS, -1),
            small_all[:, 1:3, SIDE:].reshape(LAYERS, -1),
        ],
        axis=1,
    )
    grad_out_gain = small_all[:, 0, SIDE : SIDE + DK]
    grad_out_gain = sum(branch_parts(grad_out_gain))
    shapes = (down_weight.shape, gate_up_weight.shape, out_weight.shape, qkv_weight.shape)
    grad_down, grad_gate_up, grad_out, grad_qkv = (
        table.reshape(shape).astype(F32) for table, shape in zip(big, shapes)
    )
    return (
        outputs,
        input_grad,
        grad_qkv,
        grad_conv,
        grad_beta,
        grad_out_gain,
        grad_out,
        grad_norm,
        grad_gate_up,
        grad_down,
    )


def solution(mesh):
    in_specs = (
        P("dp", None),
        P(None, None, None, "tensor"),
        P(None, None, None, "tensor"),
        P(None, None, "tensor"),
        P(),
        P(None, "tensor", None),
        P(),
        P(None, None, None, "tensor"),
        P(None, "tensor", None),
        P("dp", None),
    )
    out_specs = (
        P("dp", None),
        P("dp", None),
        P(None, None, None, "tensor"),
        P(None, None, None, "tensor"),
        P(None, None, "tensor"),
        P(),
        P(None, "tensor", None),
        P(),
        P(None, None, None, "tensor"),
        P(None, "tensor", None),
    )
    return jax.shard_map(body, mesh=mesh, in_specs=in_specs, out_specs=out_specs, check_vma=False)
```

```python
import functools
import math

import jax
import jax.numpy as jnp
from jax import lax
from jax.experimental import pallas as pl
from jax.experimental.pallas import tpu as pltpu
from jax.sharding import PartitionSpec as P

DK = 128
KCONV = 4
LAYERS = 2
LANES = 128
SIDE = 512
F32 = jnp.float32
BF16 = jnp.bfloat16
VMEM_LIMIT = 60 * 1024 * 1024


def dot_nn(a, b):
    return lax.dot_general(a, b, (((1,), (0,)), ((), ())), preferred_element_type=F32)


def dot_nt(a, b):
    return lax.dot_general(a, b, (((1,), (1,)), ((), ())), preferred_element_type=F32)


def dot_tn(a, b):
    return lax.dot_general(a, b, (((0,), (0,)), ((), ())), preferred_element_type=F32)


def halves(a):
    hi = a.astype(BF16)
    return hi, (a - hi.astype(F32)).astype(BF16)


def split_dot(dot, a, b):
    return dot(a[0], b[0]) + (dot(a[0], b[1]) + dot(a[1], b[0]))


def low(a):
    return a.astype(BF16)


def sigmoid(a):
    return 1.0 / (1.0 + jnp.exp(-a))


def rms_scale(a):
    return lax.rsqrt(jnp.mean(a * a, axis=-1, keepdims=True) + 1e-05)


def rms_back(hidden, gain, grad_normed):
    scale = rms_scale(hidden)
    weighted = gain * grad_normed
    inner = jnp.mean(hidden * weighted, axis=-1, keepdims=True)
    grad_hidden = scale * weighted - hidden * (scale * scale * scale) * inner
    rows = jnp.sum(grad_normed * hidden * scale, axis=0, keepdims=True)
    return grad_hidden, rows


def shift_down(a, count):
    if count == 0:
        return a
    row = lax.broadcasted_iota(jnp.int32, a.shape, 0)
    return jnp.where(row >= count, pltpu.roll(a, count, 0), 0.0)


def shift_up(a, count):
    if count == 0:
        return a
    length = a.shape[0]
    row = lax.broadcasted_iota(jnp.int32, a.shape, 0)
    return jnp.where(row < length - count, pltpu.roll(a, length - count, 0), 0.0)


def conv_silu(project, taps):
    total = taps[KCONV - 1 : KCONV, :] * project
    for tap in range(KCONV - 1):
        total = total + taps[tap : tap + 1, :] * shift_down(project, KCONV - 1 - tap)
    gate = sigmoid(total)
    return total, gate, total * gate


def conv_silu_rows(project, taps, rows):
    start = rows.start
    if start == 0:
        return conv_silu(project[rows], taps)[2]
    return conv_silu(project[start - 8 : rows.stop], taps)[2][8:]


def solve_back(blocks, key, gate, grad):
    half = grad.shape[0] // 2
    second = split_dot(dot_tn, blocks[1], halves(grad[half:]))
    gram = halves(dot_nt(key[half:], key[:half]))
    cross = split_dot(dot_tn, gram, halves(gate[half:] * second))
    first = split_dot(dot_tn, blocks[0], halves(grad[:half] - cross))
    return jnp.concatenate([first, second], axis=0)


def positions(length):
    row = lax.broadcasted_iota(jnp.int32, (length, length), 0)
    col = lax.broadcasted_iota(jnp.int32, (length, length), 1)
    return row, col


def unit_lower_inverse(lower_list):
    length = lower_list[0].shape[0]
    row, col = positions(length)
    eye = jnp.where(row == col, 1.0, 0.0)
    diag_list = [jnp.where(row // 4 == col // 4, lower, 0.0) for lower in lower_list]
    parts = [halves(diag) for diag in diag_list]
    squares = [split_dot(dot_nn, part, part) for part in parts]
    firsts = [eye - diag for diag in diag_list]
    inverse = [
        first + split_dot(dot_nn, halves(first), halves(square))
        for first, square in zip(firsts, squares)
    ]
    size = 4
    while size < length:
        fresh = (row // (2 * size) == col // (2 * size)) & (row // size != col // size)
        offs = [halves(jnp.where(fresh, lower, 0.0)) for lower in lower_list]
        held = [halves(inv) for inv in inverse]
        mids = [split_dot(dot_nn, inv, off) for inv, off in zip(held, offs)]
        inverse = [
            inv - split_dot(dot_nn, halves(mid), part)
            for inv, mid, part in zip(inverse, mids, held)
        ]
        size = 2 * size
    return inverse


def head_cols(head):
    return slice(head * DK, (head + 1) * DK)


KEPT = ("x", "n1", "p", "logits", "t", "u", "o", "on", "h", "n2", "gu", "z")


def kept_shapes(length, width, chans, hidden):
    heads = chans // DK
    shapes = dict(
        x=((length, width), F32),
        n1=((length, width), BF16),
        p=((3, length, chans), F32),
        logits=((length, LANES), F32),
        t=((2, heads, 2, length // 2, length // 2), BF16),
        u=((length, chans), BF16),
        o=((length, chans), F32),
        on=((length, chans), BF16),
        h=((length, width), F32),
        n2=((length, width), BF16),
        gu=((2, length, hidden), F32),
        z=((length, hidden), BF16),
    )
    return [((LAYERS, *shapes[name][0]), shapes[name][1]) for name in KEPT]


class Exchange:
    def __init__(self, slots, send_sems, recv_sems):
        self.slots, self.send_sems, self.recv_sems = slots, send_sems, recv_sems
        self.count = slots.shape[1]
        self.me = lax.axis_index("tensor")
        self.others = [
            {"tensor": lax.rem(self.me + away, self.count)} for away in range(1, self.count)
        ]
        self.pending = []

    def greet(self, others=0):
        barrier = pltpu.get_barrier_semaphore()
        for device in self.others:
            pl.semaphore_signal(
                barrier, inc=1, device_id=device, device_id_type=pl.DeviceIdType.MESH
            )
        pl.semaphore_wait(barrier, self.count - 1 + others)

    def copies(self, spot, part, rows):
        mine = self.slots.at[spot, self.me, rows]
        return [
            pltpu.make_async_remote_copy(
                src_ref=mine,
                dst_ref=mine,
                send_sem=self.send_sems.at[spot, part, away],
                recv_sem=self.recv_sems.at[spot, part, away],
                device_id=device,
                device_id_type=pl.DeviceIdType.MESH,
            )
            for away, device in enumerate(self.others)
        ]

    def give(self, spot, part, rows, value):
        self.slots[spot, self.me, rows] = value
        self.send(spot, part, rows)

    def send(self, spot, part, rows):
        for copy in self.copies(spot, part, rows):
            copy.start()
        self.pending.append((spot, part, rows))

    def take(self, spot, part, rows):
        for copy in self.copies(spot, part, rows):
            copy.wait_recv()
        total = self.slots[spot, 0, rows].astype(F32)
        for index in range(1, self.count):
            total = total + self.slots[spot, index, rows].astype(F32)
        return total

    def finish(self):
        for sent in self.pending:
            for copy in self.copies(*sent):
                copy.wait_send()


def forward_kernel(n_parts, *refs):
    (x_ref, gain_ref, taps_ref, head_gain_ref, wb_ref) = refs[:5]
    (wq_hbm, wo_hbm, wgu_hbm, wd_hbm) = refs[5:9]
    count = len(KEPT)
    outs = dict(zip(KEPT, refs[9 : 9 + count]))
    last_out = refs[9 + count]
    held = dict(zip(KEPT, refs[10 + count : 10 + 2 * count]))
    (wq, wo, wgu, wd, wb, slots, last, load_sems, keep_sems, send_sems, recv_sems) = refs[
        10 + 2 * count :
    ]
    exchange = Exchange(slots, send_sems, recv_sems)
    sources = ((wq_hbm, wq), (wo_hbm, wo), (wgu_hbm, wgu), (wd_hbm, wd))
    loads = [
        [
            pltpu.make_async_copy(source.at[level], target.at[level], load_sems.at[level, index])
            for index, (source, target) in enumerate(sources)
        ]
        for level in range(LAYERS)
    ]
    for group in loads:
        for load in group:
            load.start()
    wb[...] = jnp.zeros_like(wb)
    for level in range(LAYERS):
        wb[level, : wb_ref.shape[1]] = wb_ref[level]
    exchange.greet()
    keeps = []

    def keep(name, level):
        copy = pltpu.make_async_copy(
            held[name].at[level], outs[name].at[level], keep_sems.at[KEPT.index(name), level]
        )
        copy.start()
        keeps.append(copy)

    length = x_ref.shape[0]
    heads = wo.shape[1] // DK
    high = length // n_parts
    parts = [(part, slice(part * high, (part + 1) * high)) for part in range(n_parts)]
    row, col = positions(high)
    for level in range(LAYERS):
        head_gain = head_gain_ref[level : level + 1, :].astype(F32)
        before = []
        for part, rows in parts:
            if level == 0:
                x = x_ref[rows].astype(F32)
            else:
                x = held["h"][level - 1, rows] + exchange.take(2 * level - 1, part, rows)
            held["x"][level, rows] = x
            n1 = low(x * rms_scale(x) * gain_ref[level, 0:1, :].astype(F32))
            held["n1"][level, rows] = n1
            logits = dot_nt(n1, wb[level])
            held["logits"][level, rows] = logits
            beta = sigmoid(logits)
            if part == 0:
                loads[level][0].wait()
            acts = []
            for index in range(3):
                held["p"][level, index, rows] = dot_nn(n1, wq[level, index])
                acts.append(
                    conv_silu_rows(
                        held["p"].at[level, index], taps_ref[level, index].astype(F32), rows
                    )
                )
            lowers, scores, values, now = [], [], [], []
            for head in range(heads):
                cols = head_cols(head)
                c0, c1, c2 = (act[:, cols] for act in acts)
                q = low(c0 * lax.rsqrt(jnp.sum(c0 * c0, axis=-1, keepdims=True) + 0.001))
                k = low(c1 * lax.rsqrt(jnp.sum(c1 * c1, axis=-1, keepdims=True) + 0.001))
                v = low(c2).astype(F32)
                gate = beta[:, head : head + 1]
                value = gate * v
                for key, u in before[head : head + 1]:
                    cross = halves(gate * dot_nt(k, key))
                    value = value - dot_nn(cross[0], u[0])
                    value = value - (dot_nn(cross[0], u[1]) + dot_nn(cross[1], u[0]))
                lowers.append(jnp.where(row > col, gate * dot_nt(k, k), 0.0))
                scores.append(low(jnp.where(row >= col, dot_nt(q, k), 0.0)))
                values.append(halves(value))
                now.append((q, k))
            inverse = unit_lower_inverse(lowers)
            after = []
            for head in range(heads):
                cols = head_cols(head)
                t_hi, t_lo = halves(inverse[head])
                held["t"][level, 0, head, part] = t_hi
                held["t"][level, 1, head, part] = t_lo
                u = halves(split_dot(dot_nn, (t_hi, t_lo), values[head]))
                held["u"][level, rows, cols] = u[0]
                o = dot_nn(scores[head], u[0])
                q, k = now[head]
                for key, early in before[head : head + 1]:
                    o = o + dot_nn(low(dot_nt(q, key)), early[0])
                after.append((k, u))
                held["o"][level, rows, cols] = o
                scale = lax.rsqrt(jnp.mean(o * o, axis=-1, keepdims=True) + 0.01)
                held["on"][level, rows, cols] = low(o * scale * head_gain)
            before = after
            if part == 0:
                loads[level][1].wait()
            out = dot_nn(held["on"][level, rows], wo[level])
            exchange.give(2 * level, part, rows, low(out))
        for name in ("x", "n1", "logits", "p", "t", "u", "o", "on"):
            keep(name, level)
        for part, rows in parts:
            h = held["x"][level, rows] + exchange.take(2 * level, part, rows)
            held["h"][level, rows] = h
            n2 = low(h * rms_scale(h) * gain_ref[level, 1:2, :].astype(F32))
            held["n2"][level, rows] = n2
            if part == 0:
                loads[level][2].wait()
            g = dot_nn(n2, wgu[level, 0])
            held["gu"][level, 0, rows] = g
            u = dot_nn(n2, wgu[level, 1])
            held["gu"][level, 1, rows] = u
            z = low(g * sigmoid(g) * u)
            held["z"][level, rows] = z
            if part == 0:
                loads[level][3].wait()
            out = low(dot_nn(z, wd[level]))
            if level < LAYERS - 1:
                exchange.give(2 * level + 1, part, rows, out)
            else:
                last[rows] = out
        for name in ("h", "n2", "gu", "z"):
            keep(name, level)
    final = pltpu.make_async_copy(last, last_out, load_sems.at[0, 0])
    final.start()
    for copy in keeps:
        copy.wait()
    final.wait()
    exchange.finish()


def forward(x, norm_gain, taps, head_gain, wb, wq, wo, wgu, wd):
    length, width = x.shape
    chans, hidden = wq.shape[-1], wgu.shape[-1]
    n_tensor = lax.axis_size("tensor")
    n_parts = 2
    kept = kept_shapes(length, width, chans, hidden)
    vmem = pl.BlockSpec(memory_space=pltpu.VMEM)
    hbm = pl.BlockSpec(memory_space=pl.ANY)
    spots = 2 * LAYERS - 1
    *kept, part = pl.pallas_call(
        functools.partial(forward_kernel, n_parts),
        out_shape=(
            *(jax.ShapeDtypeStruct(*spec) for spec in kept),
            jax.ShapeDtypeStruct((length, width), BF16),
        ),
        in_specs=[vmem] * 5 + [hbm] * 4,
        out_specs=(hbm,) * (len(kept) + 1),
        scratch_shapes=[
            *(pltpu.VMEM(*spec) for spec in kept),
            pltpu.VMEM((LAYERS, 3, width, chans), BF16),
            pltpu.VMEM((LAYERS, chans, width), BF16),
            pltpu.VMEM((LAYERS, 2, width, hidden), BF16),
            pltpu.VMEM((LAYERS, hidden, width), BF16),
            pltpu.VMEM((LAYERS, LANES, width), BF16),
            pltpu.VMEM((spots, n_tensor, length, width), BF16),
            pltpu.VMEM((length, width), BF16),
            pltpu.SemaphoreType.DMA((LAYERS, 4)),
            pltpu.SemaphoreType.DMA((len(kept), LAYERS)),
            pltpu.SemaphoreType.DMA((spots, n_parts, n_tensor - 1)),
            pltpu.SemaphoreType.DMA((spots, n_parts, n_tensor - 1)),
        ],
        compiler_params=pltpu.CompilerParams(
            vmem_limit_bytes=VMEM_LIMIT, collective_id=1, has_side_effects=True
        ),
        name="forward",
    )(x, norm_gain, taps, head_gain, wb, wq, wo, wgu, wd)
    return dict(zip(KEPT, kept)), part


def back_through_norm(level, which, gain_ref, e_ref, hid_ref, adds, rows_out):
    e = e_ref[...].astype(F32)
    if not adds:
        rows_out[...] = jnp.zeros_like(rows_out)
        return e
    total = adds[0][...].astype(F32)
    for add in adds[1:]:
        total = total + add[...].astype(F32)
    gain = gain_ref[level, which : which + 1, :].astype(F32)
    grad_hidden, rows = rms_back(hid_ref[...], gain, total)
    rows_out[...] = rows
    return e + grad_hidden


def mlp_backward_kernel(level, n_add, *refs):
    (e_ref, hid_ref, *adds) = refs[: 2 + n_add]
    (gain_ref, n2_ref, gu_ref, z_ref, wgu_hbm, wd_hbm) = refs[2 + n_add : 8 + n_add]
    (e_out, rows_out, part_out, gd_out, ggu_out) = refs[8 + n_add : 13 + n_add]
    wgu, wd, dgu_ref, sems = refs[13 + n_add :]
    loads = [
        pltpu.make_async_copy(wd_hbm.at[level], wd, sems.at[0]),
        pltpu.make_async_copy(wgu_hbm.at[level], wgu, sems.at[1]),
    ]
    for load in loads:
        load.start()
    e = back_through_norm(level + 1, 0, gain_ref, e_ref, hid_ref, adds, rows_out)
    e_out[...] = e
    ef = low(e)
    loads[0].wait()
    dz = dot_nt(ef, wd[...])
    g, u = gu_ref[0], gu_ref[1]
    s = sigmoid(g)
    dgu_ref[0] = low(dz * u * (s * (1.0 + g * (1.0 - s))))
    dgu_ref[1] = low(dz * (g * s))
    loads[1].wait()
    part_out[...] = low(dot_nt(dgu_ref[0], wgu[0]) + dot_nt(dgu_ref[1], wgu[1]))
    gd_out[...] = low(dot_tn(z_ref[...], ef))
    for half in range(2):
        ggu_out[half] = low(dot_tn(n2_ref[...], dgu_ref[half]))


def mlp_backward(level, e, hid, adds, norm_gain, n2, gu, z, wgu, wd):
    length, width = e.shape
    hidden = wgu.shape[-1]
    sds = jax.ShapeDtypeStruct
    vmem = pl.BlockSpec(memory_space=pltpu.VMEM)
    hbm = pl.BlockSpec(memory_space=pl.ANY)
    return pl.pallas_call(
        functools.partial(mlp_backward_kernel, level, len(adds)),
        out_shape=(
            sds((length, width), F32),
            sds((1, width), F32),
            sds((length, width), BF16),
            sds((hidden, width), BF16),
            sds((2, width, hidden), BF16),
        ),
        in_specs=[vmem] * (6 + len(adds)) + [hbm, hbm],
        out_specs=(vmem,) * 5,
        scratch_shapes=[
            pltpu.VMEM((2, width, hidden), BF16),
            pltpu.VMEM((hidden, width), BF16),
            pltpu.VMEM((2, length, hidden), BF16),
            pltpu.SemaphoreType.DMA((2,)),
        ],
        compiler_params=pltpu.CompilerParams(vmem_limit_bytes=VMEM_LIMIT),
        name="mlp_backward",
    )(e, hid, *adds, norm_gain, n2, gu, z, wgu, wd)


def mixer_backward_kernel(level, heads, n_add, *refs):
    (e_ref, hid_ref, *adds) = refs[: 2 + n_add]
    (gain_ref, taps_ref, head_gain_ref, wb_ref, n1_ref, p_ref, logit_ref, t_ref, u_ref, o_ref) = (
        refs[2 + n_add : 12 + n_add]
    )
    (on_ref, wq_hbm, wo_hbm) = refs[12 + n_add : 15 + n_add]
    (e_out, part_out, small_out, gq_out, go_out) = refs[15 + n_add : 20 + n_add]
    wq, wo, grads, dp_ref, rows_out, wb, sems = refs[20 + n_add :]
    loads = [
        pltpu.make_async_copy(wo_hbm.at[level], wo, sems.at[0]),
        pltpu.make_async_copy(wq_hbm.at[level], wq, sems.at[1]),
    ]
    for load in loads:
        load.start()
    e = back_through_norm(level, 1, gain_ref, e_ref, hid_ref, adds, rows_out)
    e_out[...] = e
    em = low(e)
    length = e.shape[0]
    loads[0].wait()
    don = dot_nt(em, wo[...])
    go_out[...] = low(dot_tn(on_ref[...], em))
    beta = sigmoid(logit_ref[...])
    row, col = positions(length)
    lane = lax.broadcasted_iota(jnp.int32, (length, LANES), 1)
    head_gain = head_gain_ref[level : level + 1, :].astype(F32)
    convs = [conv_silu(p_ref[part], taps_ref[level, part].astype(F32)) for part in range(3)]
    gain_rows = jnp.zeros((1, DK), F32)
    dlogit = jnp.zeros((length, LANES), F32)
    for head in range(heads):
        cols = head_cols(head)
        c0, c1, c2 = (conv[2][:, cols] for conv in convs)
        rho0 = lax.rsqrt(jnp.sum(c0 * c0, axis=-1, keepdims=True) + 0.001)
        rho1 = lax.rsqrt(jnp.sum(c1 * c1, axis=-1, keepdims=True) + 0.001)
        q, k, v = low(c0 * rho0), low(c1 * rho1), low(c2).astype(F32)
        gate = beta[:, head : head + 1]
        o = o_ref[:, cols]
        scale = lax.rsqrt(jnp.mean(o * o, axis=-1, keepdims=True) + 0.01)
        dn = don[:, cols]
        weighted = dn * head_gain
        inner = jnp.mean(o * weighted, axis=-1, keepdims=True)
        do = low(scale * weighted - o * (scale * scale * scale) * inner)
        gain_rows = gain_rows + jnp.sum(dn * o * scale, axis=0, keepdims=True)
        u = u_ref[:, cols]
        score_t = low(jnp.where(row <= col, dot_nt(k, q), 0.0))
        du = dot_nn(score_t, do)
        ds = low(jnp.where(row >= col, dot_nt(do, u), 0.0))
        ds_t = low(jnp.where(row <= col, dot_nt(u, do), 0.0))
        dq = dot_nn(ds, k)
        dk = dot_nn(ds_t, q)
        blocks = [(t_ref[0, head, index], t_ref[1, head, index]) for index in range(2)]
        r = solve_back(blocks, k, gate, du)
        dv = gate * r
        dv_low = low(dv)
        gram = low(jnp.where(row > col, dot_nt(k, k), 0.0))
        w = v - dot_nn(gram, u)
        dbeta = jnp.sum(r * w, axis=-1, keepdims=True)
        dgram = jnp.where(row > col, dot_nt(dv_low, u), 0.0) + jnp.where(
            row < col, dot_nt(u, dv_low), 0.0
        )
        dk = dk - dot_nn(low(dgram), k)
        grads[0, :, cols] = rho0 * dq - c0 * (rho0 * rho0 * rho0) * jnp.sum(
            c0 * dq, axis=-1, keepdims=True
        )
        grads[1, :, cols] = rho1 * dk - c1 * (rho1 * rho1 * rho1) * jnp.sum(
            c1 * dk, axis=-1, keepdims=True
        )
        grads[2, :, cols] = dv
        dlogit = dlogit + jnp.where(lane == head, dbeta * gate * (1.0 - gate), 0.0)
    chans = grads.shape[-1]
    small_out[...] = jnp.zeros_like(small_out)
    small_out[0:1, SIDE : SIDE + DK] = gain_rows
    half = rows_out.shape[-1] // 2
    small_out[1:2, SIDE:] = rows_out[:, :half]
    small_out[2:3, SIDE:] = rows_out[:, half:]
    dlogit_low = low(dlogit)
    n1 = n1_ref[...]
    small_out[3 * KCONV : 3 * KCONV + heads, :] = dot_tn(dlogit_low, n1)[:heads, :]
    for part in range(3):
        taps = taps_ref[level, part].astype(F32)
        total, gate, _ = convs[part]
        dsum = grads[part] * (gate * (1.0 + total * (1.0 - gate)))
        p = p_ref[part]
        dp = taps[KCONV - 1 : KCONV, :] * dsum
        for tap in range(KCONV):
            back = KCONV - 1 - tap
            spot = part * KCONV + tap
            small_out[spot : spot + 1, :chans] = jnp.sum(
                dsum * shift_down(p, back), axis=0, keepdims=True
            )
            if back:
                dp = dp + taps[tap : tap + 1, :] * shift_up(dsum, back)
        dp_ref[part] = low(dp)
    loads[1].wait()
    wb[...] = jnp.zeros_like(wb)
    wb[:heads] = wb_ref[level]
    dn1 = dot_nn(dlogit_low, wb[...])
    for part in range(3):
        dn1 = dn1 + dot_nt(dp_ref[part], wq[part])
    part_out[...] = low(dn1)
    for part in range(3):
        gq_out[part] = low(dot_tn(n1, dp_ref[part]))


def mixer_backward(level, e, hid, adds, norm_gain, taps, head_gain, wb, kept, wq, wo):
    length, width = e.shape
    chans = wq.shape[-1]
    heads = chans // DK
    sds = jax.ShapeDtypeStruct
    vmem = pl.BlockSpec(memory_space=pltpu.VMEM)
    hbm = pl.BlockSpec(memory_space=pl.ANY)
    return pl.pallas_call(
        functools.partial(mixer_backward_kernel, level, heads, len(adds)),
        out_shape=(
            sds((length, width), F32),
            sds((length, width), BF16),
            sds((16, width), F32),
            sds((3, width, chans), BF16),
            sds((chans, width), BF16),
        ),
        in_specs=[vmem] * (13 + len(adds)) + [hbm, hbm],
        out_specs=(vmem,) * 5,
        scratch_shapes=[
            pltpu.VMEM((3, width, chans), BF16),
            pltpu.VMEM((chans, width), BF16),
            pltpu.VMEM((3, length, chans), F32),
            pltpu.VMEM((3, length, chans), BF16),
            pltpu.VMEM((1, width), F32),
            pltpu.VMEM((LANES, width), BF16),
            pltpu.SemaphoreType.DMA((2,)),
        ],
        compiler_params=pltpu.CompilerParams(vmem_limit_bytes=VMEM_LIMIT),
        name="mixer_backward",
    )(e, hid, *adds, norm_gain, taps, head_gain, wb, *kept, wq, wo)


def branch_parts(part):
    count = lax.axis_size("tensor")
    if count == 1:
        return (part,)
    if count == 2:
        return (part, lax.ppermute(part, "tensor", [(0, 1), (1, 0)]))
    return (lax.psum(part, "tensor"),)


def sum_over_dp(tables):
    shapes = [table.shape for table in tables]
    flat = jnp.concatenate([table.reshape(-1) for table in tables])
    size = flat.shape[0]
    count = lax.axis_size("dp")
    pad = -size % (count * 1024)
    flat = jnp.pad(flat, (0, pad))
    shard = lax.psum_scatter(flat, "dp", scatter_dimension=0, tiled=True)
    joined = lax.all_gather(shard, "dp", axis=0, tiled=True)
    pieces = []
    offset = 0
    for shape in shapes:
        size = math.prod(shape)
        pieces.append(joined[offset : offset + size].reshape(shape))
        offset = offset + size
    return pieces


def fold_spot(depth, side, core):
    return (depth * 2 + side) * 2 + core


def remote(source, target, send, recv, device):
    return pltpu.make_async_remote_copy(
        src_ref=source,
        dst_ref=target,
        send_sem=send,
        recv_sem=recv,
        device_id=device,
        device_id_type=pl.DeviceIdType.MESH,
    )


DEPTH = 4
CHUNKS = 8
STEPS = CHUNKS // 2
SLOTS = ("p1", "p2", "p3", "e1", "e2", "e3", "e4")
KINDS = (*SLOTS, "p4e", "p4y", "pf0", "pf1", "pk", "e5", "e6", "e7", "ef0", "ef1", "ek")


class Fold:
    def __init__(self, cuts, own, slots, totals, sems):
        self.cuts, self.own, self.slots, self.totals = cuts, own, slots, totals
        self.send_sems, self.recv_sems = sems
        spot = lax.axis_index("dp")
        self.core = lax.rem(spot, 2)
        side = lax.rem(lax.div(spot, 2), 2)
        depth = lax.div(spot, 4)
        self.is_mid = (depth == 1) | (depth == 2)
        self.is_end = (depth == 0) | (depth == 3)
        folded = depth + 1 - 2 * lax.rem(depth, 2)
        across = DEPTH - 1 - depth
        half = lax.div(depth, 2)
        self.partner = {"dp": fold_spot(depth, side, 1 - self.core)}
        self.beside = {"dp": fold_spot(depth, 1 - side, self.core)}
        self.folded = {"dp": fold_spot(folded, side, self.core)}
        self.across = {"dp": fold_spot(across, side, self.core)}
        self.mine = [[base * STEPS + step for step in range(STEPS)] for base in (side, half)]
        self.others = [
            [(1 - base) * STEPS + step for step in range(STEPS)] for base in (side, half)
        ]
        self.done = [0] * len(cuts)
        self.active, self.waiting = [], []

    def piece(self, index, chunk, way):
        kind, rows, cols = self.cuts[index]
        ref = self.own[index]
        if kind == "cols":
            return ref.at[
                pl.ds(pl.multiple_of(chunk * rows, rows), rows), way * cols : (way + 1) * cols
            ]
        if kind == "rows":
            start = pl.multiple_of(chunk * (2 * rows) + way * rows, rows)
            return ref.at[pl.ds(start, rows), :]
        return ref.at[
            way * rows : (way + 1) * rows, pl.ds(pl.multiple_of(chunk * cols, cols), cols)
        ]

    def spot(self, index, chunk, way):
        kind, rows, cols = self.cuts[index]
        ref = self.totals[index]
        if kind == "cols":
            start = pl.multiple_of(self.core * (2 * cols) + way * cols, cols)
            return ref.at[pl.ds(pl.multiple_of(chunk * rows, rows), rows), pl.ds(start, cols)]
        if kind == "rows":
            start = pl.multiple_of(chunk * (2 * rows) + way * rows, rows)
            return ref.at[self.core, pl.ds(start, rows), :]
        start = pl.multiple_of(self.core * (2 * rows) + way * rows, rows)
        return ref.at[pl.ds(start, rows), pl.ds(pl.multiple_of(chunk * cols, cols), cols)]

    def family(self, index):
        return index % 4 if index < SMALL else 4

    def slot(self, name, index, step):
        return self.slots[self.family(index)].at[SLOTS.index(name), step]

    def copy(self, name, index, step, kept=True):
        way = 1 if name[0] == "e" else 0
        far = name in ("p1", "pf1", "e1", "e2", "e7", "ef1")
        chunk = (self.others if far else self.mine)[way][step]
        device = self.folded
        if name in ("p1", "p4y", "e4"):
            device = self.beside
        elif name in ("p3", "e2", "e6"):
            device = self.across
        elif name[1] == "f":
            device = self.partner
        source = self.piece(index, chunk, way)
        if name in SLOTS:
            target = self.slot(name, index, step)
        else:
            target = self.spot(index, chunk, way)
            if name in ("pf1", "ef1", "e6", "e7") or not kept:
                source = target
        at = (KINDS.index(name), index, step)
        if name[1] == "k":
            return pltpu.make_async_copy(source, target, self.recv_sems.at[at])
        return remote(source, target, self.send_sems.at[at], self.recv_sems.at[at], device)

    def start(self, names, index, step, kept=True):
        for name in names:
            self.copy(name, index, step, kept).start()

    def add(self, name, index, step, chunk):
        self.copy(name, index, step).wait_recv()
        mine = self.piece(index, chunk, 1 if name[0] == "e" else 0)
        both = mine[...].astype(F32) + self.slot(name, index, step)[...].astype(F32)
        mine[...] = both.astype(mine.dtype)

    def stage_one(self, index, step):
        self.start(("p1",), index, step)

        @pl.when(self.is_end)
        def _():
            self.start(("e1",), index, step)

    def stage_two(self, index, step):
        self.add("p1", index, step, self.mine[0][step])

        @pl.when(self.is_end)
        def _():
            self.start(("p2",), index, step)

        @pl.when(self.is_mid)
        def _():
            self.add("e1", index, step, self.others[1][step])
            self.start(("e2",), index, step)

    def stage_three(self, index, step):
        @pl.when(self.is_mid)
        def _():
            self.add("p2", index, step, self.mine[0][step])
            self.start(("p3",), index, step)
            self.add("e2", index, step, self.mine[1][step])
            self.start(("e3",), index, step)

    def stage_four(self, index, step):
        @pl.when(self.is_mid)
        def _():
            self.copy("p3", index, step).wait_send()
            self.add("p3", index, step, self.mine[0][step])
            self.start(("p4e", "p4y", "pf0", "pk"), index, step)

        @pl.when(self.is_end)
        def _():
            self.add("e3", index, step, self.mine[1][step])
            self.start(("e4",), index, step)

    def stage_five(self, index, step):
        @pl.when(self.is_end)
        def _():
            self.copy("e4", index, step).wait_send()
            self.add("e4", index, step, self.mine[1][step])
            self.start(("e5", "ef0", "ek"), index, step)
            self.copy("p4e", index, step).wait_recv()
            self.start(("p4y", "pf0"), index, step, False)

    def stage_six(self, index, step):
        self.copy("p4y", index, step).wait_recv()
        self.start(("pf1",), index, step)

        @pl.when(self.is_mid)
        def _():
            self.copy("e5", index, step).wait_recv()
            self.start(("e6", "ef0"), index, step, False)

    def stage_seven(self, index, step):
        @pl.when(self.is_mid)
        def _():
            self.copy("e6", index, step).wait_recv()
            self.start(("e7", "ef1"), index, step)

    def stage_eight(self, index, step):
        @pl.when(self.is_end)
        def _():
            self.copy("e7", index, step).wait_recv()
            self.start(("ef1",), index, step)

    def settle(self, index, step):
        for name in ("p1", "p4y"):
            self.copy(name, index, step).wait_send()
        for name in ("pf0", "pf1", "ef0", "ef1"):
            self.copy(name, index, step).wait()

        @pl.when(self.is_end)
        def _():
            for name in ("e1", "p2", "e5"):
                self.copy(name, index, step).wait_send()
            self.copy("ek", index, step).wait()

        @pl.when(self.is_mid)
        def _():
            for name in ("e2", "e3", "p4e", "e6", "e7"):
                self.copy(name, index, step).wait_send()
            self.copy("pk", index, step).wait()

    def advance(self, index):
        stages = (
            self.stage_one,
            self.stage_two,
            self.stage_three,
            self.stage_four,
            self.stage_five,
            self.stage_six,
            self.stage_seven,
            self.stage_eight,
        )
        tick = self.done[index]
        self.done[index] = tick + 1
        last = STEPS + len(stages) - 1
        if tick == last:
            for step in range(STEPS):
                self.settle(index, step)
            return False
        for offset, stage in reversed(list(enumerate(stages))):
            if 0 <= tick - offset < STEPS:
                stage(index, tick - offset)
        return True

    def begin(self, index):
        if any(self.family(index) == self.family(held) for held in self.active):
            self.waiting.append(index)
        else:
            self.active.append(index)

    def serve(self, count=1):
        for _ in range(count):
            if not self.active:
                return
            index = self.active.pop(0)
            if self.advance(index):
                self.active.append(index)
                continue
            for other in self.waiting:
                if self.family(other) == self.family(index):
                    self.waiting.remove(other)
                    self.active.append(other)
                    break


def fold_cuts(n_dp, width, chans, hidden):
    if n_dp != 4 * DEPTH or width != CHUNKS * LANES or chans % (4 * LANES) or hidden % LANES:
        return None
    if any(rows % (16 * CHUNKS) for rows in (hidden, chans, width)):
        return None
    layer = [
        ("cols", hidden // CHUNKS, width // 4),
        ("rows", width // (2 * CHUNKS), hidden),
        ("cols", chans // CHUNKS, width // 4),
        ("cols", 3 * width // CHUNKS, chans // 4),
    ]
    return layer * LAYERS + [("small", 8, LANES)]


DOWN, GATE_UP, OUT, QKV = range(4)
SMALL = 4 * LAYERS
MLP_KEPT = ("gu", "z", "n2")
MIXER_KEPT = ("n1", "p", "logits", "t", "u", "o", "on", "h")
PEERS = ("z", "n2", "ef", "dgu", "n1", "on", "em", "dp")


def backward_kernel(n_parts, cuts, *refs):
    refs = list(refs)

    def taken(count):
        group = refs[:count]
        del refs[:count]
        return group

    (cot_ref, gain_ref, taps_ref, head_gain_ref, wb_ref) = taken(5)
    (part_hbm, wq_hbm, wo_hbm, wgu_hbm, wd_hbm) = taken(5)
    kept = dict(zip(KEPT, taken(len(KEPT))))
    (out_ref, in_grad_ref, *totals) = taken(2 + 5)
    own = taken(len(cuts))
    fold_slots = taken(5)
    peers = dict(zip(PEERS, taken(len(PEERS))))
    (e_ref, small, small_peer, slots, don_ref, wb, gains) = taken(7)
    (load_sems, send_sems, recv_sems, peer_sems, gain_sems) = taken(5)
    fold_sems = taken(2)

    per_table = [totals[index].at[level] for level in range(LAYERS) for index in range(4)]
    fold = Fold(cuts, own, fold_slots, [*per_table, totals[4]], fold_sems)
    core, serve = fold.core, fold.serve
    exchange = Exchange(slots, send_sems, recv_sems)
    barrier = pltpu.get_barrier_semaphore()
    for device in (fold.partner, fold.beside, fold.folded, fold.across):
        pl.semaphore_signal(barrier, inc=1, device_id=device, device_id_type=pl.DeviceIdType.MESH)
    exchange.greet(4)

    length, width = e_ref.shape
    chans = wo_hbm.shape[1]
    hidden = wd_hbm.shape[1]
    heads = chans // DK
    high = length // n_parts
    parts = [(part, slice(part * high, (part + 1) * high)) for part in range(n_parts)]
    row, col = positions(length)
    lane = lax.broadcasted_iota(jnp.int32, (length, LANES), 1)
    side = width - SIDE
    half_width, half_chans = width // 2, chans // 2

    def other_half(wide):
        return pl.ds(pl.multiple_of((1 - core) * wide, LANES), wide)

    def own_half(wide):
        return pl.ds(pl.multiple_of(core * wide, LANES), wide)

    def to_peer(name, level, source):
        spot = PEERS.index(name)
        return remote(
            source,
            peers[name].at[level],
            peer_sems.at[0, spot, level],
            peer_sems.at[1, spot, level],
            fold.partner,
        )

    top = LAYERS - 1
    early = [
        to_peer(name, level, kept[name].at[level])
        for level in reversed(range(LAYERS))
        for name in ("z", "n2", "on", "n1")
    ]
    early.insert(1, to_peer("ef", top, cot_ref.at[:, other_half(width // 2)]))
    for copy in early:
        copy.start()
    first = pltpu.make_async_copy(part_hbm, slots.at[0, exchange.me], load_sems.at[0, 0, 0])
    first.start()
    small[...] = jnp.zeros_like(small)

    def norm_step(level, which, spot, part, rows, hid):
        total = exchange.take(spot, part, rows)
        gain = gain_ref[level, which : which + 1, :].astype(F32)
        grad_hidden, sums = rms_back(hid, gain, total)
        base = 16 * level + (1 if which else 3)
        for index in range(2):
            spot_row = slice(base + index, base + index + 1)
            small[spot_row, SIDE:] += sums[:, index * side : (index + 1) * side]
        return e_ref[rows] + grad_hidden

    def mlp_stage(level):
        def scope(wgu, wd, gu, z, n2, hid, dgu, ef):
            held = dict(gu=gu, z=z, n2=n2)
            loads = {
                "wd": pltpu.make_async_copy(wd_hbm.at[level], wd, load_sems.at[level, 0, 1]),
                "wgu": pltpu.make_async_copy(wgu_hbm.at[level], wgu, load_sems.at[level, 0, 2]),
            }
            for index, name in enumerate(MLP_KEPT):
                loads[name] = pltpu.make_async_copy(
                    kept[name].at[level], held[name], load_sems.at[level, 0, 3 + index]
                )
            if level < LAYERS - 1:
                loads["hid"] = pltpu.make_async_copy(
                    kept["x"].at[level + 1], hid, load_sems.at[level, 0, 6]
                )
                loads["hid"].start()
            for name in ("z", "wd", "gu", "wgu", "n2"):
                loads[name].start()
            index = 4 * level
            if level == top:
                first.wait()
                for part, rows in parts:
                    exchange.send(0, part, rows)
                loads["z"].wait()
                for name in ("z", "ef"):
                    to_peer(name, level, peers[name].at[level]).wait_recv()
                own[index + DOWN][...] = low(
                    dot_tn(z[...], cot_ref[:, own_half(half_width)])
                    + dot_tn(peers["z"][level], peers["ef"][level])
                )
                fold.begin(index + DOWN)
            for part, rows in parts:
                serve()
                if level == LAYERS - 1:
                    e = cot_ref[rows].astype(F32)
                else:
                    if part == 0:
                        loads["hid"].wait()
                    e = norm_step(level + 1, 0, 2 * (LAYERS - 1 - level), part, rows, hid[rows])
                e_ref[rows] = e
                e_low = low(e)
                ef[rows] = e_low
                if part == 0:
                    loads["wd"].wait()
                dz = dot_nt(e_low, wd[...])
                if part == 0:
                    loads["gu"].wait()
                g, u = gu[0, rows], gu[1, rows]
                s = sigmoid(g)
                dgu[0, rows] = low(dz * u * (s * (1.0 + g * (1.0 - s))))
                dgu[1, rows] = low(dz * (g * s))
                if part == 0:
                    loads["wgu"].wait()
                partial = dot_nt(dgu[0, rows], wgu[0]) + dot_nt(dgu[1, rows], wgu[1])
                exchange.give(2 * (LAYERS - 1 - level) + 1, part, rows, low(partial))
            sends = [to_peer("dgu", level, dgu.at[1 - core])]
            if level != top:
                sends.append(to_peer("ef", level, ef.at[:, other_half(half_width)]))
            for send in sends:
                send.start()
            serve()
            loads["n2"].wait()
            for name in ("n2", "dgu"):
                to_peer(name, level, peers[name].at[level]).wait_recv()
            own[index + GATE_UP][...] = low(
                dot_tn(n2[...], dgu[core]) + dot_tn(peers["n2"][level], peers["dgu"][level])
            )
            fold.begin(index + GATE_UP)
            serve()
            if level != top:
                loads["z"].wait()
                for name in ("z", "ef"):
                    to_peer(name, level, peers[name].at[level]).wait_recv()
                own[index + DOWN][...] = low(
                    dot_tn(z[...], ef[:, own_half(half_width)])
                    + dot_tn(peers["z"][level], peers["ef"][level])
                )
                fold.begin(index + DOWN)
                serve()
            for send in sends:
                send.wait_send()

        pl.run_scoped(
            scope,
            pltpu.VMEM((2, width, hidden), BF16),
            pltpu.VMEM((hidden, width), BF16),
            pltpu.VMEM((2, length, hidden), F32),
            pltpu.VMEM((length, hidden), BF16),
            pltpu.VMEM((length, width), BF16),
            pltpu.VMEM((length, width), F32),
            pltpu.VMEM((2, length, hidden), BF16),
            pltpu.VMEM((length, width), BF16),
        )

    def mixer_stage(level):
        def scope(wq, wo, n1, p, logits, t, u_all, o_all, on, h, grads, dp, em):
            held = dict(n1=n1, p=p, logits=logits, t=t, u=u_all, o=o_all, on=on, h=h)
            loads = {
                "wo": pltpu.make_async_copy(wo_hbm.at[level], wo, load_sems.at[level, 1, 0]),
                "wq": pltpu.make_async_copy(wq_hbm.at[level], wq, load_sems.at[level, 1, 1]),
            }
            for index, name in enumerate(MIXER_KEPT):
                loads[name] = pltpu.make_async_copy(
                    kept[name].at[level], held[name], load_sems.at[level, 1, 2 + index]
                )
            for name in ("h", "wo", "p", "o", "u", "logits", "t", "wq", "n1", "on"):
                loads[name].start()
            serve()
            loads["p"].wait()
            convs = [
                conv_silu(p[index], taps_ref[level, index].astype(F32)) for index in range(3)
            ]
            spot = 2 * (LAYERS - 1 - level) + 1
            loads["h"].wait()
            if level == LAYERS - 1:
                for part, rows in parts:
                    out_ref[rows] = low(h[rows] + exchange.take(0, part, rows))
            for part, rows in parts:
                serve()
                e = norm_step(level, 1, spot, part, rows, h[rows])
                e_ref[rows] = e
                e_low = low(e)
                em[rows] = e_low
                if part == 0:
                    loads["wo"].wait()
                don_ref[rows] = dot_nt(e_low, wo[...])
            send_em = to_peer("em", level, em.at[:, other_half(half_width)])
            send_em.start()
            for name in ("o", "u", "logits", "t"):
                loads[name].wait()
            beta = sigmoid(logits[...])
            head_gain = head_gain_ref[level : level + 1, :].astype(F32)
            gain_rows = jnp.zeros((1, DK), F32)
            dlogit = jnp.zeros((length, LANES), F32)
            serve()
            for head in range(heads):
                cols = head_cols(head)
                c0, c1, c2 = (conv[2][:, cols] for conv in convs)
                rho0 = lax.rsqrt(jnp.sum(c0 * c0, axis=-1, keepdims=True) + 0.001)
                rho1 = lax.rsqrt(jnp.sum(c1 * c1, axis=-1, keepdims=True) + 0.001)
                q, k, v = low(c0 * rho0), low(c1 * rho1), low(c2).astype(F32)
                gate = beta[:, head : head + 1]
                o = o_all[:, cols]
                scale = lax.rsqrt(jnp.mean(o * o, axis=-1, keepdims=True) + 0.01)
                dn = don_ref[:, cols]
                weighted = dn * head_gain
                inner = jnp.mean(o * weighted, axis=-1, keepdims=True)
                do = low(scale * weighted - o * (scale * scale * scale) * inner)
                gain_rows = gain_rows + jnp.sum(dn * o * scale, axis=0, keepdims=True)
                u = u_all[:, cols]
                score_t = low(jnp.where(row <= col, dot_nt(k, q), 0.0))
                du = dot_nn(score_t, do)
                ds = low(jnp.where(row >= col, dot_nt(do, u), 0.0))
                ds_t = low(jnp.where(row <= col, dot_nt(u, do), 0.0))
                dq = dot_nn(ds, k)
                dk = dot_nn(ds_t, q)
                blocks = [(t[0, head, index], t[1, head, index]) for index in range(2)]
                r = solve_back(blocks, k, gate, du)
                dv = gate * r
                dv_low = low(dv)
                gram = low(jnp.where(row > col, dot_nt(k, k), 0.0))
                w = v - dot_nn(gram, u)
                dbeta = jnp.sum(r * w, axis=-1, keepdims=True)
                dgram = jnp.where(row > col, dot_nt(dv_low, u), 0.0) + jnp.where(
                    row < col, dot_nt(u, dv_low), 0.0
                )
                dk = dk - dot_nn(low(dgram), k)
                grads[0, :, cols] = rho0 * dq - c0 * (rho0 * rho0 * rho0) * jnp.sum(
                    c0 * dq, axis=-1, keepdims=True
                )
                grads[1, :, cols] = rho1 * dk - c1 * (rho1 * rho1 * rho1) * jnp.sum(
                    c1 * dk, axis=-1, keepdims=True
                )
                grads[2, :, cols] = dv
                dlogit = dlogit + jnp.where(lane == head, dbeta * gate * (1.0 - gate), 0.0)
                if head % 2:
                    serve()
            base = 16 * level
            small[base : base + 1, SIDE : SIDE + DK] = gain_rows
            for index in range(3):
                taps = taps_ref[level, index].astype(F32)
                total, gate, _ = convs[index]
                dsum = grads[index] * (gate * (1.0 + total * (1.0 - gate)))
                project = p[index]
                dproject = taps[KCONV - 1 : KCONV, :] * dsum
                for tap in range(KCONV):
                    back = KCONV - 1 - tap
                    line = base + index * KCONV + tap
                    small[line : line + 1, :chans] = jnp.sum(
                        dsum * shift_down(project, back), axis=0, keepdims=True
                    )
                    if back:
                        dproject = dproject + taps[tap : tap + 1, :] * shift_up(dsum, back)
                dp[index] = low(dproject)
            dlogit_low = low(dlogit)
            wb[...] = jnp.zeros_like(wb)
            wb[:heads] = wb_ref[level]
            loads["wq"].wait()
            for part, rows in parts:
                dn1 = dot_nn(dlogit_low[rows], wb[...])
                for index in range(3):
                    dn1 = dn1 + dot_nt(dp[index, rows], wq[index])
                exchange.give(spot + 1, part, rows, low(dn1))
            send_dp = to_peer("dp", level, dp.at[:, :, other_half(half_chans)])
            send_dp.start()
            serve()
            loads["n1"].wait()
            loads["on"].wait()
            line = base + 3 * KCONV
            small[line : line + heads, :] = dot_tn(dlogit_low, n1[...])[:heads, :]
            for name in ("em", "on", "n1", "dp"):
                to_peer(name, level, peers[name].at[level]).wait_recv()
            own[4 * level + OUT][...] = low(
                dot_tn(on[...], em[:, own_half(half_width)])
                + dot_tn(peers["on"][level], peers["em"][level])
            )
            fold.begin(4 * level + OUT)
            serve()
            for index in range(3):
                own[4 * level + QKV][index * width : (index + 1) * width] = low(
                    dot_tn(n1[...], dp[index, :, own_half(half_chans)])
                    + dot_tn(peers["n1"][level], peers["dp"][level, index])
                )
            fold.begin(4 * level + QKV)
            serve()
            send_em.wait_send()
            send_dp.wait_send()

        pl.run_scoped(
            scope,
            pltpu.VMEM((3, width, chans), BF16),
            pltpu.VMEM((chans, width), BF16),
            pltpu.VMEM((length, width), BF16),
            pltpu.VMEM((3, length, chans), F32),
            pltpu.VMEM((length, LANES), F32),
            pltpu.VMEM((2, heads, 2, length // 2, length // 2), BF16),
            pltpu.VMEM((length, chans), BF16),
            pltpu.VMEM((length, chans), F32),
            pltpu.VMEM((length, chans), BF16),
            pltpu.VMEM((length, width), F32),
            pltpu.VMEM((3, length, chans), F32),
            pltpu.VMEM((3, length, chans), BF16),
            pltpu.VMEM((length, width), BF16),
        )

    for level in reversed(range(LAYERS)):
        mlp_stage(level)
        mixer_stage(level)

    for level in range(LAYERS):
        gains[exchange.me, level : level + 1] = small[
            16 * level : 16 * level + 1, SIDE : SIDE + DK
        ]
    gain_copies = [
        remote(
            gains.at[exchange.me],
            gains.at[exchange.me],
            gain_sems.at[0, away],
            gain_sems.at[1, away],
            device,
        )
        for away, device in enumerate(exchange.others)
    ]
    for copy in gain_copies:
        copy.start()

    def last_scope(hid):
        load = pltpu.make_async_copy(kept["x"].at[0], hid, load_sems.at[0, 0, 7])
        load.start()
        serve(len(fold.active))
        load.wait()
        for part, rows in parts:
            in_grad_ref[rows] = low(norm_step(0, 0, 2 * LAYERS, part, rows, hid[rows]))

    pl.run_scoped(last_scope, pltpu.VMEM((length, width), F32))

    for copy in gain_copies:
        copy.wait()
    for level in range(LAYERS):
        total = gains[0, level : level + 1]
        for index in range(1, exchange.count):
            total = total + gains[index, level : level + 1]
        small[16 * level : 16 * level + 1, SIDE : SIDE + DK] = total

    def small_half(which):
        return small.at[pl.ds(pl.multiple_of(which * 16, 16), 16)]

    send_small = remote(
        small_half(1 - core),
        small_peer,
        load_sems.at[1, 0, 6],
        load_sems.at[1, 0, 7],
        fold.partner,
    )
    send_small.start()
    serve(len(fold.active))
    send_small.wait_recv()
    own[SMALL][...] = small_half(core)[...] + small_peer[...]
    fold.begin(SMALL)
    while fold.active:
        serve()
    send_small.wait_send()
    for copy in early:
        copy.wait_send()
    exchange.finish()


def backward(cot, part, saved, norm_gain, taps, head_gain, wb, wq, wo, wgu, wd):
    length, width = cot.shape
    chans, hidden = wq.shape[-1], wgu.shape[-1]
    heads = chans // DK
    n_tensor = lax.axis_size("tensor")
    cuts = fold_cuts(lax.axis_size("dp"), width, chans, hidden)
    n_parts = 2
    sds = jax.ShapeDtypeStruct
    vmem = pl.BlockSpec(memory_space=pltpu.VMEM)
    hbm = pl.BlockSpec(memory_space=pl.ANY)
    own, slots = [], []
    for index, (kind, rows, cols) in enumerate(cuts):
        dtype = F32 if kind == "small" else BF16
        half = {
            "cols": (rows * CHUNKS, 2 * cols),
            "rows": (2 * rows * CHUNKS, cols),
            "small": (2 * rows, cols * CHUNKS),
        }[kind]
        own.append(pltpu.VMEM(half, dtype))
        if index < 4 or index == SMALL:
            slots.append(pltpu.VMEM((len(SLOTS), STEPS, rows, cols), dtype))
    peers = dict(
        z=(length, hidden),
        n2=(length, width),
        ef=(length, width // 2),
        dgu=(length, hidden),
        n1=(length, width),
        on=(length, chans),
        em=(length, width // 2),
        dp=(3, length, chans // 2),
    )
    spots = 2 * LAYERS + 1
    return pl.pallas_call(
        functools.partial(backward_kernel, n_parts, cuts),
        out_shape=(
            sds((length, width), BF16),
            sds((length, width), BF16),
            sds((LAYERS, hidden, width), BF16),
            sds((LAYERS, 2, width, hidden), BF16),
            sds((LAYERS, chans, width), BF16),
            sds((LAYERS, 3 * width, chans), BF16),
            sds((16 * LAYERS, width), F32),
        ),
        in_specs=[vmem] * 5 + [hbm] * (5 + len(KEPT)),
        out_specs=(vmem, vmem) + (hbm,) * 5,
        scratch_shapes=[
            *own,
            *slots,
            *(pltpu.VMEM((LAYERS, *peers[name]), BF16) for name in PEERS),
            pltpu.VMEM((length, width), F32),
            pltpu.VMEM((16 * LAYERS, width), F32),
            pltpu.VMEM((16, width), F32),
            pltpu.VMEM((spots, n_tensor, length, width), BF16),
            pltpu.VMEM((length, chans), F32),
            pltpu.VMEM((LANES, width), BF16),
            pltpu.VMEM((n_tensor, 8, DK), F32),
            pltpu.SemaphoreType.DMA((LAYERS, 2, 10)),
            pltpu.SemaphoreType.DMA((spots, n_parts, n_tensor - 1)),
            pltpu.SemaphoreType.DMA((spots, n_parts, n_tensor - 1)),
            pltpu.SemaphoreType.DMA((2, len(PEERS), LAYERS)),
            pltpu.SemaphoreType.DMA((2, n_tensor - 1)),
            pltpu.SemaphoreType.DMA((len(KINDS), len(cuts), STEPS)),
            pltpu.SemaphoreType.DMA((len(KINDS), len(cuts), STEPS)),
        ],
        compiler_params=pltpu.CompilerParams(
            vmem_limit_bytes=VMEM_LIMIT, collective_id=0, has_side_effects=True
        ),
        name="backward",
    )(cot, norm_gain, taps, head_gain, wb, part, wq, wo, wgu, wd, *(saved[name] for name in KEPT))


def staged_backward(cot, part, saved, norm_gain, taps, head_gain, wb, wq, wo, wgu, wd):
    total = saved["h"][LAYERS - 1]
    for add in branch_parts(part):
        total = total + add.astype(F32)
    outputs = total.astype(BF16)
    e, hid, adds = cot, saved["x"][LAYERS - 1], ()
    gain_rows = {}
    small = [None] * LAYERS
    big = [None] * LAYERS
    for level in reversed(range(LAYERS)):
        at = {name: saved[name][level] for name in KEPT}
        mlp_kept = tuple(at[name] for name in ("n2", "gu", "z"))
        mixer_kept = tuple(at[name] for name in ("n1", "p", "logits", "t", "u", "o", "on"))
        e, rows, part, grad_down, grad_gate_up = mlp_backward(
            level, e, hid, adds, norm_gain, *mlp_kept, wgu, wd
        )
        gain_rows[level + 1] = rows
        e, part, small[level], grad_qkv, grad_out = mixer_backward(
            level,
            e,
            at["h"],
            branch_parts(part),
            norm_gain,
            taps,
            head_gain,
            wb,
            mixer_kept,
            wq,
            wo,
        )
        hid, adds = at["x"], branch_parts(part)
        big[level] = (grad_down, grad_gate_up, grad_out, grad_qkv)
    branch = adds[0].astype(F32)
    for add in adds[1:]:
        branch = branch + add.astype(F32)
    grad_hidden, rows = rms_back(hid, norm_gain[0, 0:1].astype(F32), branch)
    gain_rows[0] = rows
    input_grad = (e + grad_hidden).astype(BF16)
    side = rows.shape[-1] - SIDE
    small_all = jnp.concatenate(
        [
            small[level].at[3:5, SIDE:].set(gain_rows[level].reshape(2, side))
            for level in range(LAYERS)
        ]
    )
    gains = small_all.reshape(LAYERS, 16, -1)[:, 0, SIDE : SIDE + DK]
    gains = sum(branch_parts(gains))
    for level in range(LAYERS):
        small_all = small_all.at[16 * level, SIDE : SIDE + DK].set(gains[level])
    tables = [table for group in big for table in group]
    sums = sum_over_dp(tables)
    stacked = [jnp.stack([sums[index], sums[4 + index]]) for index in range(4)]
    return (outputs, input_grad, *stacked, lax.psum(small_all, "dp"))


def widen_kernel(heads, chans, chunks, *refs):
    count = len(chunks)
    sources, (small,) = refs[:count], refs[count : count + 1]
    targets = refs[count + 1 : 2 * count + 1]
    (conv_out, beta_out, norm_out, gain_out) = refs[2 * count + 1 : 2 * count + 5]
    came = refs[2 * count + 5 : 3 * count + 5]
    made = refs[3 * count + 5 : 4 * count + 5]
    came_sems, made_sems = refs[4 * count + 5 :]
    order = []
    for index, rows in enumerate(chunks):
        steps = sources[index].shape[0] // rows
        order += [(index, step, pl.ds(step * rows, rows)) for step in range(steps)]
    loads = [
        pltpu.make_async_copy(
            sources[index].at[rows], came[index].at[rows], came_sems.at[index, step]
        )
        for index, step, rows in order
    ]
    for load in loads:
        load.start()
    for level in range(LAYERS):
        base = 16 * level
        conv_out[level] = small[base : base + 3 * KCONV, :chans]
        beta_out[level] = small[base + 3 * KCONV : base + 3 * KCONV + heads, :]
        half = norm_out.shape[-1] // 2
        for which, line in ((0, 3), (1, 1)):
            for index in range(2):
                spot = base + line + index
                norm_out[level, which : which + 1, index * half : (index + 1) * half] = small[
                    spot : spot + 1, SIDE : SIDE + half
                ]
        gain_out[level : level + 1] = small[base : base + 1, SIDE : SIDE + DK]
    stores = {}
    for (index, step, rows), load in zip(order, loads):
        slot = step % SLOTS_OUT
        if step >= SLOTS_OUT:
            stores[(index, slot)].wait()
        load.wait()
        made[index][slot] = came[index][rows].astype(F32)
        store = pltpu.make_async_copy(
            made[index].at[slot], targets[index].at[rows], made_sems.at[index, slot]
        )
        store.start()
        stores[(index, slot)] = store
    for store in stores.values():
        store.wait()


SLOTS_OUT = 4


def widen(tables, small, heads, chans):
    views = [table.reshape(-1, table.shape[-1]) for table in tables]
    chunks = []
    for view in views:
        rows, cols = view.shape
        steps = 1
        while rows % (32 * steps) == 0 and rows // steps * cols > 400000:
            steps *= 2
        chunks.append(rows // steps)
    most = max(view.shape[0] // rows for view, rows in zip(views, chunks))
    width = small.shape[-1]
    sds = jax.ShapeDtypeStruct
    vmem = pl.BlockSpec(memory_space=pltpu.VMEM)
    hbm = pl.BlockSpec(memory_space=pl.ANY)
    count = len(views)
    moved = sum(6 * view.size for view in views)
    results = pl.pallas_call(
        functools.partial(widen_kernel, heads, chans, tuple(chunks)),
        out_shape=(
            *(sds(view.shape, F32) for view in views),
            sds((LAYERS, 3 * KCONV, chans), F32),
            sds((LAYERS, heads, width), F32),
            sds((LAYERS, 2, 2 * (width - SIDE)), F32),
            sds((LAYERS, DK), F32),
        ),
        in_specs=[hbm] * count + [vmem],
        out_specs=(hbm,) * count + (vmem,) * 4,
        scratch_shapes=[
            *(pltpu.VMEM(view.shape, view.dtype) for view in views),
            *(
                pltpu.VMEM((SLOTS_OUT, rows, view.shape[1]), F32)
                for view, rows in zip(views, chunks)
            ),
            pltpu.SemaphoreType.DMA((count, most)),
            pltpu.SemaphoreType.DMA((count, SLOTS_OUT)),
        ],
        compiler_params=pltpu.CompilerParams(vmem_limit_bytes=VMEM_LIMIT),
        cost_estimate=pl.CostEstimate(flops=0, bytes_accessed=moved, transcendentals=0),
        name="widen",
    )(*views, small)
    return (list(results[:count]), *results[count:])


def body(
    inputs,
    qkv_weight,
    conv_taps,
    beta_weight,
    out_gain,
    out_weight,
    norm_gain,
    gate_up_weight,
    down_weight,
    cotangent,
):
    heads = beta_weight.shape[-1]
    wb = jnp.swapaxes(beta_weight, 1, 2)
    saved, part = forward(
        inputs,
        norm_gain,
        conv_taps,
        out_gain,
        wb,
        qkv_weight,
        out_weight,
        gate_up_weight,
        down_weight,
    )
    length, width = inputs.shape
    chans, hidden = conv_taps.shape[-1], down_weight.shape[1]
    if fold_cuts(lax.axis_size("dp"), width, chans, hidden) is not None:
        outputs, input_grad, *big, small_all = backward(
            cotangent,
            part,
            saved,
            norm_gain,
            conv_taps,
            out_gain,
            wb,
            qkv_weight,
            out_weight,
            gate_up_weight,
            down_weight,
        )
    else:
        outputs, input_grad, *big, small_all = staged_backward(
            cotangent,
            part,
            saved,
            norm_gain,
            conv_taps,
            out_gain,
            wb,
            qkv_weight,
            out_weight,
            gate_up_weight,
            down_weight,
        )
    shapes = (down_weight.shape, gate_up_weight.shape, out_weight.shape, qkv_weight.shape)
    big, grad_conv, grad_beta, grad_norm, grad_out_gain = widen(big, small_all, heads, chans)
    grad_down, grad_gate_up, grad_out, grad_qkv = (
        table.reshape(shape) for table, shape in zip(big, shapes)
    )
    grad_conv = grad_conv.reshape(conv_taps.shape)
    grad_beta = jnp.swapaxes(grad_beta, 1, 2)
    return (
        outputs,
        input_grad,
        grad_qkv,
        grad_conv,
        grad_beta,
        grad_out_gain,
        grad_out,
        grad_norm,
        grad_gate_up,
        grad_down,
    )


def solution(mesh):
    in_specs = (
        P("dp", None),
        P(None, None, None, "tensor"),
        P(None, None, None, "tensor"),
        P(None, None, "tensor"),
        P(),
        P(None, "tensor", None),
        P(),
        P(None, None, None, "tensor"),
        P(None, "tensor", None),
        P("dp", None),
    )
    out_specs = (
        P("dp", None),
        P("dp", None),
        P(None, None, None, "tensor"),
        P(None, None, None, "tensor"),
        P(None, None, "tensor"),
        P(),
        P(None, "tensor", None),
        P(),
        P(None, None, None, "tensor"),
        P(None, "tensor", None),
    )
    return jax.shard_map(body, mesh=mesh, in_specs=in_specs, out_specs=out_specs, check_vma=False)
```

```python
import functools
import math

import jax
import jax.numpy as jnp
from jax import lax
from jax.experimental import pallas as pl
from jax.experimental.pallas import tpu as pltpu
from jax.sharding import PartitionSpec as P

DK = 128
KCONV = 4
LAYERS = 2
LANES = 128
SIDE = 512
F32 = jnp.float32
BF16 = jnp.bfloat16
VMEM_LIMIT = 60 * 1024 * 1024


def dot_nn(a, b):
    return lax.dot_general(a, b, (((1,), (0,)), ((), ())), preferred_element_type=F32)


def dot_nt(a, b):
    return lax.dot_general(a, b, (((1,), (1,)), ((), ())), preferred_element_type=F32)


def dot_tn(a, b):
    return lax.dot_general(a, b, (((0,), (0,)), ((), ())), preferred_element_type=F32)


def halves(a):
    hi = a.astype(BF16)
    return hi, (a - hi.astype(F32)).astype(BF16)


def split_dot(dot, a, b):
    return dot(a[0], b[0]) + (dot(a[0], b[1]) + dot(a[1], b[0]))


def low(a):
    return a.astype(BF16)


def sigmoid(a):
    return 1.0 / (1.0 + jnp.exp(-a))


def rms_scale(a):
    return lax.rsqrt(jnp.mean(a * a, axis=-1, keepdims=True) + 1e-05)


def rms_back(hidden, gain, grad_normed):
    scale = rms_scale(hidden)
    weighted = gain * grad_normed
    inner = jnp.mean(hidden * weighted, axis=-1, keepdims=True)
    grad_hidden = scale * weighted - hidden * (scale * scale * scale) * inner
    rows = jnp.sum(grad_normed * hidden * scale, axis=0, keepdims=True)
    return grad_hidden, rows


def shift_down(a, count):
    if count == 0:
        return a
    row = lax.broadcasted_iota(jnp.int32, a.shape, 0)
    return jnp.where(row >= count, pltpu.roll(a, count, 0), 0.0)


def shift_up(a, count):
    if count == 0:
        return a
    length = a.shape[0]
    row = lax.broadcasted_iota(jnp.int32, a.shape, 0)
    return jnp.where(row < length - count, pltpu.roll(a, length - count, 0), 0.0)


def conv_silu(project, taps):
    total = taps[KCONV - 1 : KCONV, :] * project
    for tap in range(KCONV - 1):
        total = total + taps[tap : tap + 1, :] * shift_down(project, KCONV - 1 - tap)
    gate = sigmoid(total)
    return total, gate, total * gate


def conv_silu_rows(project, taps, rows):
    start = rows.start
    if start == 0:
        return conv_silu(project[rows], taps)[2]
    return conv_silu(project[start - 8 : rows.stop], taps)[2][8:]


def solve_back(blocks, key, gate, grad):
    half = grad.shape[0] // 2
    second = split_dot(dot_tn, blocks[1], halves(grad[half:]))
    gram = halves(dot_nt(key[half:], key[:half]))
    cross = split_dot(dot_tn, gram, halves(gate[half:] * second))
    first = split_dot(dot_tn, blocks[0], halves(grad[:half] - cross))
    return jnp.concatenate([first, second], axis=0)


def positions(length):
    row = lax.broadcasted_iota(jnp.int32, (length, length), 0)
    col = lax.broadcasted_iota(jnp.int32, (length, length), 1)
    return row, col


def unit_lower_inverse(lower_list):
    length = lower_list[0].shape[0]
    row, col = positions(length)
    eye = jnp.where(row == col, 1.0, 0.0)
    diag_list = [jnp.where(row // 4 == col // 4, lower, 0.0) for lower in lower_list]
    parts = [halves(diag) for diag in diag_list]
    squares = [split_dot(dot_nn, part, part) for part in parts]
    firsts = [eye - diag for diag in diag_list]
    inverse = [
        first + split_dot(dot_nn, halves(first), halves(square))
        for first, square in zip(firsts, squares)
    ]
    size = 4
    while size < length:
        fresh = (row // (2 * size) == col // (2 * size)) & (row // size != col // size)
        offs = [halves(jnp.where(fresh, lower, 0.0)) for lower in lower_list]
        held = [halves(inv) for inv in inverse]
        mids = [split_dot(dot_nn, inv, off) for inv, off in zip(held, offs)]
        inverse = [
            inv - split_dot(dot_nn, halves(mid), part)
            for inv, mid, part in zip(inverse, mids, held)
        ]
        size = 2 * size
    return inverse


def head_cols(head):
    return slice(head * DK, (head + 1) * DK)


KEPT = ("x", "n1", "p", "logits", "t", "u", "o", "on", "h", "n2", "gu", "z")


def kept_shapes(length, width, chans, hidden):
    heads = chans // DK
    shapes = dict(
        x=((length, width), F32),
        n1=((length, width), BF16),
        p=((3, length, chans), F32),
        logits=((length, LANES), F32),
        t=((2, heads, 2, length // 2, length // 2), BF16),
        u=((length, chans), BF16),
        o=((length, chans), F32),
        on=((length, chans), BF16),
        h=((length, width), F32),
        n2=((length, width), BF16),
        gu=((2, length, hidden), F32),
        z=((length, hidden), BF16),
    )
    return [((LAYERS, *shapes[name][0]), shapes[name][1]) for name in KEPT]


class Exchange:
    def __init__(self, slots, send_sems, recv_sems):
        self.slots, self.send_sems, self.recv_sems = slots, send_sems, recv_sems
        self.count = slots.shape[1]
        self.me = lax.axis_index("tensor")
        self.others = [
            {"tensor": lax.rem(self.me + away, self.count)} for away in range(1, self.count)
        ]
        self.pending = []

    def greet(self, others=0):
        barrier = pltpu.get_barrier_semaphore()
        for device in self.others:
            pl.semaphore_signal(
                barrier, inc=1, device_id=device, device_id_type=pl.DeviceIdType.MESH
            )
        pl.semaphore_wait(barrier, self.count - 1 + others)

    def copies(self, spot, part, rows):
        mine = self.slots.at[spot, self.me, rows]
        return [
            pltpu.make_async_remote_copy(
                src_ref=mine,
                dst_ref=mine,
                send_sem=self.send_sems.at[spot, part, away],
                recv_sem=self.recv_sems.at[spot, part, away],
                device_id=device,
                device_id_type=pl.DeviceIdType.MESH,
            )
            for away, device in enumerate(self.others)
        ]

    def give(self, spot, part, rows, value):
        self.slots[spot, self.me, rows] = value
        self.send(spot, part, rows)

    def send(self, spot, part, rows):
        for copy in self.copies(spot, part, rows):
            copy.start()
        self.pending.append((spot, part, rows))

    def take(self, spot, part, rows):
        for copy in self.copies(spot, part, rows):
            copy.wait_recv()
        total = self.slots[spot, 0, rows].astype(F32)
        for index in range(1, self.count):
            total = total + self.slots[spot, index, rows].astype(F32)
        return total

    def finish(self):
        for sent in self.pending:
            for copy in self.copies(*sent):
                copy.wait_send()


def forward_kernel(n_parts, *refs):
    (x_ref, gain_ref, taps_ref, head_gain_ref, wb_ref) = refs[:5]
    (wq_hbm, wo_hbm, wgu_hbm, wd_hbm) = refs[5:9]
    count = len(KEPT)
    outs = dict(zip(KEPT, refs[9 : 9 + count]))
    last_out = refs[9 + count]
    held = dict(zip(KEPT, refs[10 + count : 10 + 2 * count]))
    (wq, wo, wgu, wd, wb, slots, last, load_sems, keep_sems, send_sems, recv_sems) = refs[
        10 + 2 * count :
    ]
    exchange = Exchange(slots, send_sems, recv_sems)
    sources = ((wq_hbm, wq), (wo_hbm, wo), (wgu_hbm, wgu), (wd_hbm, wd))
    loads = [
        [
            pltpu.make_async_copy(source.at[level], target.at[level], load_sems.at[level, index])
            for index, (source, target) in enumerate(sources)
        ]
        for level in range(LAYERS)
    ]
    for group in loads:
        for load in group:
            load.start()
    wb[...] = jnp.zeros_like(wb)
    for level in range(LAYERS):
        wb[level, : wb_ref.shape[1]] = wb_ref[level]
    exchange.greet()
    keeps = []

    def keep(name, level):
        copy = pltpu.make_async_copy(
            held[name].at[level], outs[name].at[level], keep_sems.at[KEPT.index(name), level]
        )
        copy.start()
        keeps.append(copy)

    length = x_ref.shape[0]
    heads = wo.shape[1] // DK
    high = length // n_parts
    parts = [(part, slice(part * high, (part + 1) * high)) for part in range(n_parts)]
    row, col = positions(high)
    for level in range(LAYERS):
        head_gain = head_gain_ref[level : level + 1, :].astype(F32)
        before = []
        for part, rows in parts:
            if level == 0:
                x = x_ref[rows].astype(F32)
            else:
                x = held["h"][level - 1, rows] + exchange.take(2 * level - 1, part, rows)
            held["x"][level, rows] = x
            n1 = low(x * rms_scale(x) * gain_ref[level, 0:1, :].astype(F32))
            held["n1"][level, rows] = n1
            logits = dot_nt(n1, wb[level])
            held["logits"][level, rows] = logits
            beta = sigmoid(logits)
            if part == 0:
                loads[level][0].wait()
            acts = []
            for index in range(3):
                held["p"][level, index, rows] = dot_nn(n1, wq[level, index])
                acts.append(
                    conv_silu_rows(
                        held["p"].at[level, index], taps_ref[level, index].astype(F32), rows
                    )
                )
            lowers, scores, values, now = [], [], [], []
            for head in range(heads):
                cols = head_cols(head)
                c0, c1, c2 = (act[:, cols] for act in acts)
                q = low(c0 * lax.rsqrt(jnp.sum(c0 * c0, axis=-1, keepdims=True) + 0.001))
                k = low(c1 * lax.rsqrt(jnp.sum(c1 * c1, axis=-1, keepdims=True) + 0.001))
                v = low(c2).astype(F32)
                gate = beta[:, head : head + 1]
                value = gate * v
                for key, u in before[head : head + 1]:
                    cross = halves(gate * dot_nt(k, key))
                    value = value - dot_nn(cross[0], u[0])
                    value = value - (dot_nn(cross[0], u[1]) + dot_nn(cross[1], u[0]))
                lowers.append(jnp.where(row > col, gate * dot_nt(k, k), 0.0))
                scores.append(low(jnp.where(row >= col, dot_nt(q, k), 0.0)))
                values.append(halves(value))
                now.append((q, k))
            inverse = unit_lower_inverse(lowers)
            after = []
            for head in range(heads):
                cols = head_cols(head)
                t_hi, t_lo = halves(inverse[head])
                held["t"][level, 0, head, part] = t_hi
                held["t"][level, 1, head, part] = t_lo
                u = halves(split_dot(dot_nn, (t_hi, t_lo), values[head]))
                held["u"][level, rows, cols] = u[0]
                o = dot_nn(scores[head], u[0])
                q, k = now[head]
                for key, early in before[head : head + 1]:
                    o = o + dot_nn(low(dot_nt(q, key)), early[0])
                after.append((k, u))
                held["o"][level, rows, cols] = o
                scale = lax.rsqrt(jnp.mean(o * o, axis=-1, keepdims=True) + 0.01)
                held["on"][level, rows, cols] = low(o * scale * head_gain)
            before = after
            if part == 0:
                loads[level][1].wait()
            out = dot_nn(held["on"][level, rows], wo[level])
            exchange.give(2 * level, part, rows, low(out))
        for name in ("x", "n1", "logits", "p", "t", "u", "o", "on"):
            keep(name, level)
        for part, rows in parts:
            h = held["x"][level, rows] + exchange.take(2 * level, part, rows)
            held["h"][level, rows] = h
            n2 = low(h * rms_scale(h) * gain_ref[level, 1:2, :].astype(F32))
            held["n2"][level, rows] = n2
            if part == 0:
                loads[level][2].wait()
            g = dot_nn(n2, wgu[level, 0])
            held["gu"][level, 0, rows] = g
            u = dot_nn(n2, wgu[level, 1])
            held["gu"][level, 1, rows] = u
            z = low(g * sigmoid(g) * u)
            held["z"][level, rows] = z
            if part == 0:
                loads[level][3].wait()
            out = low(dot_nn(z, wd[level]))
            if level < LAYERS - 1:
                exchange.give(2 * level + 1, part, rows, out)
            else:
                last[rows] = out
        for name in ("h", "n2", "gu", "z"):
            keep(name, level)
    final = pltpu.make_async_copy(last, last_out, load_sems.at[0, 0])
    final.start()
    for copy in keeps:
        copy.wait()
    final.wait()
    exchange.finish()


def forward(x, norm_gain, taps, head_gain, wb, wq, wo, wgu, wd):
    length, width = x.shape
    chans, hidden = wq.shape[-1], wgu.shape[-1]
    n_tensor = lax.axis_size("tensor")
    n_parts = 2
    kept = kept_shapes(length, width, chans, hidden)
    vmem = pl.BlockSpec(memory_space=pltpu.VMEM)
    hbm = pl.BlockSpec(memory_space=pl.ANY)
    spots = 2 * LAYERS - 1
    *kept, part = pl.pallas_call(
        functools.partial(forward_kernel, n_parts),
        out_shape=(
            *(jax.ShapeDtypeStruct(*spec) for spec in kept),
            jax.ShapeDtypeStruct((length, width), BF16),
        ),
        in_specs=[vmem] * 5 + [hbm] * 4,
        out_specs=(hbm,) * (len(kept) + 1),
        scratch_shapes=[
            *(pltpu.VMEM(*spec) for spec in kept),
            pltpu.VMEM((LAYERS, 3, width, chans), BF16),
            pltpu.VMEM((LAYERS, chans, width), BF16),
            pltpu.VMEM((LAYERS, 2, width, hidden), BF16),
            pltpu.VMEM((LAYERS, hidden, width), BF16),
            pltpu.VMEM((LAYERS, LANES, width), BF16),
            pltpu.VMEM((spots, n_tensor, length, width), BF16),
            pltpu.VMEM((length, width), BF16),
            pltpu.SemaphoreType.DMA((LAYERS, 4)),
            pltpu.SemaphoreType.DMA((len(kept), LAYERS)),
            pltpu.SemaphoreType.DMA((spots, n_parts, n_tensor - 1)),
            pltpu.SemaphoreType.DMA((spots, n_parts, n_tensor - 1)),
        ],
        compiler_params=pltpu.CompilerParams(
            vmem_limit_bytes=VMEM_LIMIT, collective_id=1, has_side_effects=True
        ),
        name="forward",
    )(x, norm_gain, taps, head_gain, wb, wq, wo, wgu, wd)
    return dict(zip(KEPT, kept)), part


def back_through_norm(level, which, gain_ref, e_ref, hid_ref, adds, rows_out):
    e = e_ref[...].astype(F32)
    if not adds:
        rows_out[...] = jnp.zeros_like(rows_out)
        return e
    total = adds[0][...].astype(F32)
    for add in adds[1:]:
        total = total + add[...].astype(F32)
    gain = gain_ref[level, which : which + 1, :].astype(F32)
    grad_hidden, rows = rms_back(hid_ref[...], gain, total)
    rows_out[...] = rows
    return e + grad_hidden


def mlp_backward_kernel(level, n_add, *refs):
    (e_ref, hid_ref, *adds) = refs[: 2 + n_add]
    (gain_ref, n2_ref, gu_ref, z_ref, wgu_hbm, wd_hbm) = refs[2 + n_add : 8 + n_add]
    (e_out, rows_out, part_out, gd_out, ggu_out) = refs[8 + n_add : 13 + n_add]
    wgu, wd, dgu_ref, sems = refs[13 + n_add :]
    loads = [
        pltpu.make_async_copy(wd_hbm.at[level], wd, sems.at[0]),
        pltpu.make_async_copy(wgu_hbm.at[level], wgu, sems.at[1]),
    ]
    for load in loads:
        load.start()
    e = back_through_norm(level + 1, 0, gain_ref, e_ref, hid_ref, adds, rows_out)
    e_out[...] = e
    ef = low(e)
    loads[0].wait()
    dz = dot_nt(ef, wd[...])
    g, u = gu_ref[0], gu_ref[1]
    s = sigmoid(g)
    dgu_ref[0] = low(dz * u * (s * (1.0 + g * (1.0 - s))))
    dgu_ref[1] = low(dz * (g * s))
    loads[1].wait()
    part_out[...] = low(dot_nt(dgu_ref[0], wgu[0]) + dot_nt(dgu_ref[1], wgu[1]))
    gd_out[...] = low(dot_tn(z_ref[...], ef))
    for half in range(2):
        ggu_out[half] = low(dot_tn(n2_ref[...], dgu_ref[half]))


def mlp_backward(level, e, hid, adds, norm_gain, n2, gu, z, wgu, wd):
    length, width = e.shape
    hidden = wgu.shape[-1]
    sds = jax.ShapeDtypeStruct
    vmem = pl.BlockSpec(memory_space=pltpu.VMEM)
    hbm = pl.BlockSpec(memory_space=pl.ANY)
    return pl.pallas_call(
        functools.partial(mlp_backward_kernel, level, len(adds)),
        out_shape=(
            sds((length, width), F32),
            sds((1, width), F32),
            sds((length, width), BF16),
            sds((hidden, width), BF16),
            sds((2, width, hidden), BF16),
        ),
        in_specs=[vmem] * (6 + len(adds)) + [hbm, hbm],
        out_specs=(vmem,) * 5,
        scratch_shapes=[
            pltpu.VMEM((2, width, hidden), BF16),
            pltpu.VMEM((hidden, width), BF16),
            pltpu.VMEM((2, length, hidden), BF16),
            pltpu.SemaphoreType.DMA((2,)),
        ],
        compiler_params=pltpu.CompilerParams(vmem_limit_bytes=VMEM_LIMIT),
        name="mlp_backward",
    )(e, hid, *adds, norm_gain, n2, gu, z, wgu, wd)


def mixer_backward_kernel(level, heads, n_add, *refs):
    (e_ref, hid_ref, *adds) = refs[: 2 + n_add]
    (gain_ref, taps_ref, head_gain_ref, wb_ref, n1_ref, p_ref, logit_ref, t_ref, u_ref, o_ref) = (
        refs[2 + n_add : 12 + n_add]
    )
    (on_ref, wq_hbm, wo_hbm) = refs[12 + n_add : 15 + n_add]
    (e_out, part_out, small_out, gq_out, go_out) = refs[15 + n_add : 20 + n_add]
    wq, wo, grads, dp_ref, rows_out, wb, sems = refs[20 + n_add :]
    loads = [
        pltpu.make_async_copy(wo_hbm.at[level], wo, sems.at[0]),
        pltpu.make_async_copy(wq_hbm.at[level], wq, sems.at[1]),
    ]
    for load in loads:
        load.start()
    e = back_through_norm(level, 1, gain_ref, e_ref, hid_ref, adds, rows_out)
    e_out[...] = e
    em = low(e)
    length = e.shape[0]
    loads[0].wait()
    don = dot_nt(em, wo[...])
    go_out[...] = low(dot_tn(on_ref[...], em))
    beta = sigmoid(logit_ref[...])
    row, col = positions(length)
    lane = lax.broadcasted_iota(jnp.int32, (length, LANES), 1)
    head_gain = head_gain_ref[level : level + 1, :].astype(F32)
    convs = [conv_silu(p_ref[part], taps_ref[level, part].astype(F32)) for part in range(3)]
    gain_rows = jnp.zeros((1, DK), F32)
    dlogit = jnp.zeros((length, LANES), F32)
    for head in range(heads):
        cols = head_cols(head)
        c0, c1, c2 = (conv[2][:, cols] for conv in convs)
        rho0 = lax.rsqrt(jnp.sum(c0 * c0, axis=-1, keepdims=True) + 0.001)
        rho1 = lax.rsqrt(jnp.sum(c1 * c1, axis=-1, keepdims=True) + 0.001)
        q, k, v = low(c0 * rho0), low(c1 * rho1), low(c2).astype(F32)
        gate = beta[:, head : head + 1]
        o = o_ref[:, cols]
        scale = lax.rsqrt(jnp.mean(o * o, axis=-1, keepdims=True) + 0.01)
        dn = don[:, cols]
        weighted = dn * head_gain
        inner = jnp.mean(o * weighted, axis=-1, keepdims=True)
        do = low(scale * weighted - o * (scale * scale * scale) * inner)
        gain_rows = gain_rows + jnp.sum(dn * o * scale, axis=0, keepdims=True)
        u = u_ref[:, cols]
        score_t = low(jnp.where(row <= col, dot_nt(k, q), 0.0))
        du = dot_nn(score_t, do)
        ds = low(jnp.where(row >= col, dot_nt(do, u), 0.0))
        ds_t = low(jnp.where(row <= col, dot_nt(u, do), 0.0))
        dq = dot_nn(ds, k)
        dk = dot_nn(ds_t, q)
        blocks = [(t_ref[0, head, index], t_ref[1, head, index]) for index in range(2)]
        r = solve_back(blocks, k, gate, du)
        dv = gate * r
        dv_low = low(dv)
        gram = low(jnp.where(row > col, dot_nt(k, k), 0.0))
        w = v - dot_nn(gram, u)
        dbeta = jnp.sum(r * w, axis=-1, keepdims=True)
        dgram = jnp.where(row > col, dot_nt(dv_low, u), 0.0) + jnp.where(
            row < col, dot_nt(u, dv_low), 0.0
        )
        dk = dk - dot_nn(low(dgram), k)
        grads[0, :, cols] = rho0 * dq - c0 * (rho0 * rho0 * rho0) * jnp.sum(
            c0 * dq, axis=-1, keepdims=True
        )
        grads[1, :, cols] = rho1 * dk - c1 * (rho1 * rho1 * rho1) * jnp.sum(
            c1 * dk, axis=-1, keepdims=True
        )
        grads[2, :, cols] = dv
        dlogit = dlogit + jnp.where(lane == head, dbeta * gate * (1.0 - gate), 0.0)
    chans = grads.shape[-1]
    small_out[...] = jnp.zeros_like(small_out)
    small_out[0:1, SIDE : SIDE + DK] = gain_rows
    half = rows_out.shape[-1] // 2
    small_out[1:2, SIDE:] = rows_out[:, :half]
    small_out[2:3, SIDE:] = rows_out[:, half:]
    dlogit_low = low(dlogit)
    n1 = n1_ref[...]
    small_out[3 * KCONV : 3 * KCONV + heads, :] = dot_tn(dlogit_low, n1)[:heads, :]
    for part in range(3):
        taps = taps_ref[level, part].astype(F32)
        total, gate, _ = convs[part]
        dsum = grads[part] * (gate * (1.0 + total * (1.0 - gate)))
        p = p_ref[part]
        dp = taps[KCONV - 1 : KCONV, :] * dsum
        for tap in range(KCONV):
            back = KCONV - 1 - tap
            spot = part * KCONV + tap
            small_out[spot : spot + 1, :chans] = jnp.sum(
                dsum * shift_down(p, back), axis=0, keepdims=True
            )
            if back:
                dp = dp + taps[tap : tap + 1, :] * shift_up(dsum, back)
        dp_ref[part] = low(dp)
    loads[1].wait()
    wb[...] = jnp.zeros_like(wb)
    wb[:heads] = wb_ref[level]
    dn1 = dot_nn(dlogit_low, wb[...])
    for part in range(3):
        dn1 = dn1 + dot_nt(dp_ref[part], wq[part])
    part_out[...] = low(dn1)
    for part in range(3):
        gq_out[part] = low(dot_tn(n1, dp_ref[part]))


def mixer_backward(level, e, hid, adds, norm_gain, taps, head_gain, wb, kept, wq, wo):
    length, width = e.shape
    chans = wq.shape[-1]
    heads = chans // DK
    sds = jax.ShapeDtypeStruct
    vmem = pl.BlockSpec(memory_space=pltpu.VMEM)
    hbm = pl.BlockSpec(memory_space=pl.ANY)
    return pl.pallas_call(
        functools.partial(mixer_backward_kernel, level, heads, len(adds)),
        out_shape=(
            sds((length, width), F32),
            sds((length, width), BF16),
            sds((16, width), F32),
            sds((3, width, chans), BF16),
            sds((chans, width), BF16),
        ),
        in_specs=[vmem] * (13 + len(adds)) + [hbm, hbm],
        out_specs=(vmem,) * 5,
        scratch_shapes=[
            pltpu.VMEM((3, width, chans), BF16),
            pltpu.VMEM((chans, width), BF16),
            pltpu.VMEM((3, length, chans), F32),
            pltpu.VMEM((3, length, chans), BF16),
            pltpu.VMEM((1, width), F32),
            pltpu.VMEM((LANES, width), BF16),
            pltpu.SemaphoreType.DMA((2,)),
        ],
        compiler_params=pltpu.CompilerParams(vmem_limit_bytes=VMEM_LIMIT),
        name="mixer_backward",
    )(e, hid, *adds, norm_gain, taps, head_gain, wb, *kept, wq, wo)


def branch_parts(part):
    count = lax.axis_size("tensor")
    if count == 1:
        return (part,)
    if count == 2:
        return (part, lax.ppermute(part, "tensor", [(0, 1), (1, 0)]))
    return (lax.psum(part, "tensor"),)


def sum_over_dp(tables):
    shapes = [table.shape for table in tables]
    flat = jnp.concatenate([table.reshape(-1) for table in tables])
    size = flat.shape[0]
    count = lax.axis_size("dp")
    pad = -size % (count * 1024)
    flat = jnp.pad(flat, (0, pad))
    shard = lax.psum_scatter(flat, "dp", scatter_dimension=0, tiled=True)
    joined = lax.all_gather(shard, "dp", axis=0, tiled=True)
    pieces = []
    offset = 0
    for shape in shapes:
        size = math.prod(shape)
        pieces.append(joined[offset : offset + size].reshape(shape))
        offset = offset + size
    return pieces


def fold_spot(depth, side, core):
    return (depth * 2 + side) * 2 + core


def remote(source, target, send, recv, device):
    return pltpu.make_async_remote_copy(
        src_ref=source,
        dst_ref=target,
        send_sem=send,
        recv_sem=recv,
        device_id=device,
        device_id_type=pl.DeviceIdType.MESH,
    )


DEPTH = 4
CHUNKS = 8
STEPS = CHUNKS // 2
SLOTS = ("p1", "p2", "p3", "e1", "e2", "e3", "e4")
KINDS = (*SLOTS, "p4e", "p4y", "pf0", "pf1", "pk", "e5", "e6", "e7", "ef0", "ef1", "ek")
ALIKE = dict(
    m1="e1", m2="e2", m3="e3", m4="e4", m5="e5", m6="e6", m7="e7", mf0="ef0", mf1="ef1", mk="ek"
)
AWAY = ("p1", "pf1", "e1", "e2", "e7", "ef1", "m3", "m7", "mf1")
PASSED = ("pf1", "ef1", "e6", "e7", "m7", "mf1")


class Fold:
    def __init__(self, cuts, own, slots, totals, sems):
        self.cuts, self.own, self.slots, self.totals = cuts, own, slots, totals
        self.send_sems, self.recv_sems = sems
        spot = lax.axis_index("dp")
        self.core = lax.rem(spot, 2)
        side = lax.rem(lax.div(spot, 2), 2)
        depth = lax.div(spot, 4)
        self.is_mid = (depth == 1) | (depth == 2)
        self.is_end = (depth == 0) | (depth == 3)
        folded = depth + 1 - 2 * lax.rem(depth, 2)
        across = DEPTH - 1 - depth
        half = lax.div(depth, 2)
        self.partner = {"dp": fold_spot(depth, side, 1 - self.core)}
        self.beside = {"dp": fold_spot(depth, 1 - side, self.core)}
        self.folded = {"dp": fold_spot(folded, side, self.core)}
        self.across = {"dp": fold_spot(across, side, self.core)}
        self.mine = [[base * STEPS + step for step in range(STEPS)] for base in (side, half)]
        self.others = [
            [(1 - base) * STEPS + step for step in range(STEPS)] for base in (side, half)
        ]
        self.done = [0] * len(cuts)
        self.active, self.waiting = [], []

    def rows(self, index, chunk, way):
        _, first, second, _ = self.cuts[index]
        high = second if way else first
        start = chunk * (first + second) + (first if way else 0)
        return pl.ds(pl.multiple_of(start, 16), high)

    def piece(self, index, chunk, way):
        kind, first, second, cols = self.cuts[index]
        if kind == "small":
            lanes = pl.ds(pl.multiple_of(chunk * cols, cols), cols)
            return self.own[index].at[way * first : (way + 1) * first, lanes]
        return self.own[index].at[self.rows(index, chunk, way), :]

    def spot(self, index, chunk, way):
        kind, first, second, cols = self.cuts[index]
        ref = self.totals[index]
        if kind == "small":
            start = pl.multiple_of(self.core * (2 * first) + way * first, first)
            return ref.at[pl.ds(start, first), pl.ds(pl.multiple_of(chunk * cols, cols), cols)]
        rows = self.rows(index, chunk, way)
        if kind == "rows":
            return ref.at[self.core, rows, :]
        return ref.at[rows, pl.ds(pl.multiple_of(self.core * cols, cols), cols)]

    def family(self, index):
        return index % 4 if index < SMALL else 4

    def slot(self, name, index, step):
        place = SLOTS.index(ALIKE.get(name, name))
        ref = self.slots[2 * self.family(index) + (place >= 3)]
        return ref.at[place - 3 if place >= 3 else place, step]

    def copy(self, name, index, step, kept=True):
        way = 0 if name[0] == "p" else 1
        chunk = (self.others if name in AWAY else self.mine)[way][step]
        if name in ("m1", "m2"):
            chunk = step + (STEPS if name == "m2" else 0)
        device = self.folded
        if name in ("p1", "p4y", "e4", "m4"):
            device = self.beside
        elif name in ("p3", "e2", "e6", "m3", "m5"):
            device = self.across
        elif name[1] == "f":
            device = self.partner
        source = self.piece(index, chunk, way)
        kind = ALIKE.get(name, name)
        if kind in SLOTS:
            target = self.slot(name, index, step)
        else:
            target = self.spot(index, chunk, way)
            if name in PASSED or not kept:
                source = target
        at = (KINDS.index(kind), index, step)
        if name[1] == "k":
            return pltpu.make_async_copy(source, target, self.recv_sems.at[at])
        return remote(source, target, self.send_sems.at[at], self.recv_sems.at[at], device)

    def start(self, names, index, step, kept=True):
        for name in names:
            self.copy(name, index, step, kept).start()

    def add(self, name, index, step, chunk):
        self.copy(name, index, step).wait_recv()
        mine = self.piece(index, chunk, 0 if name[0] == "p" else 1)
        both = mine[...].astype(F32) + self.slot(name, index, step)[...].astype(F32)
        mine[...] = both.astype(mine.dtype)

    def stage_one(self, index, step):
        self.start(("p1",), index, step)

        @pl.when(self.is_end)
        def _():
            self.start(("m1", "m2") if self.mid_rooted(index) else ("e1",), index, step)

    def stage_two(self, index, step):
        self.add("p1", index, step, self.mine[0][step])

        @pl.when(self.is_end)
        def _():
            self.start(("p2",), index, step)

        @pl.when(self.is_mid)
        def _():
            if self.mid_rooted(index):
                self.add("m1", index, step, step)
                self.add("m2", index, step, STEPS + step)
                self.start(("m3",), index, step)
            else:
                self.add("e1", index, step, self.others[1][step])
                self.start(("e2",), index, step)

    def stage_three(self, index, step):
        @pl.when(self.is_mid)
        def _():
            self.add("p2", index, step, self.mine[0][step])
            self.start(("p3",), index, step)
            if self.mid_rooted(index):
                self.add("m3", index, step, self.mine[1][step])
                self.start(("m4",), index, step)
            else:
                self.add("e2", index, step, self.mine[1][step])
                self.start(("e3",), index, step)

    def stage_four(self, index, step):
        @pl.when(self.is_mid)
        def _():
            if self.mid_rooted(index):
                self.copy("m4", index, step).wait_send()
                self.add("m4", index, step, self.mine[1][step])
                self.start(("m5", "m6", "mf0", "mk"), index, step)
            self.copy("p3", index, step).wait_send()
            self.add("p3", index, step, self.mine[0][step])
            self.start(("p4e", "p4y", "pf0", "pk"), index, step)

        if not self.mid_rooted(index):

            @pl.when(self.is_end)
            def _():
                self.add("e3", index, step, self.mine[1][step])
                self.start(("e4",), index, step)

    def stage_five(self, index, step):
        @pl.when(self.is_end)
        def _():
            if not self.mid_rooted(index):
                self.copy("e4", index, step).wait_send()
                self.add("e4", index, step, self.mine[1][step])
                self.start(("e5", "ef0", "ek"), index, step)
            self.copy("p4e", index, step).wait_recv()
            self.start(("p4y", "pf0"), index, step, False)

        if self.mid_rooted(index):

            @pl.when(self.is_mid)
            def _():
                self.copy("m5", index, step).wait_recv()
                self.start(("m7", "mf1"), index, step)

    def stage_six(self, index, step):
        self.copy("p4y", index, step).wait_recv()
        self.start(("pf1",), index, step)
        if self.mid_rooted(index):

            @pl.when(self.is_end)
            def _():
                self.copy("m6", index, step).wait_recv()
                self.copy("m7", index, step).wait_recv()
                self.start(("mf0", "mf1"), index, step, False)

        else:

            @pl.when(self.is_mid)
            def _():
                self.copy("e5", index, step).wait_recv()
                self.start(("e6", "ef0"), index, step, False)

    def stage_seven(self, index, step):
        @pl.when(self.is_mid)
        def _():
            self.copy("e6", index, step).wait_recv()
            self.start(("e7", "ef1"), index, step)

    def stage_eight(self, index, step):
        @pl.when(self.is_end)
        def _():
            self.copy("e7", index, step).wait_recv()
            self.start(("ef1",), index, step)

    def settle(self, index, step):
        mid_rooted = self.mid_rooted(index)
        for name in ("p1", "p4y"):
            self.copy(name, index, step).wait_send()
        for name in ("pf0", "pf1", "mf0", "mf1") if mid_rooted else ("pf0", "pf1", "ef0", "ef1"):
            self.copy(name, index, step).wait()

        @pl.when(self.is_end)
        def _():
            for name in ("m1", "m2", "p2") if mid_rooted else ("e1", "p2", "e5"):
                self.copy(name, index, step).wait_send()
            if not mid_rooted:
                self.copy("ek", index, step).wait()

        @pl.when(self.is_mid)
        def _():
            for name in ("m3", "p4e", "m5", "m6", "m7") if mid_rooted else (
                "e2",
                "e3",
                "p4e",
                "e6",
                "e7",
            ):
                self.copy(name, index, step).wait_send()
            for name in ("pk", "mk") if mid_rooted else ("pk",):
                self.copy(name, index, step).wait()

    def mid_rooted(self, index):
        return index in MID_ROOTED

    def advance(self, index):
        stages = [
            self.stage_one,
            self.stage_two,
            self.stage_three,
            self.stage_four,
            self.stage_five,
            self.stage_six,
        ]
        if not self.mid_rooted(index):
            stages += [self.stage_seven, self.stage_eight]
        tick = self.done[index]
        self.done[index] = tick + 1
        last = STEPS + len(stages) - 1
        if tick == last:
            for step in range(STEPS):
                self.settle(index, step)
            return False
        for offset, stage in reversed(list(enumerate(stages))):
            if 0 <= tick - offset < STEPS:
                stage(index, tick - offset)
        return True

    def begin(self, index):
        if any(self.family(index) == self.family(held) for held in self.active):
            self.waiting.append(index)
        else:
            self.active.append(index)

    def serve(self, count=1):
        for _ in range(count):
            if not self.active:
                return
            index = self.active.pop(0)
            if self.advance(index):
                self.active.append(index)
                continue
            for other in self.waiting:
                if self.family(other) == self.family(index):
                    self.waiting.remove(other)
                    self.active.append(other)
                    break


def fold_cuts(n_dp, width, chans, hidden):
    if n_dp != 4 * DEPTH or width != CHUNKS * LANES or chans % (2 * LANES) or hidden % LANES:
        return None
    if any(rows % (16 * CHUNKS) for rows in (hidden, chans, width)):
        return None
    layer = []
    for kind, rows, cols in (
        ("cols", hidden, width // 2),
        ("rows", width, hidden),
        ("cols", chans, width // 2),
        ("cols", 3 * width, chans // 2),
    ):
        chunk = rows // CHUNKS
        first = 16 * round(0.6 * chunk / 16)
        if not 0 < first < chunk:
            return None
        layer.append((kind, first, chunk - first, cols))
    return layer * LAYERS + [("small", 8, 8, LANES)]


DOWN, GATE_UP, OUT, QKV = range(4)
SMALL = 4 * LAYERS
MID_ROOTED = (DOWN, QKV, 4 + OUT)
MLP_KEPT = ("gu", "z", "n2")
MIXER_KEPT = ("n1", "p", "logits", "t", "u", "o", "on", "h")
PEERS = ("z", "n2", "ef", "dgu", "n1", "on", "em", "dp")


def backward_kernel(n_parts, cuts, *refs):
    refs = list(refs)

    def taken(count):
        group = refs[:count]
        del refs[:count]
        return group

    (cot_ref, gain_ref, taps_ref, head_gain_ref, wb_ref) = taken(5)
    (part_hbm, wq_hbm, wo_hbm, wgu_hbm, wd_hbm) = taken(5)
    kept = dict(zip(KEPT, taken(len(KEPT))))
    (out_ref, in_grad_ref, *totals) = taken(2 + 5)
    own = taken(len(cuts))
    fold_slots = taken(10)
    peers = dict(zip(PEERS, taken(len(PEERS))))
    (e_ref, small, small_peer, slots, don_ref, wb, gains) = taken(7)
    (load_sems, send_sems, recv_sems, peer_sems, gain_sems) = taken(5)
    fold_sems = taken(2)

    per_table = [totals[index].at[level] for level in range(LAYERS) for index in range(4)]
    fold = Fold(cuts, own, fold_slots, [*per_table, totals[4]], fold_sems)
    core, serve = fold.core, fold.serve
    exchange = Exchange(slots, send_sems, recv_sems)
    barrier = pltpu.get_barrier_semaphore()
    for device in (fold.partner, fold.beside, fold.folded, fold.across):
        pl.semaphore_signal(barrier, inc=1, device_id=device, device_id_type=pl.DeviceIdType.MESH)
    exchange.greet(4)

    length, width = e_ref.shape
    chans = wo_hbm.shape[1]
    hidden = wd_hbm.shape[1]
    heads = chans // DK
    high = length // n_parts
    parts = [(part, slice(part * high, (part + 1) * high)) for part in range(n_parts)]
    row, col = positions(length)
    lane = lax.broadcasted_iota(jnp.int32, (length, LANES), 1)
    side = width - SIDE
    half_width, half_chans = width // 2, chans // 2

    def other_half(wide):
        return pl.ds(pl.multiple_of((1 - core) * wide, LANES), wide)

    def own_half(wide):
        return pl.ds(pl.multiple_of(core * wide, LANES), wide)

    def to_peer(name, level, source):
        spot = PEERS.index(name)
        return remote(
            source,
            peers[name].at[level],
            peer_sems.at[0, spot, level],
            peer_sems.at[1, spot, level],
            fold.partner,
        )

    top = LAYERS - 1
    early = [
        to_peer(name, level, kept[name].at[level])
        for level in reversed(range(LAYERS))
        for name in ("z", "n2", "on", "n1")
    ]
    early.insert(1, to_peer("ef", top, cot_ref.at[:, other_half(width // 2)]))
    for copy in early:
        copy.start()
    first = pltpu.make_async_copy(part_hbm, slots.at[0, exchange.me], load_sems.at[0, 0, 0])
    first.start()
    small[...] = jnp.zeros_like(small)

    def norm_step(level, which, spot, part, rows, hid):
        total = exchange.take(spot, part, rows)
        gain = gain_ref[level, which : which + 1, :].astype(F32)
        grad_hidden, sums = rms_back(hid, gain, total)
        base = 16 * level + (1 if which else 3)
        for index in range(2):
            spot_row = slice(base + index, base + index + 1)
            small[spot_row, SIDE:] += sums[:, index * side : (index + 1) * side]
        return e_ref[rows] + grad_hidden

    def mlp_stage(level):
        def scope(wgu, wd, gu, z, n2, hid, dgu, ef):
            held = dict(gu=gu, z=z, n2=n2)
            loads = {
                "wd": pltpu.make_async_copy(wd_hbm.at[level], wd, load_sems.at[level, 0, 1]),
                "wgu": pltpu.make_async_copy(wgu_hbm.at[level], wgu, load_sems.at[level, 0, 2]),
            }
            for index, name in enumerate(MLP_KEPT):
                loads[name] = pltpu.make_async_copy(
                    kept[name].at[level], held[name], load_sems.at[level, 0, 3 + index]
                )
            if level < LAYERS - 1:
                loads["hid"] = pltpu.make_async_copy(
                    kept["x"].at[level + 1], hid, load_sems.at[level, 0, 6]
                )
                loads["hid"].start()
            for name in ("z", "wd", "gu", "wgu", "n2"):
                loads[name].start()
            index = 4 * level
            if level == top:
                first.wait()
                for part, rows in parts:
                    exchange.send(0, part, rows)
                loads["z"].wait()
                for name in ("z", "ef"):
                    to_peer(name, level, peers[name].at[level]).wait_recv()
                own[index + DOWN][...] = low(
                    dot_tn(z[...], cot_ref[:, own_half(half_width)])
                    + dot_tn(peers["z"][level], peers["ef"][level])
                )
                fold.begin(index + DOWN)
                serve()
            for part, rows in parts:
                if level == LAYERS - 1:
                    e = cot_ref[rows].astype(F32)
                else:
                    if part == 0:
                        loads["hid"].wait()
                    e = norm_step(level + 1, 0, 2 * (LAYERS - 1 - level), part, rows, hid[rows])
                e_ref[rows] = e
                e_low = low(e)
                ef[rows] = e_low
                if part == 0:
                    loads["wd"].wait()
                dz = dot_nt(e_low, wd[...])
                if part == 0:
                    loads["gu"].wait()
                g, u = gu[0, rows], gu[1, rows]
                s = sigmoid(g)
                dgu[0, rows] = low(dz * u * (s * (1.0 + g * (1.0 - s))))
                dgu[1, rows] = low(dz * (g * s))
                if part or level != top:
                    serve()
            sends = [to_peer("dgu", level, dgu.at[1 - core])]
            if level != top:
                sends.append(to_peer("ef", level, ef.at[:, other_half(half_width)]))
            for send in sends:
                send.start()
            loads["wgu"].wait()
            for part, rows in parts:
                partial = dot_nt(dgu[0, rows], wgu[0]) + dot_nt(dgu[1, rows], wgu[1])
                exchange.give(2 * (LAYERS - 1 - level) + 1, part, rows, low(partial))
            serve()
            loads["n2"].wait()
            for name in ("n2", "dgu"):
                to_peer(name, level, peers[name].at[level]).wait_recv()
            own[index + GATE_UP][...] = low(
                dot_tn(n2[...], dgu[core]) + dot_tn(peers["n2"][level], peers["dgu"][level])
            )
            fold.begin(index + GATE_UP)
            serve()
            if level != top:
                loads["z"].wait()
                for name in ("z", "ef"):
                    to_peer(name, level, peers[name].at[level]).wait_recv()
                own[index + DOWN][...] = low(
                    dot_tn(z[...], ef[:, own_half(half_width)])
                    + dot_tn(peers["z"][level], peers["ef"][level])
                )
                fold.begin(index + DOWN)
                serve(3)
            for send in sends:
                send.wait_send()

        pl.run_scoped(
            scope,
            pltpu.VMEM((2, width, hidden), BF16),
            pltpu.VMEM((hidden, width), BF16),
            pltpu.VMEM((2, length, hidden), F32),
            pltpu.VMEM((length, hidden), BF16),
            pltpu.VMEM((length, width), BF16),
            pltpu.VMEM((length, width), F32),
            pltpu.VMEM((2, length, hidden), BF16),
            pltpu.VMEM((length, width), BF16),
        )

    def mixer_stage(level):
        def scope(wq, wo, n1, p, logits, t, u_all, o_all, on, h, grads, dp, em):
            held = dict(n1=n1, p=p, logits=logits, t=t, u=u_all, o=o_all, on=on, h=h)
            loads = {
                "wo": pltpu.make_async_copy(wo_hbm.at[level], wo, load_sems.at[level, 1, 0]),
                "wq": pltpu.make_async_copy(wq_hbm.at[level], wq, load_sems.at[level, 1, 1]),
            }
            for index, name in enumerate(MIXER_KEPT):
                loads[name] = pltpu.make_async_copy(
                    kept[name].at[level], held[name], load_sems.at[level, 1, 2 + index]
                )
            for name in ("h", "wo", "p", "o", "u", "logits", "t", "wq", "n1", "on"):
                loads[name].start()
            loads["p"].wait()
            convs = [
                conv_silu(p[index], taps_ref[level, index].astype(F32)) for index in range(3)
            ]
            spot = 2 * (LAYERS - 1 - level) + 1
            loads["h"].wait()
            if level == LAYERS - 1:
                for part, rows in parts:
                    out_ref[rows] = low(h[rows] + exchange.take(0, part, rows))
            for part, rows in parts:
                serve()
                e = norm_step(level, 1, spot, part, rows, h[rows])
                e_ref[rows] = e
                e_low = low(e)
                em[rows] = e_low
                if part == 0:
                    loads["wo"].wait()
                don_ref[rows] = dot_nt(e_low, wo[...])
            send_em = to_peer("em", level, em.at[:, other_half(half_width)])
            send_em.start()
            for name in ("o", "u", "logits", "t"):
                loads[name].wait()
            beta = sigmoid(logits[...])
            head_gain = head_gain_ref[level : level + 1, :].astype(F32)
            gain_rows = jnp.zeros((1, DK), F32)
            dlogit = jnp.zeros((length, LANES), F32)
            serve(2)
            for head in range(heads):
                cols = head_cols(head)
                c0, c1, c2 = (conv[2][:, cols] for conv in convs)
                rho0 = lax.rsqrt(jnp.sum(c0 * c0, axis=-1, keepdims=True) + 0.001)
                rho1 = lax.rsqrt(jnp.sum(c1 * c1, axis=-1, keepdims=True) + 0.001)
                q, k, v = low(c0 * rho0), low(c1 * rho1), low(c2).astype(F32)
                gate = beta[:, head : head + 1]
                o = o_all[:, cols]
                scale = lax.rsqrt(jnp.mean(o * o, axis=-1, keepdims=True) + 0.01)
                dn = don_ref[:, cols]
                weighted = dn * head_gain
                inner = jnp.mean(o * weighted, axis=-1, keepdims=True)
                do = low(scale * weighted - o * (scale * scale * scale) * inner)
                gain_rows = gain_rows + jnp.sum(dn * o * scale, axis=0, keepdims=True)
                u = u_all[:, cols]
                score_t = low(jnp.where(row <= col, dot_nt(k, q), 0.0))
                du = dot_nn(score_t, do)
                ds = low(jnp.where(row >= col, dot_nt(do, u), 0.0))
                ds_t = low(jnp.where(row <= col, dot_nt(u, do), 0.0))
                dq = dot_nn(ds, k)
                dk = dot_nn(ds_t, q)
                blocks = [(t[0, head, index], t[1, head, index]) for index in range(2)]
                r = solve_back(blocks, k, gate, du)
                dv = gate * r
                dv_low = low(dv)
                gram = low(jnp.where(row > col, dot_nt(k, k), 0.0))
                w = v - dot_nn(gram, u)
                dbeta = jnp.sum(r * w, axis=-1, keepdims=True)
                dgram = jnp.where(row > col, dot_nt(dv_low, u), 0.0) + jnp.where(
                    row < col, dot_nt(u, dv_low), 0.0
                )
                dk = dk - dot_nn(low(dgram), k)
                grads[0, :, cols] = rho0 * dq - c0 * (rho0 * rho0 * rho0) * jnp.sum(
                    c0 * dq, axis=-1, keepdims=True
                )
                grads[1, :, cols] = rho1 * dk - c1 * (rho1 * rho1 * rho1) * jnp.sum(
                    c1 * dk, axis=-1, keepdims=True
                )
                grads[2, :, cols] = dv
                dlogit = dlogit + jnp.where(lane == head, dbeta * gate * (1.0 - gate), 0.0)
                if head % 2:
                    serve()
            base = 16 * level
            small[base : base + 1, SIDE : SIDE + DK] = gain_rows
            for index in range(3):
                taps = taps_ref[level, index].astype(F32)
                total, gate, _ = convs[index]
                dsum = grads[index] * (gate * (1.0 + total * (1.0 - gate)))
                project = p[index]
                dproject = taps[KCONV - 1 : KCONV, :] * dsum
                for tap in range(KCONV):
                    back = KCONV - 1 - tap
                    line = base + index * KCONV + tap
                    small[line : line + 1, :chans] = jnp.sum(
                        dsum * shift_down(project, back), axis=0, keepdims=True
                    )
                    if back:
                        dproject = dproject + taps[tap : tap + 1, :] * shift_up(dsum, back)
                dp[index] = low(dproject)
            dlogit_low = low(dlogit)
            wb[...] = jnp.zeros_like(wb)
            wb[:heads] = wb_ref[level]
            loads["wq"].wait()
            for part, rows in parts:
                dn1 = dot_nn(dlogit_low[rows], wb[...])
                for index in range(3):
                    dn1 = dn1 + dot_nt(dp[index, rows], wq[index])
                exchange.give(spot + 1, part, rows, low(dn1))
            send_dp = to_peer("dp", level, dp.at[:, :, other_half(half_chans)])
            send_dp.start()
            serve()
            loads["n1"].wait()
            loads["on"].wait()
            line = base + 3 * KCONV
            small[line : line + heads, :] = dot_tn(dlogit_low, n1[...])[:heads, :]
            for name in ("em", "on", "n1", "dp"):
                to_peer(name, level, peers[name].at[level]).wait_recv()
            own[4 * level + OUT][...] = low(
                dot_tn(on[...], em[:, own_half(half_width)])
                + dot_tn(peers["on"][level], peers["em"][level])
            )
            fold.begin(4 * level + OUT)
            serve()
            for index in range(3):
                own[4 * level + QKV][index * width : (index + 1) * width] = low(
                    dot_tn(n1[...], dp[index, :, own_half(half_chans)])
                    + dot_tn(peers["n1"][level], peers["dp"][level, index])
                )
            fold.begin(4 * level + QKV)
            serve(3)
            send_em.wait_send()
            send_dp.wait_send()

        pl.run_scoped(
            scope,
            pltpu.VMEM((3, width, chans), BF16),
            pltpu.VMEM((chans, width), BF16),
            pltpu.VMEM((length, width), BF16),
            pltpu.VMEM((3, length, chans), F32),
            pltpu.VMEM((length, LANES), F32),
            pltpu.VMEM((2, heads, 2, length // 2, length // 2), BF16),
            pltpu.VMEM((length, chans), BF16),
            pltpu.VMEM((length, chans), F32),
            pltpu.VMEM((length, chans), BF16),
            pltpu.VMEM((length, width), F32),
            pltpu.VMEM((3, length, chans), F32),
            pltpu.VMEM((3, length, chans), BF16),
            pltpu.VMEM((length, width), BF16),
        )

    for level in reversed(range(LAYERS)):
        mlp_stage(level)
        mixer_stage(level)

    for level in range(LAYERS):
        gains[exchange.me, level : level + 1] = small[
            16 * level : 16 * level + 1, SIDE : SIDE + DK
        ]
    gain_copies = [
        remote(
            gains.at[exchange.me],
            gains.at[exchange.me],
            gain_sems.at[0, away],
            gain_sems.at[1, away],
            device,
        )
        for away, device in enumerate(exchange.others)
    ]
    for copy in gain_copies:
        copy.start()

    def last_scope(hid):
        load = pltpu.make_async_copy(kept["x"].at[0], hid, load_sems.at[0, 0, 7])
        load.start()
        serve(4)
        load.wait()
        for part, rows in parts:
            in_grad_ref[rows] = low(norm_step(0, 0, 2 * LAYERS, part, rows, hid[rows]))

    pl.run_scoped(last_scope, pltpu.VMEM((length, width), F32))

    for copy in gain_copies:
        copy.wait()
    for level in range(LAYERS):
        total = gains[0, level : level + 1]
        for index in range(1, exchange.count):
            total = total + gains[index, level : level + 1]
        small[16 * level : 16 * level + 1, SIDE : SIDE + DK] = total

    def small_half(which):
        return small.at[pl.ds(pl.multiple_of(which * 16, 16), 16)]

    send_small = remote(
        small_half(1 - core),
        small_peer,
        load_sems.at[1, 0, 6],
        load_sems.at[1, 0, 7],
        fold.partner,
    )
    send_small.start()
    serve()
    send_small.wait_recv()
    own[SMALL][...] = small_half(core)[...] + small_peer[...]
    fold.begin(SMALL)
    while fold.active:
        serve()
    send_small.wait_send()
    for copy in early:
        copy.wait_send()
    exchange.finish()


def backward(cot, part, saved, norm_gain, taps, head_gain, wb, wq, wo, wgu, wd):
    length, width = cot.shape
    chans, hidden = wq.shape[-1], wgu.shape[-1]
    heads = chans // DK
    n_tensor = lax.axis_size("tensor")
    cuts = fold_cuts(lax.axis_size("dp"), width, chans, hidden)
    n_parts = 2
    sds = jax.ShapeDtypeStruct
    vmem = pl.BlockSpec(memory_space=pltpu.VMEM)
    hbm = pl.BlockSpec(memory_space=pl.ANY)
    own, slots = [], []
    for index, (kind, first, second, cols) in enumerate(cuts):
        dtype = F32 if kind == "small" else BF16
        own.append(
            pltpu.VMEM((16, cols * CHUNKS), dtype)
            if kind == "small"
            else pltpu.VMEM(((first + second) * CHUNKS, cols), dtype)
        )
        if index < 4 or index == SMALL:
            slots.append(pltpu.VMEM((3, STEPS, first, cols), dtype))
            slots.append(pltpu.VMEM((4, STEPS, second, cols), dtype))
    peers = dict(
        z=(length, hidden),
        n2=(length, width),
        ef=(length, width // 2),
        dgu=(length, hidden),
        n1=(length, width),
        on=(length, chans),
        em=(length, width // 2),
        dp=(3, length, chans // 2),
    )
    spots = 2 * LAYERS + 1
    return pl.pallas_call(
        functools.partial(backward_kernel, n_parts, cuts),
        out_shape=(
            sds((length, width), BF16),
            sds((length, width), BF16),
            sds((LAYERS, hidden, width), BF16),
            sds((LAYERS, 2, width, hidden), BF16),
            sds((LAYERS, chans, width), BF16),
            sds((LAYERS, 3 * width, chans), BF16),
            sds((16 * LAYERS, width), F32),
        ),
        in_specs=[vmem] * 5 + [hbm] * (5 + len(KEPT)),
        out_specs=(vmem, vmem) + (hbm,) * 5,
        scratch_shapes=[
            *own,
            *slots,
            *(pltpu.VMEM((LAYERS, *peers[name]), BF16) for name in PEERS),
            pltpu.VMEM((length, width), F32),
            pltpu.VMEM((16 * LAYERS, width), F32),
            pltpu.VMEM((16, width), F32),
            pltpu.VMEM((spots, n_tensor, length, width), BF16),
            pltpu.VMEM((length, chans), F32),
            pltpu.VMEM((LANES, width), BF16),
            pltpu.VMEM((n_tensor, 8, DK), F32),
            pltpu.SemaphoreType.DMA((LAYERS, 2, 10)),
            pltpu.SemaphoreType.DMA((spots, n_parts, n_tensor - 1)),
            pltpu.SemaphoreType.DMA((spots, n_parts, n_tensor - 1)),
            pltpu.SemaphoreType.DMA((2, len(PEERS), LAYERS)),
            pltpu.SemaphoreType.DMA((2, n_tensor - 1)),
            pltpu.SemaphoreType.DMA((len(KINDS), len(cuts), STEPS)),
            pltpu.SemaphoreType.DMA((len(KINDS), len(cuts), STEPS)),
        ],
        compiler_params=pltpu.CompilerParams(
            vmem_limit_bytes=VMEM_LIMIT, collective_id=0, has_side_effects=True
        ),
        name="backward",
    )(cot, norm_gain, taps, head_gain, wb, part, wq, wo, wgu, wd, *(saved[name] for name in KEPT))


def staged_backward(cot, part, saved, norm_gain, taps, head_gain, wb, wq, wo, wgu, wd):
    total = saved["h"][LAYERS - 1]
    for add in branch_parts(part):
        total = total + add.astype(F32)
    outputs = total.astype(BF16)
    e, hid, adds = cot, saved["x"][LAYERS - 1], ()
    gain_rows = {}
    small = [None] * LAYERS
    big = [None] * LAYERS
    for level in reversed(range(LAYERS)):
        at = {name: saved[name][level] for name in KEPT}
        mlp_kept = tuple(at[name] for name in ("n2", "gu", "z"))
        mixer_kept = tuple(at[name] for name in ("n1", "p", "logits", "t", "u", "o", "on"))
        e, rows, part, grad_down, grad_gate_up = mlp_backward(
            level, e, hid, adds, norm_gain, *mlp_kept, wgu, wd
        )
        gain_rows[level + 1] = rows
        e, part, small[level], grad_qkv, grad_out = mixer_backward(
            level,
            e,
            at["h"],
            branch_parts(part),
            norm_gain,
            taps,
            head_gain,
            wb,
            mixer_kept,
            wq,
            wo,
        )
        hid, adds = at["x"], branch_parts(part)
        big[level] = (grad_down, grad_gate_up, grad_out, grad_qkv)
    branch = adds[0].astype(F32)
    for add in adds[1:]:
        branch = branch + add.astype(F32)
    grad_hidden, rows = rms_back(hid, norm_gain[0, 0:1].astype(F32), branch)
    gain_rows[0] = rows
    input_grad = (e + grad_hidden).astype(BF16)
    side = rows.shape[-1] - SIDE
    small_all = jnp.concatenate(
        [
            small[level].at[3:5, SIDE:].set(gain_rows[level].reshape(2, side))
            for level in range(LAYERS)
        ]
    )
    gains = small_all.reshape(LAYERS, 16, -1)[:, 0, SIDE : SIDE + DK]
    gains = sum(branch_parts(gains))
    for level in range(LAYERS):
        small_all = small_all.at[16 * level, SIDE : SIDE + DK].set(gains[level])
    tables = [table for group in big for table in group]
    sums = sum_over_dp(tables)
    stacked = [jnp.stack([sums[index], sums[4 + index]]) for index in range(4)]
    return (outputs, input_grad, *stacked, lax.psum(small_all, "dp"))


def widen_kernel(heads, chans, chunks, *refs):
    count = len(chunks)
    refs = list(refs)

    def taken(number):
        group = refs[:number]
        del refs[:number]
        return group

    sources, (small, *passed) = taken(count), taken(3)
    targets, (conv_out, beta_out, norm_out, gain_out) = taken(count), taken(4)
    passed_out, came, made = taken(2), taken(count), taken(count)
    came_sems, made_sems = taken(2)
    for source, target in zip(passed, passed_out):
        target[...] = source[...]
    order = []
    for index, rows in enumerate(chunks):
        steps = sources[index].shape[0] // rows
        order += [(index, step, pl.ds(step * rows, rows)) for step in range(steps)]
    loads = [
        pltpu.make_async_copy(
            sources[index].at[rows], came[index].at[rows], came_sems.at[index, step]
        )
        for index, step, rows in order
    ]
    for load in loads:
        load.start()
    for level in range(LAYERS):
        base = 16 * level
        for index in range(3):
            line = base + index * KCONV
            conv_out[level, index] = small[line : line + KCONV, :chans]
        beta_out[level] = small[base + 3 * KCONV : base + 3 * KCONV + heads, :]
        half = norm_out.shape[-1] // 2
        for which, line in ((0, 3), (1, 1)):
            for index in range(2):
                spot = base + line + index
                norm_out[level, which : which + 1, index * half : (index + 1) * half] = small[
                    spot : spot + 1, SIDE : SIDE + half
                ]
        gain_out[level : level + 1] = small[base : base + 1, SIDE : SIDE + DK]
    stores = {}
    for (index, step, rows), load in zip(order, loads):
        slot = step % SLOTS_OUT
        if step >= SLOTS_OUT:
            stores[(index, slot)].wait()
        load.wait()
        made[index][slot] = came[index][rows].astype(F32)
        store = pltpu.make_async_copy(
            made[index].at[slot], targets[index].at[rows], made_sems.at[index, slot]
        )
        store.start()
        stores[(index, slot)] = store
    for store in stores.values():
        store.wait()


SLOTS_OUT = 4


def widen(tables, small, heads, chans, passed):
    views = [table.reshape(-1, table.shape[-1]) for table in tables]
    chunks = []
    for view in views:
        rows, cols = view.shape
        steps = 1
        while rows % (32 * steps) == 0 and rows // steps * cols > 400000:
            steps *= 2
        chunks.append(rows // steps)
    most = max(view.shape[0] // rows for view, rows in zip(views, chunks))
    width = small.shape[-1]
    sds = jax.ShapeDtypeStruct
    vmem = pl.BlockSpec(memory_space=pltpu.VMEM)
    hbm = pl.BlockSpec(memory_space=pl.ANY)
    count = len(views)
    moved = sum(6 * view.size for view in views)
    results = pl.pallas_call(
        functools.partial(widen_kernel, heads, chans, tuple(chunks)),
        out_shape=(
            *(sds(view.shape, F32) for view in views),
            sds((LAYERS, 3, KCONV, chans), F32),
            sds((LAYERS, heads, width), F32),
            sds((LAYERS, 2, 2 * (width - SIDE)), F32),
            sds((LAYERS, DK), F32),
            *(sds(array.shape, array.dtype) for array in passed),
        ),
        in_specs=[hbm] * count + [vmem] * 3,
        out_specs=(hbm,) * count + (vmem,) * 6,
        scratch_shapes=[
            *(pltpu.VMEM(view.shape, view.dtype) for view in views),
            *(
                pltpu.VMEM((SLOTS_OUT, rows, view.shape[1]), F32)
                for view, rows in zip(views, chunks)
            ),
            pltpu.SemaphoreType.DMA((count, most)),
            pltpu.SemaphoreType.DMA((count, SLOTS_OUT)),
        ],
        compiler_params=pltpu.CompilerParams(vmem_limit_bytes=VMEM_LIMIT),
        cost_estimate=pl.CostEstimate(flops=0, bytes_accessed=moved, transcendentals=0),
        name="widen",
    )(*views, small, *passed)
    return (list(results[:count]), *results[count:])


def body(
    inputs,
    qkv_weight,
    conv_taps,
    beta_weight,
    out_gain,
    out_weight,
    norm_gain,
    gate_up_weight,
    down_weight,
    cotangent,
):
    heads = beta_weight.shape[-1]
    wb = jnp.swapaxes(beta_weight, 1, 2)
    saved, part = forward(
        inputs,
        norm_gain,
        conv_taps,
        out_gain,
        wb,
        qkv_weight,
        out_weight,
        gate_up_weight,
        down_weight,
    )
    length, width = inputs.shape
    chans, hidden = conv_taps.shape[-1], down_weight.shape[1]
    if fold_cuts(lax.axis_size("dp"), width, chans, hidden) is not None:
        outputs, input_grad, *big, small_all = backward(
            cotangent,
            part,
            saved,
            norm_gain,
            conv_taps,
            out_gain,
            wb,
            qkv_weight,
            out_weight,
            gate_up_weight,
            down_weight,
        )
    else:
        outputs, input_grad, *big, small_all = staged_backward(
            cotangent,
            part,
            saved,
            norm_gain,
            conv_taps,
            out_gain,
            wb,
            qkv_weight,
            out_weight,
            gate_up_weight,
            down_weight,
        )
    shapes = (down_weight.shape, gate_up_weight.shape, out_weight.shape, qkv_weight.shape)
    big, grad_conv, grad_beta, grad_norm, grad_out_gain, outputs, input_grad = widen(
        big, small_all, heads, chans, (outputs, input_grad)
    )
    grad_down, grad_gate_up, grad_out, grad_qkv = (
        table.reshape(shape) for table, shape in zip(big, shapes)
    )
    grad_beta = jnp.swapaxes(grad_beta, 1, 2)
    return (
        outputs,
        input_grad,
        grad_qkv,
        grad_conv,
        grad_beta,
        grad_out_gain,
        grad_out,
        grad_norm,
        grad_gate_up,
        grad_down,
    )


def solution(mesh):
    in_specs = (
        P("dp", None),
        P(None, None, None, "tensor"),
        P(None, None, None, "tensor"),
        P(None, None, "tensor"),
        P(),
        P(None, "tensor", None),
        P(),
        P(None, None, None, "tensor"),
        P(None, "tensor", None),
        P("dp", None),
    )
    out_specs = (
        P("dp", None),
        P("dp", None),
        P(None, None, None, "tensor"),
        P(None, None, None, "tensor"),
        P(None, None, "tensor"),
        P(),
        P(None, "tensor", None),
        P(),
        P(None, None, None, "tensor"),
        P(None, "tensor", None),
    )
    return jax.shard_map(body, mesh=mesh, in_specs=in_specs, out_specs=out_specs, check_vma=False)
```

```python
import functools
import math

import jax
import jax.numpy as jnp
from jax import lax
from jax.experimental import pallas as pl
from jax.experimental.pallas import tpu as pltpu
from jax.sharding import PartitionSpec as P

DK = 128
KCONV = 4
LAYERS = 2
LANES = 128
SIDE = 512
F32 = jnp.float32
BF16 = jnp.bfloat16
VMEM_LIMIT = 60 * 1024 * 1024


def dot_nn(a, b):
    return lax.dot_general(a, b, (((1,), (0,)), ((), ())), preferred_element_type=F32)


def dot_nt(a, b):
    return lax.dot_general(a, b, (((1,), (1,)), ((), ())), preferred_element_type=F32)


def dot_tn(a, b):
    return lax.dot_general(a, b, (((0,), (0,)), ((), ())), preferred_element_type=F32)


def halves(a):
    hi = a.astype(BF16)
    return hi, (a - hi.astype(F32)).astype(BF16)


def split_dot(dot, a, b):
    return dot(a[0], b[0]) + (dot(a[0], b[1]) + dot(a[1], b[0]))


def low(a):
    return a.astype(BF16)


def sigmoid(a):
    return 1.0 / (1.0 + jnp.exp(-a))


def rms_scale(a):
    return lax.rsqrt(jnp.mean(a * a, axis=-1, keepdims=True) + 1e-05)


def rms_back(hidden, gain, grad_normed):
    scale = rms_scale(hidden)
    weighted = gain * grad_normed
    inner = jnp.mean(hidden * weighted, axis=-1, keepdims=True)
    grad_hidden = scale * weighted - hidden * (scale * scale * scale) * inner
    rows = jnp.sum(grad_normed * hidden * scale, axis=0, keepdims=True)
    return grad_hidden, rows


def shift_down(a, count):
    if count == 0:
        return a
    row = lax.broadcasted_iota(jnp.int32, a.shape, 0)
    return jnp.where(row >= count, pltpu.roll(a, count, 0), 0.0)


def shift_up(a, count):
    if count == 0:
        return a
    length = a.shape[0]
    row = lax.broadcasted_iota(jnp.int32, a.shape, 0)
    return jnp.where(row < length - count, pltpu.roll(a, length - count, 0), 0.0)


def conv_silu(project, taps):
    total = taps[KCONV - 1 : KCONV, :] * project
    for tap in range(KCONV - 1):
        total = total + taps[tap : tap + 1, :] * shift_down(project, KCONV - 1 - tap)
    gate = sigmoid(total)
    return total, gate, total * gate


def conv_silu_rows(project, taps, rows):
    start = rows.start
    if start == 0:
        return conv_silu(project[rows], taps)[2]
    return conv_silu(project[start - 8 : rows.stop], taps)[2][8:]


def solve_back(blocks, key, gate, grad):
    half = grad.shape[0] // 2
    second = split_dot(dot_tn, blocks[1], halves(grad[half:]))
    gram = halves(dot_nt(key[half:], key[:half]))
    cross = split_dot(dot_tn, gram, halves(gate[half:] * second))
    first = split_dot(dot_tn, blocks[0], halves(grad[:half] - cross))
    return jnp.concatenate([first, second], axis=0)


def positions(length):
    row = lax.broadcasted_iota(jnp.int32, (length, length), 0)
    col = lax.broadcasted_iota(jnp.int32, (length, length), 1)
    return row, col


def unit_lower_inverse(lower_list):
    length = lower_list[0].shape[0]
    row, col = positions(length)
    eye = jnp.where(row == col, 1.0, 0.0)
    diag_list = [jnp.where(row // 4 == col // 4, lower, 0.0) for lower in lower_list]
    parts = [halves(diag) for diag in diag_list]
    squares = [split_dot(dot_nn, part, part) for part in parts]
    firsts = [eye - diag for diag in diag_list]
    inverse = [
        first + split_dot(dot_nn, halves(first), halves(square))
        for first, square in zip(firsts, squares)
    ]
    size = 4
    while size < length:
        fresh = (row // (2 * size) == col // (2 * size)) & (row // size != col // size)
        offs = [halves(jnp.where(fresh, lower, 0.0)) for lower in lower_list]
        held = [halves(inv) for inv in inverse]
        mids = [split_dot(dot_nn, inv, off) for inv, off in zip(held, offs)]
        inverse = [
            inv - split_dot(dot_nn, halves(mid), part)
            for inv, mid, part in zip(inverse, mids, held)
        ]
        size = 2 * size
    return inverse


def head_cols(head):
    return slice(head * DK, (head + 1) * DK)


KEPT = ("x", "n1", "p", "logits", "t", "u", "o", "on", "h", "n2", "gu", "z")


def kept_shapes(length, width, chans, hidden):
    heads = chans // DK
    shapes = dict(
        x=((length, width), F32),
        n1=((length, width), BF16),
        p=((3, length, chans), F32),
        logits=((length, LANES), F32),
        t=((2, heads, 2, length // 2, length // 2), BF16),
        u=((length, chans), BF16),
        o=((length, chans), F32),
        on=((length, chans), BF16),
        h=((length, width), F32),
        n2=((length, width), BF16),
        gu=((2, length, hidden), F32),
        z=((length, hidden), BF16),
    )
    return [((LAYERS, *shapes[name][0]), shapes[name][1]) for name in KEPT]


class Exchange:
    def __init__(self, slots, send_sems, recv_sems):
        self.slots, self.send_sems, self.recv_sems = slots, send_sems, recv_sems
        self.count = slots.shape[1]
        self.me = lax.axis_index("tensor")
        self.others = [
            {"tensor": lax.rem(self.me + away, self.count)} for away in range(1, self.count)
        ]
        self.pending = []

    def greet(self, others=0):
        barrier = pltpu.get_barrier_semaphore()
        for device in self.others:
            pl.semaphore_signal(
                barrier, inc=1, device_id=device, device_id_type=pl.DeviceIdType.MESH
            )
        pl.semaphore_wait(barrier, self.count - 1 + others)

    def copies(self, spot, part, rows):
        mine = self.slots.at[spot, self.me, rows]
        return [
            pltpu.make_async_remote_copy(
                src_ref=mine,
                dst_ref=mine,
                send_sem=self.send_sems.at[spot, part, away],
                recv_sem=self.recv_sems.at[spot, part, away],
                device_id=device,
                device_id_type=pl.DeviceIdType.MESH,
            )
            for away, device in enumerate(self.others)
        ]

    def give(self, spot, part, rows, value):
        self.slots[spot, self.me, rows] = value
        self.send(spot, part, rows)

    def send(self, spot, part, rows):
        for copy in self.copies(spot, part, rows):
            copy.start()
        self.pending.append((spot, part, rows))

    def take(self, spot, part, rows):
        for copy in self.copies(spot, part, rows):
            copy.wait_recv()
        total = self.slots[spot, 0, rows].astype(F32)
        for index in range(1, self.count):
            total = total + self.slots[spot, index, rows].astype(F32)
        return total

    def finish(self):
        for sent in self.pending:
            for copy in self.copies(*sent):
                copy.wait_send()


def forward_kernel(n_parts, *refs):
    (x_ref, gain_ref, taps_ref, head_gain_ref, wb_ref) = refs[:5]
    (wq_hbm, wo_hbm, wgu_hbm, wd_hbm) = refs[5:9]
    count = len(KEPT)
    outs = dict(zip(KEPT, refs[9 : 9 + count]))
    last_out = refs[9 + count]
    held = dict(zip(KEPT, refs[10 + count : 10 + 2 * count]))
    (wq, wo, wgu, wd, wb, slots, last, load_sems, keep_sems, send_sems, recv_sems) = refs[
        10 + 2 * count :
    ]
    exchange = Exchange(slots, send_sems, recv_sems)
    sources = ((wq_hbm, wq), (wo_hbm, wo), (wgu_hbm, wgu), (wd_hbm, wd))
    loads = [
        [
            pltpu.make_async_copy(source.at[level], target.at[level], load_sems.at[level, index])
            for index, (source, target) in enumerate(sources)
        ]
        for level in range(LAYERS)
    ]
    for group in loads:
        for load in group:
            load.start()
    wb[...] = jnp.zeros_like(wb)
    for level in range(LAYERS):
        wb[level, : wb_ref.shape[1]] = wb_ref[level]
    exchange.greet()
    keeps = []

    def keep(name, level):
        copy = pltpu.make_async_copy(
            held[name].at[level], outs[name].at[level], keep_sems.at[KEPT.index(name), level]
        )
        copy.start()
        keeps.append(copy)

    length = x_ref.shape[0]
    heads = wo.shape[1] // DK
    high = length // n_parts
    parts = [(part, slice(part * high, (part + 1) * high)) for part in range(n_parts)]
    row, col = positions(high)
    for level in range(LAYERS):
        head_gain = head_gain_ref[level : level + 1, :].astype(F32)
        before = []
        for part, rows in parts:
            if level == 0:
                x = x_ref[rows].astype(F32)
            else:
                x = held["h"][level - 1, rows] + exchange.take(2 * level - 1, part, rows)
            held["x"][level, rows] = x
            n1 = low(x * rms_scale(x) * gain_ref[level, 0:1, :].astype(F32))
            held["n1"][level, rows] = n1
            logits = dot_nt(n1, wb[level])
            held["logits"][level, rows] = logits
            beta = sigmoid(logits)
            if part == 0:
                loads[level][0].wait()
            acts = []
            for index in range(3):
                held["p"][level, index, rows] = dot_nn(n1, wq[level, index])
                acts.append(
                    conv_silu_rows(
                        held["p"].at[level, index], taps_ref[level, index].astype(F32), rows
                    )
                )
            lowers, scores, values, now = [], [], [], []
            for head in range(heads):
                cols = head_cols(head)
                c0, c1, c2 = (act[:, cols] for act in acts)
                q = low(c0 * lax.rsqrt(jnp.sum(c0 * c0, axis=-1, keepdims=True) + 0.001))
                k = low(c1 * lax.rsqrt(jnp.sum(c1 * c1, axis=-1, keepdims=True) + 0.001))
                v = low(c2).astype(F32)
                gate = beta[:, head : head + 1]
                value = gate * v
                for key, u in before[head : head + 1]:
                    cross = halves(gate * dot_nt(k, key))
                    value = value - dot_nn(cross[0], u[0])
                    value = value - (dot_nn(cross[0], u[1]) + dot_nn(cross[1], u[0]))
                lowers.append(jnp.where(row > col, gate * dot_nt(k, k), 0.0))
                scores.append(low(jnp.where(row >= col, dot_nt(q, k), 0.0)))
                values.append(halves(value))
                now.append((q, k))
            inverse = unit_lower_inverse(lowers)
            after = []
            for head in range(heads):
                cols = head_cols(head)
                t_hi, t_lo = halves(inverse[head])
                held["t"][level, 0, head, part] = t_hi
                held["t"][level, 1, head, part] = t_lo
                u = halves(split_dot(dot_nn, (t_hi, t_lo), values[head]))
                held["u"][level, rows, cols] = u[0]
                o = dot_nn(scores[head], u[0])
                q, k = now[head]
                for key, early in before[head : head + 1]:
                    o = o + dot_nn(low(dot_nt(q, key)), early[0])
                after.append((k, u))
                held["o"][level, rows, cols] = o
                scale = lax.rsqrt(jnp.mean(o * o, axis=-1, keepdims=True) + 0.01)
                held["on"][level, rows, cols] = low(o * scale * head_gain)
            before = after
            if part == 0:
                loads[level][1].wait()
            out = dot_nn(held["on"][level, rows], wo[level])
            exchange.give(2 * level, part, rows, low(out))
        for name in ("x", "n1", "logits", "p", "t", "u", "o", "on"):
            keep(name, level)
        for part, rows in parts:
            h = held["x"][level, rows] + exchange.take(2 * level, part, rows)
            held["h"][level, rows] = h
            n2 = low(h * rms_scale(h) * gain_ref[level, 1:2, :].astype(F32))
            held["n2"][level, rows] = n2
            if part == 0:
                loads[level][2].wait()
            g = dot_nn(n2, wgu[level, 0])
            held["gu"][level, 0, rows] = g
            u = dot_nn(n2, wgu[level, 1])
            held["gu"][level, 1, rows] = u
            z = low(g * sigmoid(g) * u)
            held["z"][level, rows] = z
            if part == 0:
                loads[level][3].wait()
            out = low(dot_nn(z, wd[level]))
            if level < LAYERS - 1:
                exchange.give(2 * level + 1, part, rows, out)
            else:
                last[rows] = out
        for name in ("h", "n2", "gu", "z"):
            keep(name, level)
    final = pltpu.make_async_copy(last, last_out, load_sems.at[0, 0])
    final.start()
    for copy in keeps:
        copy.wait()
    final.wait()
    exchange.finish()


def forward(x, norm_gain, taps, head_gain, wb, wq, wo, wgu, wd):
    length, width = x.shape
    chans, hidden = wq.shape[-1], wgu.shape[-1]
    n_tensor = lax.axis_size("tensor")
    n_parts = 2
    kept = kept_shapes(length, width, chans, hidden)
    vmem = pl.BlockSpec(memory_space=pltpu.VMEM)
    hbm = pl.BlockSpec(memory_space=pl.ANY)
    spots = 2 * LAYERS - 1
    *kept, part = pl.pallas_call(
        functools.partial(forward_kernel, n_parts),
        out_shape=(
            *(jax.ShapeDtypeStruct(*spec) for spec in kept),
            jax.ShapeDtypeStruct((length, width), BF16),
        ),
        in_specs=[vmem] * 5 + [hbm] * 4,
        out_specs=(hbm,) * (len(kept) + 1),
        scratch_shapes=[
            *(pltpu.VMEM(*spec) for spec in kept),
            pltpu.VMEM((LAYERS, 3, width, chans), BF16),
            pltpu.VMEM((LAYERS, chans, width), BF16),
            pltpu.VMEM((LAYERS, 2, width, hidden), BF16),
            pltpu.VMEM((LAYERS, hidden, width), BF16),
            pltpu.VMEM((LAYERS, LANES, width), BF16),
            pltpu.VMEM((spots, n_tensor, length, width), BF16),
            pltpu.VMEM((length, width), BF16),
            pltpu.SemaphoreType.DMA((LAYERS, 4)),
            pltpu.SemaphoreType.DMA((len(kept), LAYERS)),
            pltpu.SemaphoreType.DMA((spots, n_parts, n_tensor - 1)),
            pltpu.SemaphoreType.DMA((spots, n_parts, n_tensor - 1)),
        ],
        compiler_params=pltpu.CompilerParams(
            vmem_limit_bytes=VMEM_LIMIT, collective_id=1, has_side_effects=True
        ),
        name="forward",
    )(x, norm_gain, taps, head_gain, wb, wq, wo, wgu, wd)
    return dict(zip(KEPT, kept)), part


def back_through_norm(level, which, gain_ref, e_ref, hid_ref, adds, rows_out):
    e = e_ref[...].astype(F32)
    if not adds:
        rows_out[...] = jnp.zeros_like(rows_out)
        return e
    total = adds[0][...].astype(F32)
    for add in adds[1:]:
        total = total + add[...].astype(F32)
    gain = gain_ref[level, which : which + 1, :].astype(F32)
    grad_hidden, rows = rms_back(hid_ref[...], gain, total)
    rows_out[...] = rows
    return e + grad_hidden


def mlp_backward_kernel(level, n_add, *refs):
    (e_ref, hid_ref, *adds) = refs[: 2 + n_add]
    (gain_ref, n2_ref, gu_ref, z_ref, wgu_hbm, wd_hbm) = refs[2 + n_add : 8 + n_add]
    (e_out, rows_out, part_out, gd_out, ggu_out) = refs[8 + n_add : 13 + n_add]
    wgu, wd, dgu_ref, sems = refs[13 + n_add :]
    loads = [
        pltpu.make_async_copy(wd_hbm.at[level], wd, sems.at[0]),
        pltpu.make_async_copy(wgu_hbm.at[level], wgu, sems.at[1]),
    ]
    for load in loads:
        load.start()
    e = back_through_norm(level + 1, 0, gain_ref, e_ref, hid_ref, adds, rows_out)
    e_out[...] = e
    ef = low(e)
    loads[0].wait()
    dz = dot_nt(ef, wd[...])
    g, u = gu_ref[0], gu_ref[1]
    s = sigmoid(g)
    dgu_ref[0] = low(dz * u * (s * (1.0 + g * (1.0 - s))))
    dgu_ref[1] = low(dz * (g * s))
    loads[1].wait()
    part_out[...] = low(dot_nt(dgu_ref[0], wgu[0]) + dot_nt(dgu_ref[1], wgu[1]))
    gd_out[...] = low(dot_tn(z_ref[...], ef))
    for half in range(2):
        ggu_out[half] = low(dot_tn(n2_ref[...], dgu_ref[half]))


def mlp_backward(level, e, hid, adds, norm_gain, n2, gu, z, wgu, wd):
    length, width = e.shape
    hidden = wgu.shape[-1]
    sds = jax.ShapeDtypeStruct
    vmem = pl.BlockSpec(memory_space=pltpu.VMEM)
    hbm = pl.BlockSpec(memory_space=pl.ANY)
    return pl.pallas_call(
        functools.partial(mlp_backward_kernel, level, len(adds)),
        out_shape=(
            sds((length, width), F32),
            sds((1, width), F32),
            sds((length, width), BF16),
            sds((hidden, width), BF16),
            sds((2, width, hidden), BF16),
        ),
        in_specs=[vmem] * (6 + len(adds)) + [hbm, hbm],
        out_specs=(vmem,) * 5,
        scratch_shapes=[
            pltpu.VMEM((2, width, hidden), BF16),
            pltpu.VMEM((hidden, width), BF16),
            pltpu.VMEM((2, length, hidden), BF16),
            pltpu.SemaphoreType.DMA((2,)),
        ],
        compiler_params=pltpu.CompilerParams(vmem_limit_bytes=VMEM_LIMIT),
        name="mlp_backward",
    )(e, hid, *adds, norm_gain, n2, gu, z, wgu, wd)


def mixer_backward_kernel(level, heads, n_add, *refs):
    (e_ref, hid_ref, *adds) = refs[: 2 + n_add]
    (gain_ref, taps_ref, head_gain_ref, wb_ref, n1_ref, p_ref, logit_ref, t_ref, u_ref, o_ref) = (
        refs[2 + n_add : 12 + n_add]
    )
    (on_ref, wq_hbm, wo_hbm) = refs[12 + n_add : 15 + n_add]
    (e_out, part_out, small_out, gq_out, go_out) = refs[15 + n_add : 20 + n_add]
    wq, wo, grads, dp_ref, rows_out, wb, sems = refs[20 + n_add :]
    loads = [
        pltpu.make_async_copy(wo_hbm.at[level], wo, sems.at[0]),
        pltpu.make_async_copy(wq_hbm.at[level], wq, sems.at[1]),
    ]
    for load in loads:
        load.start()
    e = back_through_norm(level, 1, gain_ref, e_ref, hid_ref, adds, rows_out)
    e_out[...] = e
    em = low(e)
    length = e.shape[0]
    loads[0].wait()
    don = dot_nt(em, wo[...])
    go_out[...] = low(dot_tn(on_ref[...], em))
    beta = sigmoid(logit_ref[...])
    row, col = positions(length)
    lane = lax.broadcasted_iota(jnp.int32, (length, LANES), 1)
    head_gain = head_gain_ref[level : level + 1, :].astype(F32)
    convs = [conv_silu(p_ref[part], taps_ref[level, part].astype(F32)) for part in range(3)]
    gain_rows = jnp.zeros((1, DK), F32)
    dlogit = jnp.zeros((length, LANES), F32)
    for head in range(heads):
        cols = head_cols(head)
        c0, c1, c2 = (conv[2][:, cols] for conv in convs)
        rho0 = lax.rsqrt(jnp.sum(c0 * c0, axis=-1, keepdims=True) + 0.001)
        rho1 = lax.rsqrt(jnp.sum(c1 * c1, axis=-1, keepdims=True) + 0.001)
        q, k, v = low(c0 * rho0), low(c1 * rho1), low(c2).astype(F32)
        gate = beta[:, head : head + 1]
        o = o_ref[:, cols]
        scale = lax.rsqrt(jnp.mean(o * o, axis=-1, keepdims=True) + 0.01)
        dn = don[:, cols]
        weighted = dn * head_gain
        inner = jnp.mean(o * weighted, axis=-1, keepdims=True)
        do = low(scale * weighted - o * (scale * scale * scale) * inner)
        gain_rows = gain_rows + jnp.sum(dn * o * scale, axis=0, keepdims=True)
        u = u_ref[:, cols]
        score_t = low(jnp.where(row <= col, dot_nt(k, q), 0.0))
        du = dot_nn(score_t, do)
        ds = low(jnp.where(row >= col, dot_nt(do, u), 0.0))
        ds_t = low(jnp.where(row <= col, dot_nt(u, do), 0.0))
        dq = dot_nn(ds, k)
        dk = dot_nn(ds_t, q)
        blocks = [(t_ref[0, head, index], t_ref[1, head, index]) for index in range(2)]
        r = solve_back(blocks, k, gate, du)
        dv = gate * r
        dv_low = low(dv)
        gram = low(jnp.where(row > col, dot_nt(k, k), 0.0))
        w = v - dot_nn(gram, u)
        dbeta = jnp.sum(r * w, axis=-1, keepdims=True)
        dgram = jnp.where(row > col, dot_nt(dv_low, u), 0.0) + jnp.where(
            row < col, dot_nt(u, dv_low), 0.0
        )
        dk = dk - dot_nn(low(dgram), k)
        grads[0, :, cols] = rho0 * dq - c0 * (rho0 * rho0 * rho0) * jnp.sum(
            c0 * dq, axis=-1, keepdims=True
        )
        grads[1, :, cols] = rho1 * dk - c1 * (rho1 * rho1 * rho1) * jnp.sum(
            c1 * dk, axis=-1, keepdims=True
        )
        grads[2, :, cols] = dv
        dlogit = dlogit + jnp.where(lane == head, dbeta * gate * (1.0 - gate), 0.0)
    chans = grads.shape[-1]
    small_out[...] = jnp.zeros_like(small_out)
    small_out[0:1, SIDE : SIDE + DK] = gain_rows
    half = rows_out.shape[-1] // 2
    small_out[1:2, SIDE:] = rows_out[:, :half]
    small_out[2:3, SIDE:] = rows_out[:, half:]
    dlogit_low = low(dlogit)
    n1 = n1_ref[...]
    small_out[3 * KCONV : 3 * KCONV + heads, :] = dot_tn(dlogit_low, n1)[:heads, :]
    for part in range(3):
        taps = taps_ref[level, part].astype(F32)
        total, gate, _ = convs[part]
        dsum = grads[part] * (gate * (1.0 + total * (1.0 - gate)))
        p = p_ref[part]
        dp = taps[KCONV - 1 : KCONV, :] * dsum
        for tap in range(KCONV):
            back = KCONV - 1 - tap
            spot = part * KCONV + tap
            small_out[spot : spot + 1, :chans] = jnp.sum(
                dsum * shift_down(p, back), axis=0, keepdims=True
            )
            if back:
                dp = dp + taps[tap : tap + 1, :] * shift_up(dsum, back)
        dp_ref[part] = low(dp)
    loads[1].wait()
    wb[...] = jnp.zeros_like(wb)
    wb[:heads] = wb_ref[level]
    dn1 = dot_nn(dlogit_low, wb[...])
    for part in range(3):
        dn1 = dn1 + dot_nt(dp_ref[part], wq[part])
    part_out[...] = low(dn1)
    for part in range(3):
        gq_out[part] = low(dot_tn(n1, dp_ref[part]))


def mixer_backward(level, e, hid, adds, norm_gain, taps, head_gain, wb, kept, wq, wo):
    length, width = e.shape
    chans = wq.shape[-1]
    heads = chans // DK
    sds = jax.ShapeDtypeStruct
    vmem = pl.BlockSpec(memory_space=pltpu.VMEM)
    hbm = pl.BlockSpec(memory_space=pl.ANY)
    return pl.pallas_call(
        functools.partial(mixer_backward_kernel, level, heads, len(adds)),
        out_shape=(
            sds((length, width), F32),
            sds((length, width), BF16),
            sds((16, width), F32),
            sds((3, width, chans), BF16),
            sds((chans, width), BF16),
        ),
        in_specs=[vmem] * (13 + len(adds)) + [hbm, hbm],
        out_specs=(vmem,) * 5,
        scratch_shapes=[
            pltpu.VMEM((3, width, chans), BF16),
            pltpu.VMEM((chans, width), BF16),
            pltpu.VMEM((3, length, chans), F32),
            pltpu.VMEM((3, length, chans), BF16),
            pltpu.VMEM((1, width), F32),
            pltpu.VMEM((LANES, width), BF16),
            pltpu.SemaphoreType.DMA((2,)),
        ],
        compiler_params=pltpu.CompilerParams(vmem_limit_bytes=VMEM_LIMIT),
        name="mixer_backward",
    )(e, hid, *adds, norm_gain, taps, head_gain, wb, *kept, wq, wo)


def branch_parts(part):
    count = lax.axis_size("tensor")
    if count == 1:
        return (part,)
    if count == 2:
        return (part, lax.ppermute(part, "tensor", [(0, 1), (1, 0)]))
    return (lax.psum(part, "tensor"),)


def sum_over_dp(tables):
    shapes = [table.shape for table in tables]
    flat = jnp.concatenate([table.reshape(-1) for table in tables])
    size = flat.shape[0]
    count = lax.axis_size("dp")
    pad = -size % (count * 1024)
    flat = jnp.pad(flat, (0, pad))
    shard = lax.psum_scatter(flat, "dp", scatter_dimension=0, tiled=True)
    joined = lax.all_gather(shard, "dp", axis=0, tiled=True)
    pieces = []
    offset = 0
    for shape in shapes:
        size = math.prod(shape)
        pieces.append(joined[offset : offset + size].reshape(shape))
        offset = offset + size
    return pieces


def fold_spot(depth, side, core):
    return (depth * 2 + side) * 2 + core


def remote(source, target, send, recv, device):
    return pltpu.make_async_remote_copy(
        src_ref=source,
        dst_ref=target,
        send_sem=send,
        recv_sem=recv,
        device_id=device,
        device_id_type=pl.DeviceIdType.MESH,
    )


DEPTH = 4
CHUNKS = 8
STEPS = CHUNKS // 2
SLOTS = ("p1", "p2", "p3", "e1", "e2", "e3", "e4")
KINDS = (*SLOTS, "p4e", "p4y", "pf0", "pf1", "pk", "e5", "e6", "e7", "ef0", "ef1", "ek")
ALIKE = dict(
    m1="e1", m2="e2", m3="e3", m4="e4", m5="e5", m6="e6", m7="e7", mf0="ef0", mf1="ef1", mk="ek"
)
AWAY = ("p1", "pf1", "e1", "e2", "e7", "ef1", "m3", "m7", "mf1")
PASSED = ("pf1", "ef1", "e6", "e7", "m7", "mf1")


class Fold:
    def __init__(self, cuts, own, slots, totals, sems):
        self.cuts, self.own, self.slots, self.totals = cuts, own, slots, totals
        self.send_sems, self.recv_sems = sems
        spot = lax.axis_index("dp")
        self.core = lax.rem(spot, 2)
        side = lax.rem(lax.div(spot, 2), 2)
        depth = lax.div(spot, 4)
        self.is_mid = (depth == 1) | (depth == 2)
        self.is_end = (depth == 0) | (depth == 3)
        folded = depth + 1 - 2 * lax.rem(depth, 2)
        across = DEPTH - 1 - depth
        half = lax.div(depth, 2)
        self.partner = {"dp": fold_spot(depth, side, 1 - self.core)}
        self.beside = {"dp": fold_spot(depth, 1 - side, self.core)}
        self.folded = {"dp": fold_spot(folded, side, self.core)}
        self.across = {"dp": fold_spot(across, side, self.core)}
        self.mine = [[base * STEPS + step for step in range(STEPS)] for base in (side, half)]
        self.others = [
            [(1 - base) * STEPS + step for step in range(STEPS)] for base in (side, half)
        ]
        self.done = [0] * len(cuts)
        self.active, self.waiting = [], []
        self.served = 0

    def rows(self, index, chunk, way):
        _, first, second, _ = self.cuts[index]
        high = second if way else first
        start = chunk * (first + second) + (first if way else 0)
        return pl.ds(pl.multiple_of(start, 16), high)

    def piece(self, index, chunk, way):
        kind, first, second, cols = self.cuts[index]
        if kind == "small":
            lanes = pl.ds(pl.multiple_of(chunk * cols, cols), cols)
            return self.own[index].at[way * first : (way + 1) * first, lanes]
        return self.own[index].at[self.rows(index, chunk, way), :]

    def spot(self, index, chunk, way):
        kind, first, second, cols = self.cuts[index]
        ref = self.totals[index]
        if kind == "small":
            start = pl.multiple_of(self.core * (2 * first) + way * first, first)
            return ref.at[pl.ds(start, first), pl.ds(pl.multiple_of(chunk * cols, cols), cols)]
        rows = self.rows(index, chunk, way)
        if kind == "rows":
            return ref.at[self.core, rows, :]
        return ref.at[rows, pl.ds(pl.multiple_of(self.core * cols, cols), cols)]

    def family(self, index):
        return index % 4 if index < SMALL else 4

    def slot(self, name, index, step):
        place = SLOTS.index(ALIKE.get(name, name))
        ref = self.slots[2 * self.family(index) + (place >= 3)]
        return ref.at[place - 3 if place >= 3 else place, step]

    def copy(self, name, index, step, kept=True):
        way = 0 if name[0] == "p" else 1
        chunk = (self.others if name in AWAY else self.mine)[way][step]
        if name in ("m1", "m2"):
            chunk = step + (STEPS if name == "m2" else 0)
        device = self.folded
        if name in ("p1", "p4y", "e4", "m4"):
            device = self.beside
        elif name in ("p3", "e2", "e6", "m3", "m5"):
            device = self.across
        elif name[1] == "f":
            device = self.partner
        source = self.piece(index, chunk, way)
        kind = ALIKE.get(name, name)
        if kind in SLOTS:
            target = self.slot(name, index, step)
        else:
            target = self.spot(index, chunk, way)
            if name in PASSED or not kept:
                source = target
        at = (KINDS.index(kind), index, step)
        if name[1] == "k":
            return pltpu.make_async_copy(source, target, self.recv_sems.at[at])
        return remote(source, target, self.send_sems.at[at], self.recv_sems.at[at], device)

    def start(self, names, index, step, kept=True):
        for name in names:
            self.copy(name, index, step, kept).start()

    def add(self, name, index, step, chunk):
        self.copy(name, index, step).wait_recv()
        mine = self.piece(index, chunk, 0 if name[0] == "p" else 1)
        both = mine[...].astype(F32) + self.slot(name, index, step)[...].astype(F32)
        mine[...] = both.astype(mine.dtype)

    def stage_one(self, index, step):
        self.start(("p1",), index, step)

        @pl.when(self.is_end)
        def _():
            self.start(("m1", "m2") if self.mid_rooted(index) else ("e1",), index, step)

    def stage_two(self, index, step):
        self.add("p1", index, step, self.mine[0][step])

        @pl.when(self.is_end)
        def _():
            self.start(("p2",), index, step)

        @pl.when(self.is_mid)
        def _():
            if self.mid_rooted(index):
                self.add("m1", index, step, step)
                self.add("m2", index, step, STEPS + step)
                self.start(("m3",), index, step)
            else:
                self.add("e1", index, step, self.others[1][step])
                self.start(("e2",), index, step)

    def stage_three(self, index, step):
        @pl.when(self.is_mid)
        def _():
            self.add("p2", index, step, self.mine[0][step])
            self.start(("p3",), index, step)
            if self.mid_rooted(index):
                self.add("m3", index, step, self.mine[1][step])
                self.start(("m4",), index, step)
            else:
                self.add("e2", index, step, self.mine[1][step])
                self.start(("e3",), index, step)

    def stage_four(self, index, step):
        @pl.when(self.is_mid)
        def _():
            if self.mid_rooted(index):
                self.copy("m4", index, step).wait_send()
                self.add("m4", index, step, self.mine[1][step])
                self.start(("m5", "m6", "mf0", "mk"), index, step)
            self.copy("p3", index, step).wait_send()
            self.add("p3", index, step, self.mine[0][step])
            self.start(("p4e", "p4y", "pf0", "pk"), index, step)

        if not self.mid_rooted(index):

            @pl.when(self.is_end)
            def _():
                self.add("e3", index, step, self.mine[1][step])
                self.start(("e4",), index, step)

    def stage_five(self, index, step):
        @pl.when(self.is_end)
        def _():
            if not self.mid_rooted(index):
                self.copy("e4", index, step).wait_send()
                self.add("e4", index, step, self.mine[1][step])
                self.start(("e5", "ef0", "ek"), index, step)
            self.copy("p4e", index, step).wait_recv()
            self.start(("p4y", "pf0"), index, step, False)

        if self.mid_rooted(index):

            @pl.when(self.is_mid)
            def _():
                self.copy("m5", index, step).wait_recv()
                self.start(("m7", "mf1"), index, step)

    def stage_six(self, index, step):
        self.copy("p4y", index, step).wait_recv()
        self.start(("pf1",), index, step)
        if self.mid_rooted(index):

            @pl.when(self.is_end)
            def _():
                self.copy("m6", index, step).wait_recv()
                self.copy("m7", index, step).wait_recv()
                self.start(("mf0", "mf1"), index, step, False)

        else:

            @pl.when(self.is_mid)
            def _():
                self.copy("e5", index, step).wait_recv()
                self.start(("e6", "ef0"), index, step, False)

    def stage_seven(self, index, step):
        @pl.when(self.is_mid)
        def _():
            self.copy("e6", index, step).wait_recv()
            self.start(("e7", "ef1"), index, step)

    def stage_eight(self, index, step):
        @pl.when(self.is_end)
        def _():
            self.copy("e7", index, step).wait_recv()
            self.start(("ef1",), index, step)

    def settle(self, index, step):
        mid_rooted = self.mid_rooted(index)
        for name in ("p1", "p4y"):
            self.copy(name, index, step).wait_send()
        for name in ("pf0", "pf1", "mf0", "mf1") if mid_rooted else ("pf0", "pf1", "ef0", "ef1"):
            self.copy(name, index, step).wait()

        @pl.when(self.is_end)
        def _():
            for name in ("m1", "m2", "p2") if mid_rooted else ("e1", "p2", "e5"):
                self.copy(name, index, step).wait_send()
            if not mid_rooted:
                self.copy("ek", index, step).wait()

        @pl.when(self.is_mid)
        def _():
            for name in ("m3", "p4e", "m5", "m6", "m7") if mid_rooted else (
                "e2",
                "e3",
                "p4e",
                "e6",
                "e7",
            ):
                self.copy(name, index, step).wait_send()
            for name in ("pk", "mk") if mid_rooted else ("pk",):
                self.copy(name, index, step).wait()

    def mid_rooted(self, index):
        return index in MID_ROOTED

    def advance(self, index):
        stages = [
            self.stage_one,
            self.stage_two,
            self.stage_three,
            self.stage_four,
            self.stage_five,
            self.stage_six,
        ]
        if not self.mid_rooted(index):
            stages += [self.stage_seven, self.stage_eight]
        tick = self.done[index]
        self.done[index] = tick + 1
        last = STEPS + len(stages) - 1
        if tick == last:
            for step in range(STEPS):
                self.settle(index, step)
            return False
        for offset, stage in reversed(list(enumerate(stages))):
            steps = [tick - offset]
            if offset == 0:
                ahead = AHEAD.get(index, 0)
                steps = range(ahead + 1) if tick == 0 else [tick + ahead]
            for step in steps:
                if 0 <= step < STEPS:
                    stage(index, step)
        return True

    def begin(self, index):
        if any(self.family(index) == self.family(held) for held in self.active):
            self.waiting.append(index)
        else:
            self.active.append(index)

    def serve(self, count=1):
        for _ in range(count):
            if not self.active:
                return
            index = self.active[0]
            if self.served < len(ORDER) and ORDER[self.served] in self.active:
                index = ORDER[self.served]
            self.served += 1
            self.active.remove(index)
            if self.advance(index):
                self.active.append(index)
                continue
            for other in self.waiting:
                if self.family(other) == self.family(index):
                    self.waiting.remove(other)
                    self.active.append(other)
                    break


def fold_cuts(n_dp, width, chans, hidden):
    if n_dp != 4 * DEPTH or width != CHUNKS * LANES or chans % (2 * LANES) or hidden % LANES:
        return None
    if any(rows % (16 * CHUNKS) for rows in (hidden, chans, width)):
        return None
    layer = []
    for kind, rows, cols in (
        ("cols", hidden, width // 2),
        ("rows", width, hidden),
        ("cols", chans, width // 2),
        ("cols", 3 * width, chans // 2),
    ):
        chunk = rows // CHUNKS
        first = 16 * round(0.6 * chunk / 16)
        if not 0 < first < chunk:
            return None
        layer.append((kind, first, chunk - first, cols))
    return layer * LAYERS + [("small", 8, 8, LANES)]


DOWN, GATE_UP, OUT, QKV = range(4)
SMALL = 4 * LAYERS
MID_ROOTED = (DOWN, QKV, 4 + OUT)
AHEAD = {
    DOWN: 1,
    OUT: 2,
    4 + DOWN: 2,
    4 + GATE_UP: 1,
    4 + OUT: 1,
    4 + QKV: 1,
}
ORDER = (
    4, 4, 4, 5, 4, 5, 4, 5, 4, 5, 4, 5, 6, 4, 7, 5, 4, 7, 4, 6, 5, 6, 7, 4, 4, 5, 6, 7, 0, 5,
    6, 7, 5, 6, 0, 7, 5, 6, 0, 7, 5, 6, 8, 0, 1, 7, 6, 8, 0, 1, 7, 6, 2, 8, 0, 1, 7, 8, 2, 0,
    7, 1, 8, 0, 7, 2, 1, 8, 0, 3, 1, 2, 8, 0, 3, 1, 2, 8, 3, 1, 2, 8, 3, 8, 1, 2, 8, 3, 1, 3,
    2, 1, 3, 8, 2, 1, 3, 2, 2, 3, 2, 3,
)
MLP_KEPT = ("gu", "z", "n2")
MIXER_KEPT = ("n1", "p", "logits", "t", "u", "o", "on", "h")
PEERS = ("z", "n2", "ef", "dgu", "n1", "on", "em", "dp")


def backward_kernel(n_parts, cuts, *refs):
    refs = list(refs)

    def taken(count):
        group = refs[:count]
        del refs[:count]
        return group

    (cot_ref, gain_ref, taps_ref, head_gain_ref, wb_ref) = taken(5)
    (part_hbm, wq_hbm, wo_hbm, wgu_hbm, wd_hbm) = taken(5)
    kept = dict(zip(KEPT, taken(len(KEPT))))
    (out_ref, in_grad_ref, *totals) = taken(2 + 5)
    own = taken(len(cuts))
    fold_slots = taken(10)
    peers = dict(zip(PEERS, taken(len(PEERS))))
    (e_ref, small, small_peer, slots, don_ref, wb, gains) = taken(7)
    (load_sems, send_sems, recv_sems, peer_sems, gain_sems) = taken(5)
    fold_sems = taken(2)

    per_table = [totals[index].at[level] for level in range(LAYERS) for index in range(4)]
    fold = Fold(cuts, own, fold_slots, [*per_table, totals[4]], fold_sems)
    core, serve = fold.core, fold.serve
    exchange = Exchange(slots, send_sems, recv_sems)
    barrier = pltpu.get_barrier_semaphore()
    for device in (fold.partner, fold.beside, fold.folded, fold.across):
        pl.semaphore_signal(barrier, inc=1, device_id=device, device_id_type=pl.DeviceIdType.MESH)
    exchange.greet(4)

    length, width = e_ref.shape
    chans = wo_hbm.shape[1]
    hidden = wd_hbm.shape[1]
    heads = chans // DK
    high = length // n_parts
    parts = [(part, slice(part * high, (part + 1) * high)) for part in range(n_parts)]
    row, col = positions(length)
    lane = lax.broadcasted_iota(jnp.int32, (length, LANES), 1)
    side = width - SIDE
    half_width, half_chans = width // 2, chans // 2

    def other_half(wide):
        return pl.ds(pl.multiple_of((1 - core) * wide, LANES), wide)

    def own_half(wide):
        return pl.ds(pl.multiple_of(core * wide, LANES), wide)

    def to_peer(name, level, source):
        spot = PEERS.index(name)
        return remote(
            source,
            peers[name].at[level],
            peer_sems.at[0, spot, level],
            peer_sems.at[1, spot, level],
            fold.partner,
        )

    top = LAYERS - 1
    early = [
        to_peer(name, level, kept[name].at[level])
        for level in reversed(range(LAYERS))
        for name in ("z", "n2", "on", "n1")
    ]
    early.insert(1, to_peer("ef", top, cot_ref.at[:, other_half(width // 2)]))
    for copy in early:
        copy.start()
    first = pltpu.make_async_copy(part_hbm, slots.at[0, exchange.me], load_sems.at[0, 0, 0])
    first.start()
    small[...] = jnp.zeros_like(small)

    def norm_step(level, which, spot, part, rows, hid):
        total = exchange.take(spot, part, rows)
        gain = gain_ref[level, which : which + 1, :].astype(F32)
        grad_hidden, sums = rms_back(hid, gain, total)
        base = 16 * level + (1 if which else 3)
        for index in range(2):
            spot_row = slice(base + index, base + index + 1)
            small[spot_row, SIDE:] += sums[:, index * side : (index + 1) * side]
        return e_ref[rows] + grad_hidden

    def mlp_stage(level):
        def scope(wgu, wd, gu, z, n2, hid, dgu, ef):
            held = dict(gu=gu, z=z, n2=n2)
            loads = {
                "wd": pltpu.make_async_copy(wd_hbm.at[level], wd, load_sems.at[level, 0, 1]),
                "wgu": pltpu.make_async_copy(wgu_hbm.at[level], wgu, load_sems.at[level, 0, 2]),
            }
            for index, name in enumerate(MLP_KEPT):
                loads[name] = pltpu.make_async_copy(
                    kept[name].at[level], held[name], load_sems.at[level, 0, 3 + index]
                )
            if level < LAYERS - 1:
                loads["hid"] = pltpu.make_async_copy(
                    kept["x"].at[level + 1], hid, load_sems.at[level, 0, 6]
                )
                loads["hid"].start()
            for name in ("z", "wd", "gu", "wgu", "n2"):
                loads[name].start()
            index = 4 * level
            if level == top:
                first.wait()
                for part, rows in parts:
                    exchange.send(0, part, rows)
                loads["z"].wait()
                for name in ("z", "ef"):
                    to_peer(name, level, peers[name].at[level]).wait_recv()
                own[index + DOWN][...] = low(
                    dot_tn(z[...], cot_ref[:, own_half(half_width)])
                    + dot_tn(peers["z"][level], peers["ef"][level])
                )
                fold.begin(index + DOWN)
                serve()
            for part, rows in parts:
                if level == LAYERS - 1:
                    e = cot_ref[rows].astype(F32)
                else:
                    if part == 0:
                        loads["hid"].wait()
                    e = norm_step(level + 1, 0, 2 * (LAYERS - 1 - level), part, rows, hid[rows])
                e_ref[rows] = e
                e_low = low(e)
                ef[rows] = e_low
                if part == 0:
                    loads["wd"].wait()
                dz = dot_nt(e_low, wd[...])
                if part == 0:
                    loads["gu"].wait()
                g, u = gu[0, rows], gu[1, rows]
                s = sigmoid(g)
                dgu[0, rows] = low(dz * u * (s * (1.0 + g * (1.0 - s))))
                dgu[1, rows] = low(dz * (g * s))
                if part or level != top:
                    serve()
            sends = [to_peer("dgu", level, dgu.at[1 - core])]
            if level != top:
                sends.append(to_peer("ef", level, ef.at[:, other_half(half_width)]))
            for send in sends:
                send.start()
            loads["wgu"].wait()
            for part, rows in parts:
                partial = dot_nt(dgu[0, rows], wgu[0]) + dot_nt(dgu[1, rows], wgu[1])
                exchange.give(2 * (LAYERS - 1 - level) + 1, part, rows, low(partial))
            serve()
            loads["n2"].wait()
            for name in ("n2", "dgu"):
                to_peer(name, level, peers[name].at[level]).wait_recv()
            own[index + GATE_UP][...] = low(
                dot_tn(n2[...], dgu[core]) + dot_tn(peers["n2"][level], peers["dgu"][level])
            )
            fold.begin(index + GATE_UP)
            serve()
            if level != top:
                loads["z"].wait()
                for name in ("z", "ef"):
                    to_peer(name, level, peers[name].at[level]).wait_recv()
                own[index + DOWN][...] = low(
                    dot_tn(z[...], ef[:, own_half(half_width)])
                    + dot_tn(peers["z"][level], peers["ef"][level])
                )
                fold.begin(index + DOWN)
                serve(4)
            for send in sends:
                send.wait_send()

        pl.run_scoped(
            scope,
            pltpu.VMEM((2, width, hidden), BF16),
            pltpu.VMEM((hidden, width), BF16),
            pltpu.VMEM((2, length, hidden), F32),
            pltpu.VMEM((length, hidden), BF16),
            pltpu.VMEM((length, width), BF16),
            pltpu.VMEM((length, width), F32),
            pltpu.VMEM((2, length, hidden), BF16),
            pltpu.VMEM((length, width), BF16),
        )

    def mixer_stage(level):
        def scope(wq, wo, n1, p, logits, t, u_all, o_all, on, h, grads, dp, em):
            held = dict(n1=n1, p=p, logits=logits, t=t, u=u_all, o=o_all, on=on, h=h)
            loads = {
                "wo": pltpu.make_async_copy(wo_hbm.at[level], wo, load_sems.at[level, 1, 0]),
                "wq": pltpu.make_async_copy(wq_hbm.at[level], wq, load_sems.at[level, 1, 1]),
            }
            for index, name in enumerate(MIXER_KEPT):
                loads[name] = pltpu.make_async_copy(
                    kept[name].at[level], held[name], load_sems.at[level, 1, 2 + index]
                )
            for name in ("h", "wo", "p", "o", "u", "logits", "t", "wq", "n1", "on"):
                loads[name].start()
            loads["p"].wait()
            convs = [
                conv_silu(p[index], taps_ref[level, index].astype(F32)) for index in range(3)
            ]
            spot = 2 * (LAYERS - 1 - level) + 1
            loads["h"].wait()
            if level == LAYERS - 1:
                for part, rows in parts:
                    out_ref[rows] = low(h[rows] + exchange.take(0, part, rows))
            for part, rows in parts:
                serve()
                e = norm_step(level, 1, spot, part, rows, h[rows])
                e_ref[rows] = e
                e_low = low(e)
                em[rows] = e_low
                if part == 0:
                    loads["wo"].wait()
                don_ref[rows] = dot_nt(e_low, wo[...])
            send_em = to_peer("em", level, em.at[:, other_half(half_width)])
            send_em.start()
            for name in ("o", "u", "logits", "t"):
                loads[name].wait()
            beta = sigmoid(logits[...])
            head_gain = head_gain_ref[level : level + 1, :].astype(F32)
            gain_rows = jnp.zeros((1, DK), F32)
            dlogit = jnp.zeros((length, LANES), F32)
            serve(2)
            for head in range(heads):
                cols = head_cols(head)
                c0, c1, c2 = (conv[2][:, cols] for conv in convs)
                rho0 = lax.rsqrt(jnp.sum(c0 * c0, axis=-1, keepdims=True) + 0.001)
                rho1 = lax.rsqrt(jnp.sum(c1 * c1, axis=-1, keepdims=True) + 0.001)
                q, k, v = low(c0 * rho0), low(c1 * rho1), low(c2).astype(F32)
                gate = beta[:, head : head + 1]
                o = o_all[:, cols]
                scale = lax.rsqrt(jnp.mean(o * o, axis=-1, keepdims=True) + 0.01)
                dn = don_ref[:, cols]
                weighted = dn * head_gain
                inner = jnp.mean(o * weighted, axis=-1, keepdims=True)
                do = low(scale * weighted - o * (scale * scale * scale) * inner)
                gain_rows = gain_rows + jnp.sum(dn * o * scale, axis=0, keepdims=True)
                u = u_all[:, cols]
                score_t = low(jnp.where(row <= col, dot_nt(k, q), 0.0))
                du = dot_nn(score_t, do)
                ds = low(jnp.where(row >= col, dot_nt(do, u), 0.0))
                ds_t = low(jnp.where(row <= col, dot_nt(u, do), 0.0))
                dq = dot_nn(ds, k)
                dk = dot_nn(ds_t, q)
                blocks = [(t[0, head, index], t[1, head, index]) for index in range(2)]
                r = solve_back(blocks, k, gate, du)
                dv = gate * r
                dv_low = low(dv)
                gram = low(jnp.where(row > col, dot_nt(k, k), 0.0))
                w = v - dot_nn(gram, u)
                dbeta = jnp.sum(r * w, axis=-1, keepdims=True)
                dgram = jnp.where(row > col, dot_nt(dv_low, u), 0.0) + jnp.where(
                    row < col, dot_nt(u, dv_low), 0.0
                )
                dk = dk - dot_nn(low(dgram), k)
                grads[0, :, cols] = rho0 * dq - c0 * (rho0 * rho0 * rho0) * jnp.sum(
                    c0 * dq, axis=-1, keepdims=True
                )
                grads[1, :, cols] = rho1 * dk - c1 * (rho1 * rho1 * rho1) * jnp.sum(
                    c1 * dk, axis=-1, keepdims=True
                )
                grads[2, :, cols] = dv
                dlogit = dlogit + jnp.where(lane == head, dbeta * gate * (1.0 - gate), 0.0)
                if head % 2:
                    serve()
            base = 16 * level
            small[base : base + 1, SIDE : SIDE + DK] = gain_rows
            for index in range(3):
                taps = taps_ref[level, index].astype(F32)
                total, gate, _ = convs[index]
                dsum = grads[index] * (gate * (1.0 + total * (1.0 - gate)))
                project = p[index]
                dproject = taps[KCONV - 1 : KCONV, :] * dsum
                for tap in range(KCONV):
                    back = KCONV - 1 - tap
                    line = base + index * KCONV + tap
                    small[line : line + 1, :chans] = jnp.sum(
                        dsum * shift_down(project, back), axis=0, keepdims=True
                    )
                    if back:
                        dproject = dproject + taps[tap : tap + 1, :] * shift_up(dsum, back)
                dp[index] = low(dproject)
            dlogit_low = low(dlogit)
            wb[...] = jnp.zeros_like(wb)
            wb[:heads] = wb_ref[level]
            loads["wq"].wait()
            for part, rows in parts:
                dn1 = dot_nn(dlogit_low[rows], wb[...])
                for index in range(3):
                    dn1 = dn1 + dot_nt(dp[index, rows], wq[index])
                exchange.give(spot + 1, part, rows, low(dn1))
            send_dp = to_peer("dp", level, dp.at[:, :, other_half(half_chans)])
            send_dp.start()
            serve()
            loads["n1"].wait()
            loads["on"].wait()
            line = base + 3 * KCONV
            small[line : line + heads, :] = dot_tn(dlogit_low, n1[...])[:heads, :]
            for name in ("em", "on", "n1", "dp"):
                to_peer(name, level, peers[name].at[level]).wait_recv()
            own[4 * level + OUT][...] = low(
                dot_tn(on[...], em[:, own_half(half_width)])
                + dot_tn(peers["on"][level], peers["em"][level])
            )
            fold.begin(4 * level + OUT)
            serve()
            for index in range(3):
                own[4 * level + QKV][index * width : (index + 1) * width] = low(
                    dot_tn(n1[...], dp[index, :, own_half(half_chans)])
                    + dot_tn(peers["n1"][level], peers["dp"][level, index])
                )
            fold.begin(4 * level + QKV)
            serve(3)
            send_em.wait_send()
            send_dp.wait_send()

        pl.run_scoped(
            scope,
            pltpu.VMEM((3, width, chans), BF16),
            pltpu.VMEM((chans, width), BF16),
            pltpu.VMEM((length, width), BF16),
            pltpu.VMEM((3, length, chans), F32),
            pltpu.VMEM((length, LANES), F32),
            pltpu.VMEM((2, heads, 2, length // 2, length // 2), BF16),
            pltpu.VMEM((length, chans), BF16),
            pltpu.VMEM((length, chans), F32),
            pltpu.VMEM((length, chans), BF16),
            pltpu.VMEM((length, width), F32),
            pltpu.VMEM((3, length, chans), F32),
            pltpu.VMEM((3, length, chans), BF16),
            pltpu.VMEM((length, width), BF16),
        )

    for level in reversed(range(LAYERS)):
        mlp_stage(level)
        mixer_stage(level)

    for level in range(LAYERS):
        gains[exchange.me, level : level + 1] = small[
            16 * level : 16 * level + 1, SIDE : SIDE + DK
        ]
    gain_copies = [
        remote(
            gains.at[exchange.me],
            gains.at[exchange.me],
            gain_sems.at[0, away],
            gain_sems.at[1, away],
            device,
        )
        for away, device in enumerate(exchange.others)
    ]
    for copy in gain_copies:
        copy.start()

    def last_scope(hid):
        load = pltpu.make_async_copy(kept["x"].at[0], hid, load_sems.at[0, 0, 7])
        load.start()
        serve(3)
        load.wait()
        for part, rows in parts:
            in_grad_ref[rows] = low(norm_step(0, 0, 2 * LAYERS, part, rows, hid[rows]))

    pl.run_scoped(last_scope, pltpu.VMEM((length, width), F32))

    for copy in gain_copies:
        copy.wait()
    for level in range(LAYERS):
        total = gains[0, level : level + 1]
        for index in range(1, exchange.count):
            total = total + gains[index, level : level + 1]
        small[16 * level : 16 * level + 1, SIDE : SIDE + DK] = total

    def small_half(which):
        return small.at[pl.ds(pl.multiple_of(which * 16, 16), 16)]

    send_small = remote(
        small_half(1 - core),
        small_peer,
        load_sems.at[1, 0, 6],
        load_sems.at[1, 0, 7],
        fold.partner,
    )
    send_small.start()
    serve()
    send_small.wait_recv()
    own[SMALL][...] = small_half(core)[...] + small_peer[...]
    fold.begin(SMALL)
    while fold.active:
        serve()
    send_small.wait_send()
    for copy in early:
        copy.wait_send()
    exchange.finish()


def backward(cot, part, saved, norm_gain, taps, head_gain, wb, wq, wo, wgu, wd):
    length, width = cot.shape
    chans, hidden = wq.shape[-1], wgu.shape[-1]
    heads = chans // DK
    n_tensor = lax.axis_size("tensor")
    cuts = fold_cuts(lax.axis_size("dp"), width, chans, hidden)
    n_parts = 2
    sds = jax.ShapeDtypeStruct
    vmem = pl.BlockSpec(memory_space=pltpu.VMEM)
    hbm = pl.BlockSpec(memory_space=pl.ANY)
    own, slots = [], []
    for index, (kind, first, second, cols) in enumerate(cuts):
        dtype = F32 if kind == "small" else BF16
        own.append(
            pltpu.VMEM((16, cols * CHUNKS), dtype)
            if kind == "small"
            else pltpu.VMEM(((first + second) * CHUNKS, cols), dtype)
        )
        if index < 4 or index == SMALL:
            slots.append(pltpu.VMEM((3, STEPS, first, cols), dtype))
            slots.append(pltpu.VMEM((4, STEPS, second, cols), dtype))
    peers = dict(
        z=(length, hidden),
        n2=(length, width),
        ef=(length, width // 2),
        dgu=(length, hidden),
        n1=(length, width),
        on=(length, chans),
        em=(length, width // 2),
        dp=(3, length, chans // 2),
    )
    spots = 2 * LAYERS + 1
    return pl.pallas_call(
        functools.partial(backward_kernel, n_parts, cuts),
        out_shape=(
            sds((length, width), BF16),
            sds((length, width), BF16),
            sds((LAYERS, hidden, width), BF16),
            sds((LAYERS, 2, width, hidden), BF16),
            sds((LAYERS, chans, width), BF16),
            sds((LAYERS, 3 * width, chans), BF16),
            sds((16 * LAYERS, width), F32),
        ),
        in_specs=[vmem] * 5 + [hbm] * (5 + len(KEPT)),
        out_specs=(vmem, vmem) + (hbm,) * 5,
        scratch_shapes=[
            *own,
            *slots,
            *(pltpu.VMEM((LAYERS, *peers[name]), BF16) for name in PEERS),
            pltpu.VMEM((length, width), F32),
            pltpu.VMEM((16 * LAYERS, width), F32),
            pltpu.VMEM((16, width), F32),
            pltpu.VMEM((spots, n_tensor, length, width), BF16),
            pltpu.VMEM((length, chans), F32),
            pltpu.VMEM((LANES, width), BF16),
            pltpu.VMEM((n_tensor, 8, DK), F32),
            pltpu.SemaphoreType.DMA((LAYERS, 2, 10)),
            pltpu.SemaphoreType.DMA((spots, n_parts, n_tensor - 1)),
            pltpu.SemaphoreType.DMA((spots, n_parts, n_tensor - 1)),
            pltpu.SemaphoreType.DMA((2, len(PEERS), LAYERS)),
            pltpu.SemaphoreType.DMA((2, n_tensor - 1)),
            pltpu.SemaphoreType.DMA((len(KINDS), len(cuts), STEPS)),
            pltpu.SemaphoreType.DMA((len(KINDS), len(cuts), STEPS)),
        ],
        compiler_params=pltpu.CompilerParams(
            vmem_limit_bytes=VMEM_LIMIT, collective_id=0, has_side_effects=True
        ),
        name="backward",
    )(cot, norm_gain, taps, head_gain, wb, part, wq, wo, wgu, wd, *(saved[name] for name in KEPT))


def staged_backward(cot, part, saved, norm_gain, taps, head_gain, wb, wq, wo, wgu, wd):
    total = saved["h"][LAYERS - 1]
    for add in branch_parts(part):
        total = total + add.astype(F32)
    outputs = total.astype(BF16)
    e, hid, adds = cot, saved["x"][LAYERS - 1], ()
    gain_rows = {}
    small = [None] * LAYERS
    big = [None] * LAYERS
    for level in reversed(range(LAYERS)):
        at = {name: saved[name][level] for name in KEPT}
        mlp_kept = tuple(at[name] for name in ("n2", "gu", "z"))
        mixer_kept = tuple(at[name] for name in ("n1", "p", "logits", "t", "u", "o", "on"))
        e, rows, part, grad_down, grad_gate_up = mlp_backward(
            level, e, hid, adds, norm_gain, *mlp_kept, wgu, wd
        )
        gain_rows[level + 1] = rows
        e, part, small[level], grad_qkv, grad_out = mixer_backward(
            level,
            e,
            at["h"],
            branch_parts(part),
            norm_gain,
            taps,
            head_gain,
            wb,
            mixer_kept,
            wq,
            wo,
        )
        hid, adds = at["x"], branch_parts(part)
        big[level] = (grad_down, grad_gate_up, grad_out, grad_qkv)
    branch = adds[0].astype(F32)
    for add in adds[1:]:
        branch = branch + add.astype(F32)
    grad_hidden, rows = rms_back(hid, norm_gain[0, 0:1].astype(F32), branch)
    gain_rows[0] = rows
    input_grad = (e + grad_hidden).astype(BF16)
    side = rows.shape[-1] - SIDE
    small_all = jnp.concatenate(
        [
            small[level].at[3:5, SIDE:].set(gain_rows[level].reshape(2, side))
            for level in range(LAYERS)
        ]
    )
    gains = small_all.reshape(LAYERS, 16, -1)[:, 0, SIDE : SIDE + DK]
    gains = sum(branch_parts(gains))
    for level in range(LAYERS):
        small_all = small_all.at[16 * level, SIDE : SIDE + DK].set(gains[level])
    tables = [table for group in big for table in group]
    sums = sum_over_dp(tables)
    stacked = [jnp.stack([sums[index], sums[4 + index]]) for index in range(4)]
    return (outputs, input_grad, *stacked, lax.psum(small_all, "dp"))


def widen_kernel(heads, chans, chunks, *refs):
    count = len(chunks)
    refs = list(refs)

    def taken(number):
        group = refs[:number]
        del refs[:number]
        return group

    sources, (small, *passed) = taken(count), taken(3)
    targets, (conv_out, beta_out, norm_out, gain_out) = taken(count), taken(4)
    passed_out, came, made = taken(2), taken(count), taken(count)
    came_sems, made_sems = taken(2)
    for source, target in zip(passed, passed_out):
        target[...] = source[...]
    order = []
    for index, rows in enumerate(chunks):
        steps = sources[index].shape[0] // rows
        order += [(index, step, pl.ds(step * rows, rows)) for step in range(steps)]
    loads = [
        pltpu.make_async_copy(
            sources[index].at[rows], came[index].at[rows], came_sems.at[index, step]
        )
        for index, step, rows in order
    ]
    for load in loads:
        load.start()
    for level in range(LAYERS):
        base = 16 * level
        for index in range(3):
            line = base + index * KCONV
            conv_out[level, index] = small[line : line + KCONV, :chans]
        beta_out[level] = small[base + 3 * KCONV : base + 3 * KCONV + heads, :]
        half = norm_out.shape[-1] // 2
        for which, line in ((0, 3), (1, 1)):
            for index in range(2):
                spot = base + line + index
                norm_out[level, which : which + 1, index * half : (index + 1) * half] = small[
                    spot : spot + 1, SIDE : SIDE + half
                ]
        gain_out[level : level + 1] = small[base : base + 1, SIDE : SIDE + DK]
    stores = {}
    for (index, step, rows), load in zip(order, loads):
        slot = step % SLOTS_OUT
        if step >= SLOTS_OUT:
            stores[(index, slot)].wait()
        load.wait()
        made[index][slot] = came[index][rows].astype(F32)
        store = pltpu.make_async_copy(
            made[index].at[slot], targets[index].at[rows], made_sems.at[index, slot]
        )
        store.start()
        stores[(index, slot)] = store
    for store in stores.values():
        store.wait()


SLOTS_OUT = 4


def widen(tables, small, heads, chans, passed):
    views = [table.reshape(-1, table.shape[-1]) for table in tables]
    chunks = []
    for view in views:
        rows, cols = view.shape
        steps = 1
        while rows % (32 * steps) == 0 and rows // steps * cols > 400000:
            steps *= 2
        chunks.append(rows // steps)
    most = max(view.shape[0] // rows for view, rows in zip(views, chunks))
    width = small.shape[-1]
    sds = jax.ShapeDtypeStruct
    vmem = pl.BlockSpec(memory_space=pltpu.VMEM)
    hbm = pl.BlockSpec(memory_space=pl.ANY)
    count = len(views)
    moved = sum(6 * view.size for view in views)
    results = pl.pallas_call(
        functools.partial(widen_kernel, heads, chans, tuple(chunks)),
        out_shape=(
            *(sds(view.shape, F32) for view in views),
            sds((LAYERS, 3, KCONV, chans), F32),
            sds((LAYERS, heads, width), F32),
            sds((LAYERS, 2, 2 * (width - SIDE)), F32),
            sds((LAYERS, DK), F32),
            *(sds(array.shape, array.dtype) for array in passed),
        ),
        in_specs=[hbm] * count + [vmem] * 3,
        out_specs=(hbm,) * count + (vmem,) * 6,
        scratch_shapes=[
            *(pltpu.VMEM(view.shape, view.dtype) for view in views),
            *(
                pltpu.VMEM((SLOTS_OUT, rows, view.shape[1]), F32)
                for view, rows in zip(views, chunks)
            ),
            pltpu.SemaphoreType.DMA((count, most)),
            pltpu.SemaphoreType.DMA((count, SLOTS_OUT)),
        ],
        compiler_params=pltpu.CompilerParams(vmem_limit_bytes=VMEM_LIMIT),
        cost_estimate=pl.CostEstimate(flops=0, bytes_accessed=moved, transcendentals=0),
        name="widen",
    )(*views, small, *passed)
    return (list(results[:count]), *results[count:])


def body(
    inputs,
    qkv_weight,
    conv_taps,
    beta_weight,
    out_gain,
    out_weight,
    norm_gain,
    gate_up_weight,
    down_weight,
    cotangent,
):
    heads = beta_weight.shape[-1]
    wb = jnp.swapaxes(beta_weight, 1, 2)
    saved, part = forward(
        inputs,
        norm_gain,
        conv_taps,
        out_gain,
        wb,
        qkv_weight,
        out_weight,
        gate_up_weight,
        down_weight,
    )
    length, width = inputs.shape
    chans, hidden = conv_taps.shape[-1], down_weight.shape[1]
    if fold_cuts(lax.axis_size("dp"), width, chans, hidden) is not None:
        outputs, input_grad, *big, small_all = backward(
            cotangent,
            part,
            saved,
            norm_gain,
            conv_taps,
            out_gain,
            wb,
            qkv_weight,
            out_weight,
            gate_up_weight,
            down_weight,
        )
    else:
        outputs, input_grad, *big, small_all = staged_backward(
            cotangent,
            part,
            saved,
            norm_gain,
            conv_taps,
            out_gain,
            wb,
            qkv_weight,
            out_weight,
            gate_up_weight,
            down_weight,
        )
    shapes = (down_weight.shape, gate_up_weight.shape, out_weight.shape, qkv_weight.shape)
    big, grad_conv, grad_beta, grad_norm, grad_out_gain, outputs, input_grad = widen(
        big, small_all, heads, chans, (outputs, input_grad)
    )
    grad_down, grad_gate_up, grad_out, grad_qkv = (
        table.reshape(shape) for table, shape in zip(big, shapes)
    )
    grad_beta = jnp.swapaxes(grad_beta, 1, 2)
    return (
        outputs,
        input_grad,
        grad_qkv,
        grad_conv,
        grad_beta,
        grad_out_gain,
        grad_out,
        grad_norm,
        grad_gate_up,
        grad_down,
    )


def solution(mesh):
    in_specs = (
        P("dp", None),
        P(None, None, None, "tensor"),
        P(None, None, None, "tensor"),
        P(None, None, "tensor"),
        P(),
        P(None, "tensor", None),
        P(),
        P(None, None, None, "tensor"),
        P(None, "tensor", None),
        P("dp", None),
    )
    out_specs = (
        P("dp", None),
        P("dp", None),
        P(None, None, None, "tensor"),
        P(None, None, None, "tensor"),
        P(None, None, "tensor"),
        P(),
        P(None, "tensor", None),
        P(),
        P(None, None, None, "tensor"),
        P(None, "tensor", None),
    )
    return jax.shard_map(body, mesh=mesh, in_specs=in_specs, out_specs=out_specs, check_vma=False)
```

```python
import functools
import math

import jax
import jax.numpy as jnp
from jax import lax
from jax.experimental import pallas as pl
from jax.experimental.pallas import tpu as pltpu
from jax.sharding import PartitionSpec as P

DK = 128
KCONV = 4
LAYERS = 2
LANES = 128
SIDE = 512
F32 = jnp.float32
BF16 = jnp.bfloat16
VMEM_LIMIT = 60 * 1024 * 1024


def dot_nn(a, b):
    return lax.dot_general(a, b, (((1,), (0,)), ((), ())), preferred_element_type=F32)


def dot_nt(a, b):
    return lax.dot_general(a, b, (((1,), (1,)), ((), ())), preferred_element_type=F32)


def dot_tn(a, b):
    return lax.dot_general(a, b, (((0,), (0,)), ((), ())), preferred_element_type=F32)


def halves(a):
    hi = a.astype(BF16)
    return hi, (a - hi.astype(F32)).astype(BF16)


def split_dot(dot, a, b):
    return dot(a[0], b[0]) + (dot(a[0], b[1]) + dot(a[1], b[0]))


def low(a):
    return a.astype(BF16)


def sigmoid(a):
    return 1.0 / (1.0 + jnp.exp(-a))


def rms_scale(a):
    return lax.rsqrt(jnp.mean(a * a, axis=-1, keepdims=True) + 1e-05)


def rms_back(hidden, gain, grad_normed):
    scale = rms_scale(hidden)
    weighted = gain * grad_normed
    inner = jnp.mean(hidden * weighted, axis=-1, keepdims=True)
    grad_hidden = scale * weighted - hidden * (scale * scale * scale) * inner
    rows = jnp.sum(grad_normed * hidden * scale, axis=0, keepdims=True)
    return grad_hidden, rows


def shift_down(a, count):
    if count == 0:
        return a
    row = lax.broadcasted_iota(jnp.int32, a.shape, 0)
    return jnp.where(row >= count, pltpu.roll(a, count, 0), 0.0)


def shift_up(a, count):
    if count == 0:
        return a
    length = a.shape[0]
    row = lax.broadcasted_iota(jnp.int32, a.shape, 0)
    return jnp.where(row < length - count, pltpu.roll(a, length - count, 0), 0.0)


def conv_silu(project, taps):
    total = taps[KCONV - 1 : KCONV, :] * project
    for tap in range(KCONV - 1):
        total = total + taps[tap : tap + 1, :] * shift_down(project, KCONV - 1 - tap)
    gate = sigmoid(total)
    return total, gate, total * gate


def conv_silu_rows(project, taps, rows):
    start = rows.start
    if start == 0:
        return conv_silu(project[rows], taps)[2]
    return conv_silu(project[start - 8 : rows.stop], taps)[2][8:]


def solve_back(blocks, key, gate, grad):
    half = grad.shape[0] // 2
    second = split_dot(dot_tn, blocks[1], halves(grad[half:]))
    gram = halves(dot_nt(key[half:], key[:half]))
    cross = split_dot(dot_tn, gram, halves(gate[half:] * second))
    first = split_dot(dot_tn, blocks[0], halves(grad[:half] - cross))
    return jnp.concatenate([first, second], axis=0)


def positions(length):
    row = lax.broadcasted_iota(jnp.int32, (length, length), 0)
    col = lax.broadcasted_iota(jnp.int32, (length, length), 1)
    return row, col


def unit_lower_inverse(lower_list):
    length = lower_list[0].shape[0]
    row, col = positions(length)
    eye = jnp.where(row == col, 1.0, 0.0)
    diag_list = [jnp.where(row // 4 == col // 4, lower, 0.0) for lower in lower_list]
    parts = [halves(diag) for diag in diag_list]
    squares = [split_dot(dot_nn, part, part) for part in parts]
    firsts = [eye - diag for diag in diag_list]
    inverse = [
        first + split_dot(dot_nn, halves(first), halves(square))
        for first, square in zip(firsts, squares)
    ]
    size = 4
    while size < length:
        fresh = (row // (2 * size) == col // (2 * size)) & (row // size != col // size)
        offs = [halves(jnp.where(fresh, lower, 0.0)) for lower in lower_list]
        held = [halves(inv) for inv in inverse]
        mids = [split_dot(dot_nn, inv, off) for inv, off in zip(held, offs)]
        inverse = [
            inv - split_dot(dot_nn, halves(mid), part)
            for inv, mid, part in zip(inverse, mids, held)
        ]
        size = 2 * size
    return inverse


def head_cols(head):
    return slice(head * DK, (head + 1) * DK)


KEPT = ("x", "n1", "p", "logits", "t", "u", "o", "on", "h", "n2", "gu", "z")


def kept_shapes(length, width, chans, hidden):
    heads = chans // DK
    shapes = dict(
        x=((length, width), F32),
        n1=((length, width), BF16),
        p=((3, length, chans), F32),
        logits=((length, LANES), F32),
        t=((2, heads, 2, length // 2, length // 2), BF16),
        u=((length, chans), BF16),
        o=((length, chans), F32),
        on=((length, chans), BF16),
        h=((length, width), F32),
        n2=((length, width), BF16),
        gu=((2, length, hidden), F32),
        z=((length, hidden), BF16),
    )
    return [((LAYERS, *shapes[name][0]), shapes[name][1]) for name in KEPT]


class Exchange:
    def __init__(self, slots, send_sems, recv_sems):
        self.slots, self.send_sems, self.recv_sems = slots, send_sems, recv_sems
        self.count = slots.shape[1]
        self.me = lax.axis_index("tensor")
        self.others = [
            {"tensor": lax.rem(self.me + away, self.count)} for away in range(1, self.count)
        ]
        self.pending = []

    def greet(self, others=0):
        barrier = pltpu.get_barrier_semaphore()
        for device in self.others:
            pl.semaphore_signal(
                barrier, inc=1, device_id=device, device_id_type=pl.DeviceIdType.MESH
            )
        pl.semaphore_wait(barrier, self.count - 1 + others)

    def copies(self, spot, part, rows):
        mine = self.slots.at[spot, self.me, rows]
        return [
            pltpu.make_async_remote_copy(
                src_ref=mine,
                dst_ref=mine,
                send_sem=self.send_sems.at[spot, part, away],
                recv_sem=self.recv_sems.at[spot, part, away],
                device_id=device,
                device_id_type=pl.DeviceIdType.MESH,
            )
            for away, device in enumerate(self.others)
        ]

    def give(self, spot, part, rows, value):
        self.slots[spot, self.me, rows] = value
        self.send(spot, part, rows)

    def send(self, spot, part, rows):
        for copy in self.copies(spot, part, rows):
            copy.start()
        self.pending.append((spot, part, rows))

    def take(self, spot, part, rows):
        for copy in self.copies(spot, part, rows):
            copy.wait_recv()
        total = self.slots[spot, 0, rows].astype(F32)
        for index in range(1, self.count):
            total = total + self.slots[spot, index, rows].astype(F32)
        return total

    def finish(self):
        for sent in self.pending:
            for copy in self.copies(*sent):
                copy.wait_send()


def forward_kernel(n_parts, *refs):
    (x_ref, gain_ref, taps_ref, head_gain_ref, wb_ref) = refs[:5]
    (wq_hbm, wo_hbm, wgu_hbm, wd_hbm) = refs[5:9]
    count = len(KEPT)
    outs = dict(zip(KEPT, refs[9 : 9 + count]))
    last_out = refs[9 + count]
    held = dict(zip(KEPT, refs[10 + count : 10 + 2 * count]))
    (wq, wo, wgu, wd, wb, slots, last, load_sems, keep_sems, send_sems, recv_sems) = refs[
        10 + 2 * count :
    ]
    exchange = Exchange(slots, send_sems, recv_sems)
    sources = ((wq_hbm, wq), (wo_hbm, wo), (wgu_hbm, wgu), (wd_hbm, wd))
    loads = [
        [
            pltpu.make_async_copy(source.at[level], target.at[level], load_sems.at[level, index])
            for index, (source, target) in enumerate(sources)
        ]
        for level in range(LAYERS)
    ]
    for group in loads:
        for load in group:
            load.start()
    wb[...] = jnp.zeros_like(wb)
    for level in range(LAYERS):
        wb[level, : wb_ref.shape[1]] = wb_ref[level]
    exchange.greet()
    keeps = []

    def keep(name, level, part=0, rows=None):
        at = (level,)
        if rows is not None:
            at = (level, slice(None), rows) if name == "gu" else (level, rows)
        copy = pltpu.make_async_copy(
            held[name].at[at], outs[name].at[at], keep_sems.at[KEPT.index(name), level, part]
        )
        copy.start()
        keeps.append(copy)

    length = x_ref.shape[0]
    heads = wo.shape[1] // DK
    high = length // n_parts
    parts = [(part, slice(part * high, (part + 1) * high)) for part in range(n_parts)]
    row, col = positions(high)
    for level in range(LAYERS):
        head_gain = head_gain_ref[level : level + 1, :].astype(F32)
        before = []
        for part, rows in parts:
            if level == 0:
                x = x_ref[rows].astype(F32)
            else:
                x = held["h"][level - 1, rows] + exchange.take(2 * level - 1, part, rows)
            held["x"][level, rows] = x
            n1 = low(x * rms_scale(x) * gain_ref[level, 0:1, :].astype(F32))
            held["n1"][level, rows] = n1
            logits = dot_nt(n1, wb[level])
            held["logits"][level, rows] = logits
            beta = sigmoid(logits)
            if part == 0:
                loads[level][0].wait()
            acts = []
            for index in range(3):
                held["p"][level, index, rows] = dot_nn(n1, wq[level, index])
                acts.append(
                    conv_silu_rows(
                        held["p"].at[level, index], taps_ref[level, index].astype(F32), rows
                    )
                )
            lowers, scores, values, now = [], [], [], []
            for head in range(heads):
                cols = head_cols(head)
                c0, c1, c2 = (act[:, cols] for act in acts)
                q = low(c0 * lax.rsqrt(jnp.sum(c0 * c0, axis=-1, keepdims=True) + 0.001))
                k = low(c1 * lax.rsqrt(jnp.sum(c1 * c1, axis=-1, keepdims=True) + 0.001))
                v = low(c2).astype(F32)
                gate = beta[:, head : head + 1]
                value = gate * v
                for key, u in before[head : head + 1]:
                    cross = halves(gate * dot_nt(k, key))
                    value = value - dot_nn(cross[0], u[0])
                    value = value - (dot_nn(cross[0], u[1]) + dot_nn(cross[1], u[0]))
                lowers.append(jnp.where(row > col, gate * dot_nt(k, k), 0.0))
                scores.append(low(jnp.where(row >= col, dot_nt(q, k), 0.0)))
                values.append(halves(value))
                now.append((q, k))
            inverse = unit_lower_inverse(lowers)
            after = []
            for head in range(heads):
                cols = head_cols(head)
                t_hi, t_lo = halves(inverse[head])
                held["t"][level, 0, head, part] = t_hi
                held["t"][level, 1, head, part] = t_lo
                u = halves(split_dot(dot_nn, (t_hi, t_lo), values[head]))
                held["u"][level, rows, cols] = u[0]
                o = dot_nn(scores[head], u[0])
                q, k = now[head]
                for key, early in before[head : head + 1]:
                    o = o + dot_nn(low(dot_nt(q, key)), early[0])
                after.append((k, u))
                held["o"][level, rows, cols] = o
                scale = lax.rsqrt(jnp.mean(o * o, axis=-1, keepdims=True) + 0.01)
                held["on"][level, rows, cols] = low(o * scale * head_gain)
            before = after
            if part == 0:
                loads[level][1].wait()
            out = dot_nn(held["on"][level, rows], wo[level])
            exchange.give(2 * level, part, rows, low(out))
        for name in ("x", "n1", "logits", "p", "t", "u", "o", "on"):
            keep(name, level)
        for part, rows in parts:
            h = held["x"][level, rows] + exchange.take(2 * level, part, rows)
            held["h"][level, rows] = h
            n2 = low(h * rms_scale(h) * gain_ref[level, 1:2, :].astype(F32))
            held["n2"][level, rows] = n2
            if part == 0:
                loads[level][2].wait()
            g = dot_nn(n2, wgu[level, 0])
            held["gu"][level, 0, rows] = g
            u = dot_nn(n2, wgu[level, 1])
            held["gu"][level, 1, rows] = u
            z = low(g * sigmoid(g) * u)
            held["z"][level, rows] = z
            if part == 0:
                loads[level][3].wait()
            out = low(dot_nn(z, wd[level]))
            if level < LAYERS - 1:
                exchange.give(2 * level + 1, part, rows, out)
            else:
                last[rows] = out
            for name in ("z", "h", "n2", "gu"):
                keep(name, level, part, rows)
    final = pltpu.make_async_copy(last, last_out, load_sems.at[0, 0])
    final.start()
    for copy in keeps:
        copy.wait()
    final.wait()
    exchange.finish()


def forward(x, norm_gain, taps, head_gain, wb, wq, wo, wgu, wd):
    length, width = x.shape
    chans, hidden = wq.shape[-1], wgu.shape[-1]
    n_tensor = lax.axis_size("tensor")
    n_parts = 2
    kept = kept_shapes(length, width, chans, hidden)
    vmem = pl.BlockSpec(memory_space=pltpu.VMEM)
    hbm = pl.BlockSpec(memory_space=pl.ANY)
    spots = 2 * LAYERS - 1
    *kept, part = pl.pallas_call(
        functools.partial(forward_kernel, n_parts),
        out_shape=(
            *(jax.ShapeDtypeStruct(*spec) for spec in kept),
            jax.ShapeDtypeStruct((length, width), BF16),
        ),
        in_specs=[vmem] * 5 + [hbm] * 4,
        out_specs=(hbm,) * (len(kept) + 1),
        scratch_shapes=[
            *(pltpu.VMEM(*spec) for spec in kept),
            pltpu.VMEM((LAYERS, 3, width, chans), BF16),
            pltpu.VMEM((LAYERS, chans, width), BF16),
            pltpu.VMEM((LAYERS, 2, width, hidden), BF16),
            pltpu.VMEM((LAYERS, hidden, width), BF16),
            pltpu.VMEM((LAYERS, LANES, width), BF16),
            pltpu.VMEM((spots, n_tensor, length, width), BF16),
            pltpu.VMEM((length, width), BF16),
            pltpu.SemaphoreType.DMA((LAYERS, 4)),
            pltpu.SemaphoreType.DMA((len(kept), LAYERS, n_parts)),
            pltpu.SemaphoreType.DMA((spots, n_parts, n_tensor - 1)),
            pltpu.SemaphoreType.DMA((spots, n_parts, n_tensor - 1)),
        ],
        compiler_params=pltpu.CompilerParams(
            vmem_limit_bytes=VMEM_LIMIT, collective_id=1, has_side_effects=True
        ),
        name="forward",
    )(x, norm_gain, taps, head_gain, wb, wq, wo, wgu, wd)
    return dict(zip(KEPT, kept)), part


def back_through_norm(level, which, gain_ref, e_ref, hid_ref, adds, rows_out):
    e = e_ref[...].astype(F32)
    if not adds:
        rows_out[...] = jnp.zeros_like(rows_out)
        return e
    total = adds[0][...].astype(F32)
    for add in adds[1:]:
        total = total + add[...].astype(F32)
    gain = gain_ref[level, which : which + 1, :].astype(F32)
    grad_hidden, rows = rms_back(hid_ref[...], gain, total)
    rows_out[...] = rows
    return e + grad_hidden


def mlp_backward_kernel(level, n_add, *refs):
    (e_ref, hid_ref, *adds) = refs[: 2 + n_add]
    (gain_ref, n2_ref, gu_ref, z_ref, wgu_hbm, wd_hbm) = refs[2 + n_add : 8 + n_add]
    (e_out, rows_out, part_out, gd_out, ggu_out) = refs[8 + n_add : 13 + n_add]
    wgu, wd, dgu_ref, sems = refs[13 + n_add :]
    loads = [
        pltpu.make_async_copy(wd_hbm.at[level], wd, sems.at[0]),
        pltpu.make_async_copy(wgu_hbm.at[level], wgu, sems.at[1]),
    ]
    for load in loads:
        load.start()
    e = back_through_norm(level + 1, 0, gain_ref, e_ref, hid_ref, adds, rows_out)
    e_out[...] = e
    ef = low(e)
    loads[0].wait()
    dz = dot_nt(ef, wd[...])
    g, u = gu_ref[0], gu_ref[1]
    s = sigmoid(g)
    dgu_ref[0] = low(dz * u * (s * (1.0 + g * (1.0 - s))))
    dgu_ref[1] = low(dz * (g * s))
    loads[1].wait()
    part_out[...] = low(dot_nt(dgu_ref[0], wgu[0]) + dot_nt(dgu_ref[1], wgu[1]))
    gd_out[...] = low(dot_tn(z_ref[...], ef))
    for half in range(2):
        ggu_out[half] = low(dot_tn(n2_ref[...], dgu_ref[half]))


def mlp_backward(level, e, hid, adds, norm_gain, n2, gu, z, wgu, wd):
    length, width = e.shape
    hidden = wgu.shape[-1]
    sds = jax.ShapeDtypeStruct
    vmem = pl.BlockSpec(memory_space=pltpu.VMEM)
    hbm = pl.BlockSpec(memory_space=pl.ANY)
    return pl.pallas_call(
        functools.partial(mlp_backward_kernel, level, len(adds)),
        out_shape=(
            sds((length, width), F32),
            sds((1, width), F32),
            sds((length, width), BF16),
            sds((hidden, width), BF16),
            sds((2, width, hidden), BF16),
        ),
        in_specs=[vmem] * (6 + len(adds)) + [hbm, hbm],
        out_specs=(vmem,) * 5,
        scratch_shapes=[
            pltpu.VMEM((2, width, hidden), BF16),
            pltpu.VMEM((hidden, width), BF16),
            pltpu.VMEM((2, length, hidden), BF16),
            pltpu.SemaphoreType.DMA((2,)),
        ],
        compiler_params=pltpu.CompilerParams(vmem_limit_bytes=VMEM_LIMIT),
        name="mlp_backward",
    )(e, hid, *adds, norm_gain, n2, gu, z, wgu, wd)


def mixer_backward_kernel(level, heads, n_add, *refs):
    (e_ref, hid_ref, *adds) = refs[: 2 + n_add]
    (gain_ref, taps_ref, head_gain_ref, wb_ref, n1_ref, p_ref, logit_ref, t_ref, u_ref, o_ref) = (
        refs[2 + n_add : 12 + n_add]
    )
    (on_ref, wq_hbm, wo_hbm) = refs[12 + n_add : 15 + n_add]
    (e_out, part_out, small_out, gq_out, go_out) = refs[15 + n_add : 20 + n_add]
    wq, wo, grads, dp_ref, rows_out, wb, sems = refs[20 + n_add :]
    loads = [
        pltpu.make_async_copy(wo_hbm.at[level], wo, sems.at[0]),
        pltpu.make_async_copy(wq_hbm.at[level], wq, sems.at[1]),
    ]
    for load in loads:
        load.start()
    e = back_through_norm(level, 1, gain_ref, e_ref, hid_ref, adds, rows_out)
    e_out[...] = e
    em = low(e)
    length = e.shape[0]
    loads[0].wait()
    don = dot_nt(em, wo[...])
    go_out[...] = low(dot_tn(on_ref[...], em))
    beta = sigmoid(logit_ref[...])
    row, col = positions(length)
    lane = lax.broadcasted_iota(jnp.int32, (length, LANES), 1)
    head_gain = head_gain_ref[level : level + 1, :].astype(F32)
    convs = [conv_silu(p_ref[part], taps_ref[level, part].astype(F32)) for part in range(3)]
    gain_rows = jnp.zeros((1, DK), F32)
    dlogit = jnp.zeros((length, LANES), F32)
    for head in range(heads):
        cols = head_cols(head)
        c0, c1, c2 = (conv[2][:, cols] for conv in convs)
        rho0 = lax.rsqrt(jnp.sum(c0 * c0, axis=-1, keepdims=True) + 0.001)
        rho1 = lax.rsqrt(jnp.sum(c1 * c1, axis=-1, keepdims=True) + 0.001)
        q, k, v = low(c0 * rho0), low(c1 * rho1), low(c2).astype(F32)
        gate = beta[:, head : head + 1]
        o = o_ref[:, cols]
        scale = lax.rsqrt(jnp.mean(o * o, axis=-1, keepdims=True) + 0.01)
        dn = don[:, cols]
        weighted = dn * head_gain
        inner = jnp.mean(o * weighted, axis=-1, keepdims=True)
        do = low(scale * weighted - o * (scale * scale * scale) * inner)
        gain_rows = gain_rows + jnp.sum(dn * o * scale, axis=0, keepdims=True)
        u = u_ref[:, cols]
        score_t = low(jnp.where(row <= col, dot_nt(k, q), 0.0))
        du = dot_nn(score_t, do)
        ds = low(jnp.where(row >= col, dot_nt(do, u), 0.0))
        ds_t = low(jnp.where(row <= col, dot_nt(u, do), 0.0))
        dq = dot_nn(ds, k)
        dk = dot_nn(ds_t, q)
        blocks = [(t_ref[0, head, index], t_ref[1, head, index]) for index in range(2)]
        r = solve_back(blocks, k, gate, du)
        dv = gate * r
        dv_low = low(dv)
        gram = low(jnp.where(row > col, dot_nt(k, k), 0.0))
        w = v - dot_nn(gram, u)
        dbeta = jnp.sum(r * w, axis=-1, keepdims=True)
        dgram = jnp.where(row > col, dot_nt(dv_low, u), 0.0) + jnp.where(
            row < col, dot_nt(u, dv_low), 0.0
        )
        dk = dk - dot_nn(low(dgram), k)
        grads[0, :, cols] = rho0 * dq - c0 * (rho0 * rho0 * rho0) * jnp.sum(
            c0 * dq, axis=-1, keepdims=True
        )
        grads[1, :, cols] = rho1 * dk - c1 * (rho1 * rho1 * rho1) * jnp.sum(
            c1 * dk, axis=-1, keepdims=True
        )
        grads[2, :, cols] = dv
        dlogit = dlogit + jnp.where(lane == head, dbeta * gate * (1.0 - gate), 0.0)
    chans = grads.shape[-1]
    small_out[...] = jnp.zeros_like(small_out)
    small_out[0:1, SIDE : SIDE + DK] = gain_rows
    half = rows_out.shape[-1] // 2
    small_out[1:2, SIDE:] = rows_out[:, :half]
    small_out[2:3, SIDE:] = rows_out[:, half:]
    dlogit_low = low(dlogit)
    n1 = n1_ref[...]
    small_out[3 * KCONV : 3 * KCONV + heads, :] = dot_tn(dlogit_low, n1)[:heads, :]
    for part in range(3):
        taps = taps_ref[level, part].astype(F32)
        total, gate, _ = convs[part]
        dsum = grads[part] * (gate * (1.0 + total * (1.0 - gate)))
        p = p_ref[part]
        dp = taps[KCONV - 1 : KCONV, :] * dsum
        for tap in range(KCONV):
            back = KCONV - 1 - tap
            spot = part * KCONV + tap
            small_out[spot : spot + 1, :chans] = jnp.sum(
                dsum * shift_down(p, back), axis=0, keepdims=True
            )
            if back:
                dp = dp + taps[tap : tap + 1, :] * shift_up(dsum, back)
        dp_ref[part] = low(dp)
    loads[1].wait()
    wb[...] = jnp.zeros_like(wb)
    wb[:heads] = wb_ref[level]
    dn1 = dot_nn(dlogit_low, wb[...])
    for part in range(3):
        dn1 = dn1 + dot_nt(dp_ref[part], wq[part])
    part_out[...] = low(dn1)
    for part in range(3):
        gq_out[part] = low(dot_tn(n1, dp_ref[part]))


def mixer_backward(level, e, hid, adds, norm_gain, taps, head_gain, wb, kept, wq, wo):
    length, width = e.shape
    chans = wq.shape[-1]
    heads = chans // DK
    sds = jax.ShapeDtypeStruct
    vmem = pl.BlockSpec(memory_space=pltpu.VMEM)
    hbm = pl.BlockSpec(memory_space=pl.ANY)
    return pl.pallas_call(
        functools.partial(mixer_backward_kernel, level, heads, len(adds)),
        out_shape=(
            sds((length, width), F32),
            sds((length, width), BF16),
            sds((16, width), F32),
            sds((3, width, chans), BF16),
            sds((chans, width), BF16),
        ),
        in_specs=[vmem] * (13 + len(adds)) + [hbm, hbm],
        out_specs=(vmem,) * 5,
        scratch_shapes=[
            pltpu.VMEM((3, width, chans), BF16),
            pltpu.VMEM((chans, width), BF16),
            pltpu.VMEM((3, length, chans), F32),
            pltpu.VMEM((3, length, chans), BF16),
            pltpu.VMEM((1, width), F32),
            pltpu.VMEM((LANES, width), BF16),
            pltpu.SemaphoreType.DMA((2,)),
        ],
        compiler_params=pltpu.CompilerParams(vmem_limit_bytes=VMEM_LIMIT),
        name="mixer_backward",
    )(e, hid, *adds, norm_gain, taps, head_gain, wb, *kept, wq, wo)


def branch_parts(part):
    count = lax.axis_size("tensor")
    if count == 1:
        return (part,)
    if count == 2:
        return (part, lax.ppermute(part, "tensor", [(0, 1), (1, 0)]))
    return (lax.psum(part, "tensor"),)


def sum_over_dp(tables):
    shapes = [table.shape for table in tables]
    flat = jnp.concatenate([table.reshape(-1) for table in tables])
    size = flat.shape[0]
    count = lax.axis_size("dp")
    pad = -size % (count * 1024)
    flat = jnp.pad(flat, (0, pad))
    shard = lax.psum_scatter(flat, "dp", scatter_dimension=0, tiled=True)
    joined = lax.all_gather(shard, "dp", axis=0, tiled=True)
    pieces = []
    offset = 0
    for shape in shapes:
        size = math.prod(shape)
        pieces.append(joined[offset : offset + size].reshape(shape))
        offset = offset + size
    return pieces


def fold_spot(depth, side, core):
    return (depth * 2 + side) * 2 + core


def remote(source, target, send, recv, device):
    return pltpu.make_async_remote_copy(
        src_ref=source,
        dst_ref=target,
        send_sem=send,
        recv_sem=recv,
        device_id=device,
        device_id_type=pl.DeviceIdType.MESH,
    )


DEPTH = 4
CHUNKS = 8
STEPS = CHUNKS // 2
SLOTS = ("p1", "p2", "p3", "e1", "e2", "e3", "e4")
KINDS = (*SLOTS, "p4e", "p4y", "pf0", "pf1", "pk", "e5", "e6", "e7", "ef0", "ef1", "ek")
ALIKE = dict(
    m1="e1", m2="e2", m3="e3", m4="e4", m5="e5", m6="e6", m7="e7", mf0="ef0", mf1="ef1", mk="ek"
)
AWAY = ("p1", "pf1", "e1", "e2", "e7", "ef1", "m3", "m7", "mf1")
PASSED = ("pf1", "ef1", "e6", "e7", "m7", "mf1")


class Fold:
    def __init__(self, cuts, own, slots, totals, sems):
        self.cuts, self.own, self.slots, self.totals = cuts, own, slots, totals
        self.send_sems, self.recv_sems = sems
        spot = lax.axis_index("dp")
        self.core = lax.rem(spot, 2)
        side = lax.rem(lax.div(spot, 2), 2)
        depth = lax.div(spot, 4)
        self.is_mid = (depth == 1) | (depth == 2)
        self.is_end = (depth == 0) | (depth == 3)
        folded = depth + 1 - 2 * lax.rem(depth, 2)
        across = DEPTH - 1 - depth
        half = lax.div(depth, 2)
        self.partner = {"dp": fold_spot(depth, side, 1 - self.core)}
        self.beside = {"dp": fold_spot(depth, 1 - side, self.core)}
        self.folded = {"dp": fold_spot(folded, side, self.core)}
        self.across = {"dp": fold_spot(across, side, self.core)}
        self.mine = [[base * STEPS + step for step in range(STEPS)] for base in (side, half)]
        self.others = [
            [(1 - base) * STEPS + step for step in range(STEPS)] for base in (side, half)
        ]
        self.done = [0] * len(cuts)
        self.active, self.waiting = [], []
        self.served = 0

    def rows(self, index, chunk, way):
        _, first, second, _ = self.cuts[index]
        high = second if way else first
        start = chunk * (first + second) + (first if way else 0)
        return pl.ds(pl.multiple_of(start, 16), high)

    def piece(self, index, chunk, way):
        kind, first, second, cols = self.cuts[index]
        if kind == "small":
            lanes = pl.ds(pl.multiple_of(chunk * cols, cols), cols)
            return self.own[index].at[way * first : (way + 1) * first, lanes]
        return self.own[index].at[self.rows(index, chunk, way), :]

    def spot(self, index, chunk, way):
        kind, first, second, cols = self.cuts[index]
        ref = self.totals[index]
        if kind == "small":
            start = pl.multiple_of(self.core * (2 * first) + way * first, first)
            return ref.at[pl.ds(start, first), pl.ds(pl.multiple_of(chunk * cols, cols), cols)]
        rows = self.rows(index, chunk, way)
        if kind == "rows":
            return ref.at[self.core, rows, :]
        return ref.at[rows, pl.ds(pl.multiple_of(self.core * cols, cols), cols)]

    def family(self, index):
        return index % 4 if index < SMALL else 4

    def slot(self, name, index, step):
        place = SLOTS.index(ALIKE.get(name, name))
        ref = self.slots[2 * self.family(index) + (place >= 3)]
        return ref.at[place - 3 if place >= 3 else place, step]

    def copy(self, name, index, step, kept=True):
        way = 0 if name[0] == "p" else 1
        chunk = (self.others if name in AWAY else self.mine)[way][step]
        if name in ("m1", "m2"):
            chunk = step + (STEPS if name == "m2" else 0)
        device = self.folded
        if name in ("p1", "p4y", "e4", "m4"):
            device = self.beside
        elif name in ("p3", "e2", "e6", "m3", "m5"):
            device = self.across
        elif name[1] == "f":
            device = self.partner
        source = self.piece(index, chunk, way)
        kind = ALIKE.get(name, name)
        if kind in SLOTS:
            target = self.slot(name, index, step)
        else:
            target = self.spot(index, chunk, way)
            if name in PASSED or not kept:
                source = target
        at = (KINDS.index(kind), index, step)
        if name[1] == "k":
            return pltpu.make_async_copy(source, target, self.recv_sems.at[at])
        return remote(source, target, self.send_sems.at[at], self.recv_sems.at[at], device)

    def start(self, names, index, step, kept=True):
        for name in names:
            self.copy(name, index, step, kept).start()

    def add(self, name, index, step, chunk):
        self.copy(name, index, step).wait_recv()
        mine = self.piece(index, chunk, 0 if name[0] == "p" else 1)
        both = mine[...].astype(F32) + self.slot(name, index, step)[...].astype(F32)
        mine[...] = both.astype(mine.dtype)

    def stage_one(self, index, step):
        self.start(("p1",), index, step)

        @pl.when(self.is_end)
        def _():
            self.start(("m1", "m2") if self.mid_rooted(index) else ("e1",), index, step)

    def stage_two(self, index, step):
        self.add("p1", index, step, self.mine[0][step])

        @pl.when(self.is_end)
        def _():
            self.start(("p2",), index, step)

        @pl.when(self.is_mid)
        def _():
            if self.mid_rooted(index):
                self.add("m1", index, step, step)
                self.add("m2", index, step, STEPS + step)
                self.start(("m3",), index, step)
            else:
                self.add("e1", index, step, self.others[1][step])
                self.start(("e2",), index, step)

    def stage_three(self, index, step):
        @pl.when(self.is_mid)
        def _():
            self.add("p2", index, step, self.mine[0][step])
            self.start(("p3",), index, step)
            if self.mid_rooted(index):
                self.add("m3", index, step, self.mine[1][step])
                self.start(("m4",), index, step)
            else:
                self.add("e2", index, step, self.mine[1][step])
                self.start(("e3",), index, step)

    def stage_four(self, index, step):
        @pl.when(self.is_mid)
        def _():
            if self.mid_rooted(index):
                self.copy("m4", index, step).wait_send()
                self.add("m4", index, step, self.mine[1][step])
                self.start(("m5", "m6", "mf0", "mk"), index, step)
            self.copy("p3", index, step).wait_send()
            self.add("p3", index, step, self.mine[0][step])
            self.start(("p4e", "p4y", "pf0", "pk"), index, step)

        if not self.mid_rooted(index):

            @pl.when(self.is_end)
            def _():
                self.add("e3", index, step, self.mine[1][step])
                self.start(("e4",), index, step)

    def stage_five(self, index, step):
        @pl.when(self.is_end)
        def _():
            if not self.mid_rooted(index):
                self.copy("e4", index, step).wait_send()
                self.add("e4", index, step, self.mine[1][step])
                self.start(("e5", "ef0", "ek"), index, step)
            self.copy("p4e", index, step).wait_recv()
            self.start(("p4y", "pf0"), index, step, False)

        if self.mid_rooted(index):

            @pl.when(self.is_mid)
            def _():
                self.copy("m5", index, step).wait_recv()
                self.start(("m7", "mf1"), index, step)

    def stage_six(self, index, step):
        self.copy("p4y", index, step).wait_recv()
        self.start(("pf1",), index, step)
        if self.mid_rooted(index):

            @pl.when(self.is_end)
            def _():
                self.copy("m6", index, step).wait_recv()
                self.copy("m7", index, step).wait_recv()
                self.start(("mf0", "mf1"), index, step, False)

        else:

            @pl.when(self.is_mid)
            def _():
                self.copy("e5", index, step).wait_recv()
                self.start(("e6", "ef0"), index, step, False)

    def stage_seven(self, index, step):
        @pl.when(self.is_mid)
        def _():
            self.copy("e6", index, step).wait_recv()
            self.start(("e7", "ef1"), index, step)

    def stage_eight(self, index, step):
        @pl.when(self.is_end)
        def _():
            self.copy("e7", index, step).wait_recv()
            self.start(("ef1",), index, step)

    def settle(self, index, step):
        mid_rooted = self.mid_rooted(index)
        for name in ("p1", "p4y"):
            self.copy(name, index, step).wait_send()
        for name in ("pf0", "pf1", "mf0", "mf1") if mid_rooted else ("pf0", "pf1", "ef0", "ef1"):
            self.copy(name, index, step).wait()

        @pl.when(self.is_end)
        def _():
            for name in ("m1", "m2", "p2") if mid_rooted else ("e1", "p2", "e5"):
                self.copy(name, index, step).wait_send()
            if not mid_rooted:
                self.copy("ek", index, step).wait()

        @pl.when(self.is_mid)
        def _():
            for name in ("m3", "p4e", "m5", "m6", "m7") if mid_rooted else (
                "e2",
                "e3",
                "p4e",
                "e6",
                "e7",
            ):
                self.copy(name, index, step).wait_send()
            for name in ("pk", "mk") if mid_rooted else ("pk",):
                self.copy(name, index, step).wait()

    def mid_rooted(self, index):
        return index in MID_ROOTED

    def advance(self, index):
        stages = [
            self.stage_one,
            self.stage_two,
            self.stage_three,
            self.stage_four,
            self.stage_five,
            self.stage_six,
        ]
        if not self.mid_rooted(index):
            stages += [self.stage_seven, self.stage_eight]
        tick = self.done[index]
        self.done[index] = tick + 1
        last = STEPS + len(stages) - 1
        if tick == last:
            for step in range(STEPS):
                self.settle(index, step)
            return False
        for offset, stage in reversed(list(enumerate(stages))):
            steps = [tick - offset]
            if offset == 0:
                ahead = AHEAD.get(index, 0)
                steps = range(ahead + 1) if tick == 0 else [tick + ahead]
            for step in steps:
                if 0 <= step < STEPS:
                    stage(index, step)
        return True

    def begin(self, index):
        if any(self.family(index) == self.family(held) for held in self.active):
            self.waiting.append(index)
        else:
            self.active.append(index)

    def serve(self, count=1):
        for _ in range(count):
            if not self.active:
                return
            index = self.active[0]
            if self.served < len(ORDER) and ORDER[self.served] in self.active:
                index = ORDER[self.served]
            self.served += 1
            self.active.remove(index)
            if self.advance(index):
                self.active.append(index)
                continue
            for other in self.waiting:
                if self.family(other) == self.family(index):
                    self.waiting.remove(other)
                    self.active.append(other)
                    break


def fold_cuts(n_dp, width, chans, hidden):
    if n_dp != 4 * DEPTH or width != CHUNKS * LANES or chans % (2 * LANES) or hidden % LANES:
        return None
    if any(rows % (16 * CHUNKS) for rows in (hidden, chans, width)):
        return None
    layer = []
    for kind, rows, cols in (
        ("cols", hidden, width // 2),
        ("rows", width, hidden),
        ("cols", chans, width // 2),
        ("cols", 3 * width, chans // 2),
    ):
        chunk = rows // CHUNKS
        first = 16 * round(0.6 * chunk / 16)
        if not 0 < first < chunk:
            return None
        layer.append((kind, first, chunk - first, cols))
    return layer * LAYERS + [("small", 8, 8, LANES)]


DOWN, GATE_UP, OUT, QKV = range(4)
SMALL = 4 * LAYERS
MID_ROOTED = (DOWN, QKV, 4 + OUT)
AHEAD = {
    DOWN: 1,
    OUT: 2,
    4 + DOWN: 2,
    4 + GATE_UP: 1,
    4 + OUT: 1,
    4 + QKV: 1,
}
ORDER = (
    4, 4, 4, 5, 4, 5, 4, 5, 4, 5, 4, 5, 6, 4, 7, 5, 4, 7, 6, 4, 5, 6, 7, 4, 4, 5, 6, 7, 0, 5,
    6, 7, 6, 0, 7, 5, 6, 0, 7, 5, 6, 8, 5, 0, 1, 7, 6, 8, 0, 1, 7, 6, 2, 8, 0, 1, 7, 2, 8, 0,
    7, 1, 8, 0, 7, 2, 1, 8, 0, 3, 1, 2, 8, 0, 3, 1, 2, 8, 3, 1, 2, 8, 3, 8, 1, 2, 8, 3, 1, 3,
    2, 1, 3, 8, 2, 1, 3, 2, 2, 3, 2, 3,
)
MLP_KEPT = ("gu", "z", "n2")
MIXER_KEPT = ("n1", "p", "logits", "t", "u", "o", "on", "h")
PEERS = ("z", "n2", "ef", "dgu", "n1", "on", "em", "dp")


def backward_kernel(n_parts, cuts, *refs):
    refs = list(refs)

    def taken(count):
        group = refs[:count]
        del refs[:count]
        return group

    (cot_ref, gain_ref, taps_ref, head_gain_ref, wb_ref) = taken(5)
    (part_hbm, wq_hbm, wo_hbm, wgu_hbm, wd_hbm) = taken(5)
    kept = dict(zip(KEPT, taken(len(KEPT))))
    (out_ref, in_grad_ref, *totals) = taken(2 + 5)
    own = taken(len(cuts))
    fold_slots = taken(10)
    peers = dict(zip(PEERS, taken(len(PEERS))))
    (e_ref, small, small_peer, slots, don_ref, wb, gains) = taken(7)
    (load_sems, send_sems, recv_sems, peer_sems, gain_sems) = taken(5)
    fold_sems = taken(2)

    per_table = [totals[index].at[level] for level in range(LAYERS) for index in range(4)]
    fold = Fold(cuts, own, fold_slots, [*per_table, totals[4]], fold_sems)
    core, serve = fold.core, fold.serve
    exchange = Exchange(slots, send_sems, recv_sems)
    barrier = pltpu.get_barrier_semaphore()
    for device in (fold.partner, fold.beside, fold.folded, fold.across):
        pl.semaphore_signal(barrier, inc=1, device_id=device, device_id_type=pl.DeviceIdType.MESH)
    exchange.greet(4)

    length, width = e_ref.shape
    chans = wo_hbm.shape[1]
    hidden = wd_hbm.shape[1]
    heads = chans // DK
    high = length // n_parts
    parts = [(part, slice(part * high, (part + 1) * high)) for part in range(n_parts)]
    row, col = positions(length)
    lane = lax.broadcasted_iota(jnp.int32, (length, LANES), 1)
    side = width - SIDE
    half_width, half_chans = width // 2, chans // 2

    def other_half(wide):
        return pl.ds(pl.multiple_of((1 - core) * wide, LANES), wide)

    def own_half(wide):
        return pl.ds(pl.multiple_of(core * wide, LANES), wide)

    def to_peer(name, level, source):
        spot = PEERS.index(name)
        return remote(
            source,
            peers[name].at[level],
            peer_sems.at[0, spot, level],
            peer_sems.at[1, spot, level],
            fold.partner,
        )

    top = LAYERS - 1
    early = [
        to_peer(name, level, kept[name].at[level])
        for level in reversed(range(LAYERS))
        for name in ("z", "n2", "on", "n1")
    ]
    early.insert(1, to_peer("ef", top, cot_ref.at[:, other_half(width // 2)]))
    for copy in early:
        copy.start()
    first = pltpu.make_async_copy(part_hbm, slots.at[0, exchange.me], load_sems.at[0, 0, 0])
    first.start()
    small[...] = jnp.zeros_like(small)

    def norm_step(level, which, spot, part, rows, hid):
        total = exchange.take(spot, part, rows)
        gain = gain_ref[level, which : which + 1, :].astype(F32)
        grad_hidden, sums = rms_back(hid, gain, total)
        base = 16 * level + (1 if which else 3)
        for index in range(2):
            spot_row = slice(base + index, base + index + 1)
            small[spot_row, SIDE:] += sums[:, index * side : (index + 1) * side]
        return e_ref[rows] + grad_hidden

    def mlp_stage(level):
        def scope(wgu, wd, gu, z, n2, hid, dgu, ef):
            held = dict(gu=gu, z=z, n2=n2)
            loads = {
                "wd": pltpu.make_async_copy(wd_hbm.at[level], wd, load_sems.at[level, 0, 1]),
                "wgu": pltpu.make_async_copy(wgu_hbm.at[level], wgu, load_sems.at[level, 0, 2]),
            }
            for index, name in enumerate(MLP_KEPT):
                loads[name] = pltpu.make_async_copy(
                    kept[name].at[level], held[name], load_sems.at[level, 0, 3 + index]
                )
            if level < LAYERS - 1:
                loads["hid"] = pltpu.make_async_copy(
                    kept["x"].at[level + 1], hid, load_sems.at[level, 0, 6]
                )
                loads["hid"].start()
            for name in ("z", "wd", "gu", "wgu", "n2"):
                loads[name].start()
            index = 4 * level
            if level == top:
                first.wait()
                for part, rows in parts:
                    exchange.send(0, part, rows)
                loads["z"].wait()
                for name in ("z", "ef"):
                    to_peer(name, level, peers[name].at[level]).wait_recv()
                own[index + DOWN][...] = low(
                    dot_tn(z[...], cot_ref[:, own_half(half_width)])
                    + dot_tn(peers["z"][level], peers["ef"][level])
                )
                fold.begin(index + DOWN)
                serve()
            whole = [(0, slice(0, length))]
            for part, rows in whole if level == top else parts:
                if level == LAYERS - 1:
                    e = cot_ref[rows].astype(F32)
                else:
                    if part == 0:
                        loads["hid"].wait()
                    e = norm_step(level + 1, 0, 2 * (LAYERS - 1 - level), part, rows, hid[rows])
                e_ref[rows] = e
                e_low = low(e)
                ef[rows] = e_low
                if part == 0:
                    loads["wd"].wait()
                dz = dot_nt(e_low, wd[...])
                if part == 0:
                    loads["gu"].wait()
                g, u = gu[0, rows], gu[1, rows]
                s = sigmoid(g)
                dgu[0, rows] = low(dz * u * (s * (1.0 + g * (1.0 - s))))
                dgu[1, rows] = low(dz * (g * s))
                serve()
            sends = [to_peer("dgu", level, dgu.at[1 - core])]
            if level != top:
                sends.append(to_peer("ef", level, ef.at[:, other_half(half_width)]))
            for send in sends:
                send.start()
            loads["wgu"].wait()
            for part, rows in parts:
                partial = dot_nt(dgu[0, rows], wgu[0]) + dot_nt(dgu[1, rows], wgu[1])
                exchange.give(2 * (LAYERS - 1 - level) + 1, part, rows, low(partial))
            serve()
            loads["n2"].wait()
            for name in ("n2", "dgu"):
                to_peer(name, level, peers[name].at[level]).wait_recv()
            own[index + GATE_UP][...] = low(
                dot_tn(n2[...], dgu[core]) + dot_tn(peers["n2"][level], peers["dgu"][level])
            )
            fold.begin(index + GATE_UP)
            serve()
            if level != top:
                loads["z"].wait()
                for name in ("z", "ef"):
                    to_peer(name, level, peers[name].at[level]).wait_recv()
                own[index + DOWN][...] = low(
                    dot_tn(z[...], ef[:, own_half(half_width)])
                    + dot_tn(peers["z"][level], peers["ef"][level])
                )
                fold.begin(index + DOWN)
                serve(4)
            for send in sends:
                send.wait_send()

        pl.run_scoped(
            scope,
            pltpu.VMEM((2, width, hidden), BF16),
            pltpu.VMEM((hidden, width), BF16),
            pltpu.VMEM((2, length, hidden), F32),
            pltpu.VMEM((length, hidden), BF16),
            pltpu.VMEM((length, width), BF16),
            pltpu.VMEM((length, width), F32),
            pltpu.VMEM((2, length, hidden), BF16),
            pltpu.VMEM((length, width), BF16),
        )

    def mixer_stage(level):
        def scope(wq, wo, n1, p, logits, t, u_all, o_all, on, h, grads, dp, em):
            held = dict(n1=n1, p=p, logits=logits, t=t, u=u_all, o=o_all, on=on, h=h)
            loads = {
                "wo": pltpu.make_async_copy(wo_hbm.at[level], wo, load_sems.at[level, 1, 0]),
                "wq": pltpu.make_async_copy(wq_hbm.at[level], wq, load_sems.at[level, 1, 1]),
            }
            for index, name in enumerate(MIXER_KEPT):
                loads[name] = pltpu.make_async_copy(
                    kept[name].at[level], held[name], load_sems.at[level, 1, 2 + index]
                )
            for name in ("h", "wo", "p", "o", "u", "logits", "t", "wq", "n1", "on"):
                loads[name].start()
            loads["p"].wait()
            convs = [
                conv_silu(p[index], taps_ref[level, index].astype(F32)) for index in range(3)
            ]
            spot = 2 * (LAYERS - 1 - level) + 1
            loads["h"].wait()
            if level == LAYERS - 1:
                for part, rows in parts:
                    out_ref[rows] = low(h[rows] + exchange.take(0, part, rows))
            for part, rows in parts:
                serve()
                e = norm_step(level, 1, spot, part, rows, h[rows])
                e_ref[rows] = e
                e_low = low(e)
                em[rows] = e_low
                if part == 0:
                    loads["wo"].wait()
                don_ref[rows] = dot_nt(e_low, wo[...])
            send_em = to_peer("em", level, em.at[:, other_half(half_width)])
            send_em.start()
            for name in ("o", "u", "logits", "t"):
                loads[name].wait()
            beta = sigmoid(logits[...])
            head_gain = head_gain_ref[level : level + 1, :].astype(F32)
            gain_rows = jnp.zeros((1, DK), F32)
            dlogit = jnp.zeros((length, LANES), F32)
            serve(2)
            for head in range(heads):
                cols = head_cols(head)
                c0, c1, c2 = (conv[2][:, cols] for conv in convs)
                rho0 = lax.rsqrt(jnp.sum(c0 * c0, axis=-1, keepdims=True) + 0.001)
                rho1 = lax.rsqrt(jnp.sum(c1 * c1, axis=-1, keepdims=True) + 0.001)
                q, k, v = low(c0 * rho0), low(c1 * rho1), low(c2).astype(F32)
                gate = beta[:, head : head + 1]
                o = o_all[:, cols]
                scale = lax.rsqrt(jnp.mean(o * o, axis=-1, keepdims=True) + 0.01)
                dn = don_ref[:, cols]
                weighted = dn * head_gain
                inner = jnp.mean(o * weighted, axis=-1, keepdims=True)
                do = low(scale * weighted - o * (scale * scale * scale) * inner)
                gain_rows = gain_rows + jnp.sum(dn * o * scale, axis=0, keepdims=True)
                u = u_all[:, cols]
                score_t = low(jnp.where(row <= col, dot_nt(k, q), 0.0))
                du = dot_nn(score_t, do)
                ds = low(jnp.where(row >= col, dot_nt(do, u), 0.0))
                ds_t = low(jnp.where(row <= col, dot_nt(u, do), 0.0))
                dq = dot_nn(ds, k)
                dk = dot_nn(ds_t, q)
                blocks = [(t[0, head, index], t[1, head, index]) for index in range(2)]
                r = solve_back(blocks, k, gate, du)
                dv = gate * r
                dv_low = low(dv)
                gram = low(jnp.where(row > col, dot_nt(k, k), 0.0))
                w = v - dot_nn(gram, u)
                dbeta = jnp.sum(r * w, axis=-1, keepdims=True)
                dgram = jnp.where(row > col, dot_nt(dv_low, u), 0.0) + jnp.where(
                    row < col, dot_nt(u, dv_low), 0.0
                )
                dk = dk - dot_nn(low(dgram), k)
                grads[0, :, cols] = rho0 * dq - c0 * (rho0 * rho0 * rho0) * jnp.sum(
                    c0 * dq, axis=-1, keepdims=True
                )
                grads[1, :, cols] = rho1 * dk - c1 * (rho1 * rho1 * rho1) * jnp.sum(
                    c1 * dk, axis=-1, keepdims=True
                )
                grads[2, :, cols] = dv
                dlogit = dlogit + jnp.where(lane == head, dbeta * gate * (1.0 - gate), 0.0)
                if head % 2:
                    serve()
            base = 16 * level
            small[base : base + 1, SIDE : SIDE + DK] = gain_rows
            for index in range(3):
                taps = taps_ref[level, index].astype(F32)
                total, gate, _ = convs[index]
                dsum = grads[index] * (gate * (1.0 + total * (1.0 - gate)))
                project = p[index]
                dproject = taps[KCONV - 1 : KCONV, :] * dsum
                for tap in range(KCONV):
                    back = KCONV - 1 - tap
                    line = base + index * KCONV + tap
                    small[line : line + 1, :chans] = jnp.sum(
                        dsum * shift_down(project, back), axis=0, keepdims=True
                    )
                    if back:
                        dproject = dproject + taps[tap : tap + 1, :] * shift_up(dsum, back)
                dp[index] = low(dproject)
            dlogit_low = low(dlogit)
            wb[...] = jnp.zeros_like(wb)
            wb[:heads] = wb_ref[level]
            loads["wq"].wait()
            for part, rows in parts:
                dn1 = dot_nn(dlogit_low[rows], wb[...])
                for index in range(3):
                    dn1 = dn1 + dot_nt(dp[index, rows], wq[index])
                exchange.give(spot + 1, part, rows, low(dn1))
            send_dp = to_peer("dp", level, dp.at[:, :, other_half(half_chans)])
            send_dp.start()
            serve()
            loads["n1"].wait()
            loads["on"].wait()
            line = base + 3 * KCONV
            small[line : line + heads, :] = dot_tn(dlogit_low, n1[...])[:heads, :]
            for name in ("em", "on", "n1", "dp"):
                to_peer(name, level, peers[name].at[level]).wait_recv()
            own[4 * level + OUT][...] = low(
                dot_tn(on[...], em[:, own_half(half_width)])
                + dot_tn(peers["on"][level], peers["em"][level])
            )
            fold.begin(4 * level + OUT)
            serve()
            for index in range(3):
                own[4 * level + QKV][index * width : (index + 1) * width] = low(
                    dot_tn(n1[...], dp[index, :, own_half(half_chans)])
                    + dot_tn(peers["n1"][level], peers["dp"][level, index])
                )
            fold.begin(4 * level + QKV)
            serve(3)
            send_em.wait_send()
            send_dp.wait_send()

        pl.run_scoped(
            scope,
            pltpu.VMEM((3, width, chans), BF16),
            pltpu.VMEM((chans, width), BF16),
            pltpu.VMEM((length, width), BF16),
            pltpu.VMEM((3, length, chans), F32),
            pltpu.VMEM((length, LANES), F32),
            pltpu.VMEM((2, heads, 2, length // 2, length // 2), BF16),
            pltpu.VMEM((length, chans), BF16),
            pltpu.VMEM((length, chans), F32),
            pltpu.VMEM((length, chans), BF16),
            pltpu.VMEM((length, width), F32),
            pltpu.VMEM((3, length, chans), F32),
            pltpu.VMEM((3, length, chans), BF16),
            pltpu.VMEM((length, width), BF16),
        )

    for level in reversed(range(LAYERS)):
        mlp_stage(level)
        mixer_stage(level)

    for level in range(LAYERS):
        gains[exchange.me, level : level + 1] = small[
            16 * level : 16 * level + 1, SIDE : SIDE + DK
        ]
    gain_copies = [
        remote(
            gains.at[exchange.me],
            gains.at[exchange.me],
            gain_sems.at[0, away],
            gain_sems.at[1, away],
            device,
        )
        for away, device in enumerate(exchange.others)
    ]
    for copy in gain_copies:
        copy.start()

    def last_scope(hid):
        load = pltpu.make_async_copy(kept["x"].at[0], hid, load_sems.at[0, 0, 7])
        load.start()
        serve(3)
        load.wait()
        for part, rows in parts:
            in_grad_ref[rows] = low(norm_step(0, 0, 2 * LAYERS, part, rows, hid[rows]))

    pl.run_scoped(last_scope, pltpu.VMEM((length, width), F32))

    for copy in gain_copies:
        copy.wait()
    for level in range(LAYERS):
        total = gains[0, level : level + 1]
        for index in range(1, exchange.count):
            total = total + gains[index, level : level + 1]
        small[16 * level : 16 * level + 1, SIDE : SIDE + DK] = total

    def small_half(which):
        return small.at[pl.ds(pl.multiple_of(which * 16, 16), 16)]

    send_small = remote(
        small_half(1 - core),
        small_peer,
        load_sems.at[1, 0, 6],
        load_sems.at[1, 0, 7],
        fold.partner,
    )
    send_small.start()
    serve()
    send_small.wait_recv()
    own[SMALL][...] = small_half(core)[...] + small_peer[...]
    fold.begin(SMALL)
    while fold.active:
        serve()
    send_small.wait_send()
    for copy in early:
        copy.wait_send()
    exchange.finish()


def backward(cot, part, saved, norm_gain, taps, head_gain, wb, wq, wo, wgu, wd):
    length, width = cot.shape
    chans, hidden = wq.shape[-1], wgu.shape[-1]
    heads = chans // DK
    n_tensor = lax.axis_size("tensor")
    cuts = fold_cuts(lax.axis_size("dp"), width, chans, hidden)
    n_parts = 2
    sds = jax.ShapeDtypeStruct
    vmem = pl.BlockSpec(memory_space=pltpu.VMEM)
    hbm = pl.BlockSpec(memory_space=pl.ANY)
    own, slots = [], []
    for index, (kind, first, second, cols) in enumerate(cuts):
        dtype = F32 if kind == "small" else BF16
        own.append(
            pltpu.VMEM((16, cols * CHUNKS), dtype)
            if kind == "small"
            else pltpu.VMEM(((first + second) * CHUNKS, cols), dtype)
        )
        if index < 4 or index == SMALL:
            slots.append(pltpu.VMEM((3, STEPS, first, cols), dtype))
            slots.append(pltpu.VMEM((4, STEPS, second, cols), dtype))
    peers = dict(
        z=(length, hidden),
        n2=(length, width),
        ef=(length, width // 2),
        dgu=(length, hidden),
        n1=(length, width),
        on=(length, chans),
        em=(length, width // 2),
        dp=(3, length, chans // 2),
    )
    spots = 2 * LAYERS + 1
    return pl.pallas_call(
        functools.partial(backward_kernel, n_parts, cuts),
        out_shape=(
            sds((length, width), BF16),
            sds((length, width), BF16),
            sds((LAYERS, hidden, width), BF16),
            sds((LAYERS, 2, width, hidden), BF16),
            sds((LAYERS, chans, width), BF16),
            sds((LAYERS, 3 * width, chans), BF16),
            sds((16 * LAYERS, width), F32),
        ),
        in_specs=[vmem] * 5 + [hbm] * (5 + len(KEPT)),
        out_specs=(vmem, vmem) + (hbm,) * 5,
        scratch_shapes=[
            *own,
            *slots,
            *(pltpu.VMEM((LAYERS, *peers[name]), BF16) for name in PEERS),
            pltpu.VMEM((length, width), F32),
            pltpu.VMEM((16 * LAYERS, width), F32),
            pltpu.VMEM((16, width), F32),
            pltpu.VMEM((spots, n_tensor, length, width), BF16),
            pltpu.VMEM((length, chans), F32),
            pltpu.VMEM((LANES, width), BF16),
            pltpu.VMEM((n_tensor, 8, DK), F32),
            pltpu.SemaphoreType.DMA((LAYERS, 2, 10)),
            pltpu.SemaphoreType.DMA((spots, n_parts, n_tensor - 1)),
            pltpu.SemaphoreType.DMA((spots, n_parts, n_tensor - 1)),
            pltpu.SemaphoreType.DMA((2, len(PEERS), LAYERS)),
            pltpu.SemaphoreType.DMA((2, n_tensor - 1)),
            pltpu.SemaphoreType.DMA((len(KINDS), len(cuts), STEPS)),
            pltpu.SemaphoreType.DMA((len(KINDS), len(cuts), STEPS)),
        ],
        compiler_params=pltpu.CompilerParams(
            vmem_limit_bytes=VMEM_LIMIT, collective_id=0, has_side_effects=True
        ),
        name="backward",
    )(cot, norm_gain, taps, head_gain, wb, part, wq, wo, wgu, wd, *(saved[name] for name in KEPT))


def staged_backward(cot, part, saved, norm_gain, taps, head_gain, wb, wq, wo, wgu, wd):
    total = saved["h"][LAYERS - 1]
    for add in branch_parts(part):
        total = total + add.astype(F32)
    outputs = total.astype(BF16)
    e, hid, adds = cot, saved["x"][LAYERS - 1], ()
    gain_rows = {}
    small = [None] * LAYERS
    big = [None] * LAYERS
    for level in reversed(range(LAYERS)):
        at = {name: saved[name][level] for name in KEPT}
        mlp_kept = tuple(at[name] for name in ("n2", "gu", "z"))
        mixer_kept = tuple(at[name] for name in ("n1", "p", "logits", "t", "u", "o", "on"))
        e, rows, part, grad_down, grad_gate_up = mlp_backward(
            level, e, hid, adds, norm_gain, *mlp_kept, wgu, wd
        )
        gain_rows[level + 1] = rows
        e, part, small[level], grad_qkv, grad_out = mixer_backward(
            level,
            e,
            at["h"],
            branch_parts(part),
            norm_gain,
            taps,
            head_gain,
            wb,
            mixer_kept,
            wq,
            wo,
        )
        hid, adds = at["x"], branch_parts(part)
        big[level] = (grad_down, grad_gate_up, grad_out, grad_qkv)
    branch = adds[0].astype(F32)
    for add in adds[1:]:
        branch = branch + add.astype(F32)
    grad_hidden, rows = rms_back(hid, norm_gain[0, 0:1].astype(F32), branch)
    gain_rows[0] = rows
    input_grad = (e + grad_hidden).astype(BF16)
    side = rows.shape[-1] - SIDE
    small_all = jnp.concatenate(
        [
            small[level].at[3:5, SIDE:].set(gain_rows[level].reshape(2, side))
            for level in range(LAYERS)
        ]
    )
    gains = small_all.reshape(LAYERS, 16, -1)[:, 0, SIDE : SIDE + DK]
    gains = sum(branch_parts(gains))
    for level in range(LAYERS):
        small_all = small_all.at[16 * level, SIDE : SIDE + DK].set(gains[level])
    tables = [table for group in big for table in group]
    sums = sum_over_dp(tables)
    stacked = [jnp.stack([sums[index], sums[4 + index]]) for index in range(4)]
    return (outputs, input_grad, *stacked, lax.psum(small_all, "dp"))


def widen_kernel(heads, chans, chunks, *refs):
    count = len(chunks)
    refs = list(refs)

    def taken(number):
        group = refs[:number]
        del refs[:number]
        return group

    sources, (small, *passed) = taken(count), taken(3)
    targets, (conv_out, beta_out, norm_out, gain_out) = taken(count), taken(4)
    passed_out, came, made = taken(2), taken(count), taken(count)
    through = taken(2)
    came_sems, made_sems, passed_sems = taken(3)
    order = []
    for index, rows in enumerate(chunks):
        steps = sources[index].shape[0] // rows
        order += [(index, step, pl.ds(step * rows, rows)) for step in range(steps)]
    loads = [
        pltpu.make_async_copy(
            sources[index].at[rows], came[index].at[rows], came_sems.at[index, step]
        )
        for index, step, rows in order
    ]
    for load in loads:
        load.start()
    passes = [
        [
            pltpu.make_async_copy(passed[index], through[index], passed_sems.at[0, index]),
            pltpu.make_async_copy(through[index], passed_out[index], passed_sems.at[1, index]),
        ]
        for index in range(2)
    ]
    for load, _ in passes:
        load.start()
    for level in range(LAYERS):
        base = 16 * level
        for index in range(3):
            line = base + index * KCONV
            conv_out[level, index] = small[line : line + KCONV, :chans]
        beta_out[level] = small[base + 3 * KCONV : base + 3 * KCONV + heads, :]
        half = norm_out.shape[-1] // 2
        for which, line in ((0, 3), (1, 1)):
            for index in range(2):
                spot = base + line + index
                norm_out[level, which : which + 1, index * half : (index + 1) * half] = small[
                    spot : spot + 1, SIDE : SIDE + half
                ]
        gain_out[level : level + 1] = small[base : base + 1, SIDE : SIDE + DK]
    stores = {}
    for (index, step, rows), load in zip(order, loads):
        slot = step % SLOTS_OUT
        if step >= SLOTS_OUT:
            stores[(index, slot)].wait()
        load.wait()
        made[index][slot] = came[index][rows].astype(F32)
        store = pltpu.make_async_copy(
            made[index].at[slot], targets[index].at[rows], made_sems.at[index, slot]
        )
        store.start()
        stores[(index, slot)] = store
    for load, store in passes:
        load.wait()
        store.start()
    for store in (*stores.values(), passes[0][1], passes[1][1]):
        store.wait()


SLOTS_OUT = 4


def widen(tables, small, heads, chans, passed):
    views = [table.reshape(-1, table.shape[-1]) for table in tables]
    chunks = []
    for view in views:
        rows, cols = view.shape
        steps = 1
        while rows % (32 * steps) == 0 and rows // steps * cols > 400000:
            steps *= 2
        chunks.append(rows // steps)
    most = max(view.shape[0] // rows for view, rows in zip(views, chunks))
    width = small.shape[-1]
    sds = jax.ShapeDtypeStruct
    vmem = pl.BlockSpec(memory_space=pltpu.VMEM)
    hbm = pl.BlockSpec(memory_space=pl.ANY)
    count = len(views)
    moved = sum(6 * view.size for view in views)
    results = pl.pallas_call(
        functools.partial(widen_kernel, heads, chans, tuple(chunks)),
        out_shape=(
            *(sds(view.shape, F32) for view in views),
            sds((LAYERS, 3, KCONV, chans), F32),
            sds((LAYERS, heads, width), F32),
            sds((LAYERS, 2, 2 * (width - SIDE)), F32),
            sds((LAYERS, DK), F32),
            *(sds(array.shape, array.dtype) for array in passed),
        ),
        in_specs=[hbm] * count + [vmem, hbm, hbm],
        out_specs=(hbm,) * count + (vmem,) * 4 + (hbm, hbm),
        scratch_shapes=[
            *(pltpu.VMEM(view.shape, view.dtype) for view in views),
            *(
                pltpu.VMEM((SLOTS_OUT, rows, view.shape[1]), F32)
                for view, rows in zip(views, chunks)
            ),
            *(pltpu.VMEM(array.shape, array.dtype) for array in passed),
            pltpu.SemaphoreType.DMA((count, most)),
            pltpu.SemaphoreType.DMA((count, SLOTS_OUT)),
            pltpu.SemaphoreType.DMA((2, 2)),
        ],
        compiler_params=pltpu.CompilerParams(vmem_limit_bytes=VMEM_LIMIT),
        cost_estimate=pl.CostEstimate(flops=0, bytes_accessed=moved, transcendentals=0),
        name="widen",
    )(*views, small, *passed)
    return (list(results[:count]), *results[count:])


def body(
    inputs,
    qkv_weight,
    conv_taps,
    beta_weight,
    out_gain,
    out_weight,
    norm_gain,
    gate_up_weight,
    down_weight,
    cotangent,
):
    heads = beta_weight.shape[-1]
    wb = jnp.swapaxes(beta_weight, 1, 2)
    saved, part = forward(
        inputs,
        norm_gain,
        conv_taps,
        out_gain,
        wb,
        qkv_weight,
        out_weight,
        gate_up_weight,
        down_weight,
    )
    length, width = inputs.shape
    chans, hidden = conv_taps.shape[-1], down_weight.shape[1]
    if fold_cuts(lax.axis_size("dp"), width, chans, hidden) is not None:
        outputs, input_grad, *big, small_all = backward(
            cotangent,
            part,
            saved,
            norm_gain,
            conv_taps,
            out_gain,
            wb,
            qkv_weight,
            out_weight,
            gate_up_weight,
            down_weight,
        )
    else:
        outputs, input_grad, *big, small_all = staged_backward(
            cotangent,
            part,
            saved,
            norm_gain,
            conv_taps,
            out_gain,
            wb,
            qkv_weight,
            out_weight,
            gate_up_weight,
            down_weight,
        )
    shapes = (down_weight.shape, gate_up_weight.shape, out_weight.shape, qkv_weight.shape)
    big, grad_conv, grad_beta, grad_norm, grad_out_gain, outputs, input_grad = widen(
        big, small_all, heads, chans, (outputs, input_grad)
    )
    grad_down, grad_gate_up, grad_out, grad_qkv = (
        table.reshape(shape) for table, shape in zip(big, shapes)
    )
    grad_beta = jnp.swapaxes(grad_beta, 1, 2)
    return (
        outputs,
        input_grad,
        grad_qkv,
        grad_conv,
        grad_beta,
        grad_out_gain,
        grad_out,
        grad_norm,
        grad_gate_up,
        grad_down,
    )


def solution(mesh):
    in_specs = (
        P("dp", None),
        P(None, None, None, "tensor"),
        P(None, None, None, "tensor"),
        P(None, None, "tensor"),
        P(),
        P(None, "tensor", None),
        P(),
        P(None, None, None, "tensor"),
        P(None, "tensor", None),
        P("dp", None),
    )
    out_specs = (
        P("dp", None),
        P("dp", None),
        P(None, None, None, "tensor"),
        P(None, None, None, "tensor"),
        P(None, None, "tensor"),
        P(),
        P(None, "tensor", None),
        P(),
        P(None, None, None, "tensor"),
        P(None, "tensor", None),
    )
    return jax.shard_map(body, mesh=mesh, in_specs=in_specs, out_specs=out_specs, check_vma=False)
```
